256 devices in a mesh: lon: 16 (over z, y_lo), lat: 8 (over x, y_hi), lev: 2 (over core).
Axes of the slice: x: 4, y: 4 (y_hi: 2, y_lo: 2; y = y_hi * 2 + y_lo), z: 8, core: 2. Of those that a mesh axis runs over, the one named last changes fastest.
Arguments:
- adjoint_in: float32 [9, 16, 128, 2048], P(None, 'lev', 'lat', 'lon'), may hold values from -6 to 6
- trajectory: bfloat16 [3, 9, 16, 128, 2048], P(None, None, 'lev', 'lat', 'lon'), may hold values from 0.5 to 2
- courant: float32 [2, 16, 128, 2048], P(None, 'lev', 'lat', 'lon'), may hold values from -0.4 to 0.4
- mixing: float32 [16, 128, 2048], P('lev', 'lat', 'lon'), may hold values from 0.02 to 0.2
- coag_rates: float32 [6, 16], replicated, may hold values from 0.02 to 0.2
- settle_speed: float32 [8, 9], replicated, may hold values from 0.01 to 0.2
- settle_class: int32 [16], replicated, may hold values from 0 to 7
- emis_profile: float32 [16], replicated, may hold values from 0.1 to 1
- emis_coef: float32 [9], replicated, may hold values from 0.5 to 2
- land_mask: int32 [128, 2048], P('lat', 'lon'), may hold values 0 or 1
- source_mask: int32 [128, 2048], P('lat', 'lon'), may hold values 0 or 1
Outputs:
- adjoint_out: float32 [9, 16, 128, 2048], P(None, 'lev', 'lat', 'lon')
- emis_grad: float32 [3, 128, 2048], P(None, 'lat', 'lon')
The draws below stay inside these ranges and needn't reach their ends.
All inputs are finite; a program needn't handle non-finite values. No bound on the sum of `land_mask` or of `source_mask` on one device may be relied on, other than what follows from the above.
Results may differ from the reference program's by a relative error of at most 0.0003.
Values may be sent and summed in bfloat16 or wider, within the bound.
A program may use at most 64 MiB of HBM per device.

```python
import math
import jax
import jax.numpy as jnp
from jax import lax

MODES = 3
TRACERS = 9
NCLASS = 8
STEPS = 3
NX = 2048
NY = 128
NLEV = 16


def place_ends(result, key, least, largest):
    extent = result.shape
    index_at = [jax.random.randint(jax.random.fold_in(key, axis), (), 0, extent[axis]) for axis in range(len(extent))]
    result = result.at[tuple(index_at)].set(least)
    longest = extent.index(max(extent))
    index_at[longest] = (index_at[longest] + 1) % extent[longest]
    return result.at[tuple(index_at)].set(largest)


def block_levels(own_key, shape, cuts, smallest, largest):
    def one(dim, blocks):
        heights = jax.random.uniform(jax.random.fold_in(jax.random.fold_in(own_key, 6), dim), (blocks,), jnp.float32, smallest / len(cuts), largest / len(cuts))
        return jnp.repeat(jnp.exp(heights), shape[dim] // blocks).reshape((-1,) + (1,) * (len(shape) - dim - 1))

    level = one(*cuts[0])
    for cut in cuts[1:]:
        level = level * one(*cut)
    return level


def scatter_about(own_key, shape, scale, most, split=(), kind=jnp.bfloat16):
    values = jax.random.normal(own_key, shape, jnp.float32) * scale
    if len(split) > 0:
        values = block_levels(own_key, shape, split, -0.22, 0.18) * values
    return jnp.clip(values, min=-most, max=most).astype(kind)


def setup_inputs(seed: int = 0) -> dict:
    keys = jax.random.split(jax.random.key(seed), 12)
    return {
        "adjoint_in": scatter_about(keys[0], (TRACERS, NLEV, NY, NX), 1.0, 6.0, ((1, 2), (2, 8), (3, 16)), jnp.float32),
        "trajectory": jnp.clip(0.5 + 1.5 * jax.random.uniform(keys[1], (STEPS, TRACERS, NLEV, NY, NX), jnp.float32) ** block_levels(keys[1], (STEPS, TRACERS, NLEV, NY, NX), ((2, 2), (3, 8), (4, 16)), -0.2, 0.2), 0.5, 2.0).astype(jnp.bfloat16),
        "courant": jnp.clip(jax.random.uniform(keys[2], (2, NLEV, NY, NX), jnp.float32, -0.4, 0.4) * block_levels(keys[2], (2, NLEV, NY, NX), ((1, 2), (2, 8), (3, 16)), -0.4, 0.0), -0.4, 0.4),
        "mixing": jnp.clip(jnp.exp(math.log(0.2) - 2.3025851 * jax.random.uniform(keys[3], (NLEV, NY, NX), jnp.float32) ** block_levels(keys[3], (NLEV, NY, NX), ((0, 2), (1, 8), (2, 16)), -0.2, 0.2)), 0.02, 0.2),
        "coag_rates": jnp.clip(jnp.exp(jax.random.uniform(keys[4], (6, NLEV), jnp.float32, math.log(0.02), math.log(0.2))), 0.02, 0.2),
        "settle_speed": jnp.clip(jnp.exp(jax.random.uniform(keys[5], (NCLASS, TRACERS), jnp.float32, math.log(0.01), math.log(0.2))), 0.01, 0.2),
        "settle_class": place_ends(jax.random.randint(keys[6], (NLEV,), 0, NCLASS), jax.random.fold_in(keys[6], 1), 0, NCLASS - 1).astype(jnp.int32),
        "emis_profile": jnp.clip(jnp.exp(jax.random.uniform(keys[7], (NLEV,), jnp.float32, math.log(0.1), math.log(1.0))), 0.1, 1.0),
        "emis_coef": jnp.clip(jax.random.uniform(keys[8], (TRACERS,), jnp.float32, 0.5, 2.0), 0.5, 2.0),
        "land_mask": place_ends((jax.random.randint(keys[9], (NY, NX), 0, 2) < 1).astype(jnp.int32), jax.random.fold_in(keys[9], 1), 0, 1),
        "source_mask": place_ends((jax.random.randint(keys[10], (NY, NX), 0, 3) < 1).astype(jnp.int32), jax.random.fold_in(keys[10], 1), 0, 1),
    }


def slab(field, axis, start, length):
    return lax.slice_in_dim(field, start, start + length, axis=axis)

def transport(padded, courant_pad, axis, length):
    courant_wide = courant_pad[None]
    diff_face = slab(padded, axis, 0, length + 3) - slab(padded, axis, 1, length + 3)
    face_speed = slab(courant_wide, axis, 0, length + 3)
    forward_part = jnp.maximum(face_speed, 0.0) * diff_face
    backward_part = jnp.minimum(face_speed, 0.0) * diff_face
    return -1.5 * slab(forward_part, axis, 2, length) + 0.5 * slab(forward_part, axis, 3, length) - 1.5 * slab(backward_part, axis, 1, length) + 0.5 * slab(backward_part, axis, 0, length)

def vertical(padded, mixing_pad, speeds, deposit):
    depth_count = padded.shape[1] - 2
    mixing_below = mixing_pad[:depth_count]
    mixing_above = mixing_pad[1:depth_count + 1]
    speed_level = speeds[:, :, None, None]
    centre = padded[:, 1:depth_count + 1]
    return centre * (1.0 - mixing_above - mixing_below - speed_level - deposit) + padded[:, :depth_count] * (mixing_below + speed_level) + padded[:, 2:] * mixing_above

def coag_increment(state, rates):
    rate_grid = rates[:, :, None, None]
    number = [state[0], state[3], state[6]]
    volume = [state[1], state[4], state[7]]
    moment_six = [state[2], state[5], state[8]]
    pair_rate = {(0, 1): rate_grid[3], (0, 2): rate_grid[4], (1, 2): rate_grid[5]}
    outputs = []
    for mode_index in range(3):
        d_number = -rate_grid[mode_index] * number[mode_index] * number[mode_index]
        d_volume = jnp.zeros_like(number[mode_index])
        d_moment = rate_grid[mode_index] * volume[mode_index] * volume[mode_index]
        for other_mode in range(3):
            if other_mode > mode_index:
                pair = pair_rate[mode_index, other_mode]
                d_number = d_number - pair * number[mode_index] * number[other_mode]
                d_volume = d_volume - pair * volume[mode_index] * number[other_mode]
                d_moment = d_moment - pair * moment_six[mode_index] * number[other_mode]
            if other_mode < mode_index:
                pair = pair_rate[other_mode, mode_index]
                d_volume = d_volume + pair * volume[other_mode] * number[mode_index]
                d_moment = d_moment + pair * (moment_six[other_mode] * number[mode_index] + 2.0 * volume[other_mode] * volume[mode_index])
        outputs.extend([d_number, d_volume, d_moment])
    return jnp.stack(outputs)

def coag_adjoint(adjoint, state, rates):
    primal_out, pullback = jax.vjp(lambda value: coag_increment(value, rates), state)
    return adjoint + pullback(adjoint)[0]

def emission_part(adjoint, profile, emis_coef, source):
    weighted = adjoint * (emis_coef[:, None, None, None] * profile[None, :, None, None])
    per_tracer = lax.optimization_barrier(jnp.sum(weighted, axis=1))
    per_mode = lax.optimization_barrier(jnp.sum(per_tracer.reshape(3, 3, per_tracer.shape[1], per_tracer.shape[2]), axis=1))
    return per_mode * source

def reference(adjoint_in, trajectory, courant, mixing, coag_rates, settle_speed, settle_class, emis_profile, emis_coef, land_mask, source_mask):
    east = courant[0]
    north = courant[1].at[:, -1, :].set(0.0)
    mixing_top = mixing.at[-1].set(0.0)
    choose = (settle_class[:, None] == jnp.arange(NCLASS, dtype=jnp.int32)[None, :]).astype(jnp.float32)
    speeds = jnp.dot(choose, settle_speed, precision=lax.Precision.HIGHEST).T
    surface = (jnp.arange(NLEV, dtype=jnp.int32) == 0).astype(jnp.float32)
    deposit = (0.1 + 0.3 * land_mask.astype(jnp.float32))[None] * surface[:, None, None]
    source = source_mask.astype(jnp.float32)
    mixing_pad = jnp.pad(mixing_top, ((1, 1), (0, 0), (0, 0)))
    east_pad = jnp.pad(east, ((0, 0), (0, 0), (2, 2)), mode='wrap')
    north_pad = jnp.pad(north, ((0, 0), (2, 2), (0, 0)))
    adjoint = adjoint_in
    emis_grad = jnp.zeros((MODES, NY, NX), jnp.float32)
    for step_index in range(STEPS - 1, -1, -1):
        emis_grad = emis_grad + emission_part(adjoint, emis_profile, emis_coef, source)
        adjoint = coag_adjoint(adjoint, trajectory[step_index].astype(jnp.float32), coag_rates)
        level_pad = jnp.pad(adjoint, ((0, 0), (1, 1), (0, 0), (0, 0)))
        adjoint = vertical(level_pad, mixing_pad, speeds, deposit)
        lon_pad = jnp.pad(adjoint, ((0, 0), (0, 0), (0, 0), (2, 2)), mode='wrap')
        lat_pad = jnp.pad(adjoint, ((0, 0), (0, 0), (2, 2), (0, 0)))
        adjoint = adjoint + transport(lon_pad, east_pad, 3, NX) + transport(lat_pad, north_pad, 2, NY)
    return (adjoint, emis_grad)
```

```python
import functools

import jax
import jax.numpy as jnp
from jax import lax
from jax.experimental import pallas as pl
from jax.experimental.pallas import tpu as pltpu
from jax.sharding import PartitionSpec as P

MESH = pl.DeviceIdType.MESH
PAD = 8


def with_halo(cells, axis, dim, lo, hi, closed):
    count = lax.axis_size(axis)
    ends = count if closed else count - 1
    parts = []
    if lo:
        tail = lax.slice_in_dim(cells, cells.shape[dim] - lo, cells.shape[dim], axis=dim)
        parts.append(lax.ppermute(tail, axis, [(i, (i + 1) % count) for i in range(ends)]))
    parts.append(cells)
    if hi:
        head = lax.slice_in_dim(cells, 0, hi, axis=dim)
        parts.append(lax.ppermute(head, axis, [((i + 1) % count, i) for i in range(ends)]))
    return jnp.concatenate(parts, axis=dim)


def face_weights(c_pad, dim, length):
    def at(shift):
        return lax.slice_in_dim(c_pad, 2 + shift, 2 + shift + length, axis=dim)

    return jnp.stack(
        [
            -1.5 * jnp.maximum(at(0), 0.0),
            0.5 * jnp.maximum(at(1), 0.0),
            -1.5 * jnp.minimum(at(-1), 0.0),
            0.5 * jnp.minimum(at(-2), 0.0),
        ]
    )


def kernel(
    adj_ref, traj_ref, cx_ref, cy_ref, vc_ref, src_ref, scal_ref,
    out_ref, emis_ref,
    pad_ref, at_ref, ht_ref, hb_ref, lv_ref, eo_ref, ep_ref, send_sem, recv_sem,
):
    n_t, n_z, n_y, n_x = adj_ref.shape
    steps = traj_ref.shape[0]
    rows = n_z * n_y
    lon = lax.axis_index("lon")
    lat = lax.axis_index("lat")
    lev = lax.axis_index("lev")
    n_lon = lax.axis_size("lon")
    n_lat = lax.axis_size("lat")
    right = lax.rem(lon + 1, n_lon)
    left = lax.rem(lon + n_lon - 1, n_lon)
    has_up = lat < n_lat - 1
    has_down = lat > 0
    up = jnp.minimum(lat + 1, n_lat - 1)
    down = jnp.maximum(lat - 1, 0)
    partner = 1 - lev
    edge_z = jnp.where(lev == 0, n_z - 1, 0)

    zeros_pad = jnp.zeros((n_t, n_z, PAD, n_x), jnp.float32)
    for k in range(steps):
        pad_ref[k, :, :, 0:PAD, :] = zeros_pad
        pad_ref[k, :, :, PAD + n_y : 2 * PAD + n_y, :] = zeros_pad

    barrier = pltpu.get_barrier_semaphore()
    for dev in ((lon, lat, partner), (left, lat, lev), (right, lat, lev)):
        pl.semaphore_signal(barrier, 1, device_id=dev, device_id_type=MESH)

    @pl.when(has_up)
    def _():
        pl.semaphore_signal(barrier, 1, device_id=(lon, up, lev), device_id_type=MESH)

    @pl.when(has_down)
    def _():
        pl.semaphore_signal(barrier, 1, device_id=(lon, down, lev), device_id_type=MESH)

    pl.semaphore_wait(barrier, 3 + has_up.astype(jnp.int32) + has_down.astype(jnp.int32))

    off_rate = 0
    off_speed = 6 * n_z
    off_emis = off_speed + n_t * n_z

    def rcopy(src, dst, idx, dev):
        return pltpu.make_async_remote_copy(
            src, dst, send_sem.at[idx], recv_sem.at[idx], device_id=dev, device_id_type=MESH
        )

    eo_ref[...] = jnp.zeros(eo_ref.shape, jnp.float32)
    src_mask = src_ref[...]
    lane = lax.broadcasted_iota(jnp.int32, (n_y, n_x), 1)

    for k in range(steps - 1, -1, -1):
        cur = adj_ref if k == steps - 1 else out_ref

        def coag_body(z, acc):
            lam = [cur[t, z] for t in range(n_t)]
            st = [traj_ref[k, t, z].astype(jnp.float32) for t in range(n_t)]
            new_acc = []
            for m in range(3):
                part = acc[m]
                for j in range(3):
                    part = part + scal_ref[off_emis + (3 * m + j) * n_z + z] * lam[3 * m + j]
                new_acc.append(part)
            kr = [scal_ref[off_rate + i * n_z + z] for i in range(6)]
            k0, k1, k2, k01, k02, k12 = kr
            n0, v0, w0, n1, v1, w1, n2, v2, w2 = st
            ln0, lv0, lw0, ln1, lv1, lw1, ln2, lv2, lw2 = lam
            a01 = k01 * n1
            a02 = k02 * n2
            a12 = k12 * n2
            s0 = a01 + a02
            g_n0 = ln0 * (-2.0 * k0 * n0 - s0)
            g_v0 = (
                (lv1 * a01 + lv2 * a02 - lv0 * s0)
                + 2.0 * (lw0 * (k0 * v0) + lw1 * (k01 * v1) + lw2 * (k02 * v2))
            )
            g_w0 = lw1 * a01 + lw2 * a02 - lw0 * s0
            g_n1 = (
                ln1 * (-2.0 * k1 * n1 - a12)
                - ln0 * (k01 * n0)
                + (lv1 - lv0) * (k01 * v0)
                + (lw1 - lw0) * (k01 * w0)
            )
            g_v1 = (lv2 - lv1) * a12 + 2.0 * (lw1 * (k1 * v1 + k01 * v0) + lw2 * (k12 * v2))
            g_w1 = (lw2 - lw1) * a12
            g_n2 = (
                -2.0 * k2 * n2 * ln2
                - ln0 * (k02 * n0)
                - ln1 * (k12 * n1)
                + (lv2 - lv0) * (k02 * v0)
                + (lv2 - lv1) * (k12 * v1)
                + (lw2 - lw0) * (k02 * w0)
                + (lw2 - lw1) * (k12 * w1)
            )
            g_v2 = 2.0 * lw2 * (k2 * v2 + k02 * v0 + k12 * v1)
            grads = [g_n0, g_v0, g_w0, g_n1, g_v1, g_w1, g_n2, g_v2, None]
            for t in range(n_t):
                if grads[t] is None:
                    out_ref[t, z] = lam[t]
                else:
                    out_ref[t, z] = lam[t] + grads[t]
            return tuple(new_acc)

        zero = jnp.zeros((n_y, n_x), jnp.float32)
        acc = lax.fori_loop(0, n_z, coag_body, (zero, zero, zero))
        for m in range(3):
            eo_ref[m] = eo_ref[m] + acc[m] * src_mask

        lev_copy = rcopy(
            out_ref.at[:, pl.ds(edge_z, 1)], lv_ref.at[k], k, (lon, lat, partner)
        )
        lev_copy.start()
        lev_copy.wait()

        below_ok = lev == 1
        above_ok = lev == 0

        def vert_body(i, carry):
            t = i // n_z
            z = i % n_z
            a = out_ref[t, z]
            halo = lv_ref[k, t, 0]
            a_below = jnp.where(z > 0, out_ref[t, jnp.maximum(z - 1, 0)], jnp.where(below_ok, halo, 0.0))
            a_above = jnp.where(z < n_z - 1, out_ref[t, jnp.minimum(z + 1, n_z - 1)], jnp.where(above_ok, halo, 0.0))
            s = scal_ref[off_speed + t * n_z + z]
            m_above = vc_ref[0, z]
            m_below = vc_ref[1, z]
            base = vc_ref[2, z]
            pad_ref[k, t, z, PAD : PAD + n_y, :] = (
                a * (base - s) + a_below * (m_below + s) + a_above * m_above
            )
            return carry

        lax.fori_loop(0, n_t * n_z, vert_body, 0)

        lat_up = rcopy(
            pad_ref.at[k, :, :, pl.ds(PAD + n_y - 2, 2), :],
            pad_ref.at[k, :, :, pl.ds(PAD - 2, 2), :],
            3 + k,
            (lon, up, lev),
        )
        lat_down = rcopy(
            pad_ref.at[k, :, :, pl.ds(PAD, 2), :],
            pad_ref.at[k, :, :, pl.ds(PAD + n_y, 2), :],
            6 + k,
            (lon, down, lev),
        )

        @pl.when(has_up)
        def _():
            lat_up.start()

        @pl.when(has_down)
        def _():
            lat_down.start()

        for t in range(n_t):
            blk = pad_ref[k, t, :, PAD : PAD + n_y, :].reshape(rows, n_x)
            at_ref[k, :, t * rows : (t + 1) * rows] = blk.T
        lon_right = rcopy(
            at_ref.at[k, pl.ds(n_x - 2, 2), :], ht_ref.at[k, pl.ds(n_x - 2, 2), :], 9 + k, (right, lat, lev)
        )
        lon_left = rcopy(
            at_ref.at[k, pl.ds(0, 2), :], ht_ref.at[k, pl.ds(0, 2), :], 12 + k, (left, lat, lev)
        )
        lon_right.start()
        lon_left.start()
        lon_right.wait()
        lon_left.wait()

        @pl.when(has_up)
        def _():
            lat_up.wait_send()
            lat_down.wait_recv()

        @pl.when(has_down)
        def _():
            lat_down.wait_send()
            lat_up.wait_recv()

        for t in range(n_t):
            hb_ref[t] = ht_ref[k, :, t * rows : (t + 1) * rows].T.reshape(n_z, n_y, n_x)

        def tr_body(i, carry):
            t = i // n_z
            z = i % n_z
            a = pad_ref[k, t, z, PAD : PAD + n_y, :]
            hz = hb_ref[t, z]
            y_p1 = pad_ref[k, t, z, PAD + 1 : PAD + 1 + n_y, :]
            y_p2 = pad_ref[k, t, z, PAD + 2 : PAD + 2 + n_y, :]
            y_m1 = pad_ref[k, t, z, PAD - 1 : PAD - 1 + n_y, :]
            y_m2 = pad_ref[k, t, z, PAD - 2 : PAD - 2 + n_y, :]
            x_p1 = jnp.where(lane == n_x - 1, pltpu.roll(hz, n_x - 1, 1), pltpu.roll(a, n_x - 1, 1))
            x_p2 = jnp.where(lane >= n_x - 2, pltpu.roll(hz, n_x - 2, 1), pltpu.roll(a, n_x - 2, 1))
            x_m1 = jnp.where(lane == 0, pltpu.roll(hz, 1, 1), pltpu.roll(a, 1, 1))
            x_m2 = jnp.where(lane <= 1, pltpu.roll(hz, 2, 1), pltpu.roll(a, 2, 1))
            lon_part = (
                cx_ref[0, z] * (a - x_p1)
                + cx_ref[1, z] * (x_p1 - x_p2)
                + cx_ref[2, z] * (x_m1 - a)
                + cx_ref[3, z] * (x_m2 - x_m1)
            )
            lat_part = (
                cy_ref[0, z] * (a - y_p1)
                + cy_ref[1, z] * (y_p1 - y_p2)
                + cy_ref[2, z] * (y_m1 - a)
                + cy_ref[3, z] * (y_m2 - y_m1)
            )
            out_ref[t, z] = a + lon_part + lat_part
            return carry

        lax.fori_loop(0, n_t * n_z, tr_body, 0)

    emis_copy = rcopy(eo_ref, ep_ref, 15, (lon, lat, partner))
    emis_copy.start()
    emis_copy.wait()
    emis_ref[...] = eo_ref[...] + ep_ref[...]


def shards(
    adjoint_in,
    trajectory,
    courant,
    mixing,
    coag_rates,
    settle_speed,
    settle_class,
    emis_profile,
    emis_coef,
    land_mask,
    source_mask,
):
    n_t, n_z, n_y, n_x = adjoint_in.shape
    lev_index = lax.axis_index("lev")
    lat_index = lax.axis_index("lat")
    lat_count = lax.axis_size("lat")
    level_total = settle_class.shape[0]
    level_start = lev_index * n_z
    level_global = level_start + jnp.arange(n_z, dtype=jnp.int32)
    row_global = lat_index * n_y + jnp.arange(n_y, dtype=jnp.int32)
    top_row = (row_global == n_y * lat_count - 1)[None, :, None]
    east = courant[0]
    north = jnp.where(top_row, 0.0, courant[1])
    east_pad = with_halo(east, "lon", 2, 2, 1, True)
    north_pad = with_halo(north, "lat", 1, 2, 1, False)
    cx = face_weights(east_pad, 2, n_x)
    cy = face_weights(north_pad, 1, n_y)

    mixing_top = jnp.where((level_global == level_total - 1)[:, None, None], 0.0, mixing)
    mixing_below = with_halo(mixing_top, "lev", 0, 1, 0, False)[:n_z]
    surface = (level_global == 0).astype(jnp.float32)
    deposit = (0.1 + 0.3 * land_mask.astype(jnp.float32))[None] * surface[:, None, None]
    base = 1.0 - mixing_top - mixing_below - deposit
    vc = jnp.stack([mixing_top, mixing_below, base])

    choose = (
        settle_class[:, None] == jnp.arange(settle_speed.shape[0], dtype=jnp.int32)[None, :]
    ).astype(jnp.float32)
    speeds_all = jnp.dot(choose, settle_speed, precision=lax.Precision.HIGHEST).T
    speeds_used = lax.dynamic_slice_in_dim(speeds_all, level_start, n_z, 1)
    rates_own = lax.dynamic_slice_in_dim(coag_rates, level_start, n_z, 1)
    profile_own = lax.dynamic_slice_in_dim(emis_profile, level_start, n_z, 0)
    emis_w = emis_coef[:, None] * profile_own[None, :]
    scal = jnp.concatenate([rates_own.reshape(-1), speeds_used.reshape(-1), emis_w.reshape(-1)])
    source = source_mask.astype(jnp.float32)
    steps = trajectory.shape[0]

    vmem = pl.BlockSpec(memory_space=pltpu.VMEM)
    smem = pl.BlockSpec(memory_space=pltpu.SMEM)
    return pl.pallas_call(
        kernel,
        out_shape=(
            jax.ShapeDtypeStruct(adjoint_in.shape, jnp.float32),
            jax.ShapeDtypeStruct((3, n_y, n_x), jnp.float32),
        ),
        in_specs=[vmem, vmem, vmem, vmem, vmem, vmem, smem],
        out_specs=(vmem, vmem),
        scratch_shapes=[
            pltpu.VMEM((steps, n_t, n_z, n_y + 2 * PAD, n_x), jnp.float32),
            pltpu.VMEM((steps, n_x, n_t * n_z * n_y), jnp.float32),
            pltpu.VMEM((steps, n_x, n_t * n_z * n_y), jnp.float32),
            pltpu.VMEM((n_t, n_z, n_y, n_x), jnp.float32),
            pltpu.VMEM((steps, n_t, 1, n_y, n_x), jnp.float32),
            pltpu.VMEM((3, n_y, n_x), jnp.float32),
            pltpu.VMEM((3, n_y, n_x), jnp.float32),
            pltpu.SemaphoreType.DMA((16,)),
            pltpu.SemaphoreType.DMA((16,)),
        ],
        compiler_params=pltpu.CompilerParams(
            collective_id=0, has_side_effects=True, vmem_limit_bytes=48 * 1024 * 1024
        ),
    )(adjoint_in, trajectory, cx, cy, vc, source, scal)


def solution(mesh):
    return jax.shard_map(
        shards,
        mesh=mesh,
        in_specs=(
            P(None, "lev", "lat", "lon"),
            P(None, None, "lev", "lat", "lon"),
            P(None, "lev", "lat", "lon"),
            P("lev", "lat", "lon"),
            P(),
            P(),
            P(),
            P(),
            P(),
            P("lat", "lon"),
            P("lat", "lon"),
        ),
        out_specs=(P(None, "lev", "lat", "lon"), P(None, "lat", "lon")),
        check_vma=False,
    )
```

```python
import jax
import jax.numpy as jnp
from jax import lax
from jax.experimental import pallas as pl
from jax.experimental.pallas import tpu as pltpu
from jax.sharding import PartitionSpec as P

MESH = pl.DeviceIdType.MESH
PAD = 8

S_LEV, S_UP, S_DOWN, S_RIGHT, S_LEFT = 0, 3, 6, 9, 12
S_EMIS, S_CE_R, S_CE_L, S_CN_U, S_CN_D, S_MIX = 15, 16, 17, 18, 19, 20
N_REMOTE = 21


def kernel(
    adj_hbm, traj_hbm, cour_hbm, mix_hbm, land_ref, srcm_ref,
    rates_ref, speed_ref, sclass_ref, prof_ref, ecoef_ref,
    out_ref, emis_ref,
    traj_ref, cour_ref, mix_ref, pad_ref, at_ref, ht_ref, hb_ref, lv_ref, eo_ref, ep_ref,
    cx_ref, cy_ref, vc_ref, cet_ref, ceh_ref, cyp_ref, mh_ref,
    send_sem, recv_sem, local_sem,
):
    n_t, n_z, n_y, n_x = out_ref.shape
    steps = traj_hbm.shape[0]
    rows = n_z * n_y
    lon = lax.axis_index("lon")
    lat = lax.axis_index("lat")
    lev = lax.axis_index("lev")
    n_lon = lax.axis_size("lon")
    n_lat = lax.axis_size("lat")
    right = lax.rem(lon + 1, n_lon)
    left = lax.rem(lon + n_lon - 1, n_lon)
    has_up = lat < n_lat - 1
    has_down = lat > 0
    up = jnp.minimum(lat + 1, n_lat - 1)
    down = jnp.maximum(lat - 1, 0)
    partner = 1 - lev
    low_half = lev == 0
    edge_z = jnp.where(low_half, n_z - 1, 0)
    inner_z = jnp.where(low_half, n_z - 2, 1)
    level0 = lev * n_z

    adj_in = pltpu.make_async_copy(adj_hbm, out_ref, local_sem.at[0])
    cour_in = pltpu.make_async_copy(cour_hbm, cour_ref, local_sem.at[1])
    mix_in = pltpu.make_async_copy(mix_hbm, mix_ref, local_sem.at[2])
    traj_in = [
        pltpu.make_async_copy(traj_hbm.at[k], traj_ref.at[k], local_sem.at[3 + k]) for k in range(steps)
    ]
    cour_in.start()
    mix_in.start()
    adj_in.start()
    for k in range(steps - 1, -1, -1):
        traj_in[k].start()

    zeros_pad = jnp.zeros((n_t, n_z, PAD, n_x), jnp.float32)
    for k in range(steps):
        pad_ref[k, :, :, 0:PAD, :] = zeros_pad
        pad_ref[k, :, :, PAD + n_y : 2 * PAD + n_y, :] = zeros_pad
    zeros_c = jnp.zeros((n_z, PAD, n_x), jnp.float32)
    cyp_ref[:, 0:PAD, :] = zeros_c
    cyp_ref[:, PAD + n_y : 2 * PAD + n_y, :] = zeros_c

    barrier = pltpu.get_barrier_semaphore()
    for dev in ((lon, lat, partner), (left, lat, lev), (right, lat, lev)):
        pl.semaphore_signal(barrier, 1, device_id=dev, device_id_type=MESH)

    @pl.when(has_up)
    def _():
        pl.semaphore_signal(barrier, 1, device_id=(lon, up, lev), device_id_type=MESH)

    @pl.when(has_down)
    def _():
        pl.semaphore_signal(barrier, 1, device_id=(lon, down, lev), device_id_type=MESH)

    pl.semaphore_wait(barrier, 3 + has_up.astype(jnp.int32) + has_down.astype(jnp.int32))

    def rcopy(src, dst, idx, dev):
        return pltpu.make_async_remote_copy(
            src, dst, send_sem.at[idx], recv_sem.at[idx], device_id=dev, device_id_type=MESH
        )

    lane = lax.broadcasted_iota(jnp.int32, (n_y, n_x), 1)
    row = lax.broadcasted_iota(jnp.int32, (n_y, n_x), 0)

    cour_in.wait()
    mix_in.wait()
    top_row = jnp.logical_and(lat == n_lat - 1, row == n_y - 1)
    for z in range(n_z):
        cyp_ref[z, PAD : PAD + n_y, :] = jnp.where(top_row, 0.0, cour_ref[1, z])
    cet_ref[...] = cour_ref[0].reshape(rows, n_x).T
    ce_right = rcopy(cet_ref.at[pl.ds(n_x - 2, 2), :], ceh_ref.at[pl.ds(n_x - 2, 2), :], S_CE_R, (right, lat, lev))
    ce_left = rcopy(cet_ref.at[pl.ds(0, 2), :], ceh_ref.at[pl.ds(0, 2), :], S_CE_L, (left, lat, lev))
    cn_up = rcopy(
        cyp_ref.at[:, pl.ds(PAD + n_y - 2, 2), :], cyp_ref.at[:, pl.ds(PAD - 2, 2), :], S_CN_U, (lon, up, lev)
    )
    cn_down = rcopy(
        cyp_ref.at[:, pl.ds(PAD, 2), :], cyp_ref.at[:, pl.ds(PAD + n_y, 2), :], S_CN_D, (lon, down, lev)
    )
    mix_x = rcopy(mix_ref.at[pl.ds(edge_z, 1)], mh_ref, S_MIX, (lon, lat, partner))
    mix_x.start()
    ce_right.start()
    ce_left.start()

    @pl.when(has_up)
    def _():
        cn_up.start()

    @pl.when(has_down)
    def _():
        cn_down.start()

    def build_vertical_coefficients():
        mix_x.wait()
        dep = jnp.where(low_half, 0.1 + 0.3 * land_ref[...].astype(jnp.float32), 0.0)
        below = jnp.where(low_half, 0.0, mh_ref[0])
        for z in range(n_z):
            above = mix_ref[z]
            if z == n_z - 1:
                above = jnp.where(low_half, above, 0.0)
            base = 1.0 - above - below
            if z == 0:
                base = base - dep
            vc_ref[0, z] = above
            vc_ref[1, z] = below
            vc_ref[2, z] = base
            below = above

    def build_transport_coefficients():
        ce_right.wait()
        ce_left.wait()

        @pl.when(has_up)
        def _():
            cn_up.wait_send()
            cn_down.wait_recv()

        @pl.when(has_down)
        def _():
            cn_down.wait_send()
            cn_up.wait_recv()

        he = ceh_ref[...].T.reshape(n_z, n_y, n_x)
        for z in range(n_z):
            c = cour_ref[0, z]
            hz = he[z]
            c_p1 = jnp.where(lane == n_x - 1, pltpu.roll(hz, n_x - 1, 1), pltpu.roll(c, n_x - 1, 1))
            c_m1 = jnp.where(lane == 0, pltpu.roll(hz, 1, 1), pltpu.roll(c, 1, 1))
            c_m2 = jnp.where(lane <= 1, pltpu.roll(hz, 2, 1), pltpu.roll(c, 2, 1))
            cx_ref[0, z] = -1.5 * jnp.maximum(c, 0.0)
            cx_ref[1, z] = 0.5 * jnp.maximum(c_p1, 0.0)
            cx_ref[2, z] = -1.5 * jnp.minimum(c_m1, 0.0)
            cx_ref[3, z] = 0.5 * jnp.minimum(c_m2, 0.0)
            cy_ref[0, z] = -1.5 * jnp.maximum(cyp_ref[z, PAD : PAD + n_y, :], 0.0)
            cy_ref[1, z] = 0.5 * jnp.maximum(cyp_ref[z, PAD + 1 : PAD + 1 + n_y, :], 0.0)
            cy_ref[2, z] = -1.5 * jnp.minimum(cyp_ref[z, PAD - 1 : PAD - 1 + n_y, :], 0.0)
            cy_ref[3, z] = 0.5 * jnp.minimum(cyp_ref[z, PAD - 2 : PAD - 2 + n_y, :], 0.0)

    eo_ref[...] = jnp.zeros(eo_ref.shape, jnp.float32)
    src_mask = srcm_ref[...].astype(jnp.float32)
    adj_in.wait()

    for k in range(steps - 1, -1, -1):
        traj_in[k].wait()

        def coag_level(zz, acc):
            z = jnp.where(low_half, n_z - 1 - zz, zz)
            zg = level0 + z
            lam = [out_ref[t, z] for t in range(n_t)]
            st = [traj_ref[k, t, z].astype(jnp.float32) for t in range(n_t)]
            new_acc = []
            for m in range(3):
                part = acc[m]
                for j in range(3):
                    part = part + (ecoef_ref[3 * m + j] * prof_ref[zg]) * lam[3 * m + j]
                new_acc.append(part)
            k0, k1, k2, k01, k02, k12 = [rates_ref[i, zg] for i in range(6)]
            n0, v0, w0, n1, v1, w1, n2, v2, w2 = st
            ln0, lv0, lw0, ln1, lv1, lw1, ln2, lv2, lw2 = lam
            a01 = k01 * n1
            a02 = k02 * n2
            a12 = k12 * n2
            s0 = a01 + a02
            g_n0 = ln0 * (-2.0 * k0 * n0 - s0)
            g_v0 = (
                (lv1 * a01 + lv2 * a02 - lv0 * s0)
                + 2.0 * (lw0 * (k0 * v0) + lw1 * (k01 * v1) + lw2 * (k02 * v2))
            )
            g_w0 = lw1 * a01 + lw2 * a02 - lw0 * s0
            g_n1 = (
                ln1 * (-2.0 * k1 * n1 - a12)
                - ln0 * (k01 * n0)
                + (lv1 - lv0) * (k01 * v0)
                + (lw1 - lw0) * (k01 * w0)
            )
            g_v1 = (lv2 - lv1) * a12 + 2.0 * (lw1 * (k1 * v1 + k01 * v0) + lw2 * (k12 * v2))
            g_w1 = (lw2 - lw1) * a12
            g_n2 = (
                -2.0 * k2 * n2 * ln2
                - ln0 * (k02 * n0)
                - ln1 * (k12 * n1)
                + (lv2 - lv0) * (k02 * v0)
                + (lv2 - lv1) * (k12 * v1)
                + (lw2 - lw0) * (k02 * w0)
                + (lw2 - lw1) * (k12 * w1)
            )
            g_v2 = 2.0 * lw2 * (k2 * v2 + k02 * v0 + k12 * v1)
            grads = [g_n0, g_v0, g_w0, g_n1, g_v1, g_w1, g_n2, g_v2]
            for t in range(n_t - 1):
                out_ref[t, z] = lam[t] + grads[t]
            return tuple(new_acc)

        zero = jnp.zeros((n_y, n_x), jnp.float32)
        acc = coag_level(0, (zero, zero, zero))
        lev_copy = rcopy(out_ref.at[:, pl.ds(edge_z, 1)], lv_ref.at[k], S_LEV + k, (lon, lat, partner))
        lev_copy.start()
        acc = lax.fori_loop(1, n_z, coag_level, acc)
        for m in range(3):
            eo_ref[m] = eo_ref[m] + acc[m] * src_mask

        if k == steps - 1:
            build_vertical_coefficients()

        def vert_inner(i, carry):
            t = i // (n_z - 1)
            z = i % (n_z - 1) + lev
            zg = level0 + z
            s = speed_ref[sclass_ref[zg], t]
            a = out_ref[t, z]
            a_below = jnp.where(z > 0, out_ref[t, jnp.maximum(z - 1, 0)], 0.0)
            a_above = jnp.where(z < n_z - 1, out_ref[t, jnp.minimum(z + 1, n_z - 1)], 0.0)
            pad_ref[k, t, z, PAD : PAD + n_y, :] = (
                a * (vc_ref[2, z] - s) + a_below * (vc_ref[1, z] + s) + a_above * vc_ref[0, z]
            )
            return carry

        lax.fori_loop(0, n_t * (n_z - 1), vert_inner, 0, unroll=7)
        lev_copy.wait()

        def vert_edge(t, carry):
            z = edge_z
            s = speed_ref[sclass_ref[level0 + z], t]
            a = out_ref[t, z]
            other = out_ref[t, inner_z]
            halo = lv_ref[k, t, 0]
            a_below = jnp.where(low_half, other, halo)
            a_above = jnp.where(low_half, halo, other)
            pad_ref[k, t, z, PAD : PAD + n_y, :] = (
                a * (vc_ref[2, z] - s) + a_below * (vc_ref[1, z] + s) + a_above * vc_ref[0, z]
            )
            return carry

        lax.fori_loop(0, n_t, vert_edge, 0, unroll=3)

        lat_up = rcopy(
            pad_ref.at[k, :, :, pl.ds(PAD + n_y - 2, 2), :],
            pad_ref.at[k, :, :, pl.ds(PAD - 2, 2), :],
            S_UP + k,
            (lon, up, lev),
        )
        lat_down = rcopy(
            pad_ref.at[k, :, :, pl.ds(PAD, 2), :],
            pad_ref.at[k, :, :, pl.ds(PAD + n_y, 2), :],
            S_DOWN + k,
            (lon, down, lev),
        )

        @pl.when(has_up)
        def _():
            lat_up.start()

        @pl.when(has_down)
        def _():
            lat_down.start()

        for t in range(n_t):
            blk = pad_ref[k, t, :, PAD : PAD + n_y, :].reshape(rows, n_x)
            at_ref[k, :, t * rows : (t + 1) * rows] = blk.T
        lon_right = rcopy(
            at_ref.at[k, pl.ds(n_x - 2, 2), :], ht_ref.at[k, pl.ds(n_x - 2, 2), :], S_RIGHT + k, (right, lat, lev)
        )
        lon_left = rcopy(
            at_ref.at[k, pl.ds(0, 2), :], ht_ref.at[k, pl.ds(0, 2), :], S_LEFT + k, (left, lat, lev)
        )
        lon_right.start()
        lon_left.start()

        if k == steps - 1:
            build_transport_coefficients()

        lon_right.wait()
        lon_left.wait()

        @pl.when(has_up)
        def _():
            lat_up.wait_send()
            lat_down.wait_recv()

        @pl.when(has_down)
        def _():
            lat_down.wait_send()
            lat_up.wait_recv()

        for t in range(n_t):
            hb_ref[t] = ht_ref[k, :, t * rows : (t + 1) * rows].T.reshape(n_z, n_y, n_x)

        def transport(i, carry):
            t = i // n_z
            z = i % n_z
            a = pad_ref[k, t, z, PAD : PAD + n_y, :]
            hz = hb_ref[t, z]
            y_p1 = pad_ref[k, t, z, PAD + 1 : PAD + 1 + n_y, :]
            y_p2 = pad_ref[k, t, z, PAD + 2 : PAD + 2 + n_y, :]
            y_m1 = pad_ref[k, t, z, PAD - 1 : PAD - 1 + n_y, :]
            y_m2 = pad_ref[k, t, z, PAD - 2 : PAD - 2 + n_y, :]
            x_p1 = jnp.where(lane == n_x - 1, pltpu.roll(hz, n_x - 1, 1), pltpu.roll(a, n_x - 1, 1))
            x_p2 = jnp.where(lane >= n_x - 2, pltpu.roll(hz, n_x - 2, 1), pltpu.roll(a, n_x - 2, 1))
            x_m1 = jnp.where(lane == 0, pltpu.roll(hz, 1, 1), pltpu.roll(a, 1, 1))
            x_m2 = jnp.where(lane <= 1, pltpu.roll(hz, 2, 1), pltpu.roll(a, 2, 1))
            lon_part = (
                cx_ref[0, z] * (a - x_p1)
                + cx_ref[1, z] * (x_p1 - x_p2)
                + cx_ref[2, z] * (x_m1 - a)
                + cx_ref[3, z] * (x_m2 - x_m1)
            )
            lat_part = (
                cy_ref[0, z] * (a - y_p1)
                + cy_ref[1, z] * (y_p1 - y_p2)
                + cy_ref[2, z] * (y_m1 - a)
                + cy_ref[3, z] * (y_m2 - y_m1)
            )
            out_ref[t, z] = a + lon_part + lat_part
            return carry

        lax.fori_loop(0, n_t * n_z, transport, 0, unroll=4)

    emis_copy = rcopy(eo_ref, ep_ref, S_EMIS, (lon, lat, partner))
    emis_copy.start()
    emis_copy.wait()
    emis_ref[...] = eo_ref[...] + ep_ref[...]


def shards(
    adjoint_in,
    trajectory,
    courant,
    mixing,
    coag_rates,
    settle_speed,
    settle_class,
    emis_profile,
    emis_coef,
    land_mask,
    source_mask,
):
    n_t, n_z, n_y, n_x = adjoint_in.shape
    steps = trajectory.shape[0]
    rows = n_z * n_y
    hbm = pl.BlockSpec(memory_space=pl.ANY)
    vmem = pl.BlockSpec(memory_space=pltpu.VMEM)
    smem = pl.BlockSpec(memory_space=pltpu.SMEM)
    f32 = jnp.float32
    return pl.pallas_call(
        kernel,
        out_shape=(
            jax.ShapeDtypeStruct(adjoint_in.shape, f32),
            jax.ShapeDtypeStruct((3, n_y, n_x), f32),
        ),
        in_specs=[hbm, hbm, hbm, hbm, vmem, vmem, smem, smem, smem, smem, smem],
        out_specs=(vmem, vmem),
        scratch_shapes=[
            pltpu.VMEM(trajectory.shape, trajectory.dtype),
            pltpu.VMEM(courant.shape, f32),
            pltpu.VMEM(mixing.shape, f32),
            pltpu.VMEM((steps, n_t, n_z, n_y + 2 * PAD, n_x), f32),
            pltpu.VMEM((steps, n_x, n_t * rows), f32),
            pltpu.VMEM((steps, n_x, n_t * rows), f32),
            pltpu.VMEM((n_t, n_z, n_y, n_x), f32),
            pltpu.VMEM((steps, n_t, 1, n_y, n_x), f32),
            pltpu.VMEM((3, n_y, n_x), f32),
            pltpu.VMEM((3, n_y, n_x), f32),
            pltpu.VMEM((4, n_z, n_y, n_x), f32),
            pltpu.VMEM((4, n_z, n_y, n_x), f32),
            pltpu.VMEM((3, n_z, n_y, n_x), f32),
            pltpu.VMEM((n_x, rows), f32),
            pltpu.VMEM((n_x, rows), f32),
            pltpu.VMEM((n_z, n_y + 2 * PAD, n_x), f32),
            pltpu.VMEM((1, n_y, n_x), f32),
            pltpu.SemaphoreType.DMA((N_REMOTE,)),
            pltpu.SemaphoreType.DMA((N_REMOTE,)),
            pltpu.SemaphoreType.DMA((3 + steps,)),
        ],
        compiler_params=pltpu.CompilerParams(
            collective_id=0, has_side_effects=True, vmem_limit_bytes=48 * 1024 * 1024
        ),
    )(
        adjoint_in, trajectory, courant, mixing, land_mask, source_mask,
        coag_rates, settle_speed, settle_class, emis_profile, emis_coef,
    )


def solution(mesh):
    return jax.shard_map(
        shards,
        mesh=mesh,
        in_specs=(
            P(None, "lev", "lat", "lon"),
            P(None, None, "lev", "lat", "lon"),
            P(None, "lev", "lat", "lon"),
            P("lev", "lat", "lon"),
            P(),
            P(),
            P(),
            P(),
            P(),
            P("lat", "lon"),
            P("lat", "lon"),
        ),
        out_specs=(P(None, "lev", "lat", "lon"), P(None, "lat", "lon")),
        check_vma=False,
    )
```

```python
import jax
import jax.numpy as jnp
from jax import lax
from jax.experimental import pallas as pl
from jax.experimental.pallas import tpu as pltpu
from jax.sharding import PartitionSpec as P

MESH = pl.DeviceIdType.MESH
PAD = 8

S_LEV, S_UP, S_DOWN, S_RIGHT, S_LEFT = 0, 3, 6, 9, 12
S_EMIS, S_CE_R, S_CE_L, S_CN_U, S_CN_D, S_MIX = 15, 16, 17, 18, 19, 20
N_REMOTE = 21


def kernel(
    adj_hbm, traj_hbm, cour_hbm, mix_hbm, land_hbm, srcm_hbm,
    rates_hbm, speed_hbm, sclass_hbm, prof_hbm, ecoef_hbm,
    out_hbm, emis_hbm,
    out_ref, emis_ref, land_ref, srcm_ref, rates_ref, speed_ref, sclass_ref, prof_ref, ecoef_ref,
    traj_ref, cour_ref, mix_ref, pad_ref, at_ref, ht_ref, hb_ref, lv_ref, eo_ref, ep_ref,
    cx_ref, cy_ref, vc_ref, cet_ref, ceh_ref, cyp_ref, mh_ref,
    send_sem, recv_sem, local_sem,
):
    n_t, n_z, n_y, n_x = out_ref.shape
    steps = traj_hbm.shape[0]
    rows = n_z * n_y
    lon = lax.axis_index("lon")
    lat = lax.axis_index("lat")
    lev = lax.axis_index("lev")
    n_lon = lax.axis_size("lon")
    n_lat = lax.axis_size("lat")
    right = lax.rem(lon + 1, n_lon)
    left = lax.rem(lon + n_lon - 1, n_lon)
    has_up = lat < n_lat - 1
    has_down = lat > 0
    up = jnp.minimum(lat + 1, n_lat - 1)
    down = jnp.maximum(lat - 1, 0)
    partner = 1 - lev
    low_half = lev == 0
    edge_z = jnp.where(low_half, n_z - 1, 0)
    inner_z = jnp.where(low_half, n_z - 2, 1)
    level0 = lev * n_z

    adj_in = pltpu.make_async_copy(adj_hbm, out_ref, local_sem.at[0])
    cour_in = pltpu.make_async_copy(cour_hbm, cour_ref, local_sem.at[1])
    mix_in = pltpu.make_async_copy(mix_hbm, mix_ref, local_sem.at[2])
    traj_in = [
        pltpu.make_async_copy(traj_hbm.at[k], traj_ref.at[k], local_sem.at[3 + k]) for k in range(steps)
    ]
    small_in = [
        pltpu.make_async_copy(src, dst, local_sem.at[3 + steps + i])
        for i, (src, dst) in enumerate(
            (
                (rates_hbm, rates_ref),
                (speed_hbm, speed_ref),
                (sclass_hbm, sclass_ref),
                (prof_hbm, prof_ref),
                (ecoef_hbm, ecoef_ref),
                (land_hbm, land_ref),
                (srcm_hbm, srcm_ref),
            )
        )
    ]
    for c in small_in:
        c.start()
    cour_in.start()
    mix_in.start()
    adj_in.start()
    for k in range(steps - 1, -1, -1):
        traj_in[k].start()

    zeros_pad = jnp.zeros((n_t, n_z, PAD, n_x), jnp.float32)
    for k in range(steps):
        pad_ref[k, :, :, 0:PAD, :] = zeros_pad
        pad_ref[k, :, :, PAD + n_y : 2 * PAD + n_y, :] = zeros_pad
    zeros_c = jnp.zeros((n_z, PAD, n_x), jnp.float32)
    cyp_ref[:, 0:PAD, :] = zeros_c
    cyp_ref[:, PAD + n_y : 2 * PAD + n_y, :] = zeros_c

    barrier = pltpu.get_barrier_semaphore()
    for dev in ((lon, lat, partner), (left, lat, lev), (right, lat, lev)):
        pl.semaphore_signal(barrier, 1, device_id=dev, device_id_type=MESH)

    @pl.when(has_up)
    def _():
        pl.semaphore_signal(barrier, 1, device_id=(lon, up, lev), device_id_type=MESH)

    @pl.when(has_down)
    def _():
        pl.semaphore_signal(barrier, 1, device_id=(lon, down, lev), device_id_type=MESH)

    pl.semaphore_wait(barrier, 3 + has_up.astype(jnp.int32) + has_down.astype(jnp.int32))

    def rcopy(src, dst, idx, dev):
        return pltpu.make_async_remote_copy(
            src, dst, send_sem.at[idx], recv_sem.at[idx], device_id=dev, device_id_type=MESH
        )

    lane = lax.broadcasted_iota(jnp.int32, (n_y, n_x), 1)
    row = lax.broadcasted_iota(jnp.int32, (n_y, n_x), 0)

    cour_in.wait()
    mix_in.wait()
    for c in small_in:
        c.wait()
    top_row = jnp.logical_and(lat == n_lat - 1, row == n_y - 1)
    for z in range(n_z):
        cyp_ref[z, PAD : PAD + n_y, :] = jnp.where(top_row, 0.0, cour_ref[1, z])
    cet_ref[...] = cour_ref[0].reshape(rows, n_x).T
    ce_right = rcopy(cet_ref.at[pl.ds(n_x - 2, 2), :], ceh_ref.at[pl.ds(n_x - 2, 2), :], S_CE_R, (right, lat, lev))
    ce_left = rcopy(cet_ref.at[pl.ds(0, 2), :], ceh_ref.at[pl.ds(0, 2), :], S_CE_L, (left, lat, lev))
    cn_up = rcopy(
        cyp_ref.at[:, pl.ds(PAD + n_y - 2, 2), :], cyp_ref.at[:, pl.ds(PAD - 2, 2), :], S_CN_U, (lon, up, lev)
    )
    cn_down = rcopy(
        cyp_ref.at[:, pl.ds(PAD, 2), :], cyp_ref.at[:, pl.ds(PAD + n_y, 2), :], S_CN_D, (lon, down, lev)
    )
    mix_x = rcopy(mix_ref.at[pl.ds(edge_z, 1)], mh_ref, S_MIX, (lon, lat, partner))
    mix_x.start()
    ce_right.start()
    ce_left.start()

    @pl.when(has_up)
    def _():
        cn_up.start()

    @pl.when(has_down)
    def _():
        cn_down.start()

    def build_vertical_coefficients():
        mix_x.wait()
        dep = jnp.where(low_half, 0.1 + 0.3 * land_ref[...].astype(jnp.float32), 0.0)
        below = jnp.where(low_half, 0.0, mh_ref[0])
        for z in range(n_z):
            above = mix_ref[z]
            if z == n_z - 1:
                above = jnp.where(low_half, above, 0.0)
            base = 1.0 - above - below
            if z == 0:
                base = base - dep
            vc_ref[0, z] = above
            vc_ref[1, z] = below
            vc_ref[2, z] = base
            below = above

    def build_transport_coefficients():
        ce_right.wait()
        ce_left.wait()

        @pl.when(has_up)
        def _():
            cn_up.wait_send()
            cn_down.wait_recv()

        @pl.when(has_down)
        def _():
            cn_down.wait_send()
            cn_up.wait_recv()

        he = ceh_ref[...].T.reshape(n_z, n_y, n_x)
        for z in range(n_z):
            c = cour_ref[0, z]
            hz = he[z]
            c_p1 = jnp.where(lane == n_x - 1, pltpu.roll(hz, n_x - 1, 1), pltpu.roll(c, n_x - 1, 1))
            c_m1 = jnp.where(lane == 0, pltpu.roll(hz, 1, 1), pltpu.roll(c, 1, 1))
            c_m2 = jnp.where(lane <= 1, pltpu.roll(hz, 2, 1), pltpu.roll(c, 2, 1))
            cx_ref[0, z] = -1.5 * jnp.maximum(c, 0.0)
            cx_ref[1, z] = 0.5 * jnp.maximum(c_p1, 0.0)
            cx_ref[2, z] = -1.5 * jnp.minimum(c_m1, 0.0)
            cx_ref[3, z] = 0.5 * jnp.minimum(c_m2, 0.0)
            cy_ref[0, z] = -1.5 * jnp.maximum(cyp_ref[z, PAD : PAD + n_y, :], 0.0)
            cy_ref[1, z] = 0.5 * jnp.maximum(cyp_ref[z, PAD + 1 : PAD + 1 + n_y, :], 0.0)
            cy_ref[2, z] = -1.5 * jnp.minimum(cyp_ref[z, PAD - 1 : PAD - 1 + n_y, :], 0.0)
            cy_ref[3, z] = 0.5 * jnp.minimum(cyp_ref[z, PAD - 2 : PAD - 2 + n_y, :], 0.0)

    eo_ref[...] = jnp.zeros(eo_ref.shape, jnp.float32)
    src_mask = srcm_ref[...].astype(jnp.float32)
    adj_in.wait()

    for k in range(steps - 1, -1, -1):
        traj_in[k].wait()

        def coag_level(zz, acc):
            z = jnp.where(low_half, n_z - 1 - zz, zz)
            zg = level0 + z
            lam = [out_ref[t, z] for t in range(n_t)]
            st = [traj_ref[k, t, z].astype(jnp.float32) for t in range(n_t)]
            new_acc = []
            for m in range(3):
                part = acc[m]
                for j in range(3):
                    part = part + (ecoef_ref[3 * m + j] * prof_ref[zg]) * lam[3 * m + j]
                new_acc.append(part)
            k0, k1, k2, k01, k02, k12 = [rates_ref[i, zg] for i in range(6)]
            n0, v0, w0, n1, v1, w1, n2, v2, w2 = st
            ln0, lv0, lw0, ln1, lv1, lw1, ln2, lv2, lw2 = lam
            a01 = k01 * n1
            a02 = k02 * n2
            a12 = k12 * n2
            s0 = a01 + a02
            g_n0 = ln0 * (-2.0 * k0 * n0 - s0)
            g_v0 = (
                (lv1 * a01 + lv2 * a02 - lv0 * s0)
                + 2.0 * (lw0 * (k0 * v0) + lw1 * (k01 * v1) + lw2 * (k02 * v2))
            )
            g_w0 = lw1 * a01 + lw2 * a02 - lw0 * s0
            g_n1 = (
                ln1 * (-2.0 * k1 * n1 - a12)
                - ln0 * (k01 * n0)
                + (lv1 - lv0) * (k01 * v0)
                + (lw1 - lw0) * (k01 * w0)
            )
            g_v1 = (lv2 - lv1) * a12 + 2.0 * (lw1 * (k1 * v1 + k01 * v0) + lw2 * (k12 * v2))
            g_w1 = (lw2 - lw1) * a12
            g_n2 = (
                -2.0 * k2 * n2 * ln2
                - ln0 * (k02 * n0)
                - ln1 * (k12 * n1)
                + (lv2 - lv0) * (k02 * v0)
                + (lv2 - lv1) * (k12 * v1)
                + (lw2 - lw0) * (k02 * w0)
                + (lw2 - lw1) * (k12 * w1)
            )
            g_v2 = 2.0 * lw2 * (k2 * v2 + k02 * v0 + k12 * v1)
            grads = [g_n0, g_v0, g_w0, g_n1, g_v1, g_w1, g_n2, g_v2]
            for t in range(n_t - 1):
                out_ref[t, z] = lam[t] + grads[t]
            return tuple(new_acc)

        zero = jnp.zeros((n_y, n_x), jnp.float32)
        acc = coag_level(0, (zero, zero, zero))
        lev_copy = rcopy(out_ref.at[:, pl.ds(edge_z, 1)], lv_ref.at[k], S_LEV + k, (lon, lat, partner))
        lev_copy.start()
        acc = lax.fori_loop(1, n_z, coag_level, acc)
        for m in range(3):
            eo_ref[m] = eo_ref[m] + acc[m] * src_mask

        if k == steps - 1:
            build_vertical_coefficients()

        def vert_inner(i, carry):
            t = i // (n_z - 1)
            z = i % (n_z - 1) + lev
            zg = level0 + z
            s = speed_ref[sclass_ref[zg], t]
            a = out_ref[t, z]
            a_below = jnp.where(z > 0, out_ref[t, jnp.maximum(z - 1, 0)], 0.0)
            a_above = jnp.where(z < n_z - 1, out_ref[t, jnp.minimum(z + 1, n_z - 1)], 0.0)
            pad_ref[k, t, z, PAD : PAD + n_y, :] = (
                a * (vc_ref[2, z] - s) + a_below * (vc_ref[1, z] + s) + a_above * vc_ref[0, z]
            )
            return carry

        lax.fori_loop(0, n_t * (n_z - 1), vert_inner, 0, unroll=7)
        lev_copy.wait()

        def vert_edge(t, carry):
            z = edge_z
            s = speed_ref[sclass_ref[level0 + z], t]
            a = out_ref[t, z]
            other = out_ref[t, inner_z]
            halo = lv_ref[k, t, 0]
            a_below = jnp.where(low_half, other, halo)
            a_above = jnp.where(low_half, halo, other)
            pad_ref[k, t, z, PAD : PAD + n_y, :] = (
                a * (vc_ref[2, z] - s) + a_below * (vc_ref[1, z] + s) + a_above * vc_ref[0, z]
            )
            return carry

        lax.fori_loop(0, n_t, vert_edge, 0, unroll=3)

        lat_up = rcopy(
            pad_ref.at[k, :, :, pl.ds(PAD + n_y - 2, 2), :],
            pad_ref.at[k, :, :, pl.ds(PAD - 2, 2), :],
            S_UP + k,
            (lon, up, lev),
        )
        lat_down = rcopy(
            pad_ref.at[k, :, :, pl.ds(PAD, 2), :],
            pad_ref.at[k, :, :, pl.ds(PAD + n_y, 2), :],
            S_DOWN + k,
            (lon, down, lev),
        )

        @pl.when(has_up)
        def _():
            lat_up.start()

        @pl.when(has_down)
        def _():
            lat_down.start()

        for t in range(n_t):
            blk = pad_ref[k, t, :, PAD : PAD + n_y, :].reshape(rows, n_x)
            at_ref[k, :, t * rows : (t + 1) * rows] = blk.T
        lon_right = rcopy(
            at_ref.at[k, pl.ds(n_x - 2, 2), :], ht_ref.at[k, pl.ds(n_x - 2, 2), :], S_RIGHT + k, (right, lat, lev)
        )
        lon_left = rcopy(
            at_ref.at[k, pl.ds(0, 2), :], ht_ref.at[k, pl.ds(0, 2), :], S_LEFT + k, (left, lat, lev)
        )
        lon_right.start()
        lon_left.start()

        if k == steps - 1:
            build_transport_coefficients()

        lon_right.wait()
        lon_left.wait()

        @pl.when(has_up)
        def _():
            lat_up.wait_send()
            lat_down.wait_recv()

        @pl.when(has_down)
        def _():
            lat_down.wait_send()
            lat_up.wait_recv()

        for t in range(n_t):
            hb_ref[t] = ht_ref[k, :, t * rows : (t + 1) * rows].T.reshape(n_z, n_y, n_x)

        def transport(i, carry):
            t = i // n_z
            z = i % n_z
            a = pad_ref[k, t, z, PAD : PAD + n_y, :]
            hz = hb_ref[t, z]
            y_p1 = pad_ref[k, t, z, PAD + 1 : PAD + 1 + n_y, :]
            y_p2 = pad_ref[k, t, z, PAD + 2 : PAD + 2 + n_y, :]
            y_m1 = pad_ref[k, t, z, PAD - 1 : PAD - 1 + n_y, :]
            y_m2 = pad_ref[k, t, z, PAD - 2 : PAD - 2 + n_y, :]
            x_p1 = jnp.where(lane == n_x - 1, pltpu.roll(hz, n_x - 1, 1), pltpu.roll(a, n_x - 1, 1))
            x_p2 = jnp.where(lane >= n_x - 2, pltpu.roll(hz, n_x - 2, 1), pltpu.roll(a, n_x - 2, 1))
            x_m1 = jnp.where(lane == 0, pltpu.roll(hz, 1, 1), pltpu.roll(a, 1, 1))
            x_m2 = jnp.where(lane <= 1, pltpu.roll(hz, 2, 1), pltpu.roll(a, 2, 1))
            lon_part = (
                cx_ref[0, z] * (a - x_p1)
                + cx_ref[1, z] * (x_p1 - x_p2)
                + cx_ref[2, z] * (x_m1 - a)
                + cx_ref[3, z] * (x_m2 - x_m1)
            )
            lat_part = (
                cy_ref[0, z] * (a - y_p1)
                + cy_ref[1, z] * (y_p1 - y_p2)
                + cy_ref[2, z] * (y_m1 - a)
                + cy_ref[3, z] * (y_m2 - y_m1)
            )
            out_ref[t, z] = a + lon_part + lat_part
            return carry

        lax.fori_loop(0, n_t * n_z, transport, 0, unroll=4)

    emis_copy = rcopy(eo_ref, ep_ref, S_EMIS, (lon, lat, partner))
    emis_copy.start()
    emis_copy.wait()
    emis_ref[...] = eo_ref[...] + ep_ref[...]
    out_copy = pltpu.make_async_copy(out_ref, out_hbm, local_sem.at[0])
    emis_out = pltpu.make_async_copy(emis_ref, emis_hbm, local_sem.at[1])
    out_copy.start()
    emis_out.start()
    out_copy.wait()
    emis_out.wait()


def shards(
    adjoint_in,
    trajectory,
    courant,
    mixing,
    coag_rates,
    settle_speed,
    settle_class,
    emis_profile,
    emis_coef,
    land_mask,
    source_mask,
):
    n_t, n_z, n_y, n_x = adjoint_in.shape
    steps = trajectory.shape[0]
    rows = n_z * n_y
    hbm = pl.BlockSpec(memory_space=pl.ANY)
    vmem = pl.BlockSpec(memory_space=pltpu.VMEM)
    smem = pl.BlockSpec(memory_space=pltpu.SMEM)
    f32 = jnp.float32
    return pl.pallas_call(
        kernel,
        out_shape=(
            jax.ShapeDtypeStruct(adjoint_in.shape, f32),
            jax.ShapeDtypeStruct((3, n_y, n_x), f32),
        ),
        in_specs=[hbm] * 11,
        out_specs=(hbm, hbm),
        scratch_shapes=[
            pltpu.VMEM(adjoint_in.shape, f32),
            pltpu.VMEM((3, n_y, n_x), f32),
            pltpu.VMEM(land_mask.shape, land_mask.dtype),
            pltpu.VMEM(source_mask.shape, source_mask.dtype),
            pltpu.SMEM(coag_rates.shape, f32),
            pltpu.SMEM(settle_speed.shape, f32),
            pltpu.SMEM(settle_class.shape, settle_class.dtype),
            pltpu.SMEM(emis_profile.shape, f32),
            pltpu.SMEM(emis_coef.shape, f32),
            pltpu.VMEM(trajectory.shape, trajectory.dtype),
            pltpu.VMEM(courant.shape, f32),
            pltpu.VMEM(mixing.shape, f32),
            pltpu.VMEM((steps, n_t, n_z, n_y + 2 * PAD, n_x), f32),
            pltpu.VMEM((steps, n_x, n_t * rows), f32),
            pltpu.VMEM((steps, n_x, n_t * rows), f32),
            pltpu.VMEM((n_t, n_z, n_y, n_x), f32),
            pltpu.VMEM((steps, n_t, 1, n_y, n_x), f32),
            pltpu.VMEM((3, n_y, n_x), f32),
            pltpu.VMEM((3, n_y, n_x), f32),
            pltpu.VMEM((4, n_z, n_y, n_x), f32),
            pltpu.VMEM((4, n_z, n_y, n_x), f32),
            pltpu.VMEM((3, n_z, n_y, n_x), f32),
            pltpu.VMEM((n_x, rows), f32),
            pltpu.VMEM((n_x, rows), f32),
            pltpu.VMEM((n_z, n_y + 2 * PAD, n_x), f32),
            pltpu.VMEM((1, n_y, n_x), f32),
            pltpu.SemaphoreType.DMA((N_REMOTE,)),
            pltpu.SemaphoreType.DMA((N_REMOTE,)),
            pltpu.SemaphoreType.DMA((10 + steps,)),
        ],
        compiler_params=pltpu.CompilerParams(
            collective_id=0, has_side_effects=True, vmem_limit_bytes=67043328
        ),
    )(
        adjoint_in, trajectory, courant, mixing, land_mask, source_mask,
        coag_rates, settle_speed, settle_class, emis_profile, emis_coef,
    )


def solution(mesh):
    return jax.shard_map(
        shards,
        mesh=mesh,
        in_specs=(
            P(None, "lev", "lat", "lon"),
            P(None, None, "lev", "lat", "lon"),
            P(None, "lev", "lat", "lon"),
            P("lev", "lat", "lon"),
            P(),
            P(),
            P(),
            P(),
            P(),
            P("lat", "lon"),
            P("lat", "lon"),
        ),
        out_specs=(P(None, "lev", "lat", "lon"), P(None, "lat", "lon")),
        check_vma=False,
    )
```

```python
import jax
import jax.numpy as jnp
from jax import lax
from jax.experimental import pallas as pl
from jax.experimental.pallas import tpu as pltpu
from jax.sharding import PartitionSpec as P

MESH = pl.DeviceIdType.MESH
PAD = 8

S_LEV, S_UP, S_DOWN, S_RIGHT, S_LEFT = 0, 3, 6, 9, 12
S_EMIS, S_CE_R, S_CE_L, S_CN_U, S_CN_D, S_MIX = 15, 16, 17, 18, 19, 20
N_REMOTE = 21


def kernel(
    adj_hbm, traj_hbm, cour_hbm, mix_hbm, land_hbm, srcm_hbm,
    rates_hbm, speed_hbm, sclass_hbm, prof_hbm, ecoef_hbm,
    out_hbm, emis_hbm,
    out_ref, emis_ref, land_ref, srcm_ref, rates_ref, speed_ref, sclass_ref, prof_ref, ecoef_ref,
    traj_ref, cour_ref, mix_ref, pad_ref, lh_ref, at_ref, ht_ref, hb_ref, lv_ref, eo_ref, ep_ref,
    cx_ref, cy_ref, vc_ref, cet_ref, ceh_ref, cyp_ref, mh_ref,
    send_sem, recv_sem, local_sem,
):
    n_t, n_z, n_y, n_x = out_ref.shape
    steps = traj_hbm.shape[0]
    rows = n_z * n_y
    lon = lax.axis_index("lon")
    lat = lax.axis_index("lat")
    lev = lax.axis_index("lev")
    n_lon = lax.axis_size("lon")
    n_lat = lax.axis_size("lat")
    right = lax.rem(lon + 1, n_lon)
    left = lax.rem(lon + n_lon - 1, n_lon)
    has_up = lat < n_lat - 1
    has_down = lat > 0
    up = jnp.minimum(lat + 1, n_lat - 1)
    down = jnp.maximum(lat - 1, 0)
    partner = 1 - lev
    low_half = lev == 0
    edge_z = jnp.where(low_half, n_z - 1, 0)
    inner_z = jnp.where(low_half, n_z - 2, 1)
    level0 = lev * n_z

    adj_in = pltpu.make_async_copy(adj_hbm, out_ref, local_sem.at[0])
    cour_in = pltpu.make_async_copy(cour_hbm, cour_ref, local_sem.at[1])
    mix_in = pltpu.make_async_copy(mix_hbm, mix_ref, local_sem.at[2])
    traj_in = [
        pltpu.make_async_copy(traj_hbm.at[k], traj_ref.at[k], local_sem.at[3 + k]) for k in range(steps)
    ]
    small_in = [
        pltpu.make_async_copy(src, dst, local_sem.at[3 + steps + i])
        for i, (src, dst) in enumerate(
            (
                (rates_hbm, rates_ref),
                (speed_hbm, speed_ref),
                (sclass_hbm, sclass_ref),
                (prof_hbm, prof_ref),
                (ecoef_hbm, ecoef_ref),
                (land_hbm, land_ref),
                (srcm_hbm, srcm_ref),
            )
        )
    ]
    for c in small_in:
        c.start()
    cour_in.start()
    mix_in.start()
    adj_in.start()
    for k in range(steps - 1, -1, -1):
        traj_in[k].start()

    zeros_pad = jnp.zeros((n_t, n_z, PAD, n_x), jnp.float32)
    for k in range(steps):
        pad_ref[k, :, :, 0:PAD, :] = zeros_pad
        pad_ref[k, :, :, PAD + n_y : 2 * PAD + n_y, :] = zeros_pad
        lh_ref[k] = zeros_pad
    zeros_c = jnp.zeros((n_z, PAD, n_x), jnp.float32)
    cyp_ref[:, 0:PAD, :] = zeros_c
    cyp_ref[:, PAD + n_y : 2 * PAD + n_y, :] = zeros_c

    barrier = pltpu.get_barrier_semaphore()
    for dev in ((lon, lat, partner), (left, lat, lev), (right, lat, lev)):
        pl.semaphore_signal(barrier, 1, device_id=dev, device_id_type=MESH)

    @pl.when(has_up)
    def _():
        pl.semaphore_signal(barrier, 1, device_id=(lon, up, lev), device_id_type=MESH)

    @pl.when(has_down)
    def _():
        pl.semaphore_signal(barrier, 1, device_id=(lon, down, lev), device_id_type=MESH)

    pl.semaphore_wait(barrier, 3 + has_up.astype(jnp.int32) + has_down.astype(jnp.int32))

    def rcopy(src, dst, idx, dev):
        return pltpu.make_async_remote_copy(
            src, dst, send_sem.at[idx], recv_sem.at[idx], device_id=dev, device_id_type=MESH
        )

    lane = lax.broadcasted_iota(jnp.int32, (n_y, n_x), 1)
    row = lax.broadcasted_iota(jnp.int32, (n_y, n_x), 0)

    cour_in.wait()
    mix_in.wait()
    for c in small_in:
        c.wait()
    top_row = jnp.logical_and(lat == n_lat - 1, row == n_y - 1)
    for z in range(n_z):
        cyp_ref[z, PAD : PAD + n_y, :] = jnp.where(top_row, 0.0, cour_ref[1, z])
    cet_ref[...] = cour_ref[0].reshape(rows, n_x).T
    ce_right = rcopy(cet_ref.at[pl.ds(n_x - 2, 2), :], ceh_ref.at[pl.ds(n_x - 2, 2), :], S_CE_R, (right, lat, lev))
    ce_left = rcopy(cet_ref.at[pl.ds(0, 2), :], ceh_ref.at[pl.ds(0, 2), :], S_CE_L, (left, lat, lev))
    cn_up = rcopy(
        cyp_ref.at[:, pl.ds(PAD + n_y - 2, 2), :], cyp_ref.at[:, pl.ds(PAD - 2, 2), :], S_CN_U, (lon, up, lev)
    )
    cn_down = rcopy(
        cyp_ref.at[:, pl.ds(PAD, 2), :], cyp_ref.at[:, pl.ds(PAD + n_y, 2), :], S_CN_D, (lon, down, lev)
    )
    mix_x = rcopy(mix_ref.at[pl.ds(edge_z, 1)], mh_ref, S_MIX, (lon, lat, partner))
    mix_x.start()
    ce_right.start()
    ce_left.start()

    @pl.when(has_up)
    def _():
        cn_up.start()

    @pl.when(has_down)
    def _():
        cn_down.start()

    def build_vertical_coefficients():
        mix_x.wait()
        dep = jnp.where(low_half, 0.1 + 0.3 * land_ref[...].astype(jnp.float32), 0.0)
        below = jnp.where(low_half, 0.0, mh_ref[0])
        for z in range(n_z):
            above = mix_ref[z]
            if z == n_z - 1:
                above = jnp.where(low_half, above, 0.0)
            base = 1.0 - above - below
            if z == 0:
                base = base - dep
            vc_ref[0, z] = above
            vc_ref[1, z] = below
            vc_ref[2, z] = base
            below = above

    def build_transport_coefficients():
        ce_right.wait()
        ce_left.wait()

        @pl.when(has_up)
        def _():
            cn_up.wait_send()
            cn_down.wait_recv()

        @pl.when(has_down)
        def _():
            cn_down.wait_send()
            cn_up.wait_recv()

        he = ceh_ref[...].T.reshape(n_z, n_y, n_x)
        for z in range(n_z):
            c = cour_ref[0, z]
            hz = he[z]
            c_p1 = jnp.where(lane == n_x - 1, pltpu.roll(hz, n_x - 1, 1), pltpu.roll(c, n_x - 1, 1))
            c_m1 = jnp.where(lane == 0, pltpu.roll(hz, 1, 1), pltpu.roll(c, 1, 1))
            c_m2 = jnp.where(lane <= 1, pltpu.roll(hz, 2, 1), pltpu.roll(c, 2, 1))
            cx_ref[0, z] = -1.5 * jnp.maximum(c, 0.0)
            cx_ref[1, z] = 0.5 * jnp.maximum(c_p1, 0.0)
            cx_ref[2, z] = -1.5 * jnp.minimum(c_m1, 0.0)
            cx_ref[3, z] = 0.5 * jnp.minimum(c_m2, 0.0)
            cy_ref[0, z] = -1.5 * jnp.maximum(cyp_ref[z, PAD : PAD + n_y, :], 0.0)
            cy_ref[1, z] = 0.5 * jnp.maximum(cyp_ref[z, PAD + 1 : PAD + 1 + n_y, :], 0.0)
            cy_ref[2, z] = -1.5 * jnp.minimum(cyp_ref[z, PAD - 1 : PAD - 1 + n_y, :], 0.0)
            cy_ref[3, z] = 0.5 * jnp.minimum(cyp_ref[z, PAD - 2 : PAD - 2 + n_y, :], 0.0)

    eo_ref[...] = jnp.zeros(eo_ref.shape, jnp.float32)
    src_mask = srcm_ref[...].astype(jnp.float32)
    adj_in.wait()

    for k in range(steps - 1, -1, -1):
        traj_in[k].wait()

        def coag_level(zz, acc):
            z = jnp.where(low_half, n_z - 1 - zz, zz)
            zg = level0 + z
            lam = [out_ref[t, z] for t in range(n_t)]
            st = [traj_ref[k, t, z].astype(jnp.float32) for t in range(n_t)]
            new_acc = []
            for m in range(3):
                part = acc[m]
                for j in range(3):
                    part = part + (ecoef_ref[3 * m + j] * prof_ref[zg]) * lam[3 * m + j]
                new_acc.append(part)
            k0, k1, k2, k01, k02, k12 = [rates_ref[i, zg] for i in range(6)]
            n0, v0, w0, n1, v1, w1, n2, v2, w2 = st
            ln0, lv0, lw0, ln1, lv1, lw1, ln2, lv2, lw2 = lam
            a01 = k01 * n1
            a02 = k02 * n2
            a12 = k12 * n2
            s0 = a01 + a02
            g_n0 = ln0 * (-2.0 * k0 * n0 - s0)
            g_v0 = (
                (lv1 * a01 + lv2 * a02 - lv0 * s0)
                + 2.0 * (lw0 * (k0 * v0) + lw1 * (k01 * v1) + lw2 * (k02 * v2))
            )
            g_w0 = lw1 * a01 + lw2 * a02 - lw0 * s0
            g_n1 = (
                ln1 * (-2.0 * k1 * n1 - a12)
                - ln0 * (k01 * n0)
                + (lv1 - lv0) * (k01 * v0)
                + (lw1 - lw0) * (k01 * w0)
            )
            g_v1 = (lv2 - lv1) * a12 + 2.0 * (lw1 * (k1 * v1 + k01 * v0) + lw2 * (k12 * v2))
            g_w1 = (lw2 - lw1) * a12
            g_n2 = (
                -2.0 * k2 * n2 * ln2
                - ln0 * (k02 * n0)
                - ln1 * (k12 * n1)
                + (lv2 - lv0) * (k02 * v0)
                + (lv2 - lv1) * (k12 * v1)
                + (lw2 - lw0) * (k02 * w0)
                + (lw2 - lw1) * (k12 * w1)
            )
            g_v2 = 2.0 * lw2 * (k2 * v2 + k02 * v0 + k12 * v1)
            grads = [g_n0, g_v0, g_w0, g_n1, g_v1, g_w1, g_n2, g_v2]
            for t in range(n_t - 1):
                out_ref[t, z] = lam[t] + grads[t]
            return tuple(new_acc)

        zero = jnp.zeros((n_y, n_x), jnp.float32)
        acc = coag_level(0, (zero, zero, zero))
        lev_copy = rcopy(out_ref.at[:, pl.ds(edge_z, 1)], lv_ref.at[k], S_LEV + k, (lon, lat, partner))
        lev_copy.start()
        acc = lax.fori_loop(1, n_z, coag_level, acc)
        for m in range(3):
            eo_ref[m] = eo_ref[m] + acc[m] * src_mask

        if k == steps - 1:
            build_vertical_coefficients()

        def vert_inner(i, carry):
            t = i // (n_z - 1)
            z = i % (n_z - 1) + lev
            zg = level0 + z
            s = speed_ref[sclass_ref[zg], t]
            a = out_ref[t, z]
            a_below = jnp.where(z > 0, out_ref[t, jnp.maximum(z - 1, 0)], 0.0)
            a_above = jnp.where(z < n_z - 1, out_ref[t, jnp.minimum(z + 1, n_z - 1)], 0.0)
            pad_ref[k, t, z, PAD : PAD + n_y, :] = (
                a * (vc_ref[2, z] - s) + a_below * (vc_ref[1, z] + s) + a_above * vc_ref[0, z]
            )
            return carry

        lax.fori_loop(0, n_t * (n_z - 1), vert_inner, 0, unroll=7)
        lev_copy.wait()

        def vert_edge(t, carry):
            z = edge_z
            s = speed_ref[sclass_ref[level0 + z], t]
            a = out_ref[t, z]
            other = out_ref[t, inner_z]
            halo = lv_ref[k, t, 0]
            a_below = jnp.where(low_half, other, halo)
            a_above = jnp.where(low_half, halo, other)
            pad_ref[k, t, z, PAD : PAD + n_y, :] = (
                a * (vc_ref[2, z] - s) + a_below * (vc_ref[1, z] + s) + a_above * vc_ref[0, z]
            )
            return carry

        lax.fori_loop(0, n_t, vert_edge, 0, unroll=3)

        lat_up = rcopy(
            pad_ref.at[k, :, :, pl.ds(PAD + n_y - 2, 2), :],
            lh_ref.at[k, :, :, pl.ds(0, 2), :],
            S_UP + k,
            (lon, up, lev),
        )
        lat_down = rcopy(
            pad_ref.at[k, :, :, pl.ds(PAD, 2), :],
            lh_ref.at[k, :, :, pl.ds(2, 2), :],
            S_DOWN + k,
            (lon, down, lev),
        )

        @pl.when(has_up)
        def _():
            lat_up.start()

        @pl.when(has_down)
        def _():
            lat_down.start()

        for t in range(n_t):
            blk = pad_ref[k, t, :, PAD : PAD + n_y, :].reshape(rows, n_x)
            at_ref[k, :, t * rows : (t + 1) * rows] = blk.T
        lon_right = rcopy(
            at_ref.at[k, pl.ds(n_x - 2, 2), :], ht_ref.at[k, pl.ds(n_x - 2, 2), :], S_RIGHT + k, (right, lat, lev)
        )
        lon_left = rcopy(
            at_ref.at[k, pl.ds(0, 2), :], ht_ref.at[k, pl.ds(0, 2), :], S_LEFT + k, (left, lat, lev)
        )
        lon_right.start()
        lon_left.start()

        if k == steps - 1:
            build_transport_coefficients()

        def transport(i, carry):
            t = i // n_z
            z = i % n_z
            a = pad_ref[k, t, z, PAD : PAD + n_y, :]
            y_p1 = pad_ref[k, t, z, PAD + 1 : PAD + 1 + n_y, :]
            y_p2 = pad_ref[k, t, z, PAD + 2 : PAD + 2 + n_y, :]
            y_m1 = pad_ref[k, t, z, PAD - 1 : PAD - 1 + n_y, :]
            y_m2 = pad_ref[k, t, z, PAD - 2 : PAD - 2 + n_y, :]
            x_p1 = pltpu.roll(a, n_x - 1, 1)
            x_p2 = pltpu.roll(a, n_x - 2, 1)
            x_m1 = pltpu.roll(a, 1, 1)
            x_m2 = pltpu.roll(a, 2, 1)
            lon_part = (
                cx_ref[0, z] * (a - x_p1)
                + cx_ref[1, z] * (x_p1 - x_p2)
                + cx_ref[2, z] * (x_m1 - a)
                + cx_ref[3, z] * (x_m2 - x_m1)
            )
            lat_part = (
                cy_ref[0, z] * (a - y_p1)
                + cy_ref[1, z] * (y_p1 - y_p2)
                + cy_ref[2, z] * (y_m1 - a)
                + cy_ref[3, z] * (y_m2 - y_m1)
            )
            out_ref[t, z] = a + lon_part + lat_part
            return carry

        lax.fori_loop(0, n_t * n_z, transport, 0, unroll=4)

        lon_right.wait()
        lon_left.wait()

        @pl.when(has_up)
        def _():
            lat_up.wait_send()
            lat_down.wait_recv()

        @pl.when(has_down)
        def _():
            lat_down.wait_send()
            lat_up.wait_recv()

        for t in range(n_t):
            hb_ref[t] = ht_ref[k, :, t * rows : (t + 1) * rows].T.reshape(n_z, n_y, n_x)

        def edges(i, carry):
            t = i // n_z
            z = i % n_z
            a = pad_ref[k, t, z, PAD : PAD + n_y, :]
            d = hb_ref[t, z] - a
            d_m1 = pltpu.roll(d, 1, 1)
            d_m2 = pltpu.roll(d, 2, 1)
            d_p1 = pltpu.roll(d, n_x - 1, 1)
            d_p2 = pltpu.roll(d, n_x - 2, 1)
            cx0 = cx_ref[0, z]
            cx1 = cx_ref[1, z]
            cxm1 = cx_ref[2, z]
            cxm2 = cx_ref[3, z]
            low = cxm2 * d_m2 + jnp.where(lane == 0, (cxm1 - cxm2) * d_m1, 0.0)
            high = jnp.where(lane == n_x - 1, (cx1 - cx0) * d_p1, 0.0) - cx1 * d_p2
            corr = jnp.where(lane <= 1, low, jnp.where(lane >= n_x - 2, high, 0.0))
            out_ref[t, z] = out_ref[t, z] + corr
            h = lh_ref[k, t, z, 0:4, :]
            am2 = h[0:1]
            am1 = h[1:2]
            ap1 = h[2:3]
            ap2 = h[3:4]
            c_lo = cy_ref[:, z, 0:2, :]
            c_hi = cy_ref[:, z, n_y - 2 : n_y, :]
            r0 = c_lo[2, 0:1] * am1 + c_lo[3, 0:1] * (am2 - am1)
            r1 = c_lo[3, 1:2] * am1
            r14 = -c_hi[1, 0:1] * ap1
            r15 = c_hi[1, 1:2] * (ap1 - ap2) - c_hi[0, 1:2] * ap1
            out_ref[t, z, 0:2, :] = out_ref[t, z, 0:2, :] + jnp.concatenate([r0, r1], axis=0)
            out_ref[t, z, n_y - 2 : n_y, :] = out_ref[t, z, n_y - 2 : n_y, :] + jnp.concatenate([r14, r15], axis=0)
            return carry

        lax.fori_loop(0, n_t * n_z, edges, 0, unroll=4)

    emis_copy = rcopy(eo_ref, ep_ref, S_EMIS, (lon, lat, partner))
    emis_copy.start()
    emis_copy.wait()
    emis_ref[...] = eo_ref[...] + ep_ref[...]
    out_copy = pltpu.make_async_copy(out_ref, out_hbm, local_sem.at[0])
    emis_out = pltpu.make_async_copy(emis_ref, emis_hbm, local_sem.at[1])
    out_copy.start()
    emis_out.start()
    out_copy.wait()
    emis_out.wait()


def shards(
    adjoint_in,
    trajectory,
    courant,
    mixing,
    coag_rates,
    settle_speed,
    settle_class,
    emis_profile,
    emis_coef,
    land_mask,
    source_mask,
):
    n_t, n_z, n_y, n_x = adjoint_in.shape
    steps = trajectory.shape[0]
    rows = n_z * n_y
    hbm = pl.BlockSpec(memory_space=pl.ANY)
    vmem = pl.BlockSpec(memory_space=pltpu.VMEM)
    smem = pl.BlockSpec(memory_space=pltpu.SMEM)
    f32 = jnp.float32
    return pl.pallas_call(
        kernel,
        out_shape=(
            jax.ShapeDtypeStruct(adjoint_in.shape, f32),
            jax.ShapeDtypeStruct((3, n_y, n_x), f32),
        ),
        in_specs=[hbm] * 11,
        out_specs=(hbm, hbm),
        scratch_shapes=[
            pltpu.VMEM(adjoint_in.shape, f32),
            pltpu.VMEM((3, n_y, n_x), f32),
            pltpu.VMEM(land_mask.shape, land_mask.dtype),
            pltpu.VMEM(source_mask.shape, source_mask.dtype),
            pltpu.SMEM(coag_rates.shape, f32),
            pltpu.SMEM(settle_speed.shape, f32),
            pltpu.SMEM(settle_class.shape, settle_class.dtype),
            pltpu.SMEM(emis_profile.shape, f32),
            pltpu.SMEM(emis_coef.shape, f32),
            pltpu.VMEM(trajectory.shape, trajectory.dtype),
            pltpu.VMEM(courant.shape, f32),
            pltpu.VMEM(mixing.shape, f32),
            pltpu.VMEM((steps, n_t, n_z, n_y + 2 * PAD, n_x), f32),
            pltpu.VMEM((steps, n_t, n_z, PAD, n_x), f32),
            pltpu.VMEM((steps, n_x, n_t * rows), f32),
            pltpu.VMEM((steps, n_x, n_t * rows), f32),
            pltpu.VMEM((n_t, n_z, n_y, n_x), f32),
            pltpu.VMEM((steps, n_t, 1, n_y, n_x), f32),
            pltpu.VMEM((3, n_y, n_x), f32),
            pltpu.VMEM((3, n_y, n_x), f32),
            pltpu.VMEM((4, n_z, n_y, n_x), f32),
            pltpu.VMEM((4, n_z, n_y, n_x), f32),
            pltpu.VMEM((3, n_z, n_y, n_x), f32),
            pltpu.VMEM((n_x, rows), f32),
            pltpu.VMEM((n_x, rows), f32),
            pltpu.VMEM((n_z, n_y + 2 * PAD, n_x), f32),
            pltpu.VMEM((1, n_y, n_x), f32),
            pltpu.SemaphoreType.DMA((N_REMOTE,)),
            pltpu.SemaphoreType.DMA((N_REMOTE,)),
            pltpu.SemaphoreType.DMA((10 + steps,)),
        ],
        compiler_params=pltpu.CompilerParams(
            collective_id=0, has_side_effects=True, vmem_limit_bytes=67043328
        ),
    )(
        adjoint_in, trajectory, courant, mixing, land_mask, source_mask,
        coag_rates, settle_speed, settle_class, emis_profile, emis_coef,
    )


def solution(mesh):
    return jax.shard_map(
        shards,
        mesh=mesh,
        in_specs=(
            P(None, "lev", "lat", "lon"),
            P(None, None, "lev", "lat", "lon"),
            P(None, "lev", "lat", "lon"),
            P("lev", "lat", "lon"),
            P(),
            P(),
            P(),
            P(),
            P(),
            P("lat", "lon"),
            P("lat", "lon"),
        ),
        out_specs=(P(None, "lev", "lat", "lon"), P(None, "lat", "lon")),
        check_vma=False,
    )
```

```python
import jax
import jax.numpy as jnp
from jax import lax
from jax.experimental import pallas as pl
from jax.experimental.pallas import tpu as pltpu
from jax.sharding import PartitionSpec as P

MESH = pl.DeviceIdType.MESH
PAD = 8

S_LEV, S_UP, S_DOWN, S_RIGHT, S_LEFT = 0, 3, 6, 9, 12
S_EMIS, S_CE_R, S_CE_L, S_CN_U, S_CN_D, S_MIX = 15, 16, 17, 18, 19, 20
N_REMOTE = 21


def kernel(
    adj_hbm, traj_hbm, cour_hbm, mix_hbm, land_hbm, srcm_hbm,
    rates_hbm, speed_hbm, sclass_hbm, prof_hbm, ecoef_hbm,
    out_hbm, emis_hbm,
    out_ref, emis_ref, land_ref, srcm_ref, rates_ref, speed_ref, sclass_ref, prof_ref, ecoef_ref,
    traj_ref, cour_ref, mix_ref, pad_ref, lh_ref, at_ref, ht_ref, hb_ref, lv_ref, eo_ref, ep_ref,
    cx_ref, cy_ref, vc_ref, cet_ref, ceh_ref, cyp_ref, mh_ref,
    send_sem, recv_sem, local_sem,
):
    n_t, n_z, n_y, n_x = out_ref.shape
    steps = traj_hbm.shape[0]
    rows = n_z * n_y
    lon = lax.axis_index("lon")
    lat = lax.axis_index("lat")
    lev = lax.axis_index("lev")
    n_lon = lax.axis_size("lon")
    n_lat = lax.axis_size("lat")
    right = lax.rem(lon + 1, n_lon)
    left = lax.rem(lon + n_lon - 1, n_lon)
    has_up = lat < n_lat - 1
    has_down = lat > 0
    up = jnp.minimum(lat + 1, n_lat - 1)
    down = jnp.maximum(lat - 1, 0)
    partner = 1 - lev
    low_half = lev == 0
    edge_z = jnp.where(low_half, n_z - 1, 0)
    inner_z = jnp.where(low_half, n_z - 2, 1)
    level0 = lev * n_z

    adj_in = pltpu.make_async_copy(adj_hbm, out_ref, local_sem.at[0])
    cour_in = pltpu.make_async_copy(cour_hbm, cour_ref, local_sem.at[1])
    mix_in = pltpu.make_async_copy(mix_hbm, mix_ref, local_sem.at[2])
    traj_in = [
        pltpu.make_async_copy(traj_hbm.at[k], traj_ref.at[k], local_sem.at[3 + k]) for k in range(steps)
    ]
    small_in = [
        pltpu.make_async_copy(src, dst, local_sem.at[3 + steps + i])
        for i, (src, dst) in enumerate(
            (
                (rates_hbm, rates_ref),
                (speed_hbm, speed_ref),
                (sclass_hbm, sclass_ref),
                (prof_hbm, prof_ref),
                (ecoef_hbm, ecoef_ref),
                (land_hbm, land_ref),
                (srcm_hbm, srcm_ref),
            )
        )
    ]
    for c in small_in:
        c.start()
    cour_in.start()
    mix_in.start()
    adj_in.start()
    for k in range(steps - 1, -1, -1):
        traj_in[k].start()

    zeros_pad = jnp.zeros((n_t, n_z, PAD, n_x), jnp.float32)
    for k in range(steps):
        pad_ref[k, :, :, 0:PAD, :] = zeros_pad
        pad_ref[k, :, :, PAD + n_y : 2 * PAD + n_y, :] = zeros_pad
        lh_ref[k] = zeros_pad
    zeros_c = jnp.zeros((n_z, PAD, n_x), jnp.float32)
    cyp_ref[:, 0:PAD, :] = zeros_c
    cyp_ref[:, PAD + n_y : 2 * PAD + n_y, :] = zeros_c

    barrier = pltpu.get_barrier_semaphore()
    for dev in ((lon, lat, partner), (left, lat, lev), (right, lat, lev)):
        pl.semaphore_signal(barrier, 1, device_id=dev, device_id_type=MESH)

    @pl.when(has_up)
    def _():
        pl.semaphore_signal(barrier, 1, device_id=(lon, up, lev), device_id_type=MESH)

    @pl.when(has_down)
    def _():
        pl.semaphore_signal(barrier, 1, device_id=(lon, down, lev), device_id_type=MESH)

    pl.semaphore_wait(barrier, 3 + has_up.astype(jnp.int32) + has_down.astype(jnp.int32))

    def rcopy(src, dst, idx, dev):
        return pltpu.make_async_remote_copy(
            src, dst, send_sem.at[idx], recv_sem.at[idx], device_id=dev, device_id_type=MESH
        )

    lane = lax.broadcasted_iota(jnp.int32, (n_y, n_x), 1)
    row = lax.broadcasted_iota(jnp.int32, (n_y, n_x), 0)

    cour_in.wait()
    mix_in.wait()
    for c in small_in:
        c.wait()
    top_row = jnp.logical_and(lat == n_lat - 1, row == n_y - 1)
    for z in range(n_z):
        cyp_ref[z, PAD : PAD + n_y, :] = jnp.where(top_row, 0.0, cour_ref[1, z])
    cet_ref[...] = cour_ref[0].reshape(rows, n_x).T
    ce_right = rcopy(cet_ref.at[pl.ds(n_x - 2, 2), :], ceh_ref.at[pl.ds(n_x - 2, 2), :], S_CE_R, (right, lat, lev))
    ce_left = rcopy(cet_ref.at[pl.ds(0, 2), :], ceh_ref.at[pl.ds(0, 2), :], S_CE_L, (left, lat, lev))
    cn_up = rcopy(
        cyp_ref.at[:, pl.ds(PAD + n_y - 2, 2), :], cyp_ref.at[:, pl.ds(PAD - 2, 2), :], S_CN_U, (lon, up, lev)
    )
    cn_down = rcopy(
        cyp_ref.at[:, pl.ds(PAD, 2), :], cyp_ref.at[:, pl.ds(PAD + n_y, 2), :], S_CN_D, (lon, down, lev)
    )
    mix_x = rcopy(mix_ref.at[pl.ds(edge_z, 1)], mh_ref, S_MIX, (lon, lat, partner))
    mix_x.start()
    ce_right.start()
    ce_left.start()

    @pl.when(has_up)
    def _():
        cn_up.start()

    @pl.when(has_down)
    def _():
        cn_down.start()

    def build_vertical_coefficients():
        mix_x.wait()
        dep = jnp.where(low_half, 0.1 + 0.3 * land_ref[...].astype(jnp.float32), 0.0)
        below = jnp.where(low_half, 0.0, mh_ref[0])
        for z in range(n_z):
            above = mix_ref[z]
            if z == n_z - 1:
                above = jnp.where(low_half, above, 0.0)
            base = 1.0 - above - below
            if z == 0:
                base = base - dep
            vc_ref[0, z] = above
            vc_ref[1, z] = below
            vc_ref[2, z] = base
            below = above

    def build_transport_coefficients():
        ce_right.wait()
        ce_left.wait()

        @pl.when(has_up)
        def _():
            cn_up.wait_send()
            cn_down.wait_recv()

        @pl.when(has_down)
        def _():
            cn_down.wait_send()
            cn_up.wait_recv()

        he = ceh_ref[...].T.reshape(n_z, n_y, n_x)
        for z in range(n_z):
            c = cour_ref[0, z]
            hz = he[z]
            c_p1 = jnp.where(lane == n_x - 1, pltpu.roll(hz, n_x - 1, 1), pltpu.roll(c, n_x - 1, 1))
            c_m1 = jnp.where(lane == 0, pltpu.roll(hz, 1, 1), pltpu.roll(c, 1, 1))
            c_m2 = jnp.where(lane <= 1, pltpu.roll(hz, 2, 1), pltpu.roll(c, 2, 1))
            cx_ref[0, z] = -1.5 * jnp.maximum(c, 0.0)
            cx_ref[1, z] = 0.5 * jnp.maximum(c_p1, 0.0)
            cx_ref[2, z] = -1.5 * jnp.minimum(c_m1, 0.0)
            cx_ref[3, z] = 0.5 * jnp.minimum(c_m2, 0.0)
            cy_ref[0, z] = -1.5 * jnp.maximum(cyp_ref[z, PAD : PAD + n_y, :], 0.0)
            cy_ref[1, z] = 0.5 * jnp.maximum(cyp_ref[z, PAD + 1 : PAD + 1 + n_y, :], 0.0)
            cy_ref[2, z] = -1.5 * jnp.minimum(cyp_ref[z, PAD - 1 : PAD - 1 + n_y, :], 0.0)
            cy_ref[3, z] = 0.5 * jnp.minimum(cyp_ref[z, PAD - 2 : PAD - 2 + n_y, :], 0.0)

    eo_ref[...] = jnp.zeros(eo_ref.shape, jnp.float32)
    src_mask = srcm_ref[...].astype(jnp.float32)
    adj_in.wait()

    for k in range(steps - 1, -1, -1):
        traj_in[k].wait()

        def coag_level(zz, acc):
            z = jnp.where(low_half, n_z - 1 - zz, zz)
            zg = level0 + z
            lam = [out_ref[t, z] for t in range(n_t)]
            st = [traj_ref[k, t, z].astype(jnp.float32) for t in range(n_t)]
            new_acc = []
            for m in range(3):
                part = acc[m]
                for j in range(3):
                    part = part + (ecoef_ref[3 * m + j] * prof_ref[zg]) * lam[3 * m + j]
                new_acc.append(part)
            k0, k1, k2, k01, k02, k12 = [rates_ref[i, zg] for i in range(6)]
            n0, v0, w0, n1, v1, w1, n2, v2, w2 = st
            ln0, lv0, lw0, ln1, lv1, lw1, ln2, lv2, lw2 = lam
            a01 = k01 * n1
            a02 = k02 * n2
            a12 = k12 * n2
            s0 = a01 + a02
            g_n0 = ln0 * (-2.0 * k0 * n0 - s0)
            g_v0 = (
                (lv1 * a01 + lv2 * a02 - lv0 * s0)
                + 2.0 * (lw0 * (k0 * v0) + lw1 * (k01 * v1) + lw2 * (k02 * v2))
            )
            g_w0 = lw1 * a01 + lw2 * a02 - lw0 * s0
            g_n1 = (
                ln1 * (-2.0 * k1 * n1 - a12)
                - ln0 * (k01 * n0)
                + (lv1 - lv0) * (k01 * v0)
                + (lw1 - lw0) * (k01 * w0)
            )
            g_v1 = (lv2 - lv1) * a12 + 2.0 * (lw1 * (k1 * v1 + k01 * v0) + lw2 * (k12 * v2))
            g_w1 = (lw2 - lw1) * a12
            g_n2 = (
                -2.0 * k2 * n2 * ln2
                - ln0 * (k02 * n0)
                - ln1 * (k12 * n1)
                + (lv2 - lv0) * (k02 * v0)
                + (lv2 - lv1) * (k12 * v1)
                + (lw2 - lw0) * (k02 * w0)
                + (lw2 - lw1) * (k12 * w1)
            )
            g_v2 = 2.0 * lw2 * (k2 * v2 + k02 * v0 + k12 * v1)
            grads = [g_n0, g_v0, g_w0, g_n1, g_v1, g_w1, g_n2, g_v2]
            for t in range(n_t - 1):
                out_ref[t, z] = lam[t] + grads[t]
            return tuple(new_acc)

        zero = jnp.zeros((n_y, n_x), jnp.float32)
        acc = coag_level(0, (zero, zero, zero))
        lev_copy = rcopy(out_ref.at[:, pl.ds(edge_z, 1)], lv_ref.at[k], S_LEV + k, (lon, lat, partner))
        lev_copy.start()
        acc = lax.fori_loop(1, n_z, coag_level, acc)
        for m in range(3):
            eo_ref[m] = eo_ref[m] + acc[m] * src_mask

        if k == steps - 1:
            build_vertical_coefficients()

        def vert_inner(i, carry):
            t = i // (n_z - 1)
            z = i % (n_z - 1) + lev
            zg = level0 + z
            s = speed_ref[sclass_ref[zg], t]
            a = out_ref[t, z]
            a_below = jnp.where(z > 0, out_ref[t, jnp.maximum(z - 1, 0)], 0.0)
            a_above = jnp.where(z < n_z - 1, out_ref[t, jnp.minimum(z + 1, n_z - 1)], 0.0)
            pad_ref[k, t, z, PAD : PAD + n_y, :] = (
                a * (vc_ref[2, z] - s) + a_below * (vc_ref[1, z] + s) + a_above * vc_ref[0, z]
            )
            return carry

        lax.fori_loop(0, n_t * (n_z - 1), vert_inner, 0, unroll=7)
        lev_copy.wait()

        lat_up = rcopy(
            pad_ref.at[k, :, :, pl.ds(PAD + n_y - 2, 2), :],
            lh_ref.at[k, :, :, pl.ds(0, 2), :],
            S_UP + k,
            (lon, up, lev),
        )
        lat_down = rcopy(
            pad_ref.at[k, :, :, pl.ds(PAD, 2), :],
            lh_ref.at[k, :, :, pl.ds(2, 2), :],
            S_DOWN + k,
            (lon, down, lev),
        )
        lon_right = rcopy(
            at_ref.at[k, pl.ds(n_x - 2, 2), :], ht_ref.at[k, pl.ds(n_x - 2, 2), :], S_RIGHT + k, (right, lat, lev)
        )
        lon_left = rcopy(
            at_ref.at[k, pl.ds(0, 2), :], ht_ref.at[k, pl.ds(0, 2), :], S_LEFT + k, (left, lat, lev)
        )

        for t in range(n_t):
            z = edge_z
            s = speed_ref[sclass_ref[level0 + z], t]
            a = out_ref[t, z]
            other = out_ref[t, inner_z]
            halo = lv_ref[k, t, 0]
            a_below = jnp.where(low_half, other, halo)
            a_above = jnp.where(low_half, halo, other)
            pad_ref[k, t, z, PAD : PAD + n_y, :] = (
                a * (vc_ref[2, z] - s) + a_below * (vc_ref[1, z] + s) + a_above * vc_ref[0, z]
            )
            up_t = rcopy(
                pad_ref.at[k, t, :, pl.ds(PAD + n_y - 2, 2), :],
                lh_ref.at[k, t, :, pl.ds(0, 2), :],
                S_UP + k,
                (lon, up, lev),
            )
            down_t = rcopy(
                pad_ref.at[k, t, :, pl.ds(PAD, 2), :],
                lh_ref.at[k, t, :, pl.ds(2, 2), :],
                S_DOWN + k,
                (lon, down, lev),
            )

            @pl.when(has_up)
            def _():
                up_t.start()

            @pl.when(has_down)
            def _():
                down_t.start()

            blk = pad_ref[k, t, :, PAD : PAD + n_y, :].reshape(rows, n_x)
            cols = pl.ds(t * rows, rows)
            at_ref[k, :, cols] = blk.T
            rcopy(
                at_ref.at[k, pl.ds(n_x - 2, 2), cols], ht_ref.at[k, pl.ds(n_x - 2, 2), cols], S_RIGHT + k,
                (right, lat, lev),
            ).start()
            rcopy(
                at_ref.at[k, pl.ds(0, 2), cols], ht_ref.at[k, pl.ds(0, 2), cols], S_LEFT + k, (left, lat, lev)
            ).start()

        if k == steps - 1:
            build_transport_coefficients()

        def transport(i, carry):
            t = i // n_z
            z = i % n_z
            a = pad_ref[k, t, z, PAD : PAD + n_y, :]
            y_p1 = pad_ref[k, t, z, PAD + 1 : PAD + 1 + n_y, :]
            y_p2 = pad_ref[k, t, z, PAD + 2 : PAD + 2 + n_y, :]
            y_m1 = pad_ref[k, t, z, PAD - 1 : PAD - 1 + n_y, :]
            y_m2 = pad_ref[k, t, z, PAD - 2 : PAD - 2 + n_y, :]
            x_p1 = pltpu.roll(a, n_x - 1, 1)
            x_p2 = pltpu.roll(a, n_x - 2, 1)
            x_m1 = pltpu.roll(a, 1, 1)
            x_m2 = pltpu.roll(a, 2, 1)
            lon_part = (
                cx_ref[0, z] * (a - x_p1)
                + cx_ref[1, z] * (x_p1 - x_p2)
                + cx_ref[2, z] * (x_m1 - a)
                + cx_ref[3, z] * (x_m2 - x_m1)
            )
            lat_part = (
                cy_ref[0, z] * (a - y_p1)
                + cy_ref[1, z] * (y_p1 - y_p2)
                + cy_ref[2, z] * (y_m1 - a)
                + cy_ref[3, z] * (y_m2 - y_m1)
            )
            out_ref[t, z] = a + lon_part + lat_part
            return carry

        lax.fori_loop(0, n_t * n_z, transport, 0, unroll=4)

        lon_right.wait()
        lon_left.wait()

        @pl.when(has_up)
        def _():
            lat_up.wait_send()
            lat_down.wait_recv()

        @pl.when(has_down)
        def _():
            lat_down.wait_send()
            lat_up.wait_recv()

        for t in range(n_t):
            hb_ref[t] = ht_ref[k, :, t * rows : (t + 1) * rows].T.reshape(n_z, n_y, n_x)

        def edges(i, carry):
            t = i // n_z
            z = i % n_z
            a = pad_ref[k, t, z, PAD : PAD + n_y, :]
            d = hb_ref[t, z] - a
            d_m1 = pltpu.roll(d, 1, 1)
            d_m2 = pltpu.roll(d, 2, 1)
            d_p1 = pltpu.roll(d, n_x - 1, 1)
            d_p2 = pltpu.roll(d, n_x - 2, 1)
            cx0 = cx_ref[0, z]
            cx1 = cx_ref[1, z]
            cxm1 = cx_ref[2, z]
            cxm2 = cx_ref[3, z]
            low = cxm2 * d_m2 + jnp.where(lane == 0, (cxm1 - cxm2) * d_m1, 0.0)
            high = jnp.where(lane == n_x - 1, (cx1 - cx0) * d_p1, 0.0) - cx1 * d_p2
            corr = jnp.where(lane <= 1, low, jnp.where(lane >= n_x - 2, high, 0.0))
            out_ref[t, z] = out_ref[t, z] + corr
            h = lh_ref[k, t, z, 0:4, :]
            am2 = h[0:1]
            am1 = h[1:2]
            ap1 = h[2:3]
            ap2 = h[3:4]
            c_lo = cy_ref[:, z, 0:2, :]
            c_hi = cy_ref[:, z, n_y - 2 : n_y, :]
            r0 = c_lo[2, 0:1] * am1 + c_lo[3, 0:1] * (am2 - am1)
            r1 = c_lo[3, 1:2] * am1
            r14 = -c_hi[1, 0:1] * ap1
            r15 = c_hi[1, 1:2] * (ap1 - ap2) - c_hi[0, 1:2] * ap1
            out_ref[t, z, 0:2, :] = out_ref[t, z, 0:2, :] + jnp.concatenate([r0, r1], axis=0)
            out_ref[t, z, n_y - 2 : n_y, :] = out_ref[t, z, n_y - 2 : n_y, :] + jnp.concatenate([r14, r15], axis=0)
            return carry

        lax.fori_loop(0, n_t * n_z, edges, 0, unroll=4)

    emis_copy = rcopy(eo_ref, ep_ref, S_EMIS, (lon, lat, partner))
    emis_copy.start()
    emis_copy.wait()
    emis_ref[...] = eo_ref[...] + ep_ref[...]
    out_copy = pltpu.make_async_copy(out_ref, out_hbm, local_sem.at[0])
    emis_out = pltpu.make_async_copy(emis_ref, emis_hbm, local_sem.at[1])
    out_copy.start()
    emis_out.start()
    out_copy.wait()
    emis_out.wait()


def shards(
    adjoint_in,
    trajectory,
    courant,
    mixing,
    coag_rates,
    settle_speed,
    settle_class,
    emis_profile,
    emis_coef,
    land_mask,
    source_mask,
):
    n_t, n_z, n_y, n_x = adjoint_in.shape
    steps = trajectory.shape[0]
    rows = n_z * n_y
    hbm = pl.BlockSpec(memory_space=pl.ANY)
    vmem = pl.BlockSpec(memory_space=pltpu.VMEM)
    smem = pl.BlockSpec(memory_space=pltpu.SMEM)
    f32 = jnp.float32
    return pl.pallas_call(
        kernel,
        out_shape=(
            jax.ShapeDtypeStruct(adjoint_in.shape, f32),
            jax.ShapeDtypeStruct((3, n_y, n_x), f32),
        ),
        in_specs=[hbm] * 11,
        out_specs=(hbm, hbm),
        scratch_shapes=[
            pltpu.VMEM(adjoint_in.shape, f32),
            pltpu.VMEM((3, n_y, n_x), f32),
            pltpu.VMEM(land_mask.shape, land_mask.dtype),
            pltpu.VMEM(source_mask.shape, source_mask.dtype),
            pltpu.SMEM(coag_rates.shape, f32),
            pltpu.SMEM(settle_speed.shape, f32),
            pltpu.SMEM(settle_class.shape, settle_class.dtype),
            pltpu.SMEM(emis_profile.shape, f32),
            pltpu.SMEM(emis_coef.shape, f32),
            pltpu.VMEM(trajectory.shape, trajectory.dtype),
            pltpu.VMEM(courant.shape, f32),
            pltpu.VMEM(mixing.shape, f32),
            pltpu.VMEM((steps, n_t, n_z, n_y + 2 * PAD, n_x), f32),
            pltpu.VMEM((steps, n_t, n_z, PAD, n_x), f32),
            pltpu.VMEM((steps, n_x, n_t * rows), f32),
            pltpu.VMEM((steps, n_x, n_t * rows), f32),
            pltpu.VMEM((n_t, n_z, n_y, n_x), f32),
            pltpu.VMEM((steps, n_t, 1, n_y, n_x), f32),
            pltpu.VMEM((3, n_y, n_x), f32),
            pltpu.VMEM((3, n_y, n_x), f32),
            pltpu.VMEM((4, n_z, n_y, n_x), f32),
            pltpu.VMEM((4, n_z, n_y, n_x), f32),
            pltpu.VMEM((3, n_z, n_y, n_x), f32),
            pltpu.VMEM((n_x, rows), f32),
            pltpu.VMEM((n_x, rows), f32),
            pltpu.VMEM((n_z, n_y + 2 * PAD, n_x), f32),
            pltpu.VMEM((1, n_y, n_x), f32),
            pltpu.SemaphoreType.DMA((N_REMOTE,)),
            pltpu.SemaphoreType.DMA((N_REMOTE,)),
            pltpu.SemaphoreType.DMA((10 + steps,)),
        ],
        compiler_params=pltpu.CompilerParams(
            collective_id=0, has_side_effects=True, vmem_limit_bytes=67043328
        ),
    )(
        adjoint_in, trajectory, courant, mixing, land_mask, source_mask,
        coag_rates, settle_speed, settle_class, emis_profile, emis_coef,
    )


def solution(mesh):
    return jax.shard_map(
        shards,
        mesh=mesh,
        in_specs=(
            P(None, "lev", "lat", "lon"),
            P(None, None, "lev", "lat", "lon"),
            P(None, "lev", "lat", "lon"),
            P("lev", "lat", "lon"),
            P(),
            P(),
            P(),
            P(),
            P(),
            P("lat", "lon"),
            P("lat", "lon"),
        ),
        out_specs=(P(None, "lev", "lat", "lon"), P(None, "lat", "lon")),
        check_vma=False,
    )
```

```python
import jax
import jax.numpy as jnp
from jax import lax
from jax.experimental import pallas as pl
from jax.experimental.pallas import tpu as pltpu
from jax.sharding import PartitionSpec as P

MESH = pl.DeviceIdType.MESH
PAD = 8

S_LEV, S_UP, S_DOWN, S_RIGHT, S_LEFT = 0, 3, 6, 9, 12
S_EMIS, S_CE_R, S_CE_L, S_CN_U, S_CN_D, S_MIX = 15, 16, 17, 18, 19, 20
N_REMOTE = 21


def kernel(
    adj_hbm, traj_hbm, cour_hbm, mix_hbm, land_hbm, srcm_hbm,
    rates_hbm, speed_hbm, sclass_hbm, prof_hbm, ecoef_hbm,
    out_hbm, emis_hbm,
    out_ref, emis_ref, land_ref, srcm_ref, rates_ref, speed_ref, sclass_ref, prof_ref, ecoef_ref,
    traj_ref, cour_ref, mix_ref, pad_ref, lh_ref, at_ref, ht_ref, hb_ref, lv_ref, eo_ref, ep_ref,
    cx_ref, cy_ref, vc_ref, cet_ref, ceh_ref, cyp_ref, mh_ref,
    send_sem, recv_sem, local_sem,
):
    n_t, n_z, n_y, n_x = out_ref.shape
    steps = traj_hbm.shape[0]
    rows = n_z * n_y
    lon = lax.axis_index("lon")
    lat = lax.axis_index("lat")
    lev = lax.axis_index("lev")
    n_lon = lax.axis_size("lon")
    n_lat = lax.axis_size("lat")
    right = lax.rem(lon + 1, n_lon)
    left = lax.rem(lon + n_lon - 1, n_lon)
    has_up = lat < n_lat - 1
    has_down = lat > 0
    up = jnp.minimum(lat + 1, n_lat - 1)
    down = jnp.maximum(lat - 1, 0)
    partner = 1 - lev
    low_half = lev == 0
    edge_z = jnp.where(low_half, n_z - 1, 0)
    inner_z = jnp.where(low_half, n_z - 2, 1)
    level0 = lev * n_z

    adj_in = pltpu.make_async_copy(adj_hbm, out_ref, local_sem.at[0])
    cour_in = pltpu.make_async_copy(cour_hbm, cour_ref, local_sem.at[1])
    mix_in = pltpu.make_async_copy(mix_hbm, mix_ref, local_sem.at[2])
    traj_in = [
        pltpu.make_async_copy(traj_hbm.at[k], traj_ref.at[k], local_sem.at[3 + k]) for k in range(steps)
    ]
    small_in = [
        pltpu.make_async_copy(src, dst, local_sem.at[3 + steps + i])
        for i, (src, dst) in enumerate(
            (
                (rates_hbm, rates_ref),
                (speed_hbm, speed_ref),
                (sclass_hbm, sclass_ref),
                (prof_hbm, prof_ref),
                (ecoef_hbm, ecoef_ref),
                (land_hbm, land_ref),
                (srcm_hbm, srcm_ref),
            )
        )
    ]
    for c in small_in:
        c.start()
    cour_in.start()
    mix_in.start()
    adj_in.start()
    for k in range(steps - 1, -1, -1):
        traj_in[k].start()

    zeros_pad = jnp.zeros((n_t, n_z, PAD, n_x), jnp.float32)
    for k in range(steps):
        pad_ref[k, :, :, 0:PAD, :] = zeros_pad
        pad_ref[k, :, :, PAD + n_y : 2 * PAD + n_y, :] = zeros_pad
        lh_ref[k] = zeros_pad
    zeros_c = jnp.zeros((n_z, PAD, n_x), jnp.float32)
    cyp_ref[:, 0:PAD, :] = zeros_c
    cyp_ref[:, PAD + n_y : 2 * PAD + n_y, :] = zeros_c

    def rcopy(src, dst, idx, dev):
        return pltpu.make_async_remote_copy(
            src, dst, send_sem.at[idx], recv_sem.at[idx], device_id=dev, device_id_type=MESH
        )

    lane = lax.broadcasted_iota(jnp.int32, (n_y, n_x), 1)
    row = lax.broadcasted_iota(jnp.int32, (n_y, n_x), 0)

    cour_in.wait()
    mix_in.wait()
    for c in small_in:
        c.wait()
    top_row = jnp.logical_and(lat == n_lat - 1, row == n_y - 1)
    for z in range(n_z):
        cyp_ref[z, PAD : PAD + n_y, :] = jnp.where(top_row, 0.0, cour_ref[1, z])
    cet_ref[...] = cour_ref[0].reshape(rows, n_x).T
    ce_right = rcopy(cet_ref.at[pl.ds(n_x - 2, 2), :], ceh_ref.at[pl.ds(n_x - 2, 2), :], S_CE_R, (right, lat, lev))
    ce_left = rcopy(cet_ref.at[pl.ds(0, 2), :], ceh_ref.at[pl.ds(0, 2), :], S_CE_L, (left, lat, lev))
    cn_up = rcopy(
        cyp_ref.at[:, pl.ds(PAD + n_y - 2, 2), :], cyp_ref.at[:, pl.ds(PAD - 2, 2), :], S_CN_U, (lon, up, lev)
    )
    cn_down = rcopy(
        cyp_ref.at[:, pl.ds(PAD, 2), :], cyp_ref.at[:, pl.ds(PAD + n_y, 2), :], S_CN_D, (lon, down, lev)
    )
    mix_x = rcopy(mix_ref.at[pl.ds(edge_z, 1)], mh_ref, S_MIX, (lon, lat, partner))

    def start_coefficient_halos():
        mix_x.start()
        ce_right.start()
        ce_left.start()

        @pl.when(has_up)
        def _():
            cn_up.start()

        @pl.when(has_down)
        def _():
            cn_down.start()

    def fix_vertical_coefficients():
        mix_x.wait()
        below = jnp.where(low_half, vc_ref[1, 0], mh_ref[0])
        vc_ref[1, 0] = below
        vc_ref[2, 0] = jnp.where(low_half, vc_ref[2, 0], 1.0 - vc_ref[0, 0] - below)

    def build_vertical_coefficients():
        dep = jnp.where(low_half, 0.1 + 0.3 * land_ref[...].astype(jnp.float32), 0.0)
        below = jnp.zeros((n_y, n_x), jnp.float32)
        for z in range(n_z):
            above = mix_ref[z]
            if z == n_z - 1:
                above = jnp.where(low_half, above, 0.0)
            base = 1.0 - above - below
            if z == 0:
                base = base - dep
            vc_ref[0, z] = above
            vc_ref[1, z] = below
            vc_ref[2, z] = base
            below = above

    def build_transport_coefficients():
        ce_right.wait()
        ce_left.wait()

        @pl.when(has_up)
        def _():
            cn_up.wait_send()
            cn_down.wait_recv()

        @pl.when(has_down)
        def _():
            cn_down.wait_send()
            cn_up.wait_recv()

        he = ceh_ref[...].T.reshape(n_z, n_y, n_x)
        for z in range(n_z):
            c = cour_ref[0, z]
            hz = he[z]
            c_p1 = jnp.where(lane == n_x - 1, pltpu.roll(hz, n_x - 1, 1), pltpu.roll(c, n_x - 1, 1))
            c_m1 = jnp.where(lane == 0, pltpu.roll(hz, 1, 1), pltpu.roll(c, 1, 1))
            c_m2 = jnp.where(lane <= 1, pltpu.roll(hz, 2, 1), pltpu.roll(c, 2, 1))
            cx_ref[0, z] = -1.5 * jnp.maximum(c, 0.0)
            cx_ref[1, z] = 0.5 * jnp.maximum(c_p1, 0.0)
            cx_ref[2, z] = -1.5 * jnp.minimum(c_m1, 0.0)
            cx_ref[3, z] = 0.5 * jnp.minimum(c_m2, 0.0)
            cy_ref[0, z] = -1.5 * jnp.maximum(cyp_ref[z, PAD : PAD + n_y, :], 0.0)
            cy_ref[1, z] = 0.5 * jnp.maximum(cyp_ref[z, PAD + 1 : PAD + 1 + n_y, :], 0.0)
            cy_ref[2, z] = -1.5 * jnp.minimum(cyp_ref[z, PAD - 1 : PAD - 1 + n_y, :], 0.0)
            cy_ref[3, z] = 0.5 * jnp.minimum(cyp_ref[z, PAD - 2 : PAD - 2 + n_y, :], 0.0)

    eo_ref[...] = jnp.zeros(eo_ref.shape, jnp.float32)
    src_mask = srcm_ref[...].astype(jnp.float32)
    adj_in.wait()
    build_vertical_coefficients()
    emis_copy = rcopy(eo_ref, ep_ref, S_EMIS, (lon, lat, partner))

    for k in range(steps - 1, -1, -1):
        first = k == steps - 1
        traj_in[k].wait()

        def coag_level(zz, acc):
            z = jnp.where(low_half, n_z - 1 - zz, zz)
            zg = level0 + z
            lam = [out_ref[t, z] for t in range(n_t)]
            st = [traj_ref[k, t, z].astype(jnp.float32) for t in range(n_t)]
            new_acc = []
            for m in range(3):
                part = acc[m]
                for j in range(3):
                    part = part + (ecoef_ref[3 * m + j] * prof_ref[zg]) * lam[3 * m + j]
                new_acc.append(part)
            k0, k1, k2, k01, k02, k12 = [rates_ref[i, zg] for i in range(6)]
            n0, v0, w0, n1, v1, w1, n2, v2, w2 = st
            ln0, lv0, lw0, ln1, lv1, lw1, ln2, lv2, lw2 = lam
            a01 = k01 * n1
            a02 = k02 * n2
            a12 = k12 * n2
            s0 = a01 + a02
            g_n0 = ln0 * (-2.0 * k0 * n0 - s0)
            g_v0 = (
                (lv1 * a01 + lv2 * a02 - lv0 * s0)
                + 2.0 * (lw0 * (k0 * v0) + lw1 * (k01 * v1) + lw2 * (k02 * v2))
            )
            g_w0 = lw1 * a01 + lw2 * a02 - lw0 * s0
            g_n1 = (
                ln1 * (-2.0 * k1 * n1 - a12)
                - ln0 * (k01 * n0)
                + (lv1 - lv0) * (k01 * v0)
                + (lw1 - lw0) * (k01 * w0)
            )
            g_v1 = (lv2 - lv1) * a12 + 2.0 * (lw1 * (k1 * v1 + k01 * v0) + lw2 * (k12 * v2))
            g_w1 = (lw2 - lw1) * a12
            g_n2 = (
                -2.0 * k2 * n2 * ln2
                - ln0 * (k02 * n0)
                - ln1 * (k12 * n1)
                + (lv2 - lv0) * (k02 * v0)
                + (lv2 - lv1) * (k12 * v1)
                + (lw2 - lw0) * (k02 * w0)
                + (lw2 - lw1) * (k12 * w1)
            )
            g_v2 = 2.0 * lw2 * (k2 * v2 + k02 * v0 + k12 * v1)
            grads = [g_n0, g_v0, g_w0, g_n1, g_v1, g_w1, g_n2, g_v2]
            for t in range(n_t - 1):
                out_ref[t, z] = lam[t] + grads[t]
            return tuple(new_acc)

        zero = jnp.zeros((n_y, n_x), jnp.float32)
        acc = coag_level(0, (zero, zero, zero))
        lev_copy = rcopy(out_ref.at[:, pl.ds(edge_z, 1)], lv_ref.at[k], S_LEV + k, (lon, lat, partner))
        if not first:
            lev_copy.start()
        acc = lax.fori_loop(1, n_z, coag_level, acc)
        for m in range(3):
            eo_ref[m] = eo_ref[m] + acc[m] * src_mask
        if k == 0:
            emis_copy.start()

        def vert_inner(i, carry):
            t = i // (n_z - 1)
            z = i % (n_z - 1) + lev
            zg = level0 + z
            s = speed_ref[sclass_ref[zg], t]
            a = out_ref[t, z]
            a_below = jnp.where(z > 0, out_ref[t, jnp.maximum(z - 1, 0)], 0.0)
            a_above = jnp.where(z < n_z - 1, out_ref[t, jnp.minimum(z + 1, n_z - 1)], 0.0)
            pad_ref[k, t, z, PAD : PAD + n_y, :] = (
                a * (vc_ref[2, z] - s) + a_below * (vc_ref[1, z] + s) + a_above * vc_ref[0, z]
            )
            return carry

        lax.fori_loop(0, n_t * (n_z - 1), vert_inner, 0, unroll=7)
        if first:
            barrier = pltpu.get_barrier_semaphore()
            for dev in ((lon, lat, partner), (left, lat, lev), (right, lat, lev)):
                pl.semaphore_signal(barrier, 1, device_id=dev, device_id_type=MESH)

            @pl.when(has_up)
            def _():
                pl.semaphore_signal(barrier, 1, device_id=(lon, up, lev), device_id_type=MESH)

            @pl.when(has_down)
            def _():
                pl.semaphore_signal(barrier, 1, device_id=(lon, down, lev), device_id_type=MESH)

            pl.semaphore_wait(barrier, 3 + has_up.astype(jnp.int32) + has_down.astype(jnp.int32))
            start_coefficient_halos()
            lev_copy.start()
            fix_vertical_coefficients()
        lev_copy.wait()

        lat_up = rcopy(
            pad_ref.at[k, :, :, pl.ds(PAD + n_y - 2, 2), :],
            lh_ref.at[k, :, :, pl.ds(0, 2), :],
            S_UP + k,
            (lon, up, lev),
        )
        lat_down = rcopy(
            pad_ref.at[k, :, :, pl.ds(PAD, 2), :],
            lh_ref.at[k, :, :, pl.ds(2, 2), :],
            S_DOWN + k,
            (lon, down, lev),
        )
        lon_right = rcopy(
            at_ref.at[k, pl.ds(n_x - 2, 2), :], ht_ref.at[k, pl.ds(n_x - 2, 2), :], S_RIGHT + k, (right, lat, lev)
        )
        lon_left = rcopy(
            at_ref.at[k, pl.ds(0, 2), :], ht_ref.at[k, pl.ds(0, 2), :], S_LEFT + k, (left, lat, lev)
        )

        for t in range(n_t):
            z = edge_z
            s = speed_ref[sclass_ref[level0 + z], t]
            a = out_ref[t, z]
            other = out_ref[t, inner_z]
            halo = lv_ref[k, t, 0]
            a_below = jnp.where(low_half, other, halo)
            a_above = jnp.where(low_half, halo, other)
            pad_ref[k, t, z, PAD : PAD + n_y, :] = (
                a * (vc_ref[2, z] - s) + a_below * (vc_ref[1, z] + s) + a_above * vc_ref[0, z]
            )
            up_t = rcopy(
                pad_ref.at[k, t, :, pl.ds(PAD + n_y - 2, 2), :],
                lh_ref.at[k, t, :, pl.ds(0, 2), :],
                S_UP + k,
                (lon, up, lev),
            )
            down_t = rcopy(
                pad_ref.at[k, t, :, pl.ds(PAD, 2), :],
                lh_ref.at[k, t, :, pl.ds(2, 2), :],
                S_DOWN + k,
                (lon, down, lev),
            )

            @pl.when(has_up)
            def _():
                up_t.start()

            @pl.when(has_down)
            def _():
                down_t.start()

            blk = pad_ref[k, t, :, PAD : PAD + n_y, :].reshape(rows, n_x)
            cols = pl.ds(t * rows, rows)
            at_ref[k, :, cols] = blk.T
            rcopy(
                at_ref.at[k, pl.ds(n_x - 2, 2), cols], ht_ref.at[k, pl.ds(n_x - 2, 2), cols], S_RIGHT + k,
                (right, lat, lev),
            ).start()
            rcopy(
                at_ref.at[k, pl.ds(0, 2), cols], ht_ref.at[k, pl.ds(0, 2), cols], S_LEFT + k, (left, lat, lev)
            ).start()

        if k == steps - 1:
            build_transport_coefficients()

        def transport(i, carry):
            t = i // n_z
            z = i % n_z
            a = pad_ref[k, t, z, PAD : PAD + n_y, :]
            y_p1 = pad_ref[k, t, z, PAD + 1 : PAD + 1 + n_y, :]
            y_p2 = pad_ref[k, t, z, PAD + 2 : PAD + 2 + n_y, :]
            y_m1 = pad_ref[k, t, z, PAD - 1 : PAD - 1 + n_y, :]
            y_m2 = pad_ref[k, t, z, PAD - 2 : PAD - 2 + n_y, :]
            x_p1 = pltpu.roll(a, n_x - 1, 1)
            x_p2 = pltpu.roll(a, n_x - 2, 1)
            x_m1 = pltpu.roll(a, 1, 1)
            x_m2 = pltpu.roll(a, 2, 1)
            lon_part = (
                cx_ref[0, z] * (a - x_p1)
                + cx_ref[1, z] * (x_p1 - x_p2)
                + cx_ref[2, z] * (x_m1 - a)
                + cx_ref[3, z] * (x_m2 - x_m1)
            )
            lat_part = (
                cy_ref[0, z] * (a - y_p1)
                + cy_ref[1, z] * (y_p1 - y_p2)
                + cy_ref[2, z] * (y_m1 - a)
                + cy_ref[3, z] * (y_m2 - y_m1)
            )
            out_ref[t, z] = a + lon_part + lat_part
            return carry

        lax.fori_loop(0, n_t * n_z, transport, 0, unroll=4)

        lon_right.wait()
        lon_left.wait()

        @pl.when(has_up)
        def _():
            lat_up.wait_send()
            lat_down.wait_recv()

        @pl.when(has_down)
        def _():
            lat_down.wait_send()
            lat_up.wait_recv()

        for t in range(n_t):
            hb_ref[t] = ht_ref[k, :, t * rows : (t + 1) * rows].T.reshape(n_z, n_y, n_x)

        def edges(i, carry):
            t = i // n_z
            z = i % n_z
            a = pad_ref[k, t, z, PAD : PAD + n_y, :]
            d = hb_ref[t, z] - a
            d_m1 = pltpu.roll(d, 1, 1)
            d_m2 = pltpu.roll(d, 2, 1)
            d_p1 = pltpu.roll(d, n_x - 1, 1)
            d_p2 = pltpu.roll(d, n_x - 2, 1)
            cx0 = cx_ref[0, z]
            cx1 = cx_ref[1, z]
            cxm1 = cx_ref[2, z]
            cxm2 = cx_ref[3, z]
            low = cxm2 * d_m2 + jnp.where(lane == 0, (cxm1 - cxm2) * d_m1, 0.0)
            high = jnp.where(lane == n_x - 1, (cx1 - cx0) * d_p1, 0.0) - cx1 * d_p2
            corr = jnp.where(lane <= 1, low, jnp.where(lane >= n_x - 2, high, 0.0))
            out_ref[t, z] = out_ref[t, z] + corr
            h = lh_ref[k, t, z, 0:4, :]
            am2 = h[0:1]
            am1 = h[1:2]
            ap1 = h[2:3]
            ap2 = h[3:4]
            c_lo = cy_ref[:, z, 0:2, :]
            c_hi = cy_ref[:, z, n_y - 2 : n_y, :]
            r0 = c_lo[2, 0:1] * am1 + c_lo[3, 0:1] * (am2 - am1)
            r1 = c_lo[3, 1:2] * am1
            r14 = -c_hi[1, 0:1] * ap1
            r15 = c_hi[1, 1:2] * (ap1 - ap2) - c_hi[0, 1:2] * ap1
            out_ref[t, z, 0:2, :] = out_ref[t, z, 0:2, :] + jnp.concatenate([r0, r1], axis=0)
            out_ref[t, z, n_y - 2 : n_y, :] = out_ref[t, z, n_y - 2 : n_y, :] + jnp.concatenate([r14, r15], axis=0)
            return carry

        lax.fori_loop(0, n_t * n_z, edges, 0, unroll=4)

    emis_copy.wait()
    emis_ref[...] = eo_ref[...] + ep_ref[...]
    out_copy = pltpu.make_async_copy(out_ref, out_hbm, local_sem.at[0])
    emis_out = pltpu.make_async_copy(emis_ref, emis_hbm, local_sem.at[1])
    out_copy.start()
    emis_out.start()
    out_copy.wait()
    emis_out.wait()


def shards(
    adjoint_in,
    trajectory,
    courant,
    mixing,
    coag_rates,
    settle_speed,
    settle_class,
    emis_profile,
    emis_coef,
    land_mask,
    source_mask,
):
    n_t, n_z, n_y, n_x = adjoint_in.shape
    steps = trajectory.shape[0]
    rows = n_z * n_y
    hbm = pl.BlockSpec(memory_space=pl.ANY)
    vmem = pl.BlockSpec(memory_space=pltpu.VMEM)
    smem = pl.BlockSpec(memory_space=pltpu.SMEM)
    f32 = jnp.float32
    return pl.pallas_call(
        kernel,
        out_shape=(
            jax.ShapeDtypeStruct(adjoint_in.shape, f32),
            jax.ShapeDtypeStruct((3, n_y, n_x), f32),
        ),
        in_specs=[hbm] * 11,
        out_specs=(hbm, hbm),
        scratch_shapes=[
            pltpu.VMEM(adjoint_in.shape, f32),
            pltpu.VMEM((3, n_y, n_x), f32),
            pltpu.VMEM(land_mask.shape, land_mask.dtype),
            pltpu.VMEM(source_mask.shape, source_mask.dtype),
            pltpu.SMEM(coag_rates.shape, f32),
            pltpu.SMEM(settle_speed.shape, f32),
            pltpu.SMEM(settle_class.shape, settle_class.dtype),
            pltpu.SMEM(emis_profile.shape, f32),
            pltpu.SMEM(emis_coef.shape, f32),
            pltpu.VMEM(trajectory.shape, trajectory.dtype),
            pltpu.VMEM(courant.shape, f32),
            pltpu.VMEM(mixing.shape, f32),
            pltpu.VMEM((steps, n_t, n_z, n_y + 2 * PAD, n_x), f32),
            pltpu.VMEM((steps, n_t, n_z, PAD, n_x), f32),
            pltpu.VMEM((steps, n_x, n_t * rows), f32),
            pltpu.VMEM((steps, n_x, n_t * rows), f32),
            pltpu.VMEM((n_t, n_z, n_y, n_x), f32),
            pltpu.VMEM((steps, n_t, 1, n_y, n_x), f32),
            pltpu.VMEM((3, n_y, n_x), f32),
            pltpu.VMEM((3, n_y, n_x), f32),
            pltpu.VMEM((4, n_z, n_y, n_x), f32),
            pltpu.VMEM((4, n_z, n_y, n_x), f32),
            pltpu.VMEM((3, n_z, n_y, n_x), f32),
            pltpu.VMEM((n_x, rows), f32),
            pltpu.VMEM((n_x, rows), f32),
            pltpu.VMEM((n_z, n_y + 2 * PAD, n_x), f32),
            pltpu.VMEM((1, n_y, n_x), f32),
            pltpu.SemaphoreType.DMA((N_REMOTE,)),
            pltpu.SemaphoreType.DMA((N_REMOTE,)),
            pltpu.SemaphoreType.DMA((10 + steps,)),
        ],
        compiler_params=pltpu.CompilerParams(
            collective_id=0, has_side_effects=True, vmem_limit_bytes=67043328
        ),
    )(
        adjoint_in, trajectory, courant, mixing, land_mask, source_mask,
        coag_rates, settle_speed, settle_class, emis_profile, emis_coef,
    )


def solution(mesh):
    return jax.shard_map(
        shards,
        mesh=mesh,
        in_specs=(
            P(None, "lev", "lat", "lon"),
            P(None, None, "lev", "lat", "lon"),
            P(None, "lev", "lat", "lon"),
            P("lev", "lat", "lon"),
            P(),
            P(),
            P(),
            P(),
            P(),
            P("lat", "lon"),
            P("lat", "lon"),
        ),
        out_specs=(P(None, "lev", "lat", "lon"), P(None, "lat", "lon")),
        check_vma=False,
    )
```

```python
import jax
import jax.numpy as jnp
from jax import lax
from jax.experimental import pallas as pl
from jax.experimental.pallas import tpu as pltpu
from jax.sharding import PartitionSpec as P

MESH = pl.DeviceIdType.MESH
PAD = 8

S_LEV, S_UP, S_DOWN, S_RIGHT, S_LEFT = 0, 3, 6, 9, 12
S_EMIS, S_CE_R, S_CE_L, S_CN_U, S_CN_D, S_MIX = 15, 16, 17, 18, 19, 20
N_REMOTE = 21


def kernel(
    adj_hbm, traj_hbm, cour_hbm, mix_hbm, land_hbm, srcm_hbm,
    rates_hbm, speed_hbm, sclass_hbm, prof_hbm, ecoef_hbm,
    out_hbm, emis_hbm,
    out_ref, emis_ref, land_ref, srcm_ref, rates_ref, speed_ref, sclass_ref, prof_ref, ecoef_ref,
    traj_ref, cour_ref, mix_ref, pad_ref, lh_ref, at_ref, ht_ref, hb_ref, lv_ref, eo_ref, ep_ref,
    cx_ref, cy_ref, vc_ref, cet_ref, ceh_ref, cyp_ref, mh_ref,
    send_sem, recv_sem, local_sem,
):
    n_t, n_z, n_y, n_x = out_ref.shape
    steps = traj_hbm.shape[0]
    rows = n_z * n_y
    lon = lax.axis_index("lon")
    lat = lax.axis_index("lat")
    lev = lax.axis_index("lev")
    n_lon = lax.axis_size("lon")
    n_lat = lax.axis_size("lat")
    right = lax.rem(lon + 1, n_lon)
    left = lax.rem(lon + n_lon - 1, n_lon)
    has_up = lat < n_lat - 1
    has_down = lat > 0
    up = jnp.minimum(lat + 1, n_lat - 1)
    down = jnp.maximum(lat - 1, 0)
    partner = 1 - lev
    low_half = lev == 0
    edge_z = jnp.where(low_half, n_z - 1, 0)
    inner_z = jnp.where(low_half, n_z - 2, 1)
    level0 = lev * n_z

    adj_in = pltpu.make_async_copy(adj_hbm, out_ref, local_sem.at[0])
    cour_in = pltpu.make_async_copy(cour_hbm, cour_ref, local_sem.at[1])
    mix_in = pltpu.make_async_copy(mix_hbm, mix_ref, local_sem.at[2])
    traj_in = [
        pltpu.make_async_copy(traj_hbm.at[k], traj_ref.at[k], local_sem.at[3 + k]) for k in range(steps)
    ]
    small_in = [
        pltpu.make_async_copy(src, dst, local_sem.at[3 + steps + i])
        for i, (src, dst) in enumerate(
            (
                (rates_hbm, rates_ref),
                (speed_hbm, speed_ref),
                (sclass_hbm, sclass_ref),
                (prof_hbm, prof_ref),
                (ecoef_hbm, ecoef_ref),
                (land_hbm, land_ref),
                (srcm_hbm, srcm_ref),
            )
        )
    ]
    for c in small_in:
        c.start()
    cour_in.start()
    mix_in.start()
    adj_in.start()
    for k in range(steps - 1, -1, -1):
        traj_in[k].start()

    zeros_pad = jnp.zeros((n_t, n_z, PAD, n_x), jnp.float32)
    for k in range(steps):
        pad_ref[k, :, :, 0:PAD, :] = zeros_pad
        pad_ref[k, :, :, PAD + n_y : 2 * PAD + n_y, :] = zeros_pad
        lh_ref[k] = zeros_pad
    zeros_c = jnp.zeros((n_z, PAD, n_x), jnp.float32)
    cyp_ref[:, 0:PAD, :] = zeros_c
    cyp_ref[:, PAD + n_y : 2 * PAD + n_y, :] = zeros_c

    def rcopy(src, dst, idx, dev):
        return pltpu.make_async_remote_copy(
            src, dst, send_sem.at[idx], recv_sem.at[idx], device_id=dev, device_id_type=MESH
        )

    lane = lax.broadcasted_iota(jnp.int32, (n_y, n_x), 1)
    row = lax.broadcasted_iota(jnp.int32, (n_y, n_x), 0)

    cour_in.wait()
    mix_in.wait()
    for c in small_in:
        c.wait()
    top_row = jnp.logical_and(lat == n_lat - 1, row == n_y - 1)
    for z in range(n_z):
        cyp_ref[z, PAD : PAD + n_y, :] = jnp.where(top_row, 0.0, cour_ref[1, z])
    cet_ref[...] = cour_ref[0].reshape(rows, n_x).T
    ce_right = rcopy(cet_ref.at[pl.ds(n_x - 2, 2), :], ceh_ref.at[pl.ds(n_x - 2, 2), :], S_CE_R, (right, lat, lev))
    ce_left = rcopy(cet_ref.at[pl.ds(0, 2), :], ceh_ref.at[pl.ds(0, 2), :], S_CE_L, (left, lat, lev))
    cn_up = rcopy(
        cyp_ref.at[:, pl.ds(PAD + n_y - 2, 2), :], cyp_ref.at[:, pl.ds(PAD - 2, 2), :], S_CN_U, (lon, up, lev)
    )
    cn_down = rcopy(
        cyp_ref.at[:, pl.ds(PAD, 2), :], cyp_ref.at[:, pl.ds(PAD + n_y, 2), :], S_CN_D, (lon, down, lev)
    )
    mix_x = rcopy(mix_ref.at[pl.ds(edge_z, 1)], mh_ref, S_MIX, (lon, lat, partner))

    def start_coefficient_halos():
        mix_x.start()
        ce_right.start()
        ce_left.start()

        @pl.when(has_up)
        def _():
            cn_up.start()

        @pl.when(has_down)
        def _():
            cn_down.start()

    def fix_vertical_coefficients():
        mix_x.wait()
        below = jnp.where(low_half, vc_ref[1, 0], mh_ref[0])
        vc_ref[1, 0] = below
        vc_ref[2, 0] = jnp.where(low_half, vc_ref[2, 0], 1.0 - vc_ref[0, 0] - below)

    def build_vertical_coefficients():
        dep = jnp.where(low_half, 0.1 + 0.3 * land_ref[...].astype(jnp.float32), 0.0)
        below = jnp.zeros((n_y, n_x), jnp.float32)
        for z in range(n_z):
            above = mix_ref[z]
            if z == n_z - 1:
                above = jnp.where(low_half, above, 0.0)
            base = 1.0 - above - below
            if z == 0:
                base = base - dep
            vc_ref[0, z] = above
            vc_ref[1, z] = below
            vc_ref[2, z] = base
            below = above

    def build_transport_coefficients():
        ce_right.wait()
        ce_left.wait()

        @pl.when(has_up)
        def _():
            cn_up.wait_send()
            cn_down.wait_recv()

        @pl.when(has_down)
        def _():
            cn_down.wait_send()
            cn_up.wait_recv()

        he = ceh_ref[...].T.reshape(n_z, n_y, n_x)
        for z in range(n_z):
            c = cour_ref[0, z]
            hz = he[z]
            c_p1 = jnp.where(lane == n_x - 1, pltpu.roll(hz, n_x - 1, 1), pltpu.roll(c, n_x - 1, 1))
            c_m1 = jnp.where(lane == 0, pltpu.roll(hz, 1, 1), pltpu.roll(c, 1, 1))
            c_m2 = jnp.where(lane <= 1, pltpu.roll(hz, 2, 1), pltpu.roll(c, 2, 1))
            cx_ref[0, z] = -1.5 * jnp.maximum(c, 0.0)
            cx_ref[1, z] = 0.5 * jnp.maximum(c_p1, 0.0)
            cx_ref[2, z] = -1.5 * jnp.minimum(c_m1, 0.0)
            cx_ref[3, z] = 0.5 * jnp.minimum(c_m2, 0.0)
            cy_ref[0, z] = -1.5 * jnp.maximum(cyp_ref[z, PAD : PAD + n_y, :], 0.0)
            cy_ref[1, z] = 0.5 * jnp.maximum(cyp_ref[z, PAD + 1 : PAD + 1 + n_y, :], 0.0)
            cy_ref[2, z] = -1.5 * jnp.minimum(cyp_ref[z, PAD - 1 : PAD - 1 + n_y, :], 0.0)
            cy_ref[3, z] = 0.5 * jnp.minimum(cyp_ref[z, PAD - 2 : PAD - 2 + n_y, :], 0.0)

    eo_ref[...] = jnp.zeros(eo_ref.shape, jnp.float32)
    src_mask = srcm_ref[...].astype(jnp.float32)
    adj_in.wait()
    build_vertical_coefficients()
    emis_copy = rcopy(eo_ref, ep_ref, S_EMIS, (lon, lat, partner))

    for k in range(steps - 1, -1, -1):
        first = k == steps - 1
        traj_in[k].wait()

        def coag_level(zz, acc):
            z = jnp.where(low_half, n_z - 1 - zz, zz)
            zg = level0 + z
            lam = [out_ref[t, z] for t in range(n_t)]
            st = [traj_ref[k, t, z].astype(jnp.float32) for t in range(n_t)]
            new_acc = []
            for m in range(3):
                part = acc[m]
                for j in range(3):
                    part = part + (ecoef_ref[3 * m + j] * prof_ref[zg]) * lam[3 * m + j]
                new_acc.append(part)
            k0, k1, k2, k01, k02, k12 = [rates_ref[i, zg] for i in range(6)]
            n0, v0, w0, n1, v1, w1, n2, v2, w2 = st
            ln0, lv0, lw0, ln1, lv1, lw1, ln2, lv2, lw2 = lam
            a01 = k01 * n1
            a02 = k02 * n2
            a12 = k12 * n2
            s0 = a01 + a02
            g_n0 = ln0 * (-2.0 * k0 * n0 - s0)
            g_v0 = (
                (lv1 * a01 + lv2 * a02 - lv0 * s0)
                + 2.0 * (lw0 * (k0 * v0) + lw1 * (k01 * v1) + lw2 * (k02 * v2))
            )
            g_w0 = lw1 * a01 + lw2 * a02 - lw0 * s0
            g_n1 = (
                ln1 * (-2.0 * k1 * n1 - a12)
                - ln0 * (k01 * n0)
                + (lv1 - lv0) * (k01 * v0)
                + (lw1 - lw0) * (k01 * w0)
            )
            g_v1 = (lv2 - lv1) * a12 + 2.0 * (lw1 * (k1 * v1 + k01 * v0) + lw2 * (k12 * v2))
            g_w1 = (lw2 - lw1) * a12
            g_n2 = (
                -2.0 * k2 * n2 * ln2
                - ln0 * (k02 * n0)
                - ln1 * (k12 * n1)
                + (lv2 - lv0) * (k02 * v0)
                + (lv2 - lv1) * (k12 * v1)
                + (lw2 - lw0) * (k02 * w0)
                + (lw2 - lw1) * (k12 * w1)
            )
            g_v2 = 2.0 * lw2 * (k2 * v2 + k02 * v0 + k12 * v1)
            grads = [g_n0, g_v0, g_w0, g_n1, g_v1, g_w1, g_n2, g_v2]
            for t in range(n_t - 1):
                out_ref[t, z] = lam[t] + grads[t]
            return tuple(new_acc)

        zero = jnp.zeros((n_y, n_x), jnp.float32)
        acc = coag_level(0, (zero, zero, zero))
        lev_copy = rcopy(out_ref.at[:, pl.ds(edge_z, 1)], lv_ref.at[k], S_LEV + k, (lon, lat, partner))
        if not first:
            lev_copy.start()
        acc = lax.fori_loop(1, n_z, coag_level, acc)
        for m in range(3):
            eo_ref[m] = eo_ref[m] + acc[m] * src_mask
        if k == 0:
            emis_copy.start()

        def vert_inner(i, carry):
            t = i // (n_z - 1)
            z = i % (n_z - 1) + lev
            zg = level0 + z
            s = speed_ref[sclass_ref[zg], t]
            a = out_ref[t, z]
            a_below = jnp.where(z > 0, out_ref[t, jnp.maximum(z - 1, 0)], 0.0)
            a_above = jnp.where(z < n_z - 1, out_ref[t, jnp.minimum(z + 1, n_z - 1)], 0.0)
            pad_ref[k, t, z, PAD : PAD + n_y, :] = (
                a * (vc_ref[2, z] - s) + a_below * (vc_ref[1, z] + s) + a_above * vc_ref[0, z]
            )
            return carry

        lax.fori_loop(0, n_t * (n_z - 1), vert_inner, 0, unroll=7)
        if first:
            barrier = pltpu.get_barrier_semaphore()
            for dev in ((lon, lat, partner), (left, lat, lev), (right, lat, lev)):
                pl.semaphore_signal(barrier, 1, device_id=dev, device_id_type=MESH)

            @pl.when(has_up)
            def _():
                pl.semaphore_signal(barrier, 1, device_id=(lon, up, lev), device_id_type=MESH)

            @pl.when(has_down)
            def _():
                pl.semaphore_signal(barrier, 1, device_id=(lon, down, lev), device_id_type=MESH)

            pl.semaphore_wait(barrier, 3 + has_up.astype(jnp.int32) + has_down.astype(jnp.int32))
            start_coefficient_halos()
            lev_copy.start()
            fix_vertical_coefficients()
        lev_copy.wait()

        lat_up = rcopy(
            pad_ref.at[k, :, :, pl.ds(PAD + n_y - 2, 2), :],
            lh_ref.at[k, :, :, pl.ds(0, 2), :],
            S_UP + k,
            (lon, up, lev),
        )
        lat_down = rcopy(
            pad_ref.at[k, :, :, pl.ds(PAD, 2), :],
            lh_ref.at[k, :, :, pl.ds(2, 2), :],
            S_DOWN + k,
            (lon, down, lev),
        )
        lon_right = rcopy(
            at_ref.at[k, pl.ds(n_x - 2, 2), :], ht_ref.at[k, pl.ds(n_x - 2, 2), :], S_RIGHT + k, (right, lat, lev)
        )
        lon_left = rcopy(
            at_ref.at[k, pl.ds(0, 2), :], ht_ref.at[k, pl.ds(0, 2), :], S_LEFT + k, (left, lat, lev)
        )

        for t in range(n_t):
            z = edge_z
            s = speed_ref[sclass_ref[level0 + z], t]
            a = out_ref[t, z]
            other = out_ref[t, inner_z]
            halo = lv_ref[k, t, 0]
            a_below = jnp.where(low_half, other, halo)
            a_above = jnp.where(low_half, halo, other)
            pad_ref[k, t, z, PAD : PAD + n_y, :] = (
                a * (vc_ref[2, z] - s) + a_below * (vc_ref[1, z] + s) + a_above * vc_ref[0, z]
            )
            up_t = rcopy(
                pad_ref.at[k, t, :, pl.ds(PAD + n_y - 2, 2), :],
                lh_ref.at[k, t, :, pl.ds(0, 2), :],
                S_UP + k,
                (lon, up, lev),
            )
            down_t = rcopy(
                pad_ref.at[k, t, :, pl.ds(PAD, 2), :],
                lh_ref.at[k, t, :, pl.ds(2, 2), :],
                S_DOWN + k,
                (lon, down, lev),
            )

            @pl.when(has_up)
            def _():
                up_t.start()

            @pl.when(has_down)
            def _():
                down_t.start()

            blk = pad_ref[k, t, :, PAD : PAD + n_y, :].reshape(rows, n_x)
            cols = pl.ds(t * rows, rows)
            at_ref[k, :, cols] = blk.T
            rcopy(
                at_ref.at[k, pl.ds(n_x - 2, 2), cols], ht_ref.at[k, pl.ds(n_x - 2, 2), cols], S_RIGHT + k,
                (right, lat, lev),
            ).start()
            rcopy(
                at_ref.at[k, pl.ds(0, 2), cols], ht_ref.at[k, pl.ds(0, 2), cols], S_LEFT + k, (left, lat, lev)
            ).start()

        if k == steps - 1:
            build_transport_coefficients()

        def transport(i, carry):
            t = i // n_z
            z = i % n_z
            a = pad_ref[k, t, z, PAD : PAD + n_y, :]
            y_p1 = pad_ref[k, t, z, PAD + 1 : PAD + 1 + n_y, :]
            y_p2 = pad_ref[k, t, z, PAD + 2 : PAD + 2 + n_y, :]
            y_m1 = pad_ref[k, t, z, PAD - 1 : PAD - 1 + n_y, :]
            y_m2 = pad_ref[k, t, z, PAD - 2 : PAD - 2 + n_y, :]
            x_p1 = pltpu.roll(a, n_x - 1, 1)
            x_p2 = pltpu.roll(a, n_x - 2, 1)
            x_m1 = pltpu.roll(a, 1, 1)
            x_m2 = pltpu.roll(a, 2, 1)
            lon_part = (
                cx_ref[0, z] * (a - x_p1)
                + cx_ref[1, z] * (x_p1 - x_p2)
                + cx_ref[2, z] * (x_m1 - a)
                + cx_ref[3, z] * (x_m2 - x_m1)
            )
            lat_part = (
                cy_ref[0, z] * (a - y_p1)
                + cy_ref[1, z] * (y_p1 - y_p2)
                + cy_ref[2, z] * (y_m1 - a)
                + cy_ref[3, z] * (y_m2 - y_m1)
            )
            out_ref[t, z] = a + lon_part + lat_part
            return carry

        lax.fori_loop(0, n_t * n_z, transport, 0, unroll=4)

        lon_right.wait()
        lon_left.wait()

        @pl.when(has_up)
        def _():
            lat_up.wait_send()
            lat_down.wait_recv()

        @pl.when(has_down)
        def _():
            lat_down.wait_send()
            lat_up.wait_recv()

        for t in range(n_t):
            hb_ref[t] = ht_ref[k, :, t * rows : (t + 1) * rows].T.reshape(n_z, n_y, n_x)

        def edges(i, carry):
            t = i // n_z
            z = i % n_z
            a = pad_ref[k, t, z, PAD : PAD + n_y, :]
            d = hb_ref[t, z] - a
            d_m1 = pltpu.roll(d, 1, 1)
            d_m2 = pltpu.roll(d, 2, 1)
            d_p1 = pltpu.roll(d, n_x - 1, 1)
            d_p2 = pltpu.roll(d, n_x - 2, 1)
            cx0 = cx_ref[0, z]
            cx1 = cx_ref[1, z]
            cxm1 = cx_ref[2, z]
            cxm2 = cx_ref[3, z]
            low = cxm2 * d_m2 + jnp.where(lane == 0, (cxm1 - cxm2) * d_m1, 0.0)
            high = jnp.where(lane == n_x - 1, (cx1 - cx0) * d_p1, 0.0) - cx1 * d_p2
            corr = jnp.where(lane <= 1, low, jnp.where(lane >= n_x - 2, high, 0.0))
            out_ref[t, z] = out_ref[t, z] + corr
            h = lh_ref[k, t, z, 0:4, :]
            am2 = h[0:1]
            am1 = h[1:2]
            ap1 = h[2:3]
            ap2 = h[3:4]
            c_lo = cy_ref[:, z, 0:2, :]
            c_hi = cy_ref[:, z, n_y - 2 : n_y, :]
            r0 = c_lo[2, 0:1] * am1 + c_lo[3, 0:1] * (am2 - am1)
            r1 = c_lo[3, 1:2] * am1
            r14 = -c_hi[1, 0:1] * ap1
            r15 = c_hi[1, 1:2] * (ap1 - ap2) - c_hi[0, 1:2] * ap1
            out_ref[t, z, 0:2, :] = out_ref[t, z, 0:2, :] + jnp.concatenate([r0, r1], axis=0)
            out_ref[t, z, n_y - 2 : n_y, :] = out_ref[t, z, n_y - 2 : n_y, :] + jnp.concatenate([r14, r15], axis=0)
            return carry

        lax.fori_loop(0, n_t * n_z, edges, 0, unroll=4)

    emis_copy.wait()
    emis_ref[...] = eo_ref[...] + ep_ref[...]
    out_copy = pltpu.make_async_copy(out_ref, out_hbm, local_sem.at[0])
    emis_out = pltpu.make_async_copy(emis_ref, emis_hbm, local_sem.at[1])
    out_copy.start()
    emis_out.start()
    out_copy.wait()
    emis_out.wait()


def hand_over(adj_hbm, emis_hbm, adj_out, emis_out, adj_buf, emis_buf, sem):
    ins = [
        pltpu.make_async_copy(adj_hbm, adj_buf, sem.at[0]),
        pltpu.make_async_copy(emis_hbm, emis_buf, sem.at[1]),
    ]
    for c in ins:
        c.start()
    outs = [
        pltpu.make_async_copy(adj_buf, adj_out, sem.at[2]),
        pltpu.make_async_copy(emis_buf, emis_out, sem.at[3]),
    ]
    for c, o in zip(ins, outs):
        c.wait()
        o.start()
    for o in outs:
        o.wait()


def shards(
    adjoint_in,
    trajectory,
    courant,
    mixing,
    coag_rates,
    settle_speed,
    settle_class,
    emis_profile,
    emis_coef,
    land_mask,
    source_mask,
):
    n_t, n_z, n_y, n_x = adjoint_in.shape
    steps = trajectory.shape[0]
    rows = n_z * n_y
    hbm = pl.BlockSpec(memory_space=pl.ANY)
    vmem = pl.BlockSpec(memory_space=pltpu.VMEM)
    smem = pl.BlockSpec(memory_space=pltpu.SMEM)
    f32 = jnp.float32
    adj_out, emis_out = pl.pallas_call(
        kernel,
        out_shape=(
            jax.ShapeDtypeStruct(adjoint_in.shape, f32),
            jax.ShapeDtypeStruct((3, n_y, n_x), f32),
        ),
        in_specs=[hbm] * 11,
        out_specs=(hbm, hbm),
        scratch_shapes=[
            pltpu.VMEM(adjoint_in.shape, f32),
            pltpu.VMEM((3, n_y, n_x), f32),
            pltpu.VMEM(land_mask.shape, land_mask.dtype),
            pltpu.VMEM(source_mask.shape, source_mask.dtype),
            pltpu.SMEM(coag_rates.shape, f32),
            pltpu.SMEM(settle_speed.shape, f32),
            pltpu.SMEM(settle_class.shape, settle_class.dtype),
            pltpu.SMEM(emis_profile.shape, f32),
            pltpu.SMEM(emis_coef.shape, f32),
            pltpu.VMEM(trajectory.shape, trajectory.dtype),
            pltpu.VMEM(courant.shape, f32),
            pltpu.VMEM(mixing.shape, f32),
            pltpu.VMEM((steps, n_t, n_z, n_y + 2 * PAD, n_x), f32),
            pltpu.VMEM((steps, n_t, n_z, PAD, n_x), f32),
            pltpu.VMEM((steps, n_x, n_t * rows), f32),
            pltpu.VMEM((steps, n_x, n_t * rows), f32),
            pltpu.VMEM((n_t, n_z, n_y, n_x), f32),
            pltpu.VMEM((steps, n_t, 1, n_y, n_x), f32),
            pltpu.VMEM((3, n_y, n_x), f32),
            pltpu.VMEM((3, n_y, n_x), f32),
            pltpu.VMEM((4, n_z, n_y, n_x), f32),
            pltpu.VMEM((4, n_z, n_y, n_x), f32),
            pltpu.VMEM((3, n_z, n_y, n_x), f32),
            pltpu.VMEM((n_x, rows), f32),
            pltpu.VMEM((n_x, rows), f32),
            pltpu.VMEM((n_z, n_y + 2 * PAD, n_x), f32),
            pltpu.VMEM((1, n_y, n_x), f32),
            pltpu.SemaphoreType.DMA((N_REMOTE,)),
            pltpu.SemaphoreType.DMA((N_REMOTE,)),
            pltpu.SemaphoreType.DMA((10 + steps,)),
        ],
        compiler_params=pltpu.CompilerParams(
            collective_id=0, has_side_effects=True, vmem_limit_bytes=67043328
        ),
    )(
        adjoint_in, trajectory, courant, mixing, land_mask, source_mask,
        coag_rates, settle_speed, settle_class, emis_profile, emis_coef,
    )
    return pl.pallas_call(
        hand_over,
        out_shape=(
            jax.ShapeDtypeStruct(adj_out.shape, f32),
            jax.ShapeDtypeStruct(emis_out.shape, f32),
        ),
        in_specs=[hbm, hbm],
        out_specs=(hbm, hbm),
        scratch_shapes=[
            pltpu.VMEM(adj_out.shape, f32),
            pltpu.VMEM(emis_out.shape, f32),
            pltpu.SemaphoreType.DMA((4,)),
        ],
    )(adj_out, emis_out)


def solution(mesh):
    return jax.shard_map(
        shards,
        mesh=mesh,
        in_specs=(
            P(None, "lev", "lat", "lon"),
            P(None, None, "lev", "lat", "lon"),
            P(None, "lev", "lat", "lon"),
            P("lev", "lat", "lon"),
            P(),
            P(),
            P(),
            P(),
            P(),
            P("lat", "lon"),
            P("lat", "lon"),
        ),
        out_specs=(P(None, "lev", "lat", "lon"), P(None, "lat", "lon")),
        check_vma=False,
    )
```

```python
import jax
import jax.numpy as jnp
from jax import lax
from jax.experimental import pallas as pl
from jax.experimental.pallas import tpu as pltpu
from jax.sharding import PartitionSpec as P

MESH = pl.DeviceIdType.MESH
PAD = 8

S_LEV, S_UP, S_DOWN, S_RIGHT, S_LEFT = 0, 3, 6, 9, 12
S_EMIS, S_CE_R, S_CE_L, S_CN_U, S_CN_D, S_MIX = 15, 16, 17, 18, 19, 20
N_REMOTE = 21


def kernel(
    adj_hbm, traj_hbm, cour_hbm, mix_hbm, land_hbm, srcm_hbm,
    rates_hbm, speed_hbm, sclass_hbm, prof_hbm, ecoef_hbm,
    out_hbm, emis_hbm,
    out_ref, emis_ref, land_ref, srcm_ref, rates_ref, speed_ref, sclass_ref, prof_ref, ecoef_ref,
    traj_ref, cour_ref, mix_ref, pad_ref, lh_ref, at_ref, ht_ref, hb_ref, lv_ref, eo_ref, ep_ref,
    cx_ref, cy_ref, vc_ref, cet_ref, ceh_ref, cyp_ref, mh_ref,
    send_sem, recv_sem, local_sem,
):
    n_t, n_z, n_y, n_x = out_ref.shape
    steps = traj_hbm.shape[0]
    rows = n_z * n_y
    lon = lax.axis_index("lon")
    lat = lax.axis_index("lat")
    lev = lax.axis_index("lev")
    n_lon = lax.axis_size("lon")
    n_lat = lax.axis_size("lat")
    right = lax.rem(lon + 1, n_lon)
    left = lax.rem(lon + n_lon - 1, n_lon)
    has_up = lat < n_lat - 1
    has_down = lat > 0
    up = jnp.minimum(lat + 1, n_lat - 1)
    down = jnp.maximum(lat - 1, 0)
    partner = 1 - lev
    low_half = lev == 0
    edge_z = jnp.where(low_half, n_z - 1, 0)
    inner_z = jnp.where(low_half, n_z - 2, 1)
    level0 = lev * n_z

    adj_in = pltpu.make_async_copy(adj_hbm, out_ref, local_sem.at[0])
    cour_in = pltpu.make_async_copy(cour_hbm, cour_ref, local_sem.at[1])
    mix_in = pltpu.make_async_copy(mix_hbm, mix_ref, local_sem.at[2])
    traj_in = [
        pltpu.make_async_copy(traj_hbm.at[k], traj_ref.at[k], local_sem.at[3 + k]) for k in range(steps)
    ]
    small_in = [
        pltpu.make_async_copy(src, dst, local_sem.at[3 + steps + i])
        for i, (src, dst) in enumerate(
            (
                (rates_hbm, rates_ref),
                (speed_hbm, speed_ref),
                (sclass_hbm, sclass_ref),
                (prof_hbm, prof_ref),
                (ecoef_hbm, ecoef_ref),
                (land_hbm, land_ref),
                (srcm_hbm, srcm_ref),
            )
        )
    ]
    for c in small_in:
        c.start()
    cour_in.start()
    mix_in.start()
    adj_in.start()
    for k in range(steps - 1, -1, -1):
        traj_in[k].start()

    zeros_pad = jnp.zeros((n_t, n_z, PAD, n_x), jnp.float32)
    for k in range(steps):
        pad_ref[k, :, :, 0:PAD, :] = zeros_pad
        pad_ref[k, :, :, PAD + n_y : 2 * PAD + n_y, :] = zeros_pad
        lh_ref[k] = zeros_pad
    zeros_c = jnp.zeros((n_z, PAD, n_x), jnp.float32)
    cyp_ref[:, 0:PAD, :] = zeros_c
    cyp_ref[:, PAD + n_y : 2 * PAD + n_y, :] = zeros_c

    def rcopy(src, dst, idx, dev):
        return pltpu.make_async_remote_copy(
            src, dst, send_sem.at[idx], recv_sem.at[idx], device_id=dev, device_id_type=MESH
        )

    lane = lax.broadcasted_iota(jnp.int32, (n_y, n_x), 1)
    row = lax.broadcasted_iota(jnp.int32, (n_y, n_x), 0)

    cour_in.wait()
    mix_in.wait()
    for c in small_in:
        c.wait()
    top_row = jnp.logical_and(lat == n_lat - 1, row == n_y - 1)
    for z in range(n_z):
        cyp_ref[z, PAD : PAD + n_y, :] = jnp.where(top_row, 0.0, cour_ref[1, z])
    cet_ref[...] = cour_ref[0].reshape(rows, n_x).T
    ce_right = rcopy(cet_ref.at[pl.ds(n_x - 2, 2), :], ceh_ref.at[pl.ds(n_x - 2, 2), :], S_CE_R, (right, lat, lev))
    ce_left = rcopy(cet_ref.at[pl.ds(0, 2), :], ceh_ref.at[pl.ds(0, 2), :], S_CE_L, (left, lat, lev))
    cn_up = rcopy(
        cyp_ref.at[:, pl.ds(PAD + n_y - 2, 2), :], cyp_ref.at[:, pl.ds(PAD - 2, 2), :], S_CN_U, (lon, up, lev)
    )
    cn_down = rcopy(
        cyp_ref.at[:, pl.ds(PAD, 2), :], cyp_ref.at[:, pl.ds(PAD + n_y, 2), :], S_CN_D, (lon, down, lev)
    )
    mix_x = rcopy(mix_ref.at[pl.ds(edge_z, 1)], mh_ref, S_MIX, (lon, lat, partner))

    def start_coefficient_halos():
        mix_x.start()
        ce_right.start()
        ce_left.start()

        @pl.when(has_up)
        def _():
            cn_up.start()

        @pl.when(has_down)
        def _():
            cn_down.start()

    def fix_vertical_coefficients():
        mix_x.wait()
        below = jnp.where(low_half, vc_ref[1, 0], mh_ref[0])
        vc_ref[1, 0] = below
        vc_ref[2, 0] = jnp.where(low_half, vc_ref[2, 0], 1.0 - vc_ref[0, 0] - below)

    def build_vertical_coefficients():
        dep = jnp.where(low_half, 0.1 + 0.3 * land_ref[...].astype(jnp.float32), 0.0)
        below = jnp.zeros((n_y, n_x), jnp.float32)
        for z in range(n_z):
            above = mix_ref[z]
            if z == n_z - 1:
                above = jnp.where(low_half, above, 0.0)
            base = 1.0 - above - below
            if z == 0:
                base = base - dep
            vc_ref[0, z] = above
            vc_ref[1, z] = below
            vc_ref[2, z] = base
            below = above

    def build_transport_coefficients():
        ce_right.wait()
        ce_left.wait()

        @pl.when(has_up)
        def _():
            cn_up.wait_send()
            cn_down.wait_recv()

        @pl.when(has_down)
        def _():
            cn_down.wait_send()
            cn_up.wait_recv()

        he = ceh_ref[...].T.reshape(n_z, n_y, n_x)
        for z in range(n_z):
            c = cour_ref[0, z]
            hz = he[z]
            c_p1 = jnp.where(lane == n_x - 1, pltpu.roll(hz, n_x - 1, 1), pltpu.roll(c, n_x - 1, 1))
            c_m1 = jnp.where(lane == 0, pltpu.roll(hz, 1, 1), pltpu.roll(c, 1, 1))
            c_m2 = jnp.where(lane <= 1, pltpu.roll(hz, 2, 1), pltpu.roll(c, 2, 1))
            cx_ref[0, z] = -1.5 * jnp.maximum(c, 0.0)
            cx_ref[1, z] = 0.5 * jnp.maximum(c_p1, 0.0)
            cx_ref[2, z] = -1.5 * jnp.minimum(c_m1, 0.0)
            cx_ref[3, z] = 0.5 * jnp.minimum(c_m2, 0.0)
            cy_ref[0, z] = -1.5 * jnp.maximum(cyp_ref[z, PAD : PAD + n_y, :], 0.0)
            cy_ref[1, z] = 0.5 * jnp.maximum(cyp_ref[z, PAD + 1 : PAD + 1 + n_y, :], 0.0)
            cy_ref[2, z] = -1.5 * jnp.minimum(cyp_ref[z, PAD - 1 : PAD - 1 + n_y, :], 0.0)
            cy_ref[3, z] = 0.5 * jnp.minimum(cyp_ref[z, PAD - 2 : PAD - 2 + n_y, :], 0.0)

    eo_ref[...] = jnp.zeros(eo_ref.shape, jnp.float32)
    src_mask = srcm_ref[...].astype(jnp.float32)
    adj_in.wait()
    build_vertical_coefficients()
    emis_copy = rcopy(eo_ref, ep_ref, S_EMIS, (lon, lat, partner))

    for k in range(steps - 1, -1, -1):
        first = k == steps - 1
        traj_in[k].wait()

        def coag_level(zz, acc):
            z = jnp.where(low_half, n_z - 1 - zz, zz)
            zg = level0 + z
            lam = [out_ref[t, z] for t in range(n_t)]
            st = [traj_ref[k, t, z].astype(jnp.float32) for t in range(n_t)]
            new_acc = []
            for m in range(3):
                part = acc[m]
                for j in range(3):
                    part = part + (ecoef_ref[3 * m + j] * prof_ref[zg]) * lam[3 * m + j]
                new_acc.append(part)
            k0, k1, k2, k01, k02, k12 = [rates_ref[i, zg] for i in range(6)]
            n0, v0, w0, n1, v1, w1, n2, v2, w2 = st
            ln0, lv0, lw0, ln1, lv1, lw1, ln2, lv2, lw2 = lam
            a01 = k01 * n1
            a02 = k02 * n2
            a12 = k12 * n2
            s0 = a01 + a02
            g_n0 = ln0 * (-2.0 * k0 * n0 - s0)
            g_v0 = (
                (lv1 * a01 + lv2 * a02 - lv0 * s0)
                + 2.0 * (lw0 * (k0 * v0) + lw1 * (k01 * v1) + lw2 * (k02 * v2))
            )
            g_w0 = lw1 * a01 + lw2 * a02 - lw0 * s0
            g_n1 = (
                ln1 * (-2.0 * k1 * n1 - a12)
                - ln0 * (k01 * n0)
                + (lv1 - lv0) * (k01 * v0)
                + (lw1 - lw0) * (k01 * w0)
            )
            g_v1 = (lv2 - lv1) * a12 + 2.0 * (lw1 * (k1 * v1 + k01 * v0) + lw2 * (k12 * v2))
            g_w1 = (lw2 - lw1) * a12
            g_n2 = (
                -2.0 * k2 * n2 * ln2
                - ln0 * (k02 * n0)
                - ln1 * (k12 * n1)
                + (lv2 - lv0) * (k02 * v0)
                + (lv2 - lv1) * (k12 * v1)
                + (lw2 - lw0) * (k02 * w0)
                + (lw2 - lw1) * (k12 * w1)
            )
            g_v2 = 2.0 * lw2 * (k2 * v2 + k02 * v0 + k12 * v1)
            grads = [g_n0, g_v0, g_w0, g_n1, g_v1, g_w1, g_n2, g_v2]
            for t in range(n_t - 1):
                out_ref[t, z] = lam[t] + grads[t]
            return tuple(new_acc)

        zero = jnp.zeros((n_y, n_x), jnp.float32)
        acc = coag_level(0, (zero, zero, zero))
        lev_copy = rcopy(out_ref.at[:, pl.ds(edge_z, 1)], lv_ref.at[k], S_LEV + k, (lon, lat, partner))
        if not first:
            lev_copy.start()
        acc = lax.fori_loop(1, n_z, coag_level, acc)
        for m in range(3):
            eo_ref[m] = eo_ref[m] + acc[m] * src_mask
        if k == 0:
            emis_copy.start()

        def vert_inner(t, carry):
            col = [out_ref[t, z] for z in range(n_z)]
            for z in range(n_z):
                s = speed_ref[sclass_ref[level0 + z], t]
                val = col[z] * (vc_ref[2, z] - s)
                if z > 0:
                    val = val + col[z - 1] * (vc_ref[1, z] + s)
                if z < n_z - 1:
                    val = val + col[z + 1] * vc_ref[0, z]
                pad_ref[k, t, z, PAD : PAD + n_y, :] = val
            return carry

        lax.fori_loop(0, n_t, vert_inner, 0)
        if first:
            barrier = pltpu.get_barrier_semaphore()
            for dev in ((lon, lat, partner), (left, lat, lev), (right, lat, lev)):
                pl.semaphore_signal(barrier, 1, device_id=dev, device_id_type=MESH)

            @pl.when(has_up)
            def _():
                pl.semaphore_signal(barrier, 1, device_id=(lon, up, lev), device_id_type=MESH)

            @pl.when(has_down)
            def _():
                pl.semaphore_signal(barrier, 1, device_id=(lon, down, lev), device_id_type=MESH)

            pl.semaphore_wait(barrier, 3 + has_up.astype(jnp.int32) + has_down.astype(jnp.int32))
            start_coefficient_halos()
            lev_copy.start()
            fix_vertical_coefficients()
        lev_copy.wait()

        lat_up = rcopy(
            pad_ref.at[k, :, :, pl.ds(PAD + n_y - 2, 2), :],
            lh_ref.at[k, :, :, pl.ds(0, 2), :],
            S_UP + k,
            (lon, up, lev),
        )
        lat_down = rcopy(
            pad_ref.at[k, :, :, pl.ds(PAD, 2), :],
            lh_ref.at[k, :, :, pl.ds(2, 2), :],
            S_DOWN + k,
            (lon, down, lev),
        )
        lon_right = rcopy(
            at_ref.at[k, pl.ds(n_x - 2, 2), :], ht_ref.at[k, pl.ds(n_x - 2, 2), :], S_RIGHT + k, (right, lat, lev)
        )
        lon_left = rcopy(
            at_ref.at[k, pl.ds(0, 2), :], ht_ref.at[k, pl.ds(0, 2), :], S_LEFT + k, (left, lat, lev)
        )

        for t in range(n_t):
            z = edge_z
            s = speed_ref[sclass_ref[level0 + z], t]
            a = out_ref[t, z]
            other = out_ref[t, inner_z]
            halo = lv_ref[k, t, 0]
            a_below = jnp.where(low_half, other, halo)
            a_above = jnp.where(low_half, halo, other)
            pad_ref[k, t, z, PAD : PAD + n_y, :] = (
                a * (vc_ref[2, z] - s) + a_below * (vc_ref[1, z] + s) + a_above * vc_ref[0, z]
            )
            up_t = rcopy(
                pad_ref.at[k, t, :, pl.ds(PAD + n_y - 2, 2), :],
                lh_ref.at[k, t, :, pl.ds(0, 2), :],
                S_UP + k,
                (lon, up, lev),
            )
            down_t = rcopy(
                pad_ref.at[k, t, :, pl.ds(PAD, 2), :],
                lh_ref.at[k, t, :, pl.ds(2, 2), :],
                S_DOWN + k,
                (lon, down, lev),
            )

            @pl.when(has_up)
            def _():
                up_t.start()

            @pl.when(has_down)
            def _():
                down_t.start()

            blk = pad_ref[k, t, :, PAD : PAD + n_y, :].reshape(rows, n_x)
            cols = pl.ds(t * rows, rows)
            at_ref[k, :, cols] = blk.T
            rcopy(
                at_ref.at[k, pl.ds(n_x - 2, 2), cols], ht_ref.at[k, pl.ds(n_x - 2, 2), cols], S_RIGHT + k,
                (right, lat, lev),
            ).start()
            rcopy(
                at_ref.at[k, pl.ds(0, 2), cols], ht_ref.at[k, pl.ds(0, 2), cols], S_LEFT + k, (left, lat, lev)
            ).start()

        if k == steps - 1:
            build_transport_coefficients()

        def transport(i, carry):
            t = i // n_z
            z = i % n_z
            a = pad_ref[k, t, z, PAD : PAD + n_y, :]
            y_p1 = pad_ref[k, t, z, PAD + 1 : PAD + 1 + n_y, :]
            y_p2 = pad_ref[k, t, z, PAD + 2 : PAD + 2 + n_y, :]
            y_m1 = pad_ref[k, t, z, PAD - 1 : PAD - 1 + n_y, :]
            y_m2 = pad_ref[k, t, z, PAD - 2 : PAD - 2 + n_y, :]
            x_p1 = pltpu.roll(a, n_x - 1, 1)
            x_p2 = pltpu.roll(a, n_x - 2, 1)
            x_m1 = pltpu.roll(a, 1, 1)
            x_m2 = pltpu.roll(a, 2, 1)
            lon_part = (
                cx_ref[0, z] * (a - x_p1)
                + cx_ref[1, z] * (x_p1 - x_p2)
                + cx_ref[2, z] * (x_m1 - a)
                + cx_ref[3, z] * (x_m2 - x_m1)
            )
            lat_part = (
                cy_ref[0, z] * (a - y_p1)
                + cy_ref[1, z] * (y_p1 - y_p2)
                + cy_ref[2, z] * (y_m1 - a)
                + cy_ref[3, z] * (y_m2 - y_m1)
            )
            out_ref[t, z] = a + lon_part + lat_part
            return carry

        lax.fori_loop(0, n_t * n_z, transport, 0, unroll=4)

        lon_right.wait()
        lon_left.wait()

        @pl.when(has_up)
        def _():
            lat_up.wait_send()
            lat_down.wait_recv()

        @pl.when(has_down)
        def _():
            lat_down.wait_send()
            lat_up.wait_recv()

        for t in range(n_t):
            hb_ref[t] = ht_ref[k, :, t * rows : (t + 1) * rows].T.reshape(n_z, n_y, n_x)

        def edges(i, carry):
            t = i // n_z
            z = i % n_z
            a = pad_ref[k, t, z, PAD : PAD + n_y, :]
            d = hb_ref[t, z] - a
            d_m1 = pltpu.roll(d, 1, 1)
            d_m2 = pltpu.roll(d, 2, 1)
            d_p1 = pltpu.roll(d, n_x - 1, 1)
            d_p2 = pltpu.roll(d, n_x - 2, 1)
            cx0 = cx_ref[0, z]
            cx1 = cx_ref[1, z]
            cxm1 = cx_ref[2, z]
            cxm2 = cx_ref[3, z]
            low = cxm2 * d_m2 + jnp.where(lane == 0, (cxm1 - cxm2) * d_m1, 0.0)
            high = jnp.where(lane == n_x - 1, (cx1 - cx0) * d_p1, 0.0) - cx1 * d_p2
            corr = jnp.where(lane <= 1, low, jnp.where(lane >= n_x - 2, high, 0.0))
            out_ref[t, z] = out_ref[t, z] + corr
            h = lh_ref[k, t, z, 0:4, :]
            am2 = h[0:1]
            am1 = h[1:2]
            ap1 = h[2:3]
            ap2 = h[3:4]
            c_lo = cy_ref[:, z, 0:2, :]
            c_hi = cy_ref[:, z, n_y - 2 : n_y, :]
            r0 = c_lo[2, 0:1] * am1 + c_lo[3, 0:1] * (am2 - am1)
            r1 = c_lo[3, 1:2] * am1
            r14 = -c_hi[1, 0:1] * ap1
            r15 = c_hi[1, 1:2] * (ap1 - ap2) - c_hi[0, 1:2] * ap1
            out_ref[t, z, 0:2, :] = out_ref[t, z, 0:2, :] + jnp.concatenate([r0, r1], axis=0)
            out_ref[t, z, n_y - 2 : n_y, :] = out_ref[t, z, n_y - 2 : n_y, :] + jnp.concatenate([r14, r15], axis=0)
            return carry

        lax.fori_loop(0, n_t * n_z, edges, 0, unroll=4)

    emis_copy.wait()
    emis_ref[...] = eo_ref[...] + ep_ref[...]
    out_copy = pltpu.make_async_copy(out_ref, out_hbm, local_sem.at[0])
    emis_out = pltpu.make_async_copy(emis_ref, emis_hbm, local_sem.at[1])
    out_copy.start()
    emis_out.start()
    out_copy.wait()
    emis_out.wait()


def hand_over(adj_hbm, emis_hbm, adj_out, emis_out, adj_buf, emis_buf, sem):
    ins = [
        pltpu.make_async_copy(adj_hbm, adj_buf, sem.at[0]),
        pltpu.make_async_copy(emis_hbm, emis_buf, sem.at[1]),
    ]
    for c in ins:
        c.start()
    outs = [
        pltpu.make_async_copy(adj_buf, adj_out, sem.at[2]),
        pltpu.make_async_copy(emis_buf, emis_out, sem.at[3]),
    ]
    for c, o in zip(ins, outs):
        c.wait()
        o.start()
    for o in outs:
        o.wait()


def shards(
    adjoint_in,
    trajectory,
    courant,
    mixing,
    coag_rates,
    settle_speed,
    settle_class,
    emis_profile,
    emis_coef,
    land_mask,
    source_mask,
):
    n_t, n_z, n_y, n_x = adjoint_in.shape
    steps = trajectory.shape[0]
    rows = n_z * n_y
    hbm = pl.BlockSpec(memory_space=pl.ANY)
    vmem = pl.BlockSpec(memory_space=pltpu.VMEM)
    smem = pl.BlockSpec(memory_space=pltpu.SMEM)
    f32 = jnp.float32
    adj_out, emis_out = pl.pallas_call(
        kernel,
        out_shape=(
            jax.ShapeDtypeStruct(adjoint_in.shape, f32),
            jax.ShapeDtypeStruct((3, n_y, n_x), f32),
        ),
        in_specs=[hbm] * 11,
        out_specs=(hbm, hbm),
        scratch_shapes=[
            pltpu.VMEM(adjoint_in.shape, f32),
            pltpu.VMEM((3, n_y, n_x), f32),
            pltpu.VMEM(land_mask.shape, land_mask.dtype),
            pltpu.VMEM(source_mask.shape, source_mask.dtype),
            pltpu.SMEM(coag_rates.shape, f32),
            pltpu.SMEM(settle_speed.shape, f32),
            pltpu.SMEM(settle_class.shape, settle_class.dtype),
            pltpu.SMEM(emis_profile.shape, f32),
            pltpu.SMEM(emis_coef.shape, f32),
            pltpu.VMEM(trajectory.shape, trajectory.dtype),
            pltpu.VMEM(courant.shape, f32),
            pltpu.VMEM(mixing.shape, f32),
            pltpu.VMEM((steps, n_t, n_z, n_y + 2 * PAD, n_x), f32),
            pltpu.VMEM((steps, n_t, n_z, PAD, n_x), f32),
            pltpu.VMEM((steps, n_x, n_t * rows), f32),
            pltpu.VMEM((steps, n_x, n_t * rows), f32),
            pltpu.VMEM((n_t, n_z, n_y, n_x), f32),
            pltpu.VMEM((steps, n_t, 1, n_y, n_x), f32),
            pltpu.VMEM((3, n_y, n_x), f32),
            pltpu.VMEM((3, n_y, n_x), f32),
            pltpu.VMEM((4, n_z, n_y, n_x), f32),
            pltpu.VMEM((4, n_z, n_y, n_x), f32),
            pltpu.VMEM((3, n_z, n_y, n_x), f32),
            pltpu.VMEM((n_x, rows), f32),
            pltpu.VMEM((n_x, rows), f32),
            pltpu.VMEM((n_z, n_y + 2 * PAD, n_x), f32),
            pltpu.VMEM((1, n_y, n_x), f32),
            pltpu.SemaphoreType.DMA((N_REMOTE,)),
            pltpu.SemaphoreType.DMA((N_REMOTE,)),
            pltpu.SemaphoreType.DMA((10 + steps,)),
        ],
        compiler_params=pltpu.CompilerParams(
            collective_id=0, has_side_effects=True, vmem_limit_bytes=67043328
        ),
    )(
        adjoint_in, trajectory, courant, mixing, land_mask, source_mask,
        coag_rates, settle_speed, settle_class, emis_profile, emis_coef,
    )
    return pl.pallas_call(
        hand_over,
        out_shape=(
            jax.ShapeDtypeStruct(adj_out.shape, f32),
            jax.ShapeDtypeStruct(emis_out.shape, f32),
        ),
        in_specs=[hbm, hbm],
        out_specs=(hbm, hbm),
        scratch_shapes=[
            pltpu.VMEM(adj_out.shape, f32),
            pltpu.VMEM(emis_out.shape, f32),
            pltpu.SemaphoreType.DMA((4,)),
        ],
    )(adj_out, emis_out)


def solution(mesh):
    return jax.shard_map(
        shards,
        mesh=mesh,
        in_specs=(
            P(None, "lev", "lat", "lon"),
            P(None, None, "lev", "lat", "lon"),
            P(None, "lev", "lat", "lon"),
            P("lev", "lat", "lon"),
            P(),
            P(),
            P(),
            P(),
            P(),
            P("lat", "lon"),
            P("lat", "lon"),
        ),
        out_specs=(P(None, "lev", "lat", "lon"), P(None, "lat", "lon")),
        check_vma=False,
    )
```

```python
import jax
import jax.numpy as jnp
from jax import lax
from jax.experimental import pallas as pl
from jax.experimental.pallas import tpu as pltpu
from jax.sharding import PartitionSpec as P

MESH = pl.DeviceIdType.MESH
PAD = 8

S_LEV, S_UP, S_DOWN, S_RIGHT, S_LEFT = 0, 3, 6, 9, 12
S_EMIS, S_CE_R, S_CE_L, S_CN_U, S_CN_D, S_MIX = 15, 16, 17, 18, 19, 20
N_REMOTE = 21


def kernel(
    adj_hbm, traj_hbm, cour_hbm, mix_hbm, land_hbm, srcm_hbm,
    rates_hbm, speed_hbm, sclass_hbm, prof_hbm, ecoef_hbm,
    out_hbm, emis_hbm,
    out_ref, emis_ref, land_ref, srcm_ref, rates_ref, speed_ref, sclass_ref, prof_ref, ecoef_ref,
    traj_ref, cour_ref, mix_ref, pad_ref, lh_ref, at_ref, ht_ref, hb_ref, lv_ref, eo_ref, ep_ref,
    cx_ref, cy_ref, vc_ref, cet_ref, ceh_ref, cyp_ref, mh_ref,
    send_sem, recv_sem, local_sem,
):
    n_t, n_z, n_y, n_x = out_ref.shape
    steps = traj_hbm.shape[0]
    rows = n_z * n_y
    lon = lax.axis_index("lon")
    lat = lax.axis_index("lat")
    lev = lax.axis_index("lev")
    n_lon = lax.axis_size("lon")
    n_lat = lax.axis_size("lat")
    right = lax.rem(lon + 1, n_lon)
    left = lax.rem(lon + n_lon - 1, n_lon)
    has_up = lat < n_lat - 1
    has_down = lat > 0
    up = jnp.minimum(lat + 1, n_lat - 1)
    down = jnp.maximum(lat - 1, 0)
    partner = 1 - lev
    low_half = lev == 0
    edge_z = jnp.where(low_half, n_z - 1, 0)
    inner_z = jnp.where(low_half, n_z - 2, 1)
    level0 = lev * n_z

    adj_in = pltpu.make_async_copy(adj_hbm, out_ref, local_sem.at[0])
    cour_in = pltpu.make_async_copy(cour_hbm, cour_ref, local_sem.at[1])
    mix_in = pltpu.make_async_copy(mix_hbm, mix_ref, local_sem.at[2])
    traj_in = [
        pltpu.make_async_copy(traj_hbm.at[k], traj_ref.at[k], local_sem.at[3 + k]) for k in range(steps)
    ]
    small_in = [
        pltpu.make_async_copy(src, dst, local_sem.at[3 + steps + i])
        for i, (src, dst) in enumerate(
            (
                (rates_hbm, rates_ref),
                (speed_hbm, speed_ref),
                (sclass_hbm, sclass_ref),
                (prof_hbm, prof_ref),
                (ecoef_hbm, ecoef_ref),
                (land_hbm, land_ref),
                (srcm_hbm, srcm_ref),
            )
        )
    ]
    for c in small_in:
        c.start()
    cour_in.start()
    mix_in.start()
    adj_in.start()
    for k in range(steps - 1, -1, -1):
        traj_in[k].start()

    zeros_pad = jnp.zeros((n_t, n_z, PAD, n_x), jnp.float32)
    for k in range(steps):
        pad_ref[k, :, :, 0:PAD, :] = zeros_pad
        pad_ref[k, :, :, PAD + n_y : 2 * PAD + n_y, :] = zeros_pad
        lh_ref[k] = zeros_pad
    zeros_c = jnp.zeros((n_z, PAD, n_x), jnp.float32)
    cyp_ref[:, 0:PAD, :] = zeros_c
    cyp_ref[:, PAD + n_y : 2 * PAD + n_y, :] = zeros_c

    def rcopy(src, dst, idx, dev):
        return pltpu.make_async_remote_copy(
            src, dst, send_sem.at[idx], recv_sem.at[idx], device_id=dev, device_id_type=MESH
        )

    lane = lax.broadcasted_iota(jnp.int32, (n_y, n_x), 1)
    row = lax.broadcasted_iota(jnp.int32, (n_y, n_x), 0)

    cour_in.wait()
    mix_in.wait()
    for c in small_in:
        c.wait()
    top_row = jnp.logical_and(lat == n_lat - 1, row == n_y - 1)
    for z in range(n_z):
        cyp_ref[z, PAD : PAD + n_y, :] = jnp.where(top_row, 0.0, cour_ref[1, z])
    cet_ref[...] = cour_ref[0].reshape(rows, n_x).T
    ce_right = rcopy(cet_ref.at[pl.ds(n_x - 2, 2), :], ceh_ref.at[pl.ds(n_x - 2, 2), :], S_CE_R, (right, lat, lev))
    ce_left = rcopy(cet_ref.at[pl.ds(0, 2), :], ceh_ref.at[pl.ds(0, 2), :], S_CE_L, (left, lat, lev))
    cn_up = rcopy(
        cyp_ref.at[:, pl.ds(PAD + n_y - 2, 2), :], cyp_ref.at[:, pl.ds(PAD - 2, 2), :], S_CN_U, (lon, up, lev)
    )
    cn_down = rcopy(
        cyp_ref.at[:, pl.ds(PAD, 2), :], cyp_ref.at[:, pl.ds(PAD + n_y, 2), :], S_CN_D, (lon, down, lev)
    )
    mix_x = rcopy(mix_ref.at[pl.ds(edge_z, 1)], mh_ref, S_MIX, (lon, lat, partner))

    def start_coefficient_halos():
        mix_x.start()
        ce_right.start()
        ce_left.start()

        @pl.when(has_up)
        def _():
            cn_up.start()

        @pl.when(has_down)
        def _():
            cn_down.start()

    def fix_vertical_coefficients():
        mix_x.wait()
        below = jnp.where(low_half, vc_ref[1, 0], mh_ref[0])
        vc_ref[1, 0] = below
        vc_ref[2, 0] = jnp.where(low_half, vc_ref[2, 0], 1.0 - vc_ref[0, 0] - below)

    def build_vertical_coefficients():
        dep = jnp.where(low_half, 0.1 + 0.3 * land_ref[...].astype(jnp.float32), 0.0)
        below = jnp.zeros((n_y, n_x), jnp.float32)
        for z in range(n_z):
            above = mix_ref[z]
            if z == n_z - 1:
                above = jnp.where(low_half, above, 0.0)
            base = 1.0 - above - below
            if z == 0:
                base = base - dep
            vc_ref[0, z] = above
            vc_ref[1, z] = below
            vc_ref[2, z] = base
            below = above

    def build_transport_coefficients():
        ce_right.wait()
        ce_left.wait()

        @pl.when(has_up)
        def _():
            cn_up.wait_send()
            cn_down.wait_recv()

        @pl.when(has_down)
        def _():
            cn_down.wait_send()
            cn_up.wait_recv()

        he = ceh_ref[...].T.reshape(n_z, n_y, n_x)
        for z in range(n_z):
            c = cour_ref[0, z]
            hz = he[z]
            c_p1 = jnp.where(lane == n_x - 1, pltpu.roll(hz, n_x - 1, 1), pltpu.roll(c, n_x - 1, 1))
            c_m1 = jnp.where(lane == 0, pltpu.roll(hz, 1, 1), pltpu.roll(c, 1, 1))
            c_m2 = jnp.where(lane <= 1, pltpu.roll(hz, 2, 1), pltpu.roll(c, 2, 1))
            cx_ref[0, z] = -1.5 * jnp.maximum(c, 0.0)
            cx_ref[1, z] = 0.5 * jnp.maximum(c_p1, 0.0)
            cx_ref[2, z] = -1.5 * jnp.minimum(c_m1, 0.0)
            cx_ref[3, z] = 0.5 * jnp.minimum(c_m2, 0.0)
            cy_ref[0, z] = -1.5 * jnp.maximum(cyp_ref[z, PAD : PAD + n_y, :], 0.0)
            cy_ref[1, z] = 0.5 * jnp.maximum(cyp_ref[z, PAD + 1 : PAD + 1 + n_y, :], 0.0)
            cy_ref[2, z] = -1.5 * jnp.minimum(cyp_ref[z, PAD - 1 : PAD - 1 + n_y, :], 0.0)
            cy_ref[3, z] = 0.5 * jnp.minimum(cyp_ref[z, PAD - 2 : PAD - 2 + n_y, :], 0.0)

    eo_ref[...] = jnp.zeros(eo_ref.shape, jnp.float32)
    src_mask = srcm_ref[...].astype(jnp.float32)
    adj_in.wait()
    build_vertical_coefficients()
    emis_copy = rcopy(eo_ref, ep_ref, S_EMIS, (lon, lat, partner))

    for k in range(steps - 1, -1, -1):
        first = k == steps - 1
        traj_in[k].wait()

        def coag_level(zz, acc):
            z = jnp.where(low_half, n_z - 1 - zz, zz)
            zg = level0 + z
            lam = [out_ref[t, z] for t in range(n_t)]
            st = [traj_ref[k, t, z].astype(jnp.float32) for t in range(n_t)]
            new_acc = []
            for m in range(3):
                part = acc[m]
                for j in range(3):
                    part = part + (ecoef_ref[3 * m + j] * prof_ref[zg]) * lam[3 * m + j]
                new_acc.append(part)
            k0, k1, k2, k01, k02, k12 = [rates_ref[i, zg] for i in range(6)]
            n0, v0, w0, n1, v1, w1, n2, v2, w2 = st
            ln0, lv0, lw0, ln1, lv1, lw1, ln2, lv2, lw2 = lam
            a01 = k01 * n1
            a02 = k02 * n2
            a12 = k12 * n2
            s0 = a01 + a02
            g_n0 = ln0 * (-2.0 * k0 * n0 - s0)
            g_v0 = (
                (lv1 * a01 + lv2 * a02 - lv0 * s0)
                + 2.0 * (lw0 * (k0 * v0) + lw1 * (k01 * v1) + lw2 * (k02 * v2))
            )
            g_w0 = lw1 * a01 + lw2 * a02 - lw0 * s0
            g_n1 = (
                ln1 * (-2.0 * k1 * n1 - a12)
                - ln0 * (k01 * n0)
                + (lv1 - lv0) * (k01 * v0)
                + (lw1 - lw0) * (k01 * w0)
            )
            g_v1 = (lv2 - lv1) * a12 + 2.0 * (lw1 * (k1 * v1 + k01 * v0) + lw2 * (k12 * v2))
            g_w1 = (lw2 - lw1) * a12
            g_n2 = (
                -2.0 * k2 * n2 * ln2
                - ln0 * (k02 * n0)
                - ln1 * (k12 * n1)
                + (lv2 - lv0) * (k02 * v0)
                + (lv2 - lv1) * (k12 * v1)
                + (lw2 - lw0) * (k02 * w0)
                + (lw2 - lw1) * (k12 * w1)
            )
            g_v2 = 2.0 * lw2 * (k2 * v2 + k02 * v0 + k12 * v1)
            grads = [g_n0, g_v0, g_w0, g_n1, g_v1, g_w1, g_n2, g_v2]
            for t in range(n_t - 1):
                out_ref[t, z] = lam[t] + grads[t]
            return tuple(new_acc)

        zero = jnp.zeros((n_y, n_x), jnp.float32)
        acc = coag_level(0, (zero, zero, zero))
        lev_copy = rcopy(out_ref.at[:, pl.ds(edge_z, 1)], lv_ref.at[k], S_LEV + k, (lon, lat, partner))
        if not first:
            lev_copy.start()
        acc = lax.fori_loop(1, n_z, coag_level, acc)
        for m in range(3):
            eo_ref[m] = eo_ref[m] + acc[m] * src_mask
        if k == 0:
            emis_copy.start()

        def vert_inner(t, carry):
            col = [out_ref[t, z] for z in range(n_z)]
            for z in range(n_z):
                s = speed_ref[sclass_ref[level0 + z], t]
                val = col[z] * (vc_ref[2, z] - s)
                if z > 0:
                    val = val + col[z - 1] * (vc_ref[1, z] + s)
                if z < n_z - 1:
                    val = val + col[z + 1] * vc_ref[0, z]
                pad_ref[k, t, z, PAD : PAD + n_y, :] = val
            return carry

        lax.fori_loop(0, n_t, vert_inner, 0)
        if first:
            barrier = pltpu.get_barrier_semaphore()
            for dev in ((lon, lat, partner), (left, lat, lev), (right, lat, lev)):
                pl.semaphore_signal(barrier, 1, device_id=dev, device_id_type=MESH)

            @pl.when(has_up)
            def _():
                pl.semaphore_signal(barrier, 1, device_id=(lon, up, lev), device_id_type=MESH)

            @pl.when(has_down)
            def _():
                pl.semaphore_signal(barrier, 1, device_id=(lon, down, lev), device_id_type=MESH)

            pl.semaphore_wait(barrier, 3 + has_up.astype(jnp.int32) + has_down.astype(jnp.int32))
            start_coefficient_halos()
            lev_copy.start()
            fix_vertical_coefficients()
        lev_copy.wait()

        lat_up = rcopy(
            pad_ref.at[k, :, :, pl.ds(PAD + n_y - 2, 2), :],
            lh_ref.at[k, :, :, pl.ds(0, 2), :],
            S_UP + k,
            (lon, up, lev),
        )
        lat_down = rcopy(
            pad_ref.at[k, :, :, pl.ds(PAD, 2), :],
            lh_ref.at[k, :, :, pl.ds(2, 2), :],
            S_DOWN + k,
            (lon, down, lev),
        )
        lon_right = rcopy(
            at_ref.at[k, pl.ds(n_x - 2, 2), :], ht_ref.at[k, pl.ds(n_x - 2, 2), :], S_RIGHT + k, (right, lat, lev)
        )
        lon_left = rcopy(
            at_ref.at[k, pl.ds(0, 2), :], ht_ref.at[k, pl.ds(0, 2), :], S_LEFT + k, (left, lat, lev)
        )

        for t in range(n_t):
            z = edge_z
            s = speed_ref[sclass_ref[level0 + z], t]
            a = out_ref[t, z]
            other = out_ref[t, inner_z]
            halo = lv_ref[k, t, 0]
            a_below = jnp.where(low_half, other, halo)
            a_above = jnp.where(low_half, halo, other)
            pad_ref[k, t, z, PAD : PAD + n_y, :] = (
                a * (vc_ref[2, z] - s) + a_below * (vc_ref[1, z] + s) + a_above * vc_ref[0, z]
            )
            up_t = rcopy(
                pad_ref.at[k, t, :, pl.ds(PAD + n_y - 2, 2), :],
                lh_ref.at[k, t, :, pl.ds(0, 2), :],
                S_UP + k,
                (lon, up, lev),
            )
            down_t = rcopy(
                pad_ref.at[k, t, :, pl.ds(PAD, 2), :],
                lh_ref.at[k, t, :, pl.ds(2, 2), :],
                S_DOWN + k,
                (lon, down, lev),
            )

            @pl.when(has_up)
            def _():
                up_t.start()

            @pl.when(has_down)
            def _():
                down_t.start()

            blk = pad_ref[k, t, :, PAD : PAD + n_y, :].reshape(rows, n_x)
            cols = pl.ds(t * rows, rows)
            at_ref[k, :, cols] = blk.T
            rcopy(
                at_ref.at[k, pl.ds(n_x - 2, 2), cols], ht_ref.at[k, pl.ds(n_x - 2, 2), cols], S_RIGHT + k,
                (right, lat, lev),
            ).start()
            rcopy(
                at_ref.at[k, pl.ds(0, 2), cols], ht_ref.at[k, pl.ds(0, 2), cols], S_LEFT + k, (left, lat, lev)
            ).start()

        if k == steps - 1:
            build_transport_coefficients()

        def transport(i, carry):
            t = i // n_z
            z = i % n_z
            a = pad_ref[k, t, z, PAD : PAD + n_y, :]
            y_p1 = pad_ref[k, t, z, PAD + 1 : PAD + 1 + n_y, :]
            y_p2 = pad_ref[k, t, z, PAD + 2 : PAD + 2 + n_y, :]
            y_m1 = pad_ref[k, t, z, PAD - 1 : PAD - 1 + n_y, :]
            y_m2 = pad_ref[k, t, z, PAD - 2 : PAD - 2 + n_y, :]
            x_p1 = pltpu.roll(a, n_x - 1, 1)
            x_p2 = pltpu.roll(a, n_x - 2, 1)
            x_m1 = pltpu.roll(a, 1, 1)
            x_m2 = pltpu.roll(a, 2, 1)
            lon_part = (
                cx_ref[0, z] * (a - x_p1)
                + cx_ref[1, z] * (x_p1 - x_p2)
                + cx_ref[2, z] * (x_m1 - a)
                + cx_ref[3, z] * (x_m2 - x_m1)
            )
            lat_part = (
                cy_ref[0, z] * (a - y_p1)
                + cy_ref[1, z] * (y_p1 - y_p2)
                + cy_ref[2, z] * (y_m1 - a)
                + cy_ref[3, z] * (y_m2 - y_m1)
            )
            out_ref[t, z] = a + lon_part + lat_part
            return carry

        lax.fori_loop(0, n_t * n_z, transport, 0, unroll=4)

        lon_right.wait()
        lon_left.wait()

        for t in range(n_t):
            hb_ref[t] = ht_ref[k, :, t * rows : (t + 1) * rows].T.reshape(n_z, n_y, n_x)

        def lon_edges(i, carry):
            t = i // n_z
            z = i % n_z
            a = pad_ref[k, t, z, PAD : PAD + n_y, :]
            d = hb_ref[t, z] - a
            d_m1 = pltpu.roll(d, 1, 1)
            d_m2 = pltpu.roll(d, 2, 1)
            d_p1 = pltpu.roll(d, n_x - 1, 1)
            d_p2 = pltpu.roll(d, n_x - 2, 1)
            cx0 = cx_ref[0, z]
            cx1 = cx_ref[1, z]
            cxm1 = cx_ref[2, z]
            cxm2 = cx_ref[3, z]
            low = cxm2 * d_m2 + jnp.where(lane == 0, (cxm1 - cxm2) * d_m1, 0.0)
            high = jnp.where(lane == n_x - 1, (cx1 - cx0) * d_p1, 0.0) - cx1 * d_p2
            corr = jnp.where(lane <= 1, low, jnp.where(lane >= n_x - 2, high, 0.0))
            out_ref[t, z] = out_ref[t, z] + corr
            return carry

        lax.fori_loop(0, n_t * n_z, lon_edges, 0, unroll=4)

        @pl.when(has_up)
        def _():
            lat_up.wait_send()
            lat_down.wait_recv()

        @pl.when(has_down)
        def _():
            lat_down.wait_send()
            lat_up.wait_recv()

        def lat_edges(i, carry):
            t = i // n_z
            z = i % n_z
            h = lh_ref[k, t, z, 0:4, :]
            am2 = h[0:1]
            am1 = h[1:2]
            ap1 = h[2:3]
            ap2 = h[3:4]
            c_lo = cy_ref[:, z, 0:2, :]
            c_hi = cy_ref[:, z, n_y - 2 : n_y, :]
            r0 = c_lo[2, 0:1] * am1 + c_lo[3, 0:1] * (am2 - am1)
            r1 = c_lo[3, 1:2] * am1
            r14 = -c_hi[1, 0:1] * ap1
            r15 = c_hi[1, 1:2] * (ap1 - ap2) - c_hi[0, 1:2] * ap1
            out_ref[t, z, 0:2, :] = out_ref[t, z, 0:2, :] + jnp.concatenate([r0, r1], axis=0)
            out_ref[t, z, n_y - 2 : n_y, :] = out_ref[t, z, n_y - 2 : n_y, :] + jnp.concatenate([r14, r15], axis=0)
            return carry

        lax.fori_loop(0, n_t * n_z, lat_edges, 0, unroll=4)

    emis_copy.wait()
    emis_ref[...] = eo_ref[...] + ep_ref[...]
    out_copy = pltpu.make_async_copy(out_ref, out_hbm, local_sem.at[0])
    emis_out = pltpu.make_async_copy(emis_ref, emis_hbm, local_sem.at[1])
    out_copy.start()
    emis_out.start()
    out_copy.wait()
    emis_out.wait()


def hand_over(adj_hbm, emis_hbm, adj_out, emis_out, adj_buf, emis_buf, sem):
    ins = [
        pltpu.make_async_copy(adj_hbm, adj_buf, sem.at[0]),
        pltpu.make_async_copy(emis_hbm, emis_buf, sem.at[1]),
    ]
    for c in ins:
        c.start()
    outs = [
        pltpu.make_async_copy(adj_buf, adj_out, sem.at[2]),
        pltpu.make_async_copy(emis_buf, emis_out, sem.at[3]),
    ]
    for c, o in zip(ins, outs):
        c.wait()
        o.start()
    for o in outs:
        o.wait()


def shards(
    adjoint_in,
    trajectory,
    courant,
    mixing,
    coag_rates,
    settle_speed,
    settle_class,
    emis_profile,
    emis_coef,
    land_mask,
    source_mask,
):
    n_t, n_z, n_y, n_x = adjoint_in.shape
    steps = trajectory.shape[0]
    rows = n_z * n_y
    hbm = pl.BlockSpec(memory_space=pl.ANY)
    vmem = pl.BlockSpec(memory_space=pltpu.VMEM)
    smem = pl.BlockSpec(memory_space=pltpu.SMEM)
    f32 = jnp.float32
    adj_out, emis_out = pl.pallas_call(
        kernel,
        out_shape=(
            jax.ShapeDtypeStruct(adjoint_in.shape, f32),
            jax.ShapeDtypeStruct((3, n_y, n_x), f32),
        ),
        in_specs=[hbm] * 11,
        out_specs=(hbm, hbm),
        scratch_shapes=[
            pltpu.VMEM(adjoint_in.shape, f32),
            pltpu.VMEM((3, n_y, n_x), f32),
            pltpu.VMEM(land_mask.shape, land_mask.dtype),
            pltpu.VMEM(source_mask.shape, source_mask.dtype),
            pltpu.SMEM(coag_rates.shape, f32),
            pltpu.SMEM(settle_speed.shape, f32),
            pltpu.SMEM(settle_class.shape, settle_class.dtype),
            pltpu.SMEM(emis_profile.shape, f32),
            pltpu.SMEM(emis_coef.shape, f32),
            pltpu.VMEM(trajectory.shape, trajectory.dtype),
            pltpu.VMEM(courant.shape, f32),
            pltpu.VMEM(mixing.shape, f32),
            pltpu.VMEM((steps, n_t, n_z, n_y + 2 * PAD, n_x), f32),
            pltpu.VMEM((steps, n_t, n_z, PAD, n_x), f32),
            pltpu.VMEM((steps, n_x, n_t * rows), f32),
            pltpu.VMEM((steps, n_x, n_t * rows), f32),
            pltpu.VMEM((n_t, n_z, n_y, n_x), f32),
            pltpu.VMEM((steps, n_t, 1, n_y, n_x), f32),
            pltpu.VMEM((3, n_y, n_x), f32),
            pltpu.VMEM((3, n_y, n_x), f32),
            pltpu.VMEM((4, n_z, n_y, n_x), f32),
            pltpu.VMEM((4, n_z, n_y, n_x), f32),
            pltpu.VMEM((3, n_z, n_y, n_x), f32),
            pltpu.VMEM((n_x, rows), f32),
            pltpu.VMEM((n_x, rows), f32),
            pltpu.VMEM((n_z, n_y + 2 * PAD, n_x), f32),
            pltpu.VMEM((1, n_y, n_x), f32),
            pltpu.SemaphoreType.DMA((N_REMOTE,)),
            pltpu.SemaphoreType.DMA((N_REMOTE,)),
            pltpu.SemaphoreType.DMA((10 + steps,)),
        ],
        compiler_params=pltpu.CompilerParams(
            collective_id=0, has_side_effects=True, vmem_limit_bytes=67043328
        ),
    )(
        adjoint_in, trajectory, courant, mixing, land_mask, source_mask,
        coag_rates, settle_speed, settle_class, emis_profile, emis_coef,
    )
    return pl.pallas_call(
        hand_over,
        out_shape=(
            jax.ShapeDtypeStruct(adj_out.shape, f32),
            jax.ShapeDtypeStruct(emis_out.shape, f32),
        ),
        in_specs=[hbm, hbm],
        out_specs=(hbm, hbm),
        scratch_shapes=[
            pltpu.VMEM(adj_out.shape, f32),
            pltpu.VMEM(emis_out.shape, f32),
            pltpu.SemaphoreType.DMA((4,)),
        ],
    )(adj_out, emis_out)


def solution(mesh):
    return jax.shard_map(
        shards,
        mesh=mesh,
        in_specs=(
            P(None, "lev", "lat", "lon"),
            P(None, None, "lev", "lat", "lon"),
            P(None, "lev", "lat", "lon"),
            P("lev", "lat", "lon"),
            P(),
            P(),
            P(),
            P(),
            P(),
            P("lat", "lon"),
            P("lat", "lon"),
        ),
        out_specs=(P(None, "lev", "lat", "lon"), P(None, "lat", "lon")),
        check_vma=False,
    )
```

```python
import jax
import jax.numpy as jnp
from jax import lax
from jax.experimental import pallas as pl
from jax.experimental.pallas import tpu as pltpu
from jax.sharding import PartitionSpec as P

MESH = pl.DeviceIdType.MESH
PAD = 8

S_LEV, S_UP, S_DOWN, S_RIGHT, S_LEFT = 0, 3, 6, 9, 12
S_EMIS, S_CE_R, S_CE_L, S_CN_U, S_CN_D, S_MIX = 15, 16, 17, 18, 19, 20
N_REMOTE = 21


def kernel(
    adj_hbm, traj_hbm, cour_hbm, mix_hbm, land_hbm, srcm_hbm,
    rates_hbm, speed_hbm, sclass_hbm, prof_hbm, ecoef_hbm,
    out_hbm, emis_hbm,
    out_ref, emis_ref, land_ref, srcm_ref, rates_ref, speed_ref, sclass_ref, prof_ref, ecoef_ref,
    traj_ref, cour_ref, mix_ref, pad_ref, lh_ref, at_ref, ht_ref, hb_ref, lv_ref, eo_ref, ep_ref,
    cx_ref, cy_ref, vc_ref, cet_ref, ceh_ref, cyp_ref, mh_ref,
    send_sem, recv_sem, local_sem,
):
    n_t, n_z, n_y, n_x = out_ref.shape
    steps = traj_hbm.shape[0]
    rows = n_z * n_y
    lon = lax.axis_index("lon")
    lat = lax.axis_index("lat")
    lev = lax.axis_index("lev")
    n_lon = lax.axis_size("lon")
    n_lat = lax.axis_size("lat")
    right = lax.rem(lon + 1, n_lon)
    left = lax.rem(lon + n_lon - 1, n_lon)
    has_up = lat < n_lat - 1
    has_down = lat > 0
    up = jnp.minimum(lat + 1, n_lat - 1)
    down = jnp.maximum(lat - 1, 0)
    partner = 1 - lev
    low_half = lev == 0
    edge_z = jnp.where(low_half, n_z - 1, 0)
    inner_z = jnp.where(low_half, n_z - 2, 1)
    level0 = lev * n_z

    adj_in = pltpu.make_async_copy(adj_hbm, out_ref, local_sem.at[0])
    cour_in = pltpu.make_async_copy(cour_hbm, cour_ref, local_sem.at[1])
    mix_in = pltpu.make_async_copy(mix_hbm, mix_ref, local_sem.at[2])
    traj_in = [
        pltpu.make_async_copy(traj_hbm.at[k], traj_ref.at[k], local_sem.at[3 + k]) for k in range(steps)
    ]
    small_in = [
        pltpu.make_async_copy(src, dst, local_sem.at[3 + steps + i])
        for i, (src, dst) in enumerate(
            (
                (rates_hbm, rates_ref),
                (speed_hbm, speed_ref),
                (sclass_hbm, sclass_ref),
                (prof_hbm, prof_ref),
                (ecoef_hbm, ecoef_ref),
                (land_hbm, land_ref),
                (srcm_hbm, srcm_ref),
            )
        )
    ]
    for c in small_in:
        c.start()
    cour_in.start()
    mix_in.start()
    adj_in.start()
    for k in range(steps - 1, -1, -1):
        traj_in[k].start()

    zeros_pad = jnp.zeros((n_t, n_z, PAD, n_x), jnp.float32)
    for k in range(steps):
        pad_ref[k, :, :, 0:PAD, :] = zeros_pad
        pad_ref[k, :, :, PAD + n_y : 2 * PAD + n_y, :] = zeros_pad
        lh_ref[k] = zeros_pad
    zeros_c = jnp.zeros((n_z, PAD, n_x), jnp.float32)
    cyp_ref[:, 0:PAD, :] = zeros_c
    cyp_ref[:, PAD + n_y : 2 * PAD + n_y, :] = zeros_c

    def rcopy(src, dst, idx, dev):
        return pltpu.make_async_remote_copy(
            src, dst, send_sem.at[idx], recv_sem.at[idx], device_id=dev, device_id_type=MESH
        )

    lane = lax.broadcasted_iota(jnp.int32, (n_y, n_x), 1)
    row = lax.broadcasted_iota(jnp.int32, (n_y, n_x), 0)

    cour_in.wait()
    mix_in.wait()
    for c in small_in:
        c.wait()
    top_row = jnp.logical_and(lat == n_lat - 1, row == n_y - 1)
    for z in range(n_z):
        cyp_ref[z, PAD : PAD + n_y, :] = jnp.where(top_row, 0.0, cour_ref[1, z])
    cet_ref[...] = cour_ref[0].reshape(rows, n_x).T
    ce_right = rcopy(cet_ref.at[pl.ds(n_x - 2, 2), :], ceh_ref.at[pl.ds(n_x - 2, 2), :], S_CE_R, (right, lat, lev))
    ce_left = rcopy(cet_ref.at[pl.ds(0, 2), :], ceh_ref.at[pl.ds(0, 2), :], S_CE_L, (left, lat, lev))
    cn_up = rcopy(
        cyp_ref.at[:, pl.ds(PAD + n_y - 2, 2), :], cyp_ref.at[:, pl.ds(PAD - 2, 2), :], S_CN_U, (lon, up, lev)
    )
    cn_down = rcopy(
        cyp_ref.at[:, pl.ds(PAD, 2), :], cyp_ref.at[:, pl.ds(PAD + n_y, 2), :], S_CN_D, (lon, down, lev)
    )
    mix_x = rcopy(mix_ref.at[pl.ds(edge_z, 1)], mh_ref, S_MIX, (lon, lat, partner))

    def start_coefficient_halos():
        mix_x.start()
        ce_right.start()
        ce_left.start()

        @pl.when(has_up)
        def _():
            cn_up.start()

        @pl.when(has_down)
        def _():
            cn_down.start()

    def fix_vertical_coefficients():
        mix_x.wait()
        below = jnp.where(low_half, vc_ref[1, 0], mh_ref[0])
        vc_ref[1, 0] = below
        vc_ref[2, 0] = jnp.where(low_half, vc_ref[2, 0], 1.0 - vc_ref[0, 0] - below)

    def build_vertical_coefficients():
        dep = jnp.where(low_half, 0.1 + 0.3 * land_ref[...].astype(jnp.float32), 0.0)
        below = jnp.zeros((n_y, n_x), jnp.float32)
        for z in range(n_z):
            above = mix_ref[z]
            if z == n_z - 1:
                above = jnp.where(low_half, above, 0.0)
            base = 1.0 - above - below
            if z == 0:
                base = base - dep
            vc_ref[0, z] = above
            vc_ref[1, z] = below
            vc_ref[2, z] = base
            below = above

    def build_transport_coefficients():
        ce_right.wait()
        ce_left.wait()

        @pl.when(has_up)
        def _():
            cn_up.wait_send()
            cn_down.wait_recv()

        @pl.when(has_down)
        def _():
            cn_down.wait_send()
            cn_up.wait_recv()

        he = ceh_ref[...].T.reshape(n_z, n_y, n_x)
        for z in range(n_z):
            c = cour_ref[0, z]
            hz = he[z]
            c_p1 = jnp.where(lane == n_x - 1, pltpu.roll(hz, n_x - 1, 1), pltpu.roll(c, n_x - 1, 1))
            c_m1 = jnp.where(lane == 0, pltpu.roll(hz, 1, 1), pltpu.roll(c, 1, 1))
            c_m2 = jnp.where(lane <= 1, pltpu.roll(hz, 2, 1), pltpu.roll(c, 2, 1))
            cx_ref[0, z] = -1.5 * jnp.maximum(c, 0.0)
            cx_ref[1, z] = 0.5 * jnp.maximum(c_p1, 0.0)
            cx_ref[2, z] = -1.5 * jnp.minimum(c_m1, 0.0)
            cx_ref[3, z] = 0.5 * jnp.minimum(c_m2, 0.0)
            cy_ref[0, z] = -1.5 * jnp.maximum(cyp_ref[z, PAD : PAD + n_y, :], 0.0)
            cy_ref[1, z] = 0.5 * jnp.maximum(cyp_ref[z, PAD + 1 : PAD + 1 + n_y, :], 0.0)
            cy_ref[2, z] = -1.5 * jnp.minimum(cyp_ref[z, PAD - 1 : PAD - 1 + n_y, :], 0.0)
            cy_ref[3, z] = 0.5 * jnp.minimum(cyp_ref[z, PAD - 2 : PAD - 2 + n_y, :], 0.0)

    eo_ref[...] = jnp.zeros(eo_ref.shape, jnp.float32)
    src_mask = srcm_ref[...].astype(jnp.float32)
    adj_in.wait()
    build_vertical_coefficients()
    emis_copy = rcopy(eo_ref, ep_ref, S_EMIS, (lon, lat, partner))

    for k in range(steps - 1, -1, -1):
        first = k == steps - 1
        traj_in[k].wait()

        def coag_level(zz, acc):
            z = jnp.where(low_half, n_z - 1 - zz, zz)
            zg = level0 + z
            lam = [out_ref[t, z] for t in range(n_t)]
            st = [traj_ref[k, t, z].astype(jnp.float32) for t in range(n_t)]
            new_acc = []
            for m in range(3):
                part = acc[m]
                for j in range(3):
                    part = part + (ecoef_ref[3 * m + j] * prof_ref[zg]) * lam[3 * m + j]
                new_acc.append(part)
            k0, k1, k2, k01, k02, k12 = [rates_ref[i, zg] for i in range(6)]
            n0, v0, w0, n1, v1, w1, n2, v2, w2 = st
            ln0, lv0, lw0, ln1, lv1, lw1, ln2, lv2, lw2 = lam
            a01 = k01 * n1
            a02 = k02 * n2
            a12 = k12 * n2
            s0 = a01 + a02
            g_n0 = ln0 * (-2.0 * k0 * n0 - s0)
            g_v0 = (
                (lv1 * a01 + lv2 * a02 - lv0 * s0)
                + 2.0 * (lw0 * (k0 * v0) + lw1 * (k01 * v1) + lw2 * (k02 * v2))
            )
            g_w0 = lw1 * a01 + lw2 * a02 - lw0 * s0
            g_n1 = (
                ln1 * (-2.0 * k1 * n1 - a12)
                - ln0 * (k01 * n0)
                + (lv1 - lv0) * (k01 * v0)
                + (lw1 - lw0) * (k01 * w0)
            )
            g_v1 = (lv2 - lv1) * a12 + 2.0 * (lw1 * (k1 * v1 + k01 * v0) + lw2 * (k12 * v2))
            g_w1 = (lw2 - lw1) * a12
            g_n2 = (
                -2.0 * k2 * n2 * ln2
                - ln0 * (k02 * n0)
                - ln1 * (k12 * n1)
                + (lv2 - lv0) * (k02 * v0)
                + (lv2 - lv1) * (k12 * v1)
                + (lw2 - lw0) * (k02 * w0)
                + (lw2 - lw1) * (k12 * w1)
            )
            g_v2 = 2.0 * lw2 * (k2 * v2 + k02 * v0 + k12 * v1)
            grads = [g_n0, g_v0, g_w0, g_n1, g_v1, g_w1, g_n2, g_v2]
            for t in range(n_t - 1):
                out_ref[t, z] = lam[t] + grads[t]
            return tuple(new_acc)

        zero = jnp.zeros((n_y, n_x), jnp.float32)
        acc = coag_level(0, (zero, zero, zero))
        lev_copy = rcopy(out_ref.at[:, pl.ds(edge_z, 1)], lv_ref.at[k], S_LEV + k, (lon, lat, partner))
        if not first:
            lev_copy.start()
        acc = lax.fori_loop(1, n_z, coag_level, acc)
        for m in range(3):
            eo_ref[m] = eo_ref[m] + acc[m] * src_mask
        if k == 0:
            emis_copy.start()

        def vert_inner(t, carry):
            col = [out_ref[t, z] for z in range(n_z)]
            for z in range(n_z):
                s = speed_ref[sclass_ref[level0 + z], t]
                val = col[z] * (vc_ref[2, z] - s)
                if z > 0:
                    val = val + col[z - 1] * (vc_ref[1, z] + s)
                if z < n_z - 1:
                    val = val + col[z + 1] * vc_ref[0, z]
                pad_ref[k, t, z, PAD : PAD + n_y, :] = val
            return carry

        lax.fori_loop(0, n_t, vert_inner, 0)
        if first:
            barrier = pltpu.get_barrier_semaphore()
            for dev in ((lon, lat, partner), (left, lat, lev), (right, lat, lev)):
                pl.semaphore_signal(barrier, 1, device_id=dev, device_id_type=MESH)

            @pl.when(has_up)
            def _():
                pl.semaphore_signal(barrier, 1, device_id=(lon, up, lev), device_id_type=MESH)

            @pl.when(has_down)
            def _():
                pl.semaphore_signal(barrier, 1, device_id=(lon, down, lev), device_id_type=MESH)

            pl.semaphore_wait(barrier, 3 + has_up.astype(jnp.int32) + has_down.astype(jnp.int32))
            start_coefficient_halos()
            lev_copy.start()
            fix_vertical_coefficients()
        lev_copy.wait()

        lat_up = rcopy(
            pad_ref.at[k, :, :, pl.ds(PAD + n_y - 2, 2), :],
            lh_ref.at[k, :, :, pl.ds(0, 2), :],
            S_UP + k,
            (lon, up, lev),
        )
        lat_down = rcopy(
            pad_ref.at[k, :, :, pl.ds(PAD, 2), :],
            lh_ref.at[k, :, :, pl.ds(2, 2), :],
            S_DOWN + k,
            (lon, down, lev),
        )
        lon_right = rcopy(
            at_ref.at[k, pl.ds(n_x - 2, 2), :], ht_ref.at[k, pl.ds(n_x - 2, 2), :], S_RIGHT + k, (right, lat, lev)
        )
        lon_left = rcopy(
            at_ref.at[k, pl.ds(0, 2), :], ht_ref.at[k, pl.ds(0, 2), :], S_LEFT + k, (left, lat, lev)
        )

        for t in range(n_t):
            z = edge_z
            s = speed_ref[sclass_ref[level0 + z], t]
            a = out_ref[t, z]
            other = out_ref[t, inner_z]
            halo = lv_ref[k, t, 0]
            a_below = jnp.where(low_half, other, halo)
            a_above = jnp.where(low_half, halo, other)
            pad_ref[k, t, z, PAD : PAD + n_y, :] = (
                a * (vc_ref[2, z] - s) + a_below * (vc_ref[1, z] + s) + a_above * vc_ref[0, z]
            )
            up_t = rcopy(
                pad_ref.at[k, t, :, pl.ds(PAD + n_y - 2, 2), :],
                lh_ref.at[k, t, :, pl.ds(0, 2), :],
                S_UP + k,
                (lon, up, lev),
            )
            down_t = rcopy(
                pad_ref.at[k, t, :, pl.ds(PAD, 2), :],
                lh_ref.at[k, t, :, pl.ds(2, 2), :],
                S_DOWN + k,
                (lon, down, lev),
            )

            @pl.when(has_up)
            def _():
                up_t.start()

            @pl.when(has_down)
            def _():
                down_t.start()

        for t in range(n_t):
            blk = pad_ref[k, t, :, PAD : PAD + n_y, :].reshape(rows, n_x)
            cols = pl.ds(t * rows, rows)
            at_ref[k, :, cols] = blk.T
            rcopy(
                at_ref.at[k, pl.ds(n_x - 2, 2), cols], ht_ref.at[k, pl.ds(n_x - 2, 2), cols], S_RIGHT + k,
                (right, lat, lev),
            ).start()
            rcopy(
                at_ref.at[k, pl.ds(0, 2), cols], ht_ref.at[k, pl.ds(0, 2), cols], S_LEFT + k, (left, lat, lev)
            ).start()

        if k == steps - 1:
            build_transport_coefficients()

        def transport(i, carry):
            t = i // n_z
            z = i % n_z
            a = pad_ref[k, t, z, PAD : PAD + n_y, :]
            y_p1 = pad_ref[k, t, z, PAD + 1 : PAD + 1 + n_y, :]
            y_p2 = pad_ref[k, t, z, PAD + 2 : PAD + 2 + n_y, :]
            y_m1 = pad_ref[k, t, z, PAD - 1 : PAD - 1 + n_y, :]
            y_m2 = pad_ref[k, t, z, PAD - 2 : PAD - 2 + n_y, :]
            x_p1 = pltpu.roll(a, n_x - 1, 1)
            x_p2 = pltpu.roll(a, n_x - 2, 1)
            x_m1 = pltpu.roll(a, 1, 1)
            x_m2 = pltpu.roll(a, 2, 1)
            lon_part = (
                cx_ref[0, z] * (a - x_p1)
                + cx_ref[1, z] * (x_p1 - x_p2)
                + cx_ref[2, z] * (x_m1 - a)
                + cx_ref[3, z] * (x_m2 - x_m1)
            )
            lat_part = (
                cy_ref[0, z] * (a - y_p1)
                + cy_ref[1, z] * (y_p1 - y_p2)
                + cy_ref[2, z] * (y_m1 - a)
                + cy_ref[3, z] * (y_m2 - y_m1)
            )
            out_ref[t, z] = a + lon_part + lat_part
            return carry

        lax.fori_loop(0, n_t * n_z, transport, 0, unroll=4)

        lon_right.wait()
        lon_left.wait()

        for t in range(n_t):
            hb_ref[t] = ht_ref[k, :, t * rows : (t + 1) * rows].T.reshape(n_z, n_y, n_x)

        def lon_edges(i, carry):
            t = i // n_z
            z = i % n_z
            a = pad_ref[k, t, z, PAD : PAD + n_y, :]
            d = hb_ref[t, z] - a
            d_m1 = pltpu.roll(d, 1, 1)
            d_m2 = pltpu.roll(d, 2, 1)
            d_p1 = pltpu.roll(d, n_x - 1, 1)
            d_p2 = pltpu.roll(d, n_x - 2, 1)
            cx0 = cx_ref[0, z]
            cx1 = cx_ref[1, z]
            cxm1 = cx_ref[2, z]
            cxm2 = cx_ref[3, z]
            low = cxm2 * d_m2 + jnp.where(lane == 0, (cxm1 - cxm2) * d_m1, 0.0)
            high = jnp.where(lane == n_x - 1, (cx1 - cx0) * d_p1, 0.0) - cx1 * d_p2
            corr = jnp.where(lane <= 1, low, jnp.where(lane >= n_x - 2, high, 0.0))
            out_ref[t, z] = out_ref[t, z] + corr
            return carry

        lax.fori_loop(0, n_t * n_z, lon_edges, 0, unroll=4)

        @pl.when(has_up)
        def _():
            lat_up.wait_send()
            lat_down.wait_recv()

        @pl.when(has_down)
        def _():
            lat_down.wait_send()
            lat_up.wait_recv()

        def lat_edges(i, carry):
            t = i // n_z
            z = i % n_z
            h = lh_ref[k, t, z, 0:4, :]
            am2 = h[0:1]
            am1 = h[1:2]
            ap1 = h[2:3]
            ap2 = h[3:4]
            c_lo = cy_ref[:, z, 0:2, :]
            c_hi = cy_ref[:, z, n_y - 2 : n_y, :]
            r0 = c_lo[2, 0:1] * am1 + c_lo[3, 0:1] * (am2 - am1)
            r1 = c_lo[3, 1:2] * am1
            r14 = -c_hi[1, 0:1] * ap1
            r15 = c_hi[1, 1:2] * (ap1 - ap2) - c_hi[0, 1:2] * ap1
            out_ref[t, z, 0:2, :] = out_ref[t, z, 0:2, :] + jnp.concatenate([r0, r1], axis=0)
            out_ref[t, z, n_y - 2 : n_y, :] = out_ref[t, z, n_y - 2 : n_y, :] + jnp.concatenate([r14, r15], axis=0)
            return carry

        lax.fori_loop(0, n_t * n_z, lat_edges, 0, unroll=4)

    emis_copy.wait()
    emis_ref[...] = eo_ref[...] + ep_ref[...]
    out_copy = pltpu.make_async_copy(out_ref, out_hbm, local_sem.at[0])
    emis_out = pltpu.make_async_copy(emis_ref, emis_hbm, local_sem.at[1])
    out_copy.start()
    emis_out.start()
    out_copy.wait()
    emis_out.wait()


def hand_over(adj_hbm, emis_hbm, adj_out, emis_out, adj_buf, emis_buf, sem):
    ins = [
        pltpu.make_async_copy(adj_hbm, adj_buf, sem.at[0]),
        pltpu.make_async_copy(emis_hbm, emis_buf, sem.at[1]),
    ]
    for c in ins:
        c.start()
    outs = [
        pltpu.make_async_copy(adj_buf, adj_out, sem.at[2]),
        pltpu.make_async_copy(emis_buf, emis_out, sem.at[3]),
    ]
    for c, o in zip(ins, outs):
        c.wait()
        o.start()
    for o in outs:
        o.wait()


def shards(
    adjoint_in,
    trajectory,
    courant,
    mixing,
    coag_rates,
    settle_speed,
    settle_class,
    emis_profile,
    emis_coef,
    land_mask,
    source_mask,
):
    n_t, n_z, n_y, n_x = adjoint_in.shape
    steps = trajectory.shape[0]
    rows = n_z * n_y
    hbm = pl.BlockSpec(memory_space=pl.ANY)
    vmem = pl.BlockSpec(memory_space=pltpu.VMEM)
    smem = pl.BlockSpec(memory_space=pltpu.SMEM)
    f32 = jnp.float32
    adj_out, emis_out = pl.pallas_call(
        kernel,
        out_shape=(
            jax.ShapeDtypeStruct(adjoint_in.shape, f32),
            jax.ShapeDtypeStruct((3, n_y, n_x), f32),
        ),
        in_specs=[hbm] * 11,
        out_specs=(hbm, hbm),
        scratch_shapes=[
            pltpu.VMEM(adjoint_in.shape, f32),
            pltpu.VMEM((3, n_y, n_x), f32),
            pltpu.VMEM(land_mask.shape, land_mask.dtype),
            pltpu.VMEM(source_mask.shape, source_mask.dtype),
            pltpu.SMEM(coag_rates.shape, f32),
            pltpu.SMEM(settle_speed.shape, f32),
            pltpu.SMEM(settle_class.shape, settle_class.dtype),
            pltpu.SMEM(emis_profile.shape, f32),
            pltpu.SMEM(emis_coef.shape, f32),
            pltpu.VMEM(trajectory.shape, trajectory.dtype),
            pltpu.VMEM(courant.shape, f32),
            pltpu.VMEM(mixing.shape, f32),
            pltpu.VMEM((steps, n_t, n_z, n_y + 2 * PAD, n_x), f32),
            pltpu.VMEM((steps, n_t, n_z, PAD, n_x), f32),
            pltpu.VMEM((steps, n_x, n_t * rows), f32),
            pltpu.VMEM((steps, n_x, n_t * rows), f32),
            pltpu.VMEM((n_t, n_z, n_y, n_x), f32),
            pltpu.VMEM((steps, n_t, 1, n_y, n_x), f32),
            pltpu.VMEM((3, n_y, n_x), f32),
            pltpu.VMEM((3, n_y, n_x), f32),
            pltpu.VMEM((4, n_z, n_y, n_x), f32),
            pltpu.VMEM((4, n_z, n_y, n_x), f32),
            pltpu.VMEM((3, n_z, n_y, n_x), f32),
            pltpu.VMEM((n_x, rows), f32),
            pltpu.VMEM((n_x, rows), f32),
            pltpu.VMEM((n_z, n_y + 2 * PAD, n_x), f32),
            pltpu.VMEM((1, n_y, n_x), f32),
            pltpu.SemaphoreType.DMA((N_REMOTE,)),
            pltpu.SemaphoreType.DMA((N_REMOTE,)),
            pltpu.SemaphoreType.DMA((10 + steps,)),
        ],
        compiler_params=pltpu.CompilerParams(
            collective_id=0, has_side_effects=True, vmem_limit_bytes=67043328
        ),
    )(
        adjoint_in, trajectory, courant, mixing, land_mask, source_mask,
        coag_rates, settle_speed, settle_class, emis_profile, emis_coef,
    )
    return pl.pallas_call(
        hand_over,
        out_shape=(
            jax.ShapeDtypeStruct(adj_out.shape, f32),
            jax.ShapeDtypeStruct(emis_out.shape, f32),
        ),
        in_specs=[hbm, hbm],
        out_specs=(hbm, hbm),
        scratch_shapes=[
            pltpu.VMEM(adj_out.shape, f32),
            pltpu.VMEM(emis_out.shape, f32),
            pltpu.SemaphoreType.DMA((4,)),
        ],
    )(adj_out, emis_out)


def solution(mesh):
    return jax.shard_map(
        shards,
        mesh=mesh,
        in_specs=(
            P(None, "lev", "lat", "lon"),
            P(None, None, "lev", "lat", "lon"),
            P(None, "lev", "lat", "lon"),
            P("lev", "lat", "lon"),
            P(),
            P(),
            P(),
            P(),
            P(),
            P("lat", "lon"),
            P("lat", "lon"),
        ),
        out_specs=(P(None, "lev", "lat", "lon"), P(None, "lat", "lon")),
        check_vma=False,
    )
```

```python
import jax
import jax.numpy as jnp
from jax import lax
from jax.experimental import pallas as pl
from jax.experimental.pallas import tpu as pltpu
from jax.sharding import PartitionSpec as P

MESH = pl.DeviceIdType.MESH
PAD = 8

S_LEV, S_UP, S_DOWN, S_RIGHT, S_LEFT = 0, 3, 6, 9, 12
S_EMIS, S_CE_R, S_CE_L, S_CN_U, S_CN_D, S_MIX = 15, 16, 17, 18, 19, 20
N_REMOTE = 21


def kernel(
    adj_hbm, traj_hbm, cour_hbm, mix_hbm, land_hbm, srcm_hbm,
    rates_hbm, speed_hbm, sclass_hbm, prof_hbm, ecoef_hbm,
    out_hbm, emis_hbm,
    out_ref, emis_ref, land_ref, srcm_ref, rates_ref, speed_ref, sclass_ref, prof_ref, ecoef_ref,
    traj_ref, cour_ref, mix_ref, pad_ref, lh_ref, at_ref, ht_ref, hb_ref, lv_ref, eo_ref, ep_ref,
    cx_ref, cy_ref, vc_ref, cet_ref, ceh_ref, cyp_ref, mh_ref,
    send_sem, recv_sem, local_sem,
):
    n_t, n_z, n_y, n_x = out_ref.shape
    steps = traj_hbm.shape[0]
    rows = n_z * n_y
    lon = lax.axis_index("lon")
    lat = lax.axis_index("lat")
    lev = lax.axis_index("lev")
    n_lon = lax.axis_size("lon")
    n_lat = lax.axis_size("lat")
    right = lax.rem(lon + 1, n_lon)
    left = lax.rem(lon + n_lon - 1, n_lon)
    has_up = lat < n_lat - 1
    has_down = lat > 0
    up = jnp.minimum(lat + 1, n_lat - 1)
    down = jnp.maximum(lat - 1, 0)
    partner = 1 - lev
    low_half = lev == 0
    edge_z = jnp.where(low_half, n_z - 1, 0)
    inner_z = jnp.where(low_half, n_z - 2, 1)
    level0 = lev * n_z

    adj_in = pltpu.make_async_copy(adj_hbm, out_ref, local_sem.at[0])
    cour_in = pltpu.make_async_copy(cour_hbm, cour_ref, local_sem.at[1])
    mix_in = pltpu.make_async_copy(mix_hbm, mix_ref, local_sem.at[2])
    traj_in = [
        pltpu.make_async_copy(traj_hbm.at[k], traj_ref.at[k], local_sem.at[3 + k]) for k in range(steps)
    ]
    small_in = [
        pltpu.make_async_copy(src, dst, local_sem.at[3 + steps + i])
        for i, (src, dst) in enumerate(
            (
                (rates_hbm, rates_ref),
                (speed_hbm, speed_ref),
                (sclass_hbm, sclass_ref),
                (prof_hbm, prof_ref),
                (ecoef_hbm, ecoef_ref),
                (land_hbm, land_ref),
                (srcm_hbm, srcm_ref),
            )
        )
    ]
    for c in small_in:
        c.start()
    cour_in.start()
    mix_in.start()
    adj_in.start()
    for k in range(steps - 1, -1, -1):
        traj_in[k].start()

    zeros_pad = jnp.zeros((n_t, n_z, PAD, n_x), jnp.float32)
    for k in range(steps):
        pad_ref[k, :, :, 0:PAD, :] = zeros_pad
        pad_ref[k, :, :, PAD + n_y : 2 * PAD + n_y, :] = zeros_pad
        lh_ref[k] = zeros_pad
    zeros_c = jnp.zeros((n_z, PAD, n_x), jnp.float32)
    cyp_ref[:, 0:PAD, :] = zeros_c
    cyp_ref[:, PAD + n_y : 2 * PAD + n_y, :] = zeros_c

    def rcopy(src, dst, idx, dev):
        return pltpu.make_async_remote_copy(
            src, dst, send_sem.at[idx], recv_sem.at[idx], device_id=dev, device_id_type=MESH
        )

    lane = lax.broadcasted_iota(jnp.int32, (n_y, n_x), 1)
    row = lax.broadcasted_iota(jnp.int32, (n_y, n_x), 0)

    cour_in.wait()
    mix_in.wait()
    for c in small_in:
        c.wait()
    top_row = jnp.logical_and(lat == n_lat - 1, row == n_y - 1)
    for z in range(n_z):
        cyp_ref[z, PAD : PAD + n_y, :] = jnp.where(top_row, 0.0, cour_ref[1, z])
    cet_ref[...] = cour_ref[0].reshape(rows, n_x).T
    ce_right = rcopy(cet_ref.at[pl.ds(n_x - 2, 2), :], ceh_ref.at[pl.ds(n_x - 2, 2), :], S_CE_R, (right, lat, lev))
    ce_left = rcopy(cet_ref.at[pl.ds(0, 2), :], ceh_ref.at[pl.ds(0, 2), :], S_CE_L, (left, lat, lev))
    cn_up = rcopy(
        cyp_ref.at[:, pl.ds(PAD + n_y - 2, 2), :], cyp_ref.at[:, pl.ds(PAD - 2, 2), :], S_CN_U, (lon, up, lev)
    )
    cn_down = rcopy(
        cyp_ref.at[:, pl.ds(PAD, 2), :], cyp_ref.at[:, pl.ds(PAD + n_y, 2), :], S_CN_D, (lon, down, lev)
    )
    mix_x = rcopy(mix_ref.at[pl.ds(edge_z, 1)], mh_ref, S_MIX, (lon, lat, partner))

    def start_coefficient_halos():
        mix_x.start()
        ce_right.start()
        ce_left.start()

        @pl.when(has_up)
        def _():
            cn_up.start()

        @pl.when(has_down)
        def _():
            cn_down.start()

    def fix_vertical_coefficients():
        mix_x.wait()
        below = jnp.where(low_half, vc_ref[1, 0], mh_ref[0])
        vc_ref[1, 0] = below
        vc_ref[2, 0] = jnp.where(low_half, vc_ref[2, 0], 1.0 - vc_ref[0, 0] - below)

    def build_vertical_coefficients():
        dep = jnp.where(low_half, 0.1 + 0.3 * land_ref[...].astype(jnp.float32), 0.0)
        below = jnp.zeros((n_y, n_x), jnp.float32)
        for z in range(n_z):
            above = mix_ref[z]
            if z == n_z - 1:
                above = jnp.where(low_half, above, 0.0)
            base = 1.0 - above - below
            if z == 0:
                base = base - dep
            vc_ref[0, z] = above
            vc_ref[1, z] = below
            vc_ref[2, z] = base
            below = above

    def build_transport_coefficients():
        ce_right.wait()
        ce_left.wait()

        @pl.when(has_up)
        def _():
            cn_up.wait_send()
            cn_down.wait_recv()

        @pl.when(has_down)
        def _():
            cn_down.wait_send()
            cn_up.wait_recv()

        he = ceh_ref[...].T.reshape(n_z, n_y, n_x)
        for z in range(n_z):
            c = cour_ref[0, z]
            hz = he[z]
            c_p1 = jnp.where(lane == n_x - 1, pltpu.roll(hz, n_x - 1, 1), pltpu.roll(c, n_x - 1, 1))
            c_m1 = jnp.where(lane == 0, pltpu.roll(hz, 1, 1), pltpu.roll(c, 1, 1))
            c_m2 = jnp.where(lane <= 1, pltpu.roll(hz, 2, 1), pltpu.roll(c, 2, 1))
            cx_ref[0, z] = -1.5 * jnp.maximum(c, 0.0)
            cx_ref[1, z] = 0.5 * jnp.maximum(c_p1, 0.0)
            cx_ref[2, z] = -1.5 * jnp.minimum(c_m1, 0.0)
            cx_ref[3, z] = 0.5 * jnp.minimum(c_m2, 0.0)
            cy_ref[0, z] = -1.5 * jnp.maximum(cyp_ref[z, PAD : PAD + n_y, :], 0.0)
            cy_ref[1, z] = 0.5 * jnp.maximum(cyp_ref[z, PAD + 1 : PAD + 1 + n_y, :], 0.0)
            cy_ref[2, z] = -1.5 * jnp.minimum(cyp_ref[z, PAD - 1 : PAD - 1 + n_y, :], 0.0)
            cy_ref[3, z] = 0.5 * jnp.minimum(cyp_ref[z, PAD - 2 : PAD - 2 + n_y, :], 0.0)

    eo_ref[...] = jnp.zeros(eo_ref.shape, jnp.float32)
    src_mask = srcm_ref[...].astype(jnp.float32)
    adj_in.wait()
    build_vertical_coefficients()
    emis_copy = rcopy(eo_ref, ep_ref, S_EMIS, (lon, lat, partner))

    for k in range(steps - 1, -1, -1):
        first = k == steps - 1
        traj_in[k].wait()

        def coag_level(zz, acc):
            z = jnp.where(low_half, n_z - 1 - zz, zz)
            zg = level0 + z
            lam = [out_ref[t, z] for t in range(n_t)]
            st = [traj_ref[k, t, z].astype(jnp.float32) for t in range(n_t)]
            new_acc = []
            for m in range(3):
                part = acc[m]
                for j in range(3):
                    part = part + (ecoef_ref[3 * m + j] * prof_ref[zg]) * lam[3 * m + j]
                new_acc.append(part)
            k0, k1, k2, k01, k02, k12 = [rates_ref[i, zg] for i in range(6)]
            n0, v0, w0, n1, v1, w1, n2, v2, w2 = st
            ln0, lv0, lw0, ln1, lv1, lw1, ln2, lv2, lw2 = lam
            a01 = k01 * n1
            a02 = k02 * n2
            a12 = k12 * n2
            s0 = a01 + a02
            g_n0 = ln0 * (-2.0 * k0 * n0 - s0)
            g_v0 = (
                (lv1 * a01 + lv2 * a02 - lv0 * s0)
                + 2.0 * (lw0 * (k0 * v0) + lw1 * (k01 * v1) + lw2 * (k02 * v2))
            )
            g_w0 = lw1 * a01 + lw2 * a02 - lw0 * s0
            g_n1 = (
                ln1 * (-2.0 * k1 * n1 - a12)
                - ln0 * (k01 * n0)
                + (lv1 - lv0) * (k01 * v0)
                + (lw1 - lw0) * (k01 * w0)
            )
            g_v1 = (lv2 - lv1) * a12 + 2.0 * (lw1 * (k1 * v1 + k01 * v0) + lw2 * (k12 * v2))
            g_w1 = (lw2 - lw1) * a12
            g_n2 = (
                -2.0 * k2 * n2 * ln2
                - ln0 * (k02 * n0)
                - ln1 * (k12 * n1)
                + (lv2 - lv0) * (k02 * v0)
                + (lv2 - lv1) * (k12 * v1)
                + (lw2 - lw0) * (k02 * w0)
                + (lw2 - lw1) * (k12 * w1)
            )
            g_v2 = 2.0 * lw2 * (k2 * v2 + k02 * v0 + k12 * v1)
            grads = [g_n0, g_v0, g_w0, g_n1, g_v1, g_w1, g_n2, g_v2]
            for t in range(n_t - 1):
                out_ref[t, z] = lam[t] + grads[t]
            return tuple(new_acc)

        zero = jnp.zeros((n_y, n_x), jnp.float32)
        acc = coag_level(0, (zero, zero, zero))
        lev_copy = rcopy(out_ref.at[:, pl.ds(edge_z, 1)], lv_ref.at[k], S_LEV + k, (lon, lat, partner))
        if not first:
            lev_copy.start()
        acc = lax.fori_loop(1, n_z, coag_level, acc)
        for m in range(3):
            eo_ref[m] = eo_ref[m] + acc[m] * src_mask
        if k == 0:
            emis_copy.start()

        def vert_inner(t, carry):
            col = [out_ref[t, z] for z in range(n_z)]
            for z in range(n_z):
                s = speed_ref[sclass_ref[level0 + z], t]
                val = col[z] * (vc_ref[2, z] - s)
                if z > 0:
                    val = val + col[z - 1] * (vc_ref[1, z] + s)
                if z < n_z - 1:
                    val = val + col[z + 1] * vc_ref[0, z]
                pad_ref[k, t, z, PAD : PAD + n_y, :] = val
            return carry

        lax.fori_loop(0, n_t, vert_inner, 0)
        if first:
            barrier = pltpu.get_barrier_semaphore()
            for dev in ((lon, lat, partner), (left, lat, lev), (right, lat, lev)):
                pl.semaphore_signal(barrier, 1, device_id=dev, device_id_type=MESH)

            @pl.when(has_up)
            def _():
                pl.semaphore_signal(barrier, 1, device_id=(lon, up, lev), device_id_type=MESH)

            @pl.when(has_down)
            def _():
                pl.semaphore_signal(barrier, 1, device_id=(lon, down, lev), device_id_type=MESH)

            pl.semaphore_wait(barrier, 3 + has_up.astype(jnp.int32) + has_down.astype(jnp.int32))
            start_coefficient_halos()
            lev_copy.start()
            fix_vertical_coefficients()
        lev_copy.wait()

        lat_up = rcopy(
            pad_ref.at[k, :, :, pl.ds(PAD + n_y - 2, 2), :],
            lh_ref.at[k, :, :, pl.ds(0, 2), :],
            S_UP + k,
            (lon, up, lev),
        )
        lat_down = rcopy(
            pad_ref.at[k, :, :, pl.ds(PAD, 2), :],
            lh_ref.at[k, :, :, pl.ds(2, 2), :],
            S_DOWN + k,
            (lon, down, lev),
        )
        lon_right = rcopy(
            at_ref.at[k, pl.ds(n_x - 2, 2), :], ht_ref.at[k, pl.ds(n_x - 2, 2), :], S_RIGHT + k, (right, lat, lev)
        )
        lon_left = rcopy(
            at_ref.at[k, pl.ds(0, 2), :], ht_ref.at[k, pl.ds(0, 2), :], S_LEFT + k, (left, lat, lev)
        )

        for t in range(n_t):
            z = edge_z
            s = speed_ref[sclass_ref[level0 + z], t]
            a = out_ref[t, z]
            other = out_ref[t, inner_z]
            halo = lv_ref[k, t, 0]
            a_below = jnp.where(low_half, other, halo)
            a_above = jnp.where(low_half, halo, other)
            pad_ref[k, t, z, PAD : PAD + n_y, :] = (
                a * (vc_ref[2, z] - s) + a_below * (vc_ref[1, z] + s) + a_above * vc_ref[0, z]
            )
            up_t = rcopy(
                pad_ref.at[k, t, :, pl.ds(PAD + n_y - 2, 2), :],
                lh_ref.at[k, t, :, pl.ds(0, 2), :],
                S_UP + k,
                (lon, up, lev),
            )
            down_t = rcopy(
                pad_ref.at[k, t, :, pl.ds(PAD, 2), :],
                lh_ref.at[k, t, :, pl.ds(2, 2), :],
                S_DOWN + k,
                (lon, down, lev),
            )

            @pl.when(has_up)
            def _():
                up_t.start()

            @pl.when(has_down)
            def _():
                down_t.start()

        for t in range(n_t):
            blk = pad_ref[k, t, :, PAD : PAD + n_y, :].reshape(rows, n_x)
            cols = pl.ds(t * rows, rows)
            at_ref[k, :, cols] = blk.T
            rcopy(
                at_ref.at[k, pl.ds(n_x - 2, 2), cols], ht_ref.at[k, pl.ds(n_x - 2, 2), cols], S_RIGHT + k,
                (right, lat, lev),
            ).start()
            rcopy(
                at_ref.at[k, pl.ds(0, 2), cols], ht_ref.at[k, pl.ds(0, 2), cols], S_LEFT + k, (left, lat, lev)
            ).start()

        if k == steps - 1:
            build_transport_coefficients()

        def transport(i, carry):
            t = i // n_z
            z = i % n_z
            a = pad_ref[k, t, z, PAD : PAD + n_y, :]
            y_p1 = pad_ref[k, t, z, PAD + 1 : PAD + 1 + n_y, :]
            y_p2 = pad_ref[k, t, z, PAD + 2 : PAD + 2 + n_y, :]
            y_m1 = pad_ref[k, t, z, PAD - 1 : PAD - 1 + n_y, :]
            y_m2 = pad_ref[k, t, z, PAD - 2 : PAD - 2 + n_y, :]
            x_p1 = pltpu.roll(a, n_x - 1, 1)
            x_p2 = pltpu.roll(a, n_x - 2, 1)
            x_m1 = pltpu.roll(a, 1, 1)
            x_m2 = pltpu.roll(a, 2, 1)
            lon_part = (
                cx_ref[0, z] * (a - x_p1)
                + cx_ref[1, z] * (x_p1 - x_p2)
                + cx_ref[2, z] * (x_m1 - a)
                + cx_ref[3, z] * (x_m2 - x_m1)
            )
            lat_part = (
                cy_ref[0, z] * (a - y_p1)
                + cy_ref[1, z] * (y_p1 - y_p2)
                + cy_ref[2, z] * (y_m1 - a)
                + cy_ref[3, z] * (y_m2 - y_m1)
            )
            out_ref[t, z] = a + lon_part + lat_part
            return carry

        lax.fori_loop(0, n_t * n_z, transport, 0, unroll=4)

        lon_right.wait()
        lon_left.wait()

        def lon_edges(t, carry):
            cols = pl.ds(pl.multiple_of(t * rows, rows), rows)
            h_t = ht_ref[k, :, cols].T.reshape(n_z, n_y, n_x)
            for z in range(n_z):
                a = pad_ref[k, t, z, PAD : PAD + n_y, :]
                d = h_t[z] - a
                d_m1 = pltpu.roll(d, 1, 1)
                d_m2 = pltpu.roll(d, 2, 1)
                d_p1 = pltpu.roll(d, n_x - 1, 1)
                d_p2 = pltpu.roll(d, n_x - 2, 1)
                cx0 = cx_ref[0, z]
                cx1 = cx_ref[1, z]
                cxm1 = cx_ref[2, z]
                cxm2 = cx_ref[3, z]
                low = cxm2 * d_m2 + jnp.where(lane == 0, (cxm1 - cxm2) * d_m1, 0.0)
                high = jnp.where(lane == n_x - 1, (cx1 - cx0) * d_p1, 0.0) - cx1 * d_p2
                corr = jnp.where(lane <= 1, low, jnp.where(lane >= n_x - 2, high, 0.0))
                out_ref[t, z] = out_ref[t, z] + corr
            return carry

        lax.fori_loop(0, n_t, lon_edges, 0)

        @pl.when(has_up)
        def _():
            lat_up.wait_send()
            lat_down.wait_recv()

        @pl.when(has_down)
        def _():
            lat_down.wait_send()
            lat_up.wait_recv()

        def lat_edges(i, carry):
            t = i // n_z
            z = i % n_z
            h = lh_ref[k, t, z, 0:4, :]
            am2 = h[0:1]
            am1 = h[1:2]
            ap1 = h[2:3]
            ap2 = h[3:4]
            c_lo = cy_ref[:, z, 0:2, :]
            c_hi = cy_ref[:, z, n_y - 2 : n_y, :]
            r0 = c_lo[2, 0:1] * am1 + c_lo[3, 0:1] * (am2 - am1)
            r1 = c_lo[3, 1:2] * am1
            r14 = -c_hi[1, 0:1] * ap1
            r15 = c_hi[1, 1:2] * (ap1 - ap2) - c_hi[0, 1:2] * ap1
            out_ref[t, z, 0:2, :] = out_ref[t, z, 0:2, :] + jnp.concatenate([r0, r1], axis=0)
            out_ref[t, z, n_y - 2 : n_y, :] = out_ref[t, z, n_y - 2 : n_y, :] + jnp.concatenate([r14, r15], axis=0)
            return carry

        lax.fori_loop(0, n_t * n_z, lat_edges, 0, unroll=4)

    emis_copy.wait()
    emis_ref[...] = eo_ref[...] + ep_ref[...]
    out_copy = pltpu.make_async_copy(out_ref, out_hbm, local_sem.at[0])
    emis_out = pltpu.make_async_copy(emis_ref, emis_hbm, local_sem.at[1])
    out_copy.start()
    emis_out.start()
    out_copy.wait()
    emis_out.wait()


def hand_over(adj_hbm, emis_hbm, adj_out, emis_out, adj_buf, emis_buf, sem):
    ins = [
        pltpu.make_async_copy(adj_hbm, adj_buf, sem.at[0]),
        pltpu.make_async_copy(emis_hbm, emis_buf, sem.at[1]),
    ]
    for c in ins:
        c.start()
    outs = [
        pltpu.make_async_copy(adj_buf, adj_out, sem.at[2]),
        pltpu.make_async_copy(emis_buf, emis_out, sem.at[3]),
    ]
    for c, o in zip(ins, outs):
        c.wait()
        o.start()
    for o in outs:
        o.wait()


def shards(
    adjoint_in,
    trajectory,
    courant,
    mixing,
    coag_rates,
    settle_speed,
    settle_class,
    emis_profile,
    emis_coef,
    land_mask,
    source_mask,
):
    n_t, n_z, n_y, n_x = adjoint_in.shape
    steps = trajectory.shape[0]
    rows = n_z * n_y
    hbm = pl.BlockSpec(memory_space=pl.ANY)
    vmem = pl.BlockSpec(memory_space=pltpu.VMEM)
    smem = pl.BlockSpec(memory_space=pltpu.SMEM)
    f32 = jnp.float32
    adj_out, emis_out = pl.pallas_call(
        kernel,
        out_shape=(
            jax.ShapeDtypeStruct(adjoint_in.shape, f32),
            jax.ShapeDtypeStruct((3, n_y, n_x), f32),
        ),
        in_specs=[hbm] * 11,
        out_specs=(hbm, hbm),
        scratch_shapes=[
            pltpu.VMEM(adjoint_in.shape, f32),
            pltpu.VMEM((3, n_y, n_x), f32),
            pltpu.VMEM(land_mask.shape, land_mask.dtype),
            pltpu.VMEM(source_mask.shape, source_mask.dtype),
            pltpu.SMEM(coag_rates.shape, f32),
            pltpu.SMEM(settle_speed.shape, f32),
            pltpu.SMEM(settle_class.shape, settle_class.dtype),
            pltpu.SMEM(emis_profile.shape, f32),
            pltpu.SMEM(emis_coef.shape, f32),
            pltpu.VMEM(trajectory.shape, trajectory.dtype),
            pltpu.VMEM(courant.shape, f32),
            pltpu.VMEM(mixing.shape, f32),
            pltpu.VMEM((steps, n_t, n_z, n_y + 2 * PAD, n_x), f32),
            pltpu.VMEM((steps, n_t, n_z, PAD, n_x), f32),
            pltpu.VMEM((steps, n_x, n_t * rows), f32),
            pltpu.VMEM((steps, n_x, n_t * rows), f32),
            pltpu.VMEM((n_t, n_z, n_y, n_x), f32),
            pltpu.VMEM((steps, n_t, 1, n_y, n_x), f32),
            pltpu.VMEM((3, n_y, n_x), f32),
            pltpu.VMEM((3, n_y, n_x), f32),
            pltpu.VMEM((4, n_z, n_y, n_x), f32),
            pltpu.VMEM((4, n_z, n_y, n_x), f32),
            pltpu.VMEM((3, n_z, n_y, n_x), f32),
            pltpu.VMEM((n_x, rows), f32),
            pltpu.VMEM((n_x, rows), f32),
            pltpu.VMEM((n_z, n_y + 2 * PAD, n_x), f32),
            pltpu.VMEM((1, n_y, n_x), f32),
            pltpu.SemaphoreType.DMA((N_REMOTE,)),
            pltpu.SemaphoreType.DMA((N_REMOTE,)),
            pltpu.SemaphoreType.DMA((10 + steps,)),
        ],
        compiler_params=pltpu.CompilerParams(
            collective_id=0, has_side_effects=True, vmem_limit_bytes=67043328
        ),
    )(
        adjoint_in, trajectory, courant, mixing, land_mask, source_mask,
        coag_rates, settle_speed, settle_class, emis_profile, emis_coef,
    )
    return pl.pallas_call(
        hand_over,
        out_shape=(
            jax.ShapeDtypeStruct(adj_out.shape, f32),
            jax.ShapeDtypeStruct(emis_out.shape, f32),
        ),
        in_specs=[hbm, hbm],
        out_specs=(hbm, hbm),
        scratch_shapes=[
            pltpu.VMEM(adj_out.shape, f32),
            pltpu.VMEM(emis_out.shape, f32),
            pltpu.SemaphoreType.DMA((4,)),
        ],
    )(adj_out, emis_out)


def solution(mesh):
    return jax.shard_map(
        shards,
        mesh=mesh,
        in_specs=(
            P(None, "lev", "lat", "lon"),
            P(None, None, "lev", "lat", "lon"),
            P(None, "lev", "lat", "lon"),
            P("lev", "lat", "lon"),
            P(),
            P(),
            P(),
            P(),
            P(),
            P("lat", "lon"),
            P("lat", "lon"),
        ),
        out_specs=(P(None, "lev", "lat", "lon"), P(None, "lat", "lon")),
        check_vma=False,
    )
```

```python
import jax
import jax.numpy as jnp
from jax import lax
from jax.experimental import pallas as pl
from jax.experimental.pallas import tpu as pltpu
from jax.sharding import PartitionSpec as P

MESH = pl.DeviceIdType.MESH
PAD = 8

S_LEV, S_UP, S_DOWN, S_RIGHT, S_LEFT = 0, 3, 6, 9, 12
S_EMIS, S_CE_R, S_CE_L, S_CN_U, S_CN_D, S_MIX = 15, 16, 17, 18, 19, 20
N_REMOTE = 21


def kernel(
    adj_hbm, traj_hbm, cour_hbm, mix_hbm, land_hbm, srcm_hbm,
    rates_hbm, speed_hbm, sclass_hbm, prof_hbm, ecoef_hbm,
    out_hbm, emis_hbm,
    out_ref, emis_ref, land_ref, srcm_ref, rates_ref, speed_ref, sclass_ref, prof_ref, ecoef_ref,
    traj_ref, cour_ref, mix_ref, pad_ref, lh_ref, at_ref, ht_ref, hb_ref, lv_ref, eo_ref, ep_ref,
    cx_ref, cy_ref, vc_ref, cet_ref, ceh_ref, cyp_ref, mh_ref,
    send_sem, recv_sem, local_sem,
):
    n_t, n_z, n_y, n_x = out_ref.shape
    steps = traj_hbm.shape[0]
    rows = n_z * n_y
    lon = lax.axis_index("lon")
    lat = lax.axis_index("lat")
    lev = lax.axis_index("lev")
    n_lon = lax.axis_size("lon")
    n_lat = lax.axis_size("lat")
    right = lax.rem(lon + 1, n_lon)
    left = lax.rem(lon + n_lon - 1, n_lon)
    has_up = lat < n_lat - 1
    has_down = lat > 0
    up = jnp.minimum(lat + 1, n_lat - 1)
    down = jnp.maximum(lat - 1, 0)
    partner = 1 - lev
    low_half = lev == 0
    edge_z = jnp.where(low_half, n_z - 1, 0)
    inner_z = jnp.where(low_half, n_z - 2, 1)
    level0 = lev * n_z

    adj_in = pltpu.make_async_copy(adj_hbm, out_ref, local_sem.at[0])
    cour_in = pltpu.make_async_copy(cour_hbm, cour_ref, local_sem.at[1])
    mix_in = pltpu.make_async_copy(mix_hbm, mix_ref, local_sem.at[2])
    traj_in = [
        pltpu.make_async_copy(traj_hbm.at[k], traj_ref.at[k], local_sem.at[3 + k]) for k in range(steps)
    ]
    small_in = [
        pltpu.make_async_copy(src, dst, local_sem.at[3 + steps + i])
        for i, (src, dst) in enumerate(
            (
                (rates_hbm, rates_ref),
                (speed_hbm, speed_ref),
                (sclass_hbm, sclass_ref),
                (prof_hbm, prof_ref),
                (ecoef_hbm, ecoef_ref),
                (land_hbm, land_ref),
                (srcm_hbm, srcm_ref),
            )
        )
    ]
    for c in small_in:
        c.start()
    cour_in.start()
    mix_in.start()
    adj_in.start()
    for k in range(steps - 1, -1, -1):
        traj_in[k].start()

    zeros_pad = jnp.zeros((n_t, n_z, PAD, n_x), jnp.float32)
    for k in range(steps):
        pad_ref[k, :, :, 0:PAD, :] = zeros_pad
        pad_ref[k, :, :, PAD + n_y : 2 * PAD + n_y, :] = zeros_pad
        lh_ref[k] = zeros_pad
    zeros_c = jnp.zeros((n_z, PAD, n_x), jnp.float32)
    cyp_ref[:, 0:PAD, :] = zeros_c
    cyp_ref[:, PAD + n_y : 2 * PAD + n_y, :] = zeros_c

    def rcopy(src, dst, idx, dev):
        return pltpu.make_async_remote_copy(
            src, dst, send_sem.at[idx], recv_sem.at[idx], device_id=dev, device_id_type=MESH
        )

    lane = lax.broadcasted_iota(jnp.int32, (n_y, n_x), 1)
    row = lax.broadcasted_iota(jnp.int32, (n_y, n_x), 0)

    cour_in.wait()
    mix_in.wait()
    for c in small_in:
        c.wait()
    top_row = jnp.logical_and(lat == n_lat - 1, row == n_y - 1)
    for z in range(n_z):
        cyp_ref[z, PAD : PAD + n_y, :] = jnp.where(top_row, 0.0, cour_ref[1, z])
    cet_ref[...] = cour_ref[0].reshape(rows, n_x).T
    ce_right = rcopy(cet_ref.at[pl.ds(n_x - 2, 2), :], ceh_ref.at[pl.ds(n_x - 2, 2), :], S_CE_R, (right, lat, lev))
    ce_left = rcopy(cet_ref.at[pl.ds(0, 2), :], ceh_ref.at[pl.ds(0, 2), :], S_CE_L, (left, lat, lev))
    cn_up = rcopy(
        cyp_ref.at[:, pl.ds(PAD + n_y - 2, 2), :], cyp_ref.at[:, pl.ds(PAD - 2, 2), :], S_CN_U, (lon, up, lev)
    )
    cn_down = rcopy(
        cyp_ref.at[:, pl.ds(PAD, 2), :], cyp_ref.at[:, pl.ds(PAD + n_y, 2), :], S_CN_D, (lon, down, lev)
    )
    mix_x = rcopy(mix_ref.at[pl.ds(edge_z, 1)], mh_ref, S_MIX, (lon, lat, partner))

    def start_coefficient_halos():
        mix_x.start()
        ce_right.start()
        ce_left.start()

        @pl.when(has_up)
        def _():
            cn_up.start()

        @pl.when(has_down)
        def _():
            cn_down.start()

    def fix_vertical_coefficients():
        mix_x.wait()
        below = jnp.where(low_half, vc_ref[1, 0], mh_ref[0])
        vc_ref[1, 0] = below
        vc_ref[2, 0] = jnp.where(low_half, vc_ref[2, 0], 1.0 - vc_ref[0, 0] - below)

    def build_vertical_coefficients():
        dep = jnp.where(low_half, 0.1 + 0.3 * land_ref[...].astype(jnp.float32), 0.0)
        below = jnp.zeros((n_y, n_x), jnp.float32)
        for z in range(n_z):
            above = mix_ref[z]
            if z == n_z - 1:
                above = jnp.where(low_half, above, 0.0)
            base = 1.0 - above - below
            if z == 0:
                base = base - dep
            vc_ref[0, z] = above
            vc_ref[1, z] = below
            vc_ref[2, z] = base
            below = above

    def build_transport_coefficients():
        ce_right.wait()
        ce_left.wait()

        @pl.when(has_up)
        def _():
            cn_up.wait_send()
            cn_down.wait_recv()

        @pl.when(has_down)
        def _():
            cn_down.wait_send()
            cn_up.wait_recv()

        he = ceh_ref[...].T.reshape(n_z, n_y, n_x)
        for z in range(n_z):
            c = cour_ref[0, z]
            hz = he[z]
            c_p1 = jnp.where(lane == n_x - 1, pltpu.roll(hz, n_x - 1, 1), pltpu.roll(c, n_x - 1, 1))
            c_m1 = jnp.where(lane == 0, pltpu.roll(hz, 1, 1), pltpu.roll(c, 1, 1))
            c_m2 = jnp.where(lane <= 1, pltpu.roll(hz, 2, 1), pltpu.roll(c, 2, 1))
            cx_ref[0, z] = -1.5 * jnp.maximum(c, 0.0)
            cx_ref[1, z] = 0.5 * jnp.maximum(c_p1, 0.0)
            cx_ref[2, z] = -1.5 * jnp.minimum(c_m1, 0.0)
            cx_ref[3, z] = 0.5 * jnp.minimum(c_m2, 0.0)
            cy_ref[0, z] = -1.5 * jnp.maximum(cyp_ref[z, PAD : PAD + n_y, :], 0.0)
            cy_ref[1, z] = 0.5 * jnp.maximum(cyp_ref[z, PAD + 1 : PAD + 1 + n_y, :], 0.0)
            cy_ref[2, z] = -1.5 * jnp.minimum(cyp_ref[z, PAD - 1 : PAD - 1 + n_y, :], 0.0)
            cy_ref[3, z] = 0.5 * jnp.minimum(cyp_ref[z, PAD - 2 : PAD - 2 + n_y, :], 0.0)

    eo_ref[...] = jnp.zeros(eo_ref.shape, jnp.float32)
    src_mask = srcm_ref[...].astype(jnp.float32)
    adj_in.wait()
    build_vertical_coefficients()
    emis_copy = rcopy(eo_ref, ep_ref, S_EMIS, (lon, lat, partner))

    for k in range(steps - 1, -1, -1):
        first = k == steps - 1
        traj_in[k].wait()

        def coag_level(zz, acc):
            z = jnp.where(low_half, n_z - 1 - zz, zz)
            zg = level0 + z
            lam = [out_ref[t, z] for t in range(n_t)]
            st = [traj_ref[k, t, z].astype(jnp.float32) for t in range(n_t)]
            new_acc = []
            for m in range(3):
                part = acc[m]
                for j in range(3):
                    part = part + (ecoef_ref[3 * m + j] * prof_ref[zg]) * lam[3 * m + j]
                new_acc.append(part)
            k0, k1, k2, k01, k02, k12 = [rates_ref[i, zg] for i in range(6)]
            n0, v0, w0, n1, v1, w1, n2, v2, w2 = st
            ln0, lv0, lw0, ln1, lv1, lw1, ln2, lv2, lw2 = lam
            a01 = k01 * n1
            a02 = k02 * n2
            a12 = k12 * n2
            s0 = a01 + a02
            g_n0 = ln0 * (-2.0 * k0 * n0 - s0)
            g_v0 = (
                (lv1 * a01 + lv2 * a02 - lv0 * s0)
                + 2.0 * (lw0 * (k0 * v0) + lw1 * (k01 * v1) + lw2 * (k02 * v2))
            )
            g_w0 = lw1 * a01 + lw2 * a02 - lw0 * s0
            g_n1 = (
                ln1 * (-2.0 * k1 * n1 - a12)
                - ln0 * (k01 * n0)
                + (lv1 - lv0) * (k01 * v0)
                + (lw1 - lw0) * (k01 * w0)
            )
            g_v1 = (lv2 - lv1) * a12 + 2.0 * (lw1 * (k1 * v1 + k01 * v0) + lw2 * (k12 * v2))
            g_w1 = (lw2 - lw1) * a12
            g_n2 = (
                -2.0 * k2 * n2 * ln2
                - ln0 * (k02 * n0)
                - ln1 * (k12 * n1)
                + (lv2 - lv0) * (k02 * v0)
                + (lv2 - lv1) * (k12 * v1)
                + (lw2 - lw0) * (k02 * w0)
                + (lw2 - lw1) * (k12 * w1)
            )
            g_v2 = 2.0 * lw2 * (k2 * v2 + k02 * v0 + k12 * v1)
            grads = [g_n0, g_v0, g_w0, g_n1, g_v1, g_w1, g_n2, g_v2]
            for t in range(n_t - 1):
                out_ref[t, z] = lam[t] + grads[t]
            return tuple(new_acc)

        zero = jnp.zeros((n_y, n_x), jnp.float32)
        acc = coag_level(0, (zero, zero, zero))
        lev_copy = rcopy(out_ref.at[:, pl.ds(edge_z, 1)], lv_ref.at[k], S_LEV + k, (lon, lat, partner))
        if not first:
            lev_copy.start()
        acc = lax.fori_loop(1, n_z, coag_level, acc)
        for m in range(3):
            eo_ref[m] = eo_ref[m] + acc[m] * src_mask
        if k == 0:
            emis_copy.start()

        def vert_inner(t, carry):
            col = [out_ref[t, z] for z in range(n_z)]
            for z in range(n_z):
                s = speed_ref[sclass_ref[level0 + z], t]
                val = col[z] * (vc_ref[2, z] - s)
                if z > 0:
                    val = val + col[z - 1] * (vc_ref[1, z] + s)
                if z < n_z - 1:
                    val = val + col[z + 1] * vc_ref[0, z]
                pad_ref[k, t, z, PAD : PAD + n_y, :] = val
            return carry

        lax.fori_loop(0, n_t, vert_inner, 0)
        if first:
            barrier = pltpu.get_barrier_semaphore()
            for dev in ((lon, lat, partner), (left, lat, lev), (right, lat, lev)):
                pl.semaphore_signal(barrier, 1, device_id=dev, device_id_type=MESH)

            @pl.when(has_up)
            def _():
                pl.semaphore_signal(barrier, 1, device_id=(lon, up, lev), device_id_type=MESH)

            @pl.when(has_down)
            def _():
                pl.semaphore_signal(barrier, 1, device_id=(lon, down, lev), device_id_type=MESH)

            pl.semaphore_wait(barrier, 3 + has_up.astype(jnp.int32) + has_down.astype(jnp.int32))
            start_coefficient_halos()
            lev_copy.start()
            fix_vertical_coefficients()
        lev_copy.wait()

        lat_up = rcopy(
            pad_ref.at[k, :, :, pl.ds(PAD + n_y - 2, 2), :],
            lh_ref.at[k, :, :, pl.ds(0, 2), :],
            S_UP + k,
            (lon, up, lev),
        )
        lat_down = rcopy(
            pad_ref.at[k, :, :, pl.ds(PAD, 2), :],
            lh_ref.at[k, :, :, pl.ds(2, 2), :],
            S_DOWN + k,
            (lon, down, lev),
        )
        lon_right = rcopy(
            at_ref.at[k, pl.ds(n_x - 2, 2), :], ht_ref.at[k, pl.ds(n_x - 2, 2), :], S_RIGHT + k, (right, lat, lev)
        )
        lon_left = rcopy(
            at_ref.at[k, pl.ds(0, 2), :], ht_ref.at[k, pl.ds(0, 2), :], S_LEFT + k, (left, lat, lev)
        )

        for t in range(n_t):
            z = edge_z
            s = speed_ref[sclass_ref[level0 + z], t]
            a = out_ref[t, z]
            other = out_ref[t, inner_z]
            halo = lv_ref[k, t, 0]
            a_below = jnp.where(low_half, other, halo)
            a_above = jnp.where(low_half, halo, other)
            pad_ref[k, t, z, PAD : PAD + n_y, :] = (
                a * (vc_ref[2, z] - s) + a_below * (vc_ref[1, z] + s) + a_above * vc_ref[0, z]
            )
            up_t = rcopy(
                pad_ref.at[k, t, :, pl.ds(PAD + n_y - 2, 2), :],
                lh_ref.at[k, t, :, pl.ds(0, 2), :],
                S_UP + k,
                (lon, up, lev),
            )
            down_t = rcopy(
                pad_ref.at[k, t, :, pl.ds(PAD, 2), :],
                lh_ref.at[k, t, :, pl.ds(2, 2), :],
                S_DOWN + k,
                (lon, down, lev),
            )

            @pl.when(has_up)
            def _():
                up_t.start()

            @pl.when(has_down)
            def _():
                down_t.start()

        for t in range(n_t):
            blk = pad_ref[k, t, :, PAD : PAD + n_y, :].reshape(rows, n_x)
            cols = pl.ds(t * rows, rows)
            at_ref[k, :, cols] = blk.T
            rcopy(
                at_ref.at[k, pl.ds(n_x - 2, 2), cols], ht_ref.at[k, pl.ds(n_x - 2, 2), cols], S_RIGHT + k,
                (right, lat, lev),
            ).start()
            rcopy(
                at_ref.at[k, pl.ds(0, 2), cols], ht_ref.at[k, pl.ds(0, 2), cols], S_LEFT + k, (left, lat, lev)
            ).start()

        if k == steps - 1:
            build_transport_coefficients()

        def transport(i, carry):
            t = i // n_z
            z = i % n_z
            a = pad_ref[k, t, z, PAD : PAD + n_y, :]
            y_p1 = pad_ref[k, t, z, PAD + 1 : PAD + 1 + n_y, :]
            y_p2 = pad_ref[k, t, z, PAD + 2 : PAD + 2 + n_y, :]
            y_m1 = pad_ref[k, t, z, PAD - 1 : PAD - 1 + n_y, :]
            y_m2 = pad_ref[k, t, z, PAD - 2 : PAD - 2 + n_y, :]
            x_p1 = pltpu.roll(a, n_x - 1, 1)
            x_p2 = pltpu.roll(a, n_x - 2, 1)
            x_m1 = pltpu.roll(a, 1, 1)
            x_m2 = pltpu.roll(a, 2, 1)
            lon_part = (
                cx_ref[0, z] * (a - x_p1)
                + cx_ref[1, z] * (x_p1 - x_p2)
                + cx_ref[2, z] * (x_m1 - a)
                + cx_ref[3, z] * (x_m2 - x_m1)
            )
            lat_part = (
                cy_ref[0, z] * (a - y_p1)
                + cy_ref[1, z] * (y_p1 - y_p2)
                + cy_ref[2, z] * (y_m1 - a)
                + cy_ref[3, z] * (y_m2 - y_m1)
            )
            out_ref[t, z] = a + lon_part + lat_part
            return carry

        lax.fori_loop(0, n_t * n_z, transport, 0, unroll=4)

        lon_right.wait()
        lon_left.wait()

        def lon_edges(t, carry):
            cols = pl.ds(pl.multiple_of(t * rows, rows), rows)
            h_t = ht_ref[k, :, cols].T.reshape(n_z, n_y, n_x)
            for z in range(n_z):
                a = pad_ref[k, t, z, PAD : PAD + n_y, :]
                d = h_t[z] - a
                d_m1 = pltpu.roll(d, 1, 1)
                d_m2 = pltpu.roll(d, 2, 1)
                d_p1 = pltpu.roll(d, n_x - 1, 1)
                d_p2 = pltpu.roll(d, n_x - 2, 1)
                cx0 = cx_ref[0, z]
                cx1 = cx_ref[1, z]
                cxm1 = cx_ref[2, z]
                cxm2 = cx_ref[3, z]
                low = cxm2 * d_m2 + jnp.where(lane == 0, (cxm1 - cxm2) * d_m1, 0.0)
                high = jnp.where(lane == n_x - 1, (cx1 - cx0) * d_p1, 0.0) - cx1 * d_p2
                corr = jnp.where(lane <= 1, low, jnp.where(lane >= n_x - 2, high, 0.0))
                out_ref[t, z] = out_ref[t, z] + corr
            return carry

        lax.fori_loop(0, n_t, lon_edges, 0)

        @pl.when(has_up)
        def _():
            lat_up.wait_send()
            lat_down.wait_recv()

        @pl.when(has_down)
        def _():
            lat_down.wait_send()
            lat_up.wait_recv()

        def lat_edges(t, carry):
            for z in range(n_z):
                h = lh_ref[k, t, z, 0:4, :]
                am2 = h[0:1]
                am1 = h[1:2]
                ap1 = h[2:3]
                ap2 = h[3:4]
                c_lo = cy_ref[:, z, 0:2, :]
                c_hi = cy_ref[:, z, n_y - 2 : n_y, :]
                r0 = c_lo[2, 0:1] * am1 + c_lo[3, 0:1] * (am2 - am1)
                r1 = c_lo[3, 1:2] * am1
                r14 = -c_hi[1, 0:1] * ap1
                r15 = c_hi[1, 1:2] * (ap1 - ap2) - c_hi[0, 1:2] * ap1
                out_ref[t, z, 0:2, :] = out_ref[t, z, 0:2, :] + jnp.concatenate([r0, r1], axis=0)
                out_ref[t, z, n_y - 2 : n_y, :] = out_ref[t, z, n_y - 2 : n_y, :] + jnp.concatenate([r14, r15], axis=0)
            return carry

        lax.fori_loop(0, n_t, lat_edges, 0)

    emis_copy.wait()
    emis_ref[...] = eo_ref[...] + ep_ref[...]
    out_copy = pltpu.make_async_copy(out_ref, out_hbm, local_sem.at[0])
    emis_out = pltpu.make_async_copy(emis_ref, emis_hbm, local_sem.at[1])
    out_copy.start()
    emis_out.start()
    out_copy.wait()
    emis_out.wait()


def hand_over(adj_hbm, emis_hbm, adj_out, emis_out, adj_buf, emis_buf, sem):
    ins = [
        pltpu.make_async_copy(adj_hbm, adj_buf, sem.at[0]),
        pltpu.make_async_copy(emis_hbm, emis_buf, sem.at[1]),
    ]
    for c in ins:
        c.start()
    outs = [
        pltpu.make_async_copy(adj_buf, adj_out, sem.at[2]),
        pltpu.make_async_copy(emis_buf, emis_out, sem.at[3]),
    ]
    for c, o in zip(ins, outs):
        c.wait()
        o.start()
    for o in outs:
        o.wait()


def shards(
    adjoint_in,
    trajectory,
    courant,
    mixing,
    coag_rates,
    settle_speed,
    settle_class,
    emis_profile,
    emis_coef,
    land_mask,
    source_mask,
):
    n_t, n_z, n_y, n_x = adjoint_in.shape
    steps = trajectory.shape[0]
    rows = n_z * n_y
    hbm = pl.BlockSpec(memory_space=pl.ANY)
    vmem = pl.BlockSpec(memory_space=pltpu.VMEM)
    smem = pl.BlockSpec(memory_space=pltpu.SMEM)
    f32 = jnp.float32
    adj_out, emis_out = pl.pallas_call(
        kernel,
        out_shape=(
            jax.ShapeDtypeStruct(adjoint_in.shape, f32),
            jax.ShapeDtypeStruct((3, n_y, n_x), f32),
        ),
        in_specs=[hbm] * 11,
        out_specs=(hbm, hbm),
        scratch_shapes=[
            pltpu.VMEM(adjoint_in.shape, f32),
            pltpu.VMEM((3, n_y, n_x), f32),
            pltpu.VMEM(land_mask.shape, land_mask.dtype),
            pltpu.VMEM(source_mask.shape, source_mask.dtype),
            pltpu.SMEM(coag_rates.shape, f32),
            pltpu.SMEM(settle_speed.shape, f32),
            pltpu.SMEM(settle_class.shape, settle_class.dtype),
            pltpu.SMEM(emis_profile.shape, f32),
            pltpu.SMEM(emis_coef.shape, f32),
            pltpu.VMEM(trajectory.shape, trajectory.dtype),
            pltpu.VMEM(courant.shape, f32),
            pltpu.VMEM(mixing.shape, f32),
            pltpu.VMEM((steps, n_t, n_z, n_y + 2 * PAD, n_x), f32),
            pltpu.VMEM((steps, n_t, n_z, PAD, n_x), f32),
            pltpu.VMEM((steps, n_x, n_t * rows), f32),
            pltpu.VMEM((steps, n_x, n_t * rows), f32),
            pltpu.VMEM((n_t, n_z, n_y, n_x), f32),
            pltpu.VMEM((steps, n_t, 1, n_y, n_x), f32),
            pltpu.VMEM((3, n_y, n_x), f32),
            pltpu.VMEM((3, n_y, n_x), f32),
            pltpu.VMEM((4, n_z, n_y, n_x), f32),
            pltpu.VMEM((4, n_z, n_y, n_x), f32),
            pltpu.VMEM((3, n_z, n_y, n_x), f32),
            pltpu.VMEM((n_x, rows), f32),
            pltpu.VMEM((n_x, rows), f32),
            pltpu.VMEM((n_z, n_y + 2 * PAD, n_x), f32),
            pltpu.VMEM((1, n_y, n_x), f32),
            pltpu.SemaphoreType.DMA((N_REMOTE,)),
            pltpu.SemaphoreType.DMA((N_REMOTE,)),
            pltpu.SemaphoreType.DMA((10 + steps,)),
        ],
        compiler_params=pltpu.CompilerParams(
            collective_id=0, has_side_effects=True, vmem_limit_bytes=67043328
        ),
    )(
        adjoint_in, trajectory, courant, mixing, land_mask, source_mask,
        coag_rates, settle_speed, settle_class, emis_profile, emis_coef,
    )
    return pl.pallas_call(
        hand_over,
        out_shape=(
            jax.ShapeDtypeStruct(adj_out.shape, f32),
            jax.ShapeDtypeStruct(emis_out.shape, f32),
        ),
        in_specs=[hbm, hbm],
        out_specs=(hbm, hbm),
        scratch_shapes=[
            pltpu.VMEM(adj_out.shape, f32),
            pltpu.VMEM(emis_out.shape, f32),
            pltpu.SemaphoreType.DMA((4,)),
        ],
    )(adj_out, emis_out)


def solution(mesh):
    return jax.shard_map(
        shards,
        mesh=mesh,
        in_specs=(
            P(None, "lev", "lat", "lon"),
            P(None, None, "lev", "lat", "lon"),
            P(None, "lev", "lat", "lon"),
            P("lev", "lat", "lon"),
            P(),
            P(),
            P(),
            P(),
            P(),
            P("lat", "lon"),
            P("lat", "lon"),
        ),
        out_specs=(P(None, "lev", "lat", "lon"), P(None, "lat", "lon")),
        check_vma=False,
    )
```

```python
import jax
import jax.numpy as jnp
from jax import lax
from jax.experimental import pallas as pl
from jax.experimental.pallas import tpu as pltpu
from jax.sharding import PartitionSpec as P

MESH = pl.DeviceIdType.MESH
PAD = 8

S_LEV, S_UP, S_DOWN, S_RIGHT, S_LEFT = 0, 3, 6, 9, 12
S_EMIS, S_CE_R, S_CE_L, S_CN_U, S_CN_D, S_MIX = 15, 16, 17, 18, 19, 20
N_REMOTE = 21


def kernel(
    adj_hbm, traj_hbm, cour_hbm, mix_hbm, land_hbm, srcm_hbm,
    rates_hbm, speed_hbm, sclass_hbm, prof_hbm, ecoef_hbm,
    out_hbm, emis_hbm,
    out_ref, emis_ref, land_ref, srcm_ref, rates_ref, speed_ref, sclass_ref, prof_ref, ecoef_ref,
    traj_ref, cour_ref, mix_ref, pad_ref, lh_ref, at_ref, ht_ref, hb_ref, lv_ref, eo_ref, ep_ref,
    cx_ref, cy_ref, vc_ref, cet_ref, ceh_ref, cyp_ref, mh_ref,
    send_sem, recv_sem, local_sem,
):
    n_t, n_z, n_y, n_x = out_ref.shape
    steps = traj_hbm.shape[0]
    rows = n_z * n_y
    lon = lax.axis_index("lon")
    lat = lax.axis_index("lat")
    lev = lax.axis_index("lev")
    n_lon = lax.axis_size("lon")
    n_lat = lax.axis_size("lat")
    right = lax.rem(lon + 1, n_lon)
    left = lax.rem(lon + n_lon - 1, n_lon)
    has_up = lat < n_lat - 1
    has_down = lat > 0
    up = jnp.minimum(lat + 1, n_lat - 1)
    down = jnp.maximum(lat - 1, 0)
    partner = 1 - lev
    low_half = lev == 0
    edge_z = jnp.where(low_half, n_z - 1, 0)
    inner_z = jnp.where(low_half, n_z - 2, 1)
    level0 = lev * n_z

    adj_in = pltpu.make_async_copy(adj_hbm, out_ref, local_sem.at[0])
    cour_in = pltpu.make_async_copy(cour_hbm, cour_ref, local_sem.at[1])
    mix_in = pltpu.make_async_copy(mix_hbm, mix_ref, local_sem.at[2])
    traj_in = [
        pltpu.make_async_copy(traj_hbm.at[k], traj_ref.at[k], local_sem.at[3 + k]) for k in range(steps)
    ]
    small_in = [
        pltpu.make_async_copy(src, dst, local_sem.at[3 + steps + i])
        for i, (src, dst) in enumerate(
            (
                (rates_hbm, rates_ref),
                (speed_hbm, speed_ref),
                (sclass_hbm, sclass_ref),
                (prof_hbm, prof_ref),
                (ecoef_hbm, ecoef_ref),
                (land_hbm, land_ref),
                (srcm_hbm, srcm_ref),
            )
        )
    ]
    for c in small_in:
        c.start()
    cour_in.start()
    mix_in.start()
    adj_in.start()
    for k in range(steps - 1, -1, -1):
        traj_in[k].start()

    zeros_pad = jnp.zeros((n_t, n_z, PAD, n_x), jnp.float32)
    for k in range(steps):
        pad_ref[k, :, :, 0:PAD, :] = zeros_pad
        pad_ref[k, :, :, PAD + n_y : 2 * PAD + n_y, :] = zeros_pad
        lh_ref[k] = zeros_pad
    zeros_c = jnp.zeros((n_z, PAD, n_x), jnp.float32)
    cyp_ref[:, 0:PAD, :] = zeros_c
    cyp_ref[:, PAD + n_y : 2 * PAD + n_y, :] = zeros_c

    def rcopy(src, dst, idx, dev):
        return pltpu.make_async_remote_copy(
            src, dst, send_sem.at[idx], recv_sem.at[idx], device_id=dev, device_id_type=MESH
        )

    lane = lax.broadcasted_iota(jnp.int32, (n_y, n_x), 1)
    row = lax.broadcasted_iota(jnp.int32, (n_y, n_x), 0)

    cour_in.wait()
    mix_in.wait()
    for c in small_in:
        c.wait()
    top_row = jnp.logical_and(lat == n_lat - 1, row == n_y - 1)
    for z in range(n_z):
        cyp_ref[z, PAD : PAD + n_y, :] = jnp.where(top_row, 0.0, cour_ref[1, z])
    cet_ref[...] = cour_ref[0].reshape(rows, n_x).T
    ce_right = rcopy(cet_ref.at[pl.ds(n_x - 2, 2), :], ceh_ref.at[pl.ds(n_x - 2, 2), :], S_CE_R, (right, lat, lev))
    ce_left = rcopy(cet_ref.at[pl.ds(0, 2), :], ceh_ref.at[pl.ds(0, 2), :], S_CE_L, (left, lat, lev))
    cn_up = rcopy(
        cyp_ref.at[:, pl.ds(PAD + n_y - 2, 2), :], cyp_ref.at[:, pl.ds(PAD - 2, 2), :], S_CN_U, (lon, up, lev)
    )
    cn_down = rcopy(
        cyp_ref.at[:, pl.ds(PAD, 2), :], cyp_ref.at[:, pl.ds(PAD + n_y, 2), :], S_CN_D, (lon, down, lev)
    )
    mix_x = rcopy(mix_ref.at[pl.ds(edge_z, 1)], mh_ref, S_MIX, (lon, lat, partner))

    def start_coefficient_halos():
        mix_x.start()
        ce_right.start()
        ce_left.start()

        @pl.when(has_up)
        def _():
            cn_up.start()

        @pl.when(has_down)
        def _():
            cn_down.start()

    def fix_vertical_coefficients():
        mix_x.wait()
        below = jnp.where(low_half, vc_ref[1, 0], mh_ref[0])
        vc_ref[1, 0] = below
        vc_ref[2, 0] = jnp.where(low_half, vc_ref[2, 0], 1.0 - vc_ref[0, 0] - below)

    def build_vertical_coefficients():
        dep = jnp.where(low_half, 0.1 + 0.3 * land_ref[...].astype(jnp.float32), 0.0)
        below = jnp.zeros((n_y, n_x), jnp.float32)
        for z in range(n_z):
            above = mix_ref[z]
            if z == n_z - 1:
                above = jnp.where(low_half, above, 0.0)
            base = 1.0 - above - below
            if z == 0:
                base = base - dep
            vc_ref[0, z] = above
            vc_ref[1, z] = below
            vc_ref[2, z] = base
            below = above

    def build_transport_coefficients():
        ce_right.wait()
        ce_left.wait()

        @pl.when(has_up)
        def _():
            cn_up.wait_send()
            cn_down.wait_recv()

        @pl.when(has_down)
        def _():
            cn_down.wait_send()
            cn_up.wait_recv()

        he = ceh_ref[...].T.reshape(n_z, n_y, n_x)
        for z in range(n_z):
            c = cour_ref[0, z]
            hz = he[z]
            c_p1 = jnp.where(lane == n_x - 1, pltpu.roll(hz, n_x - 1, 1), pltpu.roll(c, n_x - 1, 1))
            c_m1 = jnp.where(lane == 0, pltpu.roll(hz, 1, 1), pltpu.roll(c, 1, 1))
            c_m2 = jnp.where(lane <= 1, pltpu.roll(hz, 2, 1), pltpu.roll(c, 2, 1))
            cx_ref[0, z] = -1.5 * jnp.maximum(c, 0.0)
            cx_ref[1, z] = 0.5 * jnp.maximum(c_p1, 0.0)
            cx_ref[2, z] = -1.5 * jnp.minimum(c_m1, 0.0)
            cx_ref[3, z] = 0.5 * jnp.minimum(c_m2, 0.0)
            cy_ref[0, z] = -1.5 * jnp.maximum(cyp_ref[z, PAD : PAD + n_y, :], 0.0)
            cy_ref[1, z] = 0.5 * jnp.maximum(cyp_ref[z, PAD + 1 : PAD + 1 + n_y, :], 0.0)
            cy_ref[2, z] = -1.5 * jnp.minimum(cyp_ref[z, PAD - 1 : PAD - 1 + n_y, :], 0.0)
            cy_ref[3, z] = 0.5 * jnp.minimum(cyp_ref[z, PAD - 2 : PAD - 2 + n_y, :], 0.0)

    eo_ref[...] = jnp.zeros(eo_ref.shape, jnp.float32)
    src_mask = srcm_ref[...].astype(jnp.float32)
    adj_in.wait()
    build_vertical_coefficients()
    emis_copy = rcopy(eo_ref, ep_ref, S_EMIS, (lon, lat, partner))

    for k in range(steps - 1, -1, -1):
        first = k == steps - 1
        traj_in[k].wait()

        def coag_level(zz, acc):
            z = jnp.where(low_half, n_z - 1 - zz, zz)
            zg = level0 + z
            lam = [out_ref[t, z] for t in range(n_t)]
            st = [traj_ref[k, t, z].astype(jnp.float32) for t in range(n_t)]
            new_acc = []
            for m in range(3):
                part = acc[m]
                for j in range(3):
                    part = part + (ecoef_ref[3 * m + j] * prof_ref[zg]) * lam[3 * m + j]
                new_acc.append(part)
            k0, k1, k2, k01, k02, k12 = [rates_ref[i, zg] for i in range(6)]
            n0, v0, w0, n1, v1, w1, n2, v2, w2 = st
            ln0, lv0, lw0, ln1, lv1, lw1, ln2, lv2, lw2 = lam
            a01 = k01 * n1
            a02 = k02 * n2
            a12 = k12 * n2
            s0 = a01 + a02
            g_n0 = ln0 * (-2.0 * k0 * n0 - s0)
            g_v0 = (
                (lv1 * a01 + lv2 * a02 - lv0 * s0)
                + 2.0 * (lw0 * (k0 * v0) + lw1 * (k01 * v1) + lw2 * (k02 * v2))
            )
            g_w0 = lw1 * a01 + lw2 * a02 - lw0 * s0
            g_n1 = (
                ln1 * (-2.0 * k1 * n1 - a12)
                - ln0 * (k01 * n0)
                + (lv1 - lv0) * (k01 * v0)
                + (lw1 - lw0) * (k01 * w0)
            )
            g_v1 = (lv2 - lv1) * a12 + 2.0 * (lw1 * (k1 * v1 + k01 * v0) + lw2 * (k12 * v2))
            g_w1 = (lw2 - lw1) * a12
            g_n2 = (
                -2.0 * k2 * n2 * ln2
                - ln0 * (k02 * n0)
                - ln1 * (k12 * n1)
                + (lv2 - lv0) * (k02 * v0)
                + (lv2 - lv1) * (k12 * v1)
                + (lw2 - lw0) * (k02 * w0)
                + (lw2 - lw1) * (k12 * w1)
            )
            g_v2 = 2.0 * lw2 * (k2 * v2 + k02 * v0 + k12 * v1)
            grads = [g_n0, g_v0, g_w0, g_n1, g_v1, g_w1, g_n2, g_v2]
            for t in range(n_t - 1):
                out_ref[t, z] = lam[t] + grads[t]
            return tuple(new_acc)

        zero = jnp.zeros((n_y, n_x), jnp.float32)
        acc = coag_level(0, (zero, zero, zero))
        lev_copy = rcopy(out_ref.at[:, pl.ds(edge_z, 1)], lv_ref.at[k], S_LEV + k, (lon, lat, partner))
        if not first:
            lev_copy.start()
        acc = lax.fori_loop(1, n_z, coag_level, acc)
        for m in range(3):
            eo_ref[m] = eo_ref[m] + acc[m] * src_mask
        if k == 0:
            emis_copy.start()

        def vert_inner(t, carry):
            col = [out_ref[t, z] for z in range(n_z)]
            for z in range(n_z):
                s = speed_ref[sclass_ref[level0 + z], t]
                val = col[z] * (vc_ref[2, z] - s)
                if z > 0:
                    val = val + col[z - 1] * (vc_ref[1, z] + s)
                if z < n_z - 1:
                    val = val + col[z + 1] * vc_ref[0, z]
                pad_ref[k, t, z, PAD : PAD + n_y, :] = val
            return carry

        lax.fori_loop(0, n_t, vert_inner, 0)
        if first:
            barrier = pltpu.get_barrier_semaphore()
            for dev in ((lon, lat, partner), (left, lat, lev), (right, lat, lev)):
                pl.semaphore_signal(barrier, 1, device_id=dev, device_id_type=MESH)

            @pl.when(has_up)
            def _():
                pl.semaphore_signal(barrier, 1, device_id=(lon, up, lev), device_id_type=MESH)

            @pl.when(has_down)
            def _():
                pl.semaphore_signal(barrier, 1, device_id=(lon, down, lev), device_id_type=MESH)

            pl.semaphore_wait(barrier, 3 + has_up.astype(jnp.int32) + has_down.astype(jnp.int32))
            start_coefficient_halos()
            lev_copy.start()
            fix_vertical_coefficients()
        lev_copy.wait()

        lat_up = rcopy(
            pad_ref.at[k, :, :, pl.ds(PAD + n_y - 2, 2), :],
            lh_ref.at[k, :, :, pl.ds(0, 2), :],
            S_UP + k,
            (lon, up, lev),
        )
        lat_down = rcopy(
            pad_ref.at[k, :, :, pl.ds(PAD, 2), :],
            lh_ref.at[k, :, :, pl.ds(2, 2), :],
            S_DOWN + k,
            (lon, down, lev),
        )
        lon_right = rcopy(
            at_ref.at[k, pl.ds(n_x - 2, 2), :], ht_ref.at[k, pl.ds(n_x - 2, 2), :], S_RIGHT + k, (right, lat, lev)
        )
        lon_left = rcopy(
            at_ref.at[k, pl.ds(0, 2), :], ht_ref.at[k, pl.ds(0, 2), :], S_LEFT + k, (left, lat, lev)
        )

        for t in range(n_t):
            z = edge_z
            s = speed_ref[sclass_ref[level0 + z], t]
            a = out_ref[t, z]
            other = out_ref[t, inner_z]
            halo = lv_ref[k, t, 0]
            a_below = jnp.where(low_half, other, halo)
            a_above = jnp.where(low_half, halo, other)
            pad_ref[k, t, z, PAD : PAD + n_y, :] = (
                a * (vc_ref[2, z] - s) + a_below * (vc_ref[1, z] + s) + a_above * vc_ref[0, z]
            )
            up_t = rcopy(
                pad_ref.at[k, t, :, pl.ds(PAD + n_y - 2, 2), :],
                lh_ref.at[k, t, :, pl.ds(0, 2), :],
                S_UP + k,
                (lon, up, lev),
            )
            down_t = rcopy(
                pad_ref.at[k, t, :, pl.ds(PAD, 2), :],
                lh_ref.at[k, t, :, pl.ds(2, 2), :],
                S_DOWN + k,
                (lon, down, lev),
            )

            @pl.when(has_up)
            def _():
                up_t.start()

            @pl.when(has_down)
            def _():
                down_t.start()

        for t in range(n_t):
            blk = pad_ref[k, t, :, PAD : PAD + n_y, :].reshape(rows, n_x)
            cols = pl.ds(t * rows, rows)
            at_ref[k, :, cols] = blk.T
            rcopy(
                at_ref.at[k, pl.ds(n_x - 2, 2), cols], ht_ref.at[k, pl.ds(n_x - 2, 2), cols], S_RIGHT + k,
                (right, lat, lev),
            ).start()
            rcopy(
                at_ref.at[k, pl.ds(0, 2), cols], ht_ref.at[k, pl.ds(0, 2), cols], S_LEFT + k, (left, lat, lev)
            ).start()

        if k == steps - 1:
            build_transport_coefficients()

        def transport(t, carry):
            for z in range(n_z):
                a = pad_ref[k, t, z, PAD : PAD + n_y, :]
                y_p1 = pad_ref[k, t, z, PAD + 1 : PAD + 1 + n_y, :]
                y_p2 = pad_ref[k, t, z, PAD + 2 : PAD + 2 + n_y, :]
                y_m1 = pad_ref[k, t, z, PAD - 1 : PAD - 1 + n_y, :]
                y_m2 = pad_ref[k, t, z, PAD - 2 : PAD - 2 + n_y, :]
                x_p1 = pltpu.roll(a, n_x - 1, 1)
                x_p2 = pltpu.roll(a, n_x - 2, 1)
                x_m1 = pltpu.roll(a, 1, 1)
                x_m2 = pltpu.roll(a, 2, 1)
                lon_part = (
                    cx_ref[0, z] * (a - x_p1)
                    + cx_ref[1, z] * (x_p1 - x_p2)
                    + cx_ref[2, z] * (x_m1 - a)
                    + cx_ref[3, z] * (x_m2 - x_m1)
                )
                lat_part = (
                    cy_ref[0, z] * (a - y_p1)
                    + cy_ref[1, z] * (y_p1 - y_p2)
                    + cy_ref[2, z] * (y_m1 - a)
                    + cy_ref[3, z] * (y_m2 - y_m1)
                )
                out_ref[t, z] = a + lon_part + lat_part
            return carry

        lax.fori_loop(0, n_t, transport, 0)

        lon_right.wait()
        lon_left.wait()

        def lon_edges(t, carry):
            cols = pl.ds(pl.multiple_of(t * rows, rows), rows)
            h_t = ht_ref[k, :, cols].T.reshape(n_z, n_y, n_x)
            for z in range(n_z):
                a = pad_ref[k, t, z, PAD : PAD + n_y, :]
                d = h_t[z] - a
                d_m1 = pltpu.roll(d, 1, 1)
                d_m2 = pltpu.roll(d, 2, 1)
                d_p1 = pltpu.roll(d, n_x - 1, 1)
                d_p2 = pltpu.roll(d, n_x - 2, 1)
                cx0 = cx_ref[0, z]
                cx1 = cx_ref[1, z]
                cxm1 = cx_ref[2, z]
                cxm2 = cx_ref[3, z]
                low = cxm2 * d_m2 + jnp.where(lane == 0, (cxm1 - cxm2) * d_m1, 0.0)
                high = jnp.where(lane == n_x - 1, (cx1 - cx0) * d_p1, 0.0) - cx1 * d_p2
                corr = jnp.where(lane <= 1, low, jnp.where(lane >= n_x - 2, high, 0.0))
                out_ref[t, z] = out_ref[t, z] + corr
            return carry

        lax.fori_loop(0, n_t, lon_edges, 0)

        @pl.when(has_up)
        def _():
            lat_up.wait_send()
            lat_down.wait_recv()

        @pl.when(has_down)
        def _():
            lat_down.wait_send()
            lat_up.wait_recv()

        def lat_edges(t, carry):
            for z in range(n_z):
                h = lh_ref[k, t, z, 0:4, :]
                am2 = h[0:1]
                am1 = h[1:2]
                ap1 = h[2:3]
                ap2 = h[3:4]
                c_lo = cy_ref[:, z, 0:2, :]
                c_hi = cy_ref[:, z, n_y - 2 : n_y, :]
                r0 = c_lo[2, 0:1] * am1 + c_lo[3, 0:1] * (am2 - am1)
                r1 = c_lo[3, 1:2] * am1
                r14 = -c_hi[1, 0:1] * ap1
                r15 = c_hi[1, 1:2] * (ap1 - ap2) - c_hi[0, 1:2] * ap1
                out_ref[t, z, 0:2, :] = out_ref[t, z, 0:2, :] + jnp.concatenate([r0, r1], axis=0)
                out_ref[t, z, n_y - 2 : n_y, :] = out_ref[t, z, n_y - 2 : n_y, :] + jnp.concatenate([r14, r15], axis=0)
            return carry

        lax.fori_loop(0, n_t, lat_edges, 0)

    emis_copy.wait()
    emis_ref[...] = eo_ref[...] + ep_ref[...]
    out_copy = pltpu.make_async_copy(out_ref, out_hbm, local_sem.at[0])
    emis_out = pltpu.make_async_copy(emis_ref, emis_hbm, local_sem.at[1])
    out_copy.start()
    emis_out.start()
    out_copy.wait()
    emis_out.wait()


def hand_over(adj_hbm, emis_hbm, adj_out, emis_out, adj_buf, emis_buf, sem):
    ins = [
        pltpu.make_async_copy(adj_hbm, adj_buf, sem.at[0]),
        pltpu.make_async_copy(emis_hbm, emis_buf, sem.at[1]),
    ]
    for c in ins:
        c.start()
    outs = [
        pltpu.make_async_copy(adj_buf, adj_out, sem.at[2]),
        pltpu.make_async_copy(emis_buf, emis_out, sem.at[3]),
    ]
    for c, o in zip(ins, outs):
        c.wait()
        o.start()
    for o in outs:
        o.wait()


def shards(
    adjoint_in,
    trajectory,
    courant,
    mixing,
    coag_rates,
    settle_speed,
    settle_class,
    emis_profile,
    emis_coef,
    land_mask,
    source_mask,
):
    n_t, n_z, n_y, n_x = adjoint_in.shape
    steps = trajectory.shape[0]
    rows = n_z * n_y
    hbm = pl.BlockSpec(memory_space=pl.ANY)
    vmem = pl.BlockSpec(memory_space=pltpu.VMEM)
    smem = pl.BlockSpec(memory_space=pltpu.SMEM)
    f32 = jnp.float32
    adj_out, emis_out = pl.pallas_call(
        kernel,
        out_shape=(
            jax.ShapeDtypeStruct(adjoint_in.shape, f32),
            jax.ShapeDtypeStruct((3, n_y, n_x), f32),
        ),
        in_specs=[hbm] * 11,
        out_specs=(hbm, hbm),
        scratch_shapes=[
            pltpu.VMEM(adjoint_in.shape, f32),
            pltpu.VMEM((3, n_y, n_x), f32),
            pltpu.VMEM(land_mask.shape, land_mask.dtype),
            pltpu.VMEM(source_mask.shape, source_mask.dtype),
            pltpu.SMEM(coag_rates.shape, f32),
            pltpu.SMEM(settle_speed.shape, f32),
            pltpu.SMEM(settle_class.shape, settle_class.dtype),
            pltpu.SMEM(emis_profile.shape, f32),
            pltpu.SMEM(emis_coef.shape, f32),
            pltpu.VMEM(trajectory.shape, trajectory.dtype),
            pltpu.VMEM(courant.shape, f32),
            pltpu.VMEM(mixing.shape, f32),
            pltpu.VMEM((steps, n_t, n_z, n_y + 2 * PAD, n_x), f32),
            pltpu.VMEM((steps, n_t, n_z, PAD, n_x), f32),
            pltpu.VMEM((steps, n_x, n_t * rows), f32),
            pltpu.VMEM((steps, n_x, n_t * rows), f32),
            pltpu.VMEM((n_t, n_z, n_y, n_x), f32),
            pltpu.VMEM((steps, n_t, 1, n_y, n_x), f32),
            pltpu.VMEM((3, n_y, n_x), f32),
            pltpu.VMEM((3, n_y, n_x), f32),
            pltpu.VMEM((4, n_z, n_y, n_x), f32),
            pltpu.VMEM((4, n_z, n_y, n_x), f32),
            pltpu.VMEM((3, n_z, n_y, n_x), f32),
            pltpu.VMEM((n_x, rows), f32),
            pltpu.VMEM((n_x, rows), f32),
            pltpu.VMEM((n_z, n_y + 2 * PAD, n_x), f32),
            pltpu.VMEM((1, n_y, n_x), f32),
            pltpu.SemaphoreType.DMA((N_REMOTE,)),
            pltpu.SemaphoreType.DMA((N_REMOTE,)),
            pltpu.SemaphoreType.DMA((10 + steps,)),
        ],
        compiler_params=pltpu.CompilerParams(
            collective_id=0, has_side_effects=True, vmem_limit_bytes=67043328
        ),
    )(
        adjoint_in, trajectory, courant, mixing, land_mask, source_mask,
        coag_rates, settle_speed, settle_class, emis_profile, emis_coef,
    )
    return pl.pallas_call(
        hand_over,
        out_shape=(
            jax.ShapeDtypeStruct(adj_out.shape, f32),
            jax.ShapeDtypeStruct(emis_out.shape, f32),
        ),
        in_specs=[hbm, hbm],
        out_specs=(hbm, hbm),
        scratch_shapes=[
            pltpu.VMEM(adj_out.shape, f32),
            pltpu.VMEM(emis_out.shape, f32),
            pltpu.SemaphoreType.DMA((4,)),
        ],
    )(adj_out, emis_out)


def solution(mesh):
    return jax.shard_map(
        shards,
        mesh=mesh,
        in_specs=(
            P(None, "lev", "lat", "lon"),
            P(None, None, "lev", "lat", "lon"),
            P(None, "lev", "lat", "lon"),
            P("lev", "lat", "lon"),
            P(),
            P(),
            P(),
            P(),
            P(),
            P("lat", "lon"),
            P("lat", "lon"),
        ),
        out_specs=(P(None, "lev", "lat", "lon"), P(None, "lat", "lon")),
        check_vma=False,
    )
```

```python
import jax
import jax.numpy as jnp
from jax import lax
from jax.experimental import pallas as pl
from jax.experimental.pallas import tpu as pltpu
from jax.sharding import PartitionSpec as P

MESH = pl.DeviceIdType.MESH
PAD = 8

S_LEV, S_UP, S_DOWN, S_RIGHT, S_LEFT = 0, 3, 6, 9, 12
S_EMIS, S_CE_R, S_CE_L, S_CN_U, S_CN_D, S_MIX = 15, 16, 17, 18, 19, 20
N_REMOTE = 21


def kernel(
    adj_hbm, traj_hbm, cour_hbm, mix_hbm, land_hbm, srcm_hbm,
    rates_hbm, speed_hbm, sclass_hbm, prof_hbm, ecoef_hbm,
    out_hbm, emis_hbm,
    out_ref, emis_ref, land_ref, srcm_ref, rates_ref, speed_ref, sclass_ref, prof_ref, ecoef_ref,
    traj_ref, cour_ref, mix_ref, pad_ref, lh_ref, at_ref, ht_ref, hb_ref, lv_ref, eo_ref, ep_ref,
    cx_ref, cy_ref, vc_ref, cet_ref, ceh_ref, cyp_ref, mh_ref,
    send_sem, recv_sem, local_sem,
):
    n_t, n_z, n_y, n_x = out_ref.shape
    steps = traj_hbm.shape[0]
    rows = n_z * n_y
    lon = lax.axis_index("lon")
    lat = lax.axis_index("lat")
    lev = lax.axis_index("lev")
    n_lon = lax.axis_size("lon")
    n_lat = lax.axis_size("lat")
    right = lax.rem(lon + 1, n_lon)
    left = lax.rem(lon + n_lon - 1, n_lon)
    has_up = lat < n_lat - 1
    has_down = lat > 0
    up = jnp.minimum(lat + 1, n_lat - 1)
    down = jnp.maximum(lat - 1, 0)
    partner = 1 - lev
    low_half = lev == 0
    edge_z = jnp.where(low_half, n_z - 1, 0)
    inner_z = jnp.where(low_half, n_z - 2, 1)
    level0 = lev * n_z

    adj_in = pltpu.make_async_copy(adj_hbm, out_ref, local_sem.at[0])
    cour_in = pltpu.make_async_copy(cour_hbm, cour_ref, local_sem.at[1])
    mix_in = pltpu.make_async_copy(mix_hbm, mix_ref, local_sem.at[2])
    traj_in = [
        pltpu.make_async_copy(traj_hbm.at[k], traj_ref.at[k], local_sem.at[3 + k]) for k in range(steps)
    ]
    small_in = [
        pltpu.make_async_copy(src, dst, local_sem.at[3 + steps + i])
        for i, (src, dst) in enumerate(
            (
                (rates_hbm, rates_ref),
                (speed_hbm, speed_ref),
                (sclass_hbm, sclass_ref),
                (prof_hbm, prof_ref),
                (ecoef_hbm, ecoef_ref),
                (land_hbm, land_ref),
                (srcm_hbm, srcm_ref),
            )
        )
    ]
    for c in small_in:
        c.start()
    cour_in.start()
    mix_in.start()
    adj_in.start()
    for k in range(steps - 1, -1, -1):
        traj_in[k].start()

    zeros_pad = jnp.zeros((n_t, n_z, PAD, n_x), jnp.float32)
    for k in range(steps):
        pad_ref[k, :, :, 0:PAD, :] = zeros_pad
        pad_ref[k, :, :, PAD + n_y : 2 * PAD + n_y, :] = zeros_pad
        lh_ref[k] = zeros_pad
    zeros_c = jnp.zeros((n_z, PAD, n_x), jnp.float32)
    cyp_ref[:, 0:PAD, :] = zeros_c
    cyp_ref[:, PAD + n_y : 2 * PAD + n_y, :] = zeros_c

    def rcopy(src, dst, idx, dev):
        return pltpu.make_async_remote_copy(
            src, dst, send_sem.at[idx], recv_sem.at[idx], device_id=dev, device_id_type=MESH
        )

    lane = lax.broadcasted_iota(jnp.int32, (n_y, n_x), 1)
    row = lax.broadcasted_iota(jnp.int32, (n_y, n_x), 0)

    cour_in.wait()
    mix_in.wait()
    for c in small_in:
        c.wait()
    top_row = jnp.logical_and(lat == n_lat - 1, row == n_y - 1)
    for z in range(n_z):
        cyp_ref[z, PAD : PAD + n_y, :] = jnp.where(top_row, 0.0, cour_ref[1, z])
    cet_ref[...] = cour_ref[0].reshape(rows, n_x).T
    ce_right = rcopy(cet_ref.at[pl.ds(n_x - 2, 2), :], ceh_ref.at[pl.ds(n_x - 2, 2), :], S_CE_R, (right, lat, lev))
    ce_left = rcopy(cet_ref.at[pl.ds(0, 2), :], ceh_ref.at[pl.ds(0, 2), :], S_CE_L, (left, lat, lev))
    cn_up = rcopy(
        cyp_ref.at[:, pl.ds(PAD + n_y - 2, 2), :], cyp_ref.at[:, pl.ds(PAD - 2, 2), :], S_CN_U, (lon, up, lev)
    )
    cn_down = rcopy(
        cyp_ref.at[:, pl.ds(PAD, 2), :], cyp_ref.at[:, pl.ds(PAD + n_y, 2), :], S_CN_D, (lon, down, lev)
    )
    mix_x = rcopy(mix_ref.at[pl.ds(edge_z, 1)], mh_ref, S_MIX, (lon, lat, partner))

    def start_coefficient_halos():
        mix_x.start()
        ce_right.start()
        ce_left.start()

        @pl.when(has_up)
        def _():
            cn_up.start()

        @pl.when(has_down)
        def _():
            cn_down.start()

    def fix_vertical_coefficients():
        mix_x.wait()
        below = jnp.where(low_half, vc_ref[1, 0], mh_ref[0])
        vc_ref[1, 0] = below
        vc_ref[2, 0] = jnp.where(low_half, vc_ref[2, 0], 1.0 - vc_ref[0, 0] - below)

    def build_vertical_coefficients():
        dep = jnp.where(low_half, 0.1 + 0.3 * land_ref[...].astype(jnp.float32), 0.0)
        below = jnp.zeros((n_y, n_x), jnp.float32)
        for z in range(n_z):
            above = mix_ref[z]
            if z == n_z - 1:
                above = jnp.where(low_half, above, 0.0)
            base = 1.0 - above - below
            if z == 0:
                base = base - dep
            vc_ref[0, z] = above
            vc_ref[1, z] = below
            vc_ref[2, z] = base
            below = above

    def build_transport_coefficients():
        ce_right.wait()
        ce_left.wait()

        @pl.when(has_up)
        def _():
            cn_up.wait_send()
            cn_down.wait_recv()

        @pl.when(has_down)
        def _():
            cn_down.wait_send()
            cn_up.wait_recv()

        he = ceh_ref[...].T.reshape(n_z, n_y, n_x)
        for z in range(n_z):
            c = cour_ref[0, z]
            hz = he[z]
            c_p1 = jnp.where(lane == n_x - 1, pltpu.roll(hz, n_x - 1, 1), pltpu.roll(c, n_x - 1, 1))
            c_m1 = jnp.where(lane == 0, pltpu.roll(hz, 1, 1), pltpu.roll(c, 1, 1))
            c_m2 = jnp.where(lane <= 1, pltpu.roll(hz, 2, 1), pltpu.roll(c, 2, 1))
            cx_ref[0, z] = -1.5 * jnp.maximum(c, 0.0)
            cx_ref[1, z] = 0.5 * jnp.maximum(c_p1, 0.0)
            cx_ref[2, z] = -1.5 * jnp.minimum(c_m1, 0.0)
            cx_ref[3, z] = 0.5 * jnp.minimum(c_m2, 0.0)
            cy_ref[0, z] = -1.5 * jnp.maximum(cyp_ref[z, PAD : PAD + n_y, :], 0.0)
            cy_ref[1, z] = 0.5 * jnp.maximum(cyp_ref[z, PAD + 1 : PAD + 1 + n_y, :], 0.0)
            cy_ref[2, z] = -1.5 * jnp.minimum(cyp_ref[z, PAD - 1 : PAD - 1 + n_y, :], 0.0)
            cy_ref[3, z] = 0.5 * jnp.minimum(cyp_ref[z, PAD - 2 : PAD - 2 + n_y, :], 0.0)

    eo_ref[...] = jnp.zeros(eo_ref.shape, jnp.float32)
    src_mask = srcm_ref[...].astype(jnp.float32)
    adj_in.wait()
    build_vertical_coefficients()
    emis_copy = rcopy(eo_ref, ep_ref, S_EMIS, (lon, lat, partner))

    for k in range(steps - 1, -1, -1):
        first = k == steps - 1
        traj_in[k].wait()

        def coag_level(zz, acc):
            z = jnp.where(low_half, n_z - 1 - zz, zz)
            zg = level0 + z
            lam = [out_ref[t, z] for t in range(n_t)]
            st = [traj_ref[k, t, z].astype(jnp.float32) for t in range(n_t)]
            new_acc = []
            for m in range(3):
                part = acc[m]
                for j in range(3):
                    part = part + (ecoef_ref[3 * m + j] * prof_ref[zg]) * lam[3 * m + j]
                new_acc.append(part)
            k0, k1, k2, k01, k02, k12 = [rates_ref[i, zg] for i in range(6)]
            n0, v0, w0, n1, v1, w1, n2, v2, w2 = st
            ln0, lv0, lw0, ln1, lv1, lw1, ln2, lv2, lw2 = lam
            a01 = k01 * n1
            a02 = k02 * n2
            a12 = k12 * n2
            s0 = a01 + a02
            g_n0 = ln0 * (-2.0 * k0 * n0 - s0)
            g_v0 = (
                (lv1 * a01 + lv2 * a02 - lv0 * s0)
                + 2.0 * (lw0 * (k0 * v0) + lw1 * (k01 * v1) + lw2 * (k02 * v2))
            )
            g_w0 = lw1 * a01 + lw2 * a02 - lw0 * s0
            g_n1 = (
                ln1 * (-2.0 * k1 * n1 - a12)
                - ln0 * (k01 * n0)
                + (lv1 - lv0) * (k01 * v0)
                + (lw1 - lw0) * (k01 * w0)
            )
            g_v1 = (lv2 - lv1) * a12 + 2.0 * (lw1 * (k1 * v1 + k01 * v0) + lw2 * (k12 * v2))
            g_w1 = (lw2 - lw1) * a12
            g_n2 = (
                -2.0 * k2 * n2 * ln2
                - ln0 * (k02 * n0)
                - ln1 * (k12 * n1)
                + (lv2 - lv0) * (k02 * v0)
                + (lv2 - lv1) * (k12 * v1)
                + (lw2 - lw0) * (k02 * w0)
                + (lw2 - lw1) * (k12 * w1)
            )
            g_v2 = 2.0 * lw2 * (k2 * v2 + k02 * v0 + k12 * v1)
            grads = [g_n0, g_v0, g_w0, g_n1, g_v1, g_w1, g_n2, g_v2]
            for t in range(n_t - 1):
                out_ref[t, z] = lam[t] + grads[t]
            return tuple(new_acc)

        zero = jnp.zeros((n_y, n_x), jnp.float32)
        acc = coag_level(0, (zero, zero, zero))
        lev_copy = rcopy(out_ref.at[:, pl.ds(edge_z, 1)], lv_ref.at[k], S_LEV + k, (lon, lat, partner))
        if not first:
            lev_copy.start()
        acc = lax.fori_loop(1, n_z, coag_level, acc, unroll=True)
        for m in range(3):
            eo_ref[m] = eo_ref[m] + acc[m] * src_mask
        if k == 0:
            emis_copy.start()

        def vert_inner(t, carry):
            col = [out_ref[t, z] for z in range(n_z)]
            for z in range(n_z):
                s = speed_ref[sclass_ref[level0 + z], t]
                val = col[z] * (vc_ref[2, z] - s)
                if z > 0:
                    val = val + col[z - 1] * (vc_ref[1, z] + s)
                if z < n_z - 1:
                    val = val + col[z + 1] * vc_ref[0, z]
                pad_ref[k, t, z, PAD : PAD + n_y, :] = val
            return carry

        lax.fori_loop(0, n_t, vert_inner, 0)
        if first:
            barrier = pltpu.get_barrier_semaphore()
            for dev in ((lon, lat, partner), (left, lat, lev), (right, lat, lev)):
                pl.semaphore_signal(barrier, 1, device_id=dev, device_id_type=MESH)

            @pl.when(has_up)
            def _():
                pl.semaphore_signal(barrier, 1, device_id=(lon, up, lev), device_id_type=MESH)

            @pl.when(has_down)
            def _():
                pl.semaphore_signal(barrier, 1, device_id=(lon, down, lev), device_id_type=MESH)

            pl.semaphore_wait(barrier, 3 + has_up.astype(jnp.int32) + has_down.astype(jnp.int32))
            start_coefficient_halos()
            lev_copy.start()
            fix_vertical_coefficients()
        lev_copy.wait()

        lat_up = rcopy(
            pad_ref.at[k, :, :, pl.ds(PAD + n_y - 2, 2), :],
            lh_ref.at[k, :, :, pl.ds(0, 2), :],
            S_UP + k,
            (lon, up, lev),
        )
        lat_down = rcopy(
            pad_ref.at[k, :, :, pl.ds(PAD, 2), :],
            lh_ref.at[k, :, :, pl.ds(2, 2), :],
            S_DOWN + k,
            (lon, down, lev),
        )
        lon_right = rcopy(
            at_ref.at[k, pl.ds(n_x - 2, 2), :], ht_ref.at[k, pl.ds(n_x - 2, 2), :], S_RIGHT + k, (right, lat, lev)
        )
        lon_left = rcopy(
            at_ref.at[k, pl.ds(0, 2), :], ht_ref.at[k, pl.ds(0, 2), :], S_LEFT + k, (left, lat, lev)
        )

        for t in range(n_t):
            z = edge_z
            s = speed_ref[sclass_ref[level0 + z], t]
            a = out_ref[t, z]
            other = out_ref[t, inner_z]
            halo = lv_ref[k, t, 0]
            a_below = jnp.where(low_half, other, halo)
            a_above = jnp.where(low_half, halo, other)
            pad_ref[k, t, z, PAD : PAD + n_y, :] = (
                a * (vc_ref[2, z] - s) + a_below * (vc_ref[1, z] + s) + a_above * vc_ref[0, z]
            )
            up_t = rcopy(
                pad_ref.at[k, t, :, pl.ds(PAD + n_y - 2, 2), :],
                lh_ref.at[k, t, :, pl.ds(0, 2), :],
                S_UP + k,
                (lon, up, lev),
            )
            down_t = rcopy(
                pad_ref.at[k, t, :, pl.ds(PAD, 2), :],
                lh_ref.at[k, t, :, pl.ds(2, 2), :],
                S_DOWN + k,
                (lon, down, lev),
            )

            @pl.when(has_up)
            def _():
                up_t.start()

            @pl.when(has_down)
            def _():
                down_t.start()

        for t in range(n_t):
            blk = pad_ref[k, t, :, PAD : PAD + n_y, :].reshape(rows, n_x)
            cols = pl.ds(t * rows, rows)
            at_ref[k, :, cols] = blk.T
            rcopy(
                at_ref.at[k, pl.ds(n_x - 2, 2), cols], ht_ref.at[k, pl.ds(n_x - 2, 2), cols], S_RIGHT + k,
                (right, lat, lev),
            ).start()
            rcopy(
                at_ref.at[k, pl.ds(0, 2), cols], ht_ref.at[k, pl.ds(0, 2), cols], S_LEFT + k, (left, lat, lev)
            ).start()

        if k == steps - 1:
            build_transport_coefficients()

        def transport(t, carry):
            for z in range(n_z):
                a = pad_ref[k, t, z, PAD : PAD + n_y, :]
                y_p1 = pad_ref[k, t, z, PAD + 1 : PAD + 1 + n_y, :]
                y_p2 = pad_ref[k, t, z, PAD + 2 : PAD + 2 + n_y, :]
                y_m1 = pad_ref[k, t, z, PAD - 1 : PAD - 1 + n_y, :]
                y_m2 = pad_ref[k, t, z, PAD - 2 : PAD - 2 + n_y, :]
                x_p1 = pltpu.roll(a, n_x - 1, 1)
                x_p2 = pltpu.roll(a, n_x - 2, 1)
                x_m1 = pltpu.roll(a, 1, 1)
                x_m2 = pltpu.roll(a, 2, 1)
                lon_part = (
                    cx_ref[0, z] * (a - x_p1)
                    + cx_ref[1, z] * (x_p1 - x_p2)
                    + cx_ref[2, z] * (x_m1 - a)
                    + cx_ref[3, z] * (x_m2 - x_m1)
                )
                lat_part = (
                    cy_ref[0, z] * (a - y_p1)
                    + cy_ref[1, z] * (y_p1 - y_p2)
                    + cy_ref[2, z] * (y_m1 - a)
                    + cy_ref[3, z] * (y_m2 - y_m1)
                )
                out_ref[t, z] = a + lon_part + lat_part
            return carry

        lax.fori_loop(0, n_t, transport, 0)

        lon_right.wait()
        lon_left.wait()

        def lon_edges(t, carry):
            cols = pl.ds(pl.multiple_of(t * rows, rows), rows)
            h_t = ht_ref[k, :, cols].T.reshape(n_z, n_y, n_x)
            for z in range(n_z):
                a = pad_ref[k, t, z, PAD : PAD + n_y, :]
                d = h_t[z] - a
                d_m1 = pltpu.roll(d, 1, 1)
                d_m2 = pltpu.roll(d, 2, 1)
                d_p1 = pltpu.roll(d, n_x - 1, 1)
                d_p2 = pltpu.roll(d, n_x - 2, 1)
                cx0 = cx_ref[0, z]
                cx1 = cx_ref[1, z]
                cxm1 = cx_ref[2, z]
                cxm2 = cx_ref[3, z]
                low = cxm2 * d_m2 + jnp.where(lane == 0, (cxm1 - cxm2) * d_m1, 0.0)
                high = jnp.where(lane == n_x - 1, (cx1 - cx0) * d_p1, 0.0) - cx1 * d_p2
                corr = jnp.where(lane <= 1, low, jnp.where(lane >= n_x - 2, high, 0.0))
                out_ref[t, z] = out_ref[t, z] + corr
            return carry

        lax.fori_loop(0, n_t, lon_edges, 0)

        @pl.when(has_up)
        def _():
            lat_up.wait_send()
            lat_down.wait_recv()

        @pl.when(has_down)
        def _():
            lat_down.wait_send()
            lat_up.wait_recv()

        def lat_edges(t, carry):
            for z in range(n_z):
                h = lh_ref[k, t, z, 0:4, :]
                am2 = h[0:1]
                am1 = h[1:2]
                ap1 = h[2:3]
                ap2 = h[3:4]
                c_lo = cy_ref[:, z, 0:2, :]
                c_hi = cy_ref[:, z, n_y - 2 : n_y, :]
                r0 = c_lo[2, 0:1] * am1 + c_lo[3, 0:1] * (am2 - am1)
                r1 = c_lo[3, 1:2] * am1
                r14 = -c_hi[1, 0:1] * ap1
                r15 = c_hi[1, 1:2] * (ap1 - ap2) - c_hi[0, 1:2] * ap1
                out_ref[t, z, 0:2, :] = out_ref[t, z, 0:2, :] + jnp.concatenate([r0, r1], axis=0)
                out_ref[t, z, n_y - 2 : n_y, :] = out_ref[t, z, n_y - 2 : n_y, :] + jnp.concatenate([r14, r15], axis=0)
            return carry

        lax.fori_loop(0, n_t, lat_edges, 0)

    emis_copy.wait()
    emis_ref[...] = eo_ref[...] + ep_ref[...]
    out_copy = pltpu.make_async_copy(out_ref, out_hbm, local_sem.at[0])
    emis_out = pltpu.make_async_copy(emis_ref, emis_hbm, local_sem.at[1])
    out_copy.start()
    emis_out.start()
    out_copy.wait()
    emis_out.wait()


def hand_over(adj_hbm, emis_hbm, adj_out, emis_out, adj_buf, emis_buf, sem):
    ins = [
        pltpu.make_async_copy(adj_hbm, adj_buf, sem.at[0]),
        pltpu.make_async_copy(emis_hbm, emis_buf, sem.at[1]),
    ]
    for c in ins:
        c.start()
    outs = [
        pltpu.make_async_copy(adj_buf, adj_out, sem.at[2]),
        pltpu.make_async_copy(emis_buf, emis_out, sem.at[3]),
    ]
    for c, o in zip(ins, outs):
        c.wait()
        o.start()
    for o in outs:
        o.wait()


def shards(
    adjoint_in,
    trajectory,
    courant,
    mixing,
    coag_rates,
    settle_speed,
    settle_class,
    emis_profile,
    emis_coef,
    land_mask,
    source_mask,
):
    n_t, n_z, n_y, n_x = adjoint_in.shape
    steps = trajectory.shape[0]
    rows = n_z * n_y
    hbm = pl.BlockSpec(memory_space=pl.ANY)
    vmem = pl.BlockSpec(memory_space=pltpu.VMEM)
    smem = pl.BlockSpec(memory_space=pltpu.SMEM)
    f32 = jnp.float32
    adj_out, emis_out = pl.pallas_call(
        kernel,
        out_shape=(
            jax.ShapeDtypeStruct(adjoint_in.shape, f32),
            jax.ShapeDtypeStruct((3, n_y, n_x), f32),
        ),
        in_specs=[hbm] * 11,
        out_specs=(hbm, hbm),
        scratch_shapes=[
            pltpu.VMEM(adjoint_in.shape, f32),
            pltpu.VMEM((3, n_y, n_x), f32),
            pltpu.VMEM(land_mask.shape, land_mask.dtype),
            pltpu.VMEM(source_mask.shape, source_mask.dtype),
            pltpu.SMEM(coag_rates.shape, f32),
            pltpu.SMEM(settle_speed.shape, f32),
            pltpu.SMEM(settle_class.shape, settle_class.dtype),
            pltpu.SMEM(emis_profile.shape, f32),
            pltpu.SMEM(emis_coef.shape, f32),
            pltpu.VMEM(trajectory.shape, trajectory.dtype),
            pltpu.VMEM(courant.shape, f32),
            pltpu.VMEM(mixing.shape, f32),
            pltpu.VMEM((steps, n_t, n_z, n_y + 2 * PAD, n_x), f32),
            pltpu.VMEM((steps, n_t, n_z, PAD, n_x), f32),
            pltpu.VMEM((steps, n_x, n_t * rows), f32),
            pltpu.VMEM((steps, n_x, n_t * rows), f32),
            pltpu.VMEM((n_t, n_z, n_y, n_x), f32),
            pltpu.VMEM((steps, n_t, 1, n_y, n_x), f32),
            pltpu.VMEM((3, n_y, n_x), f32),
            pltpu.VMEM((3, n_y, n_x), f32),
            pltpu.VMEM((4, n_z, n_y, n_x), f32),
            pltpu.VMEM((4, n_z, n_y, n_x), f32),
            pltpu.VMEM((3, n_z, n_y, n_x), f32),
            pltpu.VMEM((n_x, rows), f32),
            pltpu.VMEM((n_x, rows), f32),
            pltpu.VMEM((n_z, n_y + 2 * PAD, n_x), f32),
            pltpu.VMEM((1, n_y, n_x), f32),
            pltpu.SemaphoreType.DMA((N_REMOTE,)),
            pltpu.SemaphoreType.DMA((N_REMOTE,)),
            pltpu.SemaphoreType.DMA((10 + steps,)),
        ],
        compiler_params=pltpu.CompilerParams(
            collective_id=0, has_side_effects=True, vmem_limit_bytes=67043328
        ),
    )(
        adjoint_in, trajectory, courant, mixing, land_mask, source_mask,
        coag_rates, settle_speed, settle_class, emis_profile, emis_coef,
    )
    return pl.pallas_call(
        hand_over,
        out_shape=(
            jax.ShapeDtypeStruct(adj_out.shape, f32),
            jax.ShapeDtypeStruct(emis_out.shape, f32),
        ),
        in_specs=[hbm, hbm],
        out_specs=(hbm, hbm),
        scratch_shapes=[
            pltpu.VMEM(adj_out.shape, f32),
            pltpu.VMEM(emis_out.shape, f32),
            pltpu.SemaphoreType.DMA((4,)),
        ],
    )(adj_out, emis_out)


def solution(mesh):
    return jax.shard_map(
        shards,
        mesh=mesh,
        in_specs=(
            P(None, "lev", "lat", "lon"),
            P(None, None, "lev", "lat", "lon"),
            P(None, "lev", "lat", "lon"),
            P("lev", "lat", "lon"),
            P(),
            P(),
            P(),
            P(),
            P(),
            P("lat", "lon"),
            P("lat", "lon"),
        ),
        out_specs=(P(None, "lev", "lat", "lon"), P(None, "lat", "lon")),
        check_vma=False,
    )
```

```python
import jax
import jax.numpy as jnp
from jax import lax
from jax.experimental import pallas as pl
from jax.experimental.pallas import tpu as pltpu
from jax.sharding import PartitionSpec as P

MESH = pl.DeviceIdType.MESH
PAD = 8

S_LEV, S_UP, S_DOWN, S_RIGHT, S_LEFT = 0, 3, 6, 9, 12
S_EMIS, S_CE_R, S_CE_L, S_CN_U, S_CN_D, S_MIX = 15, 16, 17, 18, 19, 20
N_REMOTE = 21


def kernel(
    adj_hbm, traj_hbm, cour_hbm, mix_hbm, land_hbm, srcm_hbm,
    rates_hbm, speed_hbm, sclass_hbm, prof_hbm, ecoef_hbm,
    out_hbm, emis_hbm,
    out_ref, emis_ref, land_ref, srcm_ref, rates_ref, speed_ref, sclass_ref, prof_ref, ecoef_ref,
    traj_ref, cour_ref, mix_ref, pad_ref, lh_ref, at_ref, ht_ref, hb_ref, lv_ref, eo_ref, ep_ref,
    cx_ref, cy_ref, vc_ref, cet_ref, ceh_ref, cyp_ref, mh_ref, tw_ref,
    send_sem, recv_sem, local_sem,
):
    n_t, n_z, n_y, n_x = out_ref.shape
    steps = traj_hbm.shape[0]
    rows = n_z * n_y
    lon = lax.axis_index("lon")
    lat = lax.axis_index("lat")
    lev = lax.axis_index("lev")
    n_lon = lax.axis_size("lon")
    n_lat = lax.axis_size("lat")
    right = lax.rem(lon + 1, n_lon)
    left = lax.rem(lon + n_lon - 1, n_lon)
    has_up = lat < n_lat - 1
    has_down = lat > 0
    up = jnp.minimum(lat + 1, n_lat - 1)
    down = jnp.maximum(lat - 1, 0)
    partner = 1 - lev
    low_half = lev == 0
    edge_z = jnp.where(low_half, n_z - 1, 0)
    inner_z = jnp.where(low_half, n_z - 2, 1)
    level0 = lev * n_z

    adj_in = pltpu.make_async_copy(adj_hbm, out_ref, local_sem.at[0])
    cour_in = pltpu.make_async_copy(cour_hbm, cour_ref, local_sem.at[1])
    mix_in = pltpu.make_async_copy(mix_hbm, mix_ref, local_sem.at[2])
    traj_in = [
        pltpu.make_async_copy(traj_hbm.at[k], traj_ref.at[k], local_sem.at[3 + k]) for k in range(steps)
    ]
    small_in = [
        pltpu.make_async_copy(src, dst, local_sem.at[3 + steps + i])
        for i, (src, dst) in enumerate(
            (
                (rates_hbm, rates_ref),
                (speed_hbm, speed_ref),
                (sclass_hbm, sclass_ref),
                (prof_hbm, prof_ref),
                (ecoef_hbm, ecoef_ref),
                (land_hbm, land_ref),
                (srcm_hbm, srcm_ref),
            )
        )
    ]
    for c in small_in:
        c.start()
    cour_in.start()
    mix_in.start()
    adj_in.start()
    for k in range(steps - 1, -1, -1):
        traj_in[k].start()

    zeros_pad = jnp.zeros((n_t, n_z, PAD, n_x), jnp.float32)
    for k in range(steps):
        pad_ref[k, :, :, 0:PAD, :] = zeros_pad
        pad_ref[k, :, :, PAD + n_y : 2 * PAD + n_y, :] = zeros_pad
        lh_ref[k] = zeros_pad
    zeros_c = jnp.zeros((n_z, PAD, n_x), jnp.float32)
    cyp_ref[:, 0:PAD, :] = zeros_c
    cyp_ref[:, PAD + n_y : 2 * PAD + n_y, :] = zeros_c

    def rcopy(src, dst, idx, dev):
        return pltpu.make_async_remote_copy(
            src, dst, send_sem.at[idx], recv_sem.at[idx], device_id=dev, device_id_type=MESH
        )

    lane = lax.broadcasted_iota(jnp.int32, (n_y, n_x), 1)
    row = lax.broadcasted_iota(jnp.int32, (n_y, n_x), 0)

    cour_in.wait()
    mix_in.wait()
    for c in small_in:
        c.wait()
    top_row = jnp.logical_and(lat == n_lat - 1, row == n_y - 1)
    for z in range(n_z):
        cyp_ref[z, PAD : PAD + n_y, :] = jnp.where(top_row, 0.0, cour_ref[1, z])
    cet_ref[...] = cour_ref[0].reshape(rows, n_x).T
    ce_right = rcopy(cet_ref.at[pl.ds(n_x - 2, 2), :], ceh_ref.at[pl.ds(n_x - 2, 2), :], S_CE_R, (right, lat, lev))
    ce_left = rcopy(cet_ref.at[pl.ds(0, 2), :], ceh_ref.at[pl.ds(0, 2), :], S_CE_L, (left, lat, lev))
    cn_up = rcopy(
        cyp_ref.at[:, pl.ds(PAD + n_y - 2, 2), :], cyp_ref.at[:, pl.ds(PAD - 2, 2), :], S_CN_U, (lon, up, lev)
    )
    cn_down = rcopy(
        cyp_ref.at[:, pl.ds(PAD, 2), :], cyp_ref.at[:, pl.ds(PAD + n_y, 2), :], S_CN_D, (lon, down, lev)
    )
    mix_x = rcopy(mix_ref.at[pl.ds(edge_z, 1)], mh_ref, S_MIX, (lon, lat, partner))

    def start_coefficient_halos():
        mix_x.start()
        ce_right.start()
        ce_left.start()

        @pl.when(has_up)
        def _():
            cn_up.start()

        @pl.when(has_down)
        def _():
            cn_down.start()

    def fix_vertical_coefficients():
        mix_x.wait()
        below = jnp.where(low_half, vc_ref[1, 0], mh_ref[0])
        vc_ref[1, 0] = below
        vc_ref[2, 0] = jnp.where(low_half, vc_ref[2, 0], 1.0 - vc_ref[0, 0] - below)

    def build_vertical_coefficients():
        dep = jnp.where(low_half, 0.1 + 0.3 * land_ref[...].astype(jnp.float32), 0.0)
        below = jnp.zeros((n_y, n_x), jnp.float32)
        for z in range(n_z):
            above = mix_ref[z]
            if z == n_z - 1:
                above = jnp.where(low_half, above, 0.0)
            base = 1.0 - above - below
            if z == 0:
                base = base - dep
            vc_ref[0, z] = above
            vc_ref[1, z] = below
            vc_ref[2, z] = base
            below = above

    def build_transport_coefficients():
        ce_right.wait()
        ce_left.wait()

        @pl.when(has_up)
        def _():
            cn_up.wait_send()
            cn_down.wait_recv()

        @pl.when(has_down)
        def _():
            cn_down.wait_send()
            cn_up.wait_recv()

        he = ceh_ref[...].T.reshape(n_z, n_y, n_x)
        for z in range(n_z):
            c = cour_ref[0, z]
            hz = he[z]
            c_p1 = jnp.where(lane == n_x - 1, pltpu.roll(hz, n_x - 1, 1), pltpu.roll(c, n_x - 1, 1))
            c_m1 = jnp.where(lane == 0, pltpu.roll(hz, 1, 1), pltpu.roll(c, 1, 1))
            c_m2 = jnp.where(lane <= 1, pltpu.roll(hz, 2, 1), pltpu.roll(c, 2, 1))
            cx_ref[0, z] = -1.5 * jnp.maximum(c, 0.0)
            cx_ref[1, z] = 0.5 * jnp.maximum(c_p1, 0.0)
            cx_ref[2, z] = -1.5 * jnp.minimum(c_m1, 0.0)
            cx_ref[3, z] = 0.5 * jnp.minimum(c_m2, 0.0)
            cy_ref[0, z] = -1.5 * jnp.maximum(cyp_ref[z, PAD : PAD + n_y, :], 0.0)
            cy_ref[1, z] = 0.5 * jnp.maximum(cyp_ref[z, PAD + 1 : PAD + 1 + n_y, :], 0.0)
            cy_ref[2, z] = -1.5 * jnp.minimum(cyp_ref[z, PAD - 1 : PAD - 1 + n_y, :], 0.0)
            cy_ref[3, z] = 0.5 * jnp.minimum(cyp_ref[z, PAD - 2 : PAD - 2 + n_y, :], 0.0)
            x0, x1, xm1, xm2 = (cx_ref[i, z] for i in range(4))
            y0, y1, ym1, ym2 = (cy_ref[i, z] for i in range(4))
            tw_ref[0, z] = 1.0 + (x0 - xm1) + (y0 - ym1)
            tw_ref[1, z] = x1 - x0
            tw_ref[2, z] = -x1
            tw_ref[3, z] = xm1 - xm2
            tw_ref[4, z] = xm2
            tw_ref[5, z] = y1 - y0
            tw_ref[6, z] = -y1
            tw_ref[7, z] = ym1 - ym2
            tw_ref[8, z] = ym2

    eo_ref[...] = jnp.zeros(eo_ref.shape, jnp.float32)
    src_mask = srcm_ref[...].astype(jnp.float32)
    adj_in.wait()
    build_vertical_coefficients()
    emis_copy = rcopy(eo_ref, ep_ref, S_EMIS, (lon, lat, partner))

    for k in range(steps - 1, -1, -1):
        first = k == steps - 1
        traj_in[k].wait()

        def coag_level(zz, acc):
            z = jnp.where(low_half, n_z - 1 - zz, zz)
            zg = level0 + z
            lam = [out_ref[t, z] for t in range(n_t)]
            st = [traj_ref[k, t, z].astype(jnp.float32) for t in range(n_t)]
            new_acc = []
            for m in range(3):
                part = acc[m]
                for j in range(3):
                    part = part + (ecoef_ref[3 * m + j] * prof_ref[zg]) * lam[3 * m + j]
                new_acc.append(part)
            k0, k1, k2, k01, k02, k12 = [rates_ref[i, zg] for i in range(6)]
            n0, v0, w0, n1, v1, w1, n2, v2, w2 = st
            ln0, lv0, lw0, ln1, lv1, lw1, ln2, lv2, lw2 = lam
            a01 = k01 * n1
            a02 = k02 * n2
            a12 = k12 * n2
            s0 = a01 + a02
            g_n0 = ln0 * (-2.0 * k0 * n0 - s0)
            g_v0 = (
                (lv1 * a01 + lv2 * a02 - lv0 * s0)
                + 2.0 * (lw0 * (k0 * v0) + lw1 * (k01 * v1) + lw2 * (k02 * v2))
            )
            g_w0 = lw1 * a01 + lw2 * a02 - lw0 * s0
            g_n1 = (
                ln1 * (-2.0 * k1 * n1 - a12)
                - ln0 * (k01 * n0)
                + (lv1 - lv0) * (k01 * v0)
                + (lw1 - lw0) * (k01 * w0)
            )
            g_v1 = (lv2 - lv1) * a12 + 2.0 * (lw1 * (k1 * v1 + k01 * v0) + lw2 * (k12 * v2))
            g_w1 = (lw2 - lw1) * a12
            g_n2 = (
                -2.0 * k2 * n2 * ln2
                - ln0 * (k02 * n0)
                - ln1 * (k12 * n1)
                + (lv2 - lv0) * (k02 * v0)
                + (lv2 - lv1) * (k12 * v1)
                + (lw2 - lw0) * (k02 * w0)
                + (lw2 - lw1) * (k12 * w1)
            )
            g_v2 = 2.0 * lw2 * (k2 * v2 + k02 * v0 + k12 * v1)
            grads = [g_n0, g_v0, g_w0, g_n1, g_v1, g_w1, g_n2, g_v2]
            for t in range(n_t - 1):
                out_ref[t, z] = lam[t] + grads[t]
            return tuple(new_acc)

        zero = jnp.zeros((n_y, n_x), jnp.float32)
        acc = coag_level(0, (zero, zero, zero))
        lev_copy = rcopy(out_ref.at[:, pl.ds(edge_z, 1)], lv_ref.at[k], S_LEV + k, (lon, lat, partner))
        if not first:
            lev_copy.start()
        acc = lax.fori_loop(1, n_z, coag_level, acc)
        for m in range(3):
            eo_ref[m] = eo_ref[m] + acc[m] * src_mask
        if k == 0:
            emis_copy.start()

        def vert_inner(t, carry):
            col = [out_ref[t, z] for z in range(n_z)]
            for z in range(n_z):
                s = speed_ref[sclass_ref[level0 + z], t]
                val = col[z] * (vc_ref[2, z] - s)
                if z > 0:
                    val = val + col[z - 1] * (vc_ref[1, z] + s)
                if z < n_z - 1:
                    val = val + col[z + 1] * vc_ref[0, z]
                pad_ref[k, t, z, PAD : PAD + n_y, :] = val
            return carry

        lax.fori_loop(0, n_t, vert_inner, 0)
        if first:
            barrier = pltpu.get_barrier_semaphore()
            for dev in ((lon, lat, partner), (left, lat, lev), (right, lat, lev)):
                pl.semaphore_signal(barrier, 1, device_id=dev, device_id_type=MESH)

            @pl.when(has_up)
            def _():
                pl.semaphore_signal(barrier, 1, device_id=(lon, up, lev), device_id_type=MESH)

            @pl.when(has_down)
            def _():
                pl.semaphore_signal(barrier, 1, device_id=(lon, down, lev), device_id_type=MESH)

            pl.semaphore_wait(barrier, 3 + has_up.astype(jnp.int32) + has_down.astype(jnp.int32))
            start_coefficient_halos()
            lev_copy.start()
            fix_vertical_coefficients()
        lev_copy.wait()

        lat_up = rcopy(
            pad_ref.at[k, :, :, pl.ds(PAD + n_y - 2, 2), :],
            lh_ref.at[k, :, :, pl.ds(0, 2), :],
            S_UP + k,
            (lon, up, lev),
        )
        lat_down = rcopy(
            pad_ref.at[k, :, :, pl.ds(PAD, 2), :],
            lh_ref.at[k, :, :, pl.ds(2, 2), :],
            S_DOWN + k,
            (lon, down, lev),
        )
        lon_right = rcopy(
            at_ref.at[k, pl.ds(n_x - 2, 2), :], ht_ref.at[k, pl.ds(n_x - 2, 2), :], S_RIGHT + k, (right, lat, lev)
        )
        lon_left = rcopy(
            at_ref.at[k, pl.ds(0, 2), :], ht_ref.at[k, pl.ds(0, 2), :], S_LEFT + k, (left, lat, lev)
        )

        for t in range(n_t):
            z = edge_z
            s = speed_ref[sclass_ref[level0 + z], t]
            a = out_ref[t, z]
            other = out_ref[t, inner_z]
            halo = lv_ref[k, t, 0]
            a_below = jnp.where(low_half, other, halo)
            a_above = jnp.where(low_half, halo, other)
            pad_ref[k, t, z, PAD : PAD + n_y, :] = (
                a * (vc_ref[2, z] - s) + a_below * (vc_ref[1, z] + s) + a_above * vc_ref[0, z]
            )
            up_t = rcopy(
                pad_ref.at[k, t, :, pl.ds(PAD + n_y - 2, 2), :],
                lh_ref.at[k, t, :, pl.ds(0, 2), :],
                S_UP + k,
                (lon, up, lev),
            )
            down_t = rcopy(
                pad_ref.at[k, t, :, pl.ds(PAD, 2), :],
                lh_ref.at[k, t, :, pl.ds(2, 2), :],
                S_DOWN + k,
                (lon, down, lev),
            )

            @pl.when(has_up)
            def _():
                up_t.start()

            @pl.when(has_down)
            def _():
                down_t.start()

        for t in range(n_t):
            blk = pad_ref[k, t, :, PAD : PAD + n_y, :].reshape(rows, n_x)
            cols = pl.ds(t * rows, rows)
            at_ref[k, :, cols] = blk.T
            rcopy(
                at_ref.at[k, pl.ds(n_x - 2, 2), cols], ht_ref.at[k, pl.ds(n_x - 2, 2), cols], S_RIGHT + k,
                (right, lat, lev),
            ).start()
            rcopy(
                at_ref.at[k, pl.ds(0, 2), cols], ht_ref.at[k, pl.ds(0, 2), cols], S_LEFT + k, (left, lat, lev)
            ).start()

        if k == steps - 1:
            build_transport_coefficients()

        def transport(t, carry):
            for z in range(n_z):
                a = pad_ref[k, t, z, PAD : PAD + n_y, :]
                y_p1 = pad_ref[k, t, z, PAD + 1 : PAD + 1 + n_y, :]
                y_p2 = pad_ref[k, t, z, PAD + 2 : PAD + 2 + n_y, :]
                y_m1 = pad_ref[k, t, z, PAD - 1 : PAD - 1 + n_y, :]
                y_m2 = pad_ref[k, t, z, PAD - 2 : PAD - 2 + n_y, :]
                x_p1 = pltpu.roll(a, n_x - 1, 1)
                x_p2 = pltpu.roll(a, n_x - 2, 1)
                x_m1 = pltpu.roll(a, 1, 1)
                x_m2 = pltpu.roll(a, 2, 1)
                out_ref[t, z] = (
                    (tw_ref[0, z] * a + tw_ref[1, z] * x_p1 + tw_ref[2, z] * x_p2)
                    + (tw_ref[3, z] * x_m1 + tw_ref[4, z] * x_m2)
                    + (tw_ref[5, z] * y_p1 + tw_ref[6, z] * y_p2)
                    + (tw_ref[7, z] * y_m1 + tw_ref[8, z] * y_m2)
                )
            return carry

        lax.fori_loop(0, n_t, transport, 0)

        lon_right.wait()
        lon_left.wait()

        def lon_edges(t, carry):
            cols = pl.ds(pl.multiple_of(t * rows, rows), rows)
            h_t = ht_ref[k, :, cols].T.reshape(n_z, n_y, n_x)
            for z in range(n_z):
                a = pad_ref[k, t, z, PAD : PAD + n_y, :]
                d = h_t[z] - a
                d_m1 = pltpu.roll(d, 1, 1)
                d_m2 = pltpu.roll(d, 2, 1)
                d_p1 = pltpu.roll(d, n_x - 1, 1)
                d_p2 = pltpu.roll(d, n_x - 2, 1)
                cx0 = cx_ref[0, z]
                cx1 = cx_ref[1, z]
                cxm1 = cx_ref[2, z]
                cxm2 = cx_ref[3, z]
                low = cxm2 * d_m2 + jnp.where(lane == 0, (cxm1 - cxm2) * d_m1, 0.0)
                high = jnp.where(lane == n_x - 1, (cx1 - cx0) * d_p1, 0.0) - cx1 * d_p2
                corr = jnp.where(lane <= 1, low, jnp.where(lane >= n_x - 2, high, 0.0))
                out_ref[t, z] = out_ref[t, z] + corr
            return carry

        lax.fori_loop(0, n_t, lon_edges, 0)

        @pl.when(has_up)
        def _():
            lat_up.wait_send()
            lat_down.wait_recv()

        @pl.when(has_down)
        def _():
            lat_down.wait_send()
            lat_up.wait_recv()

        def lat_edges(t, carry):
            for z in range(n_z):
                h = lh_ref[k, t, z, 0:4, :]
                am2 = h[0:1]
                am1 = h[1:2]
                ap1 = h[2:3]
                ap2 = h[3:4]
                c_lo = cy_ref[:, z, 0:2, :]
                c_hi = cy_ref[:, z, n_y - 2 : n_y, :]
                r0 = c_lo[2, 0:1] * am1 + c_lo[3, 0:1] * (am2 - am1)
                r1 = c_lo[3, 1:2] * am1
                r14 = -c_hi[1, 0:1] * ap1
                r15 = c_hi[1, 1:2] * (ap1 - ap2) - c_hi[0, 1:2] * ap1
                out_ref[t, z, 0:2, :] = out_ref[t, z, 0:2, :] + jnp.concatenate([r0, r1], axis=0)
                out_ref[t, z, n_y - 2 : n_y, :] = out_ref[t, z, n_y - 2 : n_y, :] + jnp.concatenate([r14, r15], axis=0)
            return carry

        lax.fori_loop(0, n_t, lat_edges, 0)

    emis_copy.wait()
    emis_ref[...] = eo_ref[...] + ep_ref[...]
    out_copy = pltpu.make_async_copy(out_ref, out_hbm, local_sem.at[0])
    emis_out = pltpu.make_async_copy(emis_ref, emis_hbm, local_sem.at[1])
    out_copy.start()
    emis_out.start()
    out_copy.wait()
    emis_out.wait()


def hand_over(adj_hbm, emis_hbm, adj_out, emis_out, adj_buf, emis_buf, sem):
    ins = [
        pltpu.make_async_copy(adj_hbm, adj_buf, sem.at[0]),
        pltpu.make_async_copy(emis_hbm, emis_buf, sem.at[1]),
    ]
    for c in ins:
        c.start()
    outs = [
        pltpu.make_async_copy(adj_buf, adj_out, sem.at[2]),
        pltpu.make_async_copy(emis_buf, emis_out, sem.at[3]),
    ]
    for c, o in zip(ins, outs):
        c.wait()
        o.start()
    for o in outs:
        o.wait()


def shards(
    adjoint_in,
    trajectory,
    courant,
    mixing,
    coag_rates,
    settle_speed,
    settle_class,
    emis_profile,
    emis_coef,
    land_mask,
    source_mask,
):
    n_t, n_z, n_y, n_x = adjoint_in.shape
    steps = trajectory.shape[0]
    rows = n_z * n_y
    hbm = pl.BlockSpec(memory_space=pl.ANY)
    vmem = pl.BlockSpec(memory_space=pltpu.VMEM)
    smem = pl.BlockSpec(memory_space=pltpu.SMEM)
    f32 = jnp.float32
    adj_out, emis_out = pl.pallas_call(
        kernel,
        out_shape=(
            jax.ShapeDtypeStruct(adjoint_in.shape, f32),
            jax.ShapeDtypeStruct((3, n_y, n_x), f32),
        ),
        in_specs=[hbm] * 11,
        out_specs=(hbm, hbm),
        scratch_shapes=[
            pltpu.VMEM(adjoint_in.shape, f32),
            pltpu.VMEM((3, n_y, n_x), f32),
            pltpu.VMEM(land_mask.shape, land_mask.dtype),
            pltpu.VMEM(source_mask.shape, source_mask.dtype),
            pltpu.SMEM(coag_rates.shape, f32),
            pltpu.SMEM(settle_speed.shape, f32),
            pltpu.SMEM(settle_class.shape, settle_class.dtype),
            pltpu.SMEM(emis_profile.shape, f32),
            pltpu.SMEM(emis_coef.shape, f32),
            pltpu.VMEM(trajectory.shape, trajectory.dtype),
            pltpu.VMEM(courant.shape, f32),
            pltpu.VMEM(mixing.shape, f32),
            pltpu.VMEM((steps, n_t, n_z, n_y + 2 * PAD, n_x), f32),
            pltpu.VMEM((steps, n_t, n_z, PAD, n_x), f32),
            pltpu.VMEM((steps, n_x, n_t * rows), f32),
            pltpu.VMEM((steps, n_x, n_t * rows), f32),
            pltpu.VMEM((n_t, n_z, n_y, n_x), f32),
            pltpu.VMEM((steps, n_t, 1, n_y, n_x), f32),
            pltpu.VMEM((3, n_y, n_x), f32),
            pltpu.VMEM((3, n_y, n_x), f32),
            pltpu.VMEM((4, n_z, n_y, n_x), f32),
            pltpu.VMEM((4, n_z, n_y, n_x), f32),
            pltpu.VMEM((3, n_z, n_y, n_x), f32),
            pltpu.VMEM((n_x, rows), f32),
            pltpu.VMEM((n_x, rows), f32),
            pltpu.VMEM((n_z, n_y + 2 * PAD, n_x), f32),
            pltpu.VMEM((1, n_y, n_x), f32),
            pltpu.VMEM((9, n_z, n_y, n_x), f32),
            pltpu.SemaphoreType.DMA((N_REMOTE,)),
            pltpu.SemaphoreType.DMA((N_REMOTE,)),
            pltpu.SemaphoreType.DMA((10 + steps,)),
        ],
        compiler_params=pltpu.CompilerParams(
            collective_id=0, has_side_effects=True, vmem_limit_bytes=67043328
        ),
    )(
        adjoint_in, trajectory, courant, mixing, land_mask, source_mask,
        coag_rates, settle_speed, settle_class, emis_profile, emis_coef,
    )
    return pl.pallas_call(
        hand_over,
        out_shape=(
            jax.ShapeDtypeStruct(adj_out.shape, f32),
            jax.ShapeDtypeStruct(emis_out.shape, f32),
        ),
        in_specs=[hbm, hbm],
        out_specs=(hbm, hbm),
        scratch_shapes=[
            pltpu.VMEM(adj_out.shape, f32),
            pltpu.VMEM(emis_out.shape, f32),
            pltpu.SemaphoreType.DMA((4,)),
        ],
    )(adj_out, emis_out)


def solution(mesh):
    return jax.shard_map(
        shards,
        mesh=mesh,
        in_specs=(
            P(None, "lev", "lat", "lon"),
            P(None, None, "lev", "lat", "lon"),
            P(None, "lev", "lat", "lon"),
            P("lev", "lat", "lon"),
            P(),
            P(),
            P(),
            P(),
            P(),
            P("lat", "lon"),
            P("lat", "lon"),
        ),
        out_specs=(P(None, "lev", "lat", "lon"), P(None, "lat", "lon")),
        check_vma=False,
    )
```

```python
import jax
import jax.numpy as jnp
from jax import lax
from jax.experimental import pallas as pl
from jax.experimental.pallas import tpu as pltpu
from jax.sharding import PartitionSpec as P

MESH = pl.DeviceIdType.MESH
PAD = 8

S_LEV, S_UP, S_DOWN, S_RIGHT, S_LEFT = 0, 3, 6, 9, 12
S_EMIS, S_CE_R, S_CE_L, S_CN_U, S_CN_D, S_MIX = 15, 16, 17, 18, 19, 20
N_REMOTE = 21


def kernel(
    adj_hbm, traj_hbm, cour_hbm, mix_hbm, land_hbm, srcm_hbm,
    rates_hbm, speed_hbm, sclass_hbm, prof_hbm, ecoef_hbm,
    out_hbm, emis_hbm,
    out_ref, emis_ref, land_ref, srcm_ref, rates_ref, speed_ref, sclass_ref, prof_ref, ecoef_ref,
    traj_ref, cour_ref, mix_ref, pad_ref, lh_ref, at_ref, ht_ref, hb_ref, lv_ref, eo_ref, ep_ref,
    cx_ref, cy_ref, vc_ref, cet_ref, ceh_ref, cyp_ref, mh_ref,
    send_sem, recv_sem, local_sem,
):
    n_t, n_z, n_y, n_x = out_ref.shape
    steps = traj_hbm.shape[0]
    rows = n_z * n_y
    lon = lax.axis_index("lon")
    lat = lax.axis_index("lat")
    lev = lax.axis_index("lev")
    n_lon = lax.axis_size("lon")
    n_lat = lax.axis_size("lat")
    right = lax.rem(lon + 1, n_lon)
    left = lax.rem(lon + n_lon - 1, n_lon)
    has_up = lat < n_lat - 1
    has_down = lat > 0
    up = jnp.minimum(lat + 1, n_lat - 1)
    down = jnp.maximum(lat - 1, 0)
    partner = 1 - lev
    low_half = lev == 0
    edge_z = jnp.where(low_half, n_z - 1, 0)
    inner_z = jnp.where(low_half, n_z - 2, 1)
    level0 = lev * n_z

    adj_in = pltpu.make_async_copy(adj_hbm, out_ref, local_sem.at[0])
    cour_in = pltpu.make_async_copy(cour_hbm, cour_ref, local_sem.at[1])
    mix_in = pltpu.make_async_copy(mix_hbm, mix_ref, local_sem.at[2])
    traj_in = [
        pltpu.make_async_copy(traj_hbm.at[k], traj_ref.at[k], local_sem.at[3 + k]) for k in range(steps)
    ]
    small_in = [
        pltpu.make_async_copy(src, dst, local_sem.at[3 + steps + i])
        for i, (src, dst) in enumerate(
            (
                (rates_hbm, rates_ref),
                (speed_hbm, speed_ref),
                (sclass_hbm, sclass_ref),
                (prof_hbm, prof_ref),
                (ecoef_hbm, ecoef_ref),
                (land_hbm, land_ref),
                (srcm_hbm, srcm_ref),
            )
        )
    ]
    for c in small_in:
        c.start()
    cour_in.start()
    mix_in.start()
    adj_in.start()
    for k in range(steps - 1, -1, -1):
        traj_in[k].start()

    zeros_pad = jnp.zeros((n_t, n_z, PAD, n_x), jnp.float32)
    for k in range(steps):
        pad_ref[k, :, :, 0:PAD, :] = zeros_pad
        pad_ref[k, :, :, PAD + n_y : 2 * PAD + n_y, :] = zeros_pad
        lh_ref[k] = zeros_pad
    zeros_c = jnp.zeros((n_z, PAD, n_x), jnp.float32)
    cyp_ref[:, 0:PAD, :] = zeros_c
    cyp_ref[:, PAD + n_y : 2 * PAD + n_y, :] = zeros_c

    def rcopy(src, dst, idx, dev):
        return pltpu.make_async_remote_copy(
            src, dst, send_sem.at[idx], recv_sem.at[idx], device_id=dev, device_id_type=MESH
        )

    lane = lax.broadcasted_iota(jnp.int32, (n_y, n_x), 1)
    row = lax.broadcasted_iota(jnp.int32, (n_y, n_x), 0)

    cour_in.wait()
    mix_in.wait()
    for c in small_in:
        c.wait()
    top_row = jnp.logical_and(lat == n_lat - 1, row == n_y - 1)
    for z in range(n_z):
        cyp_ref[z, PAD : PAD + n_y, :] = jnp.where(top_row, 0.0, cour_ref[1, z])
    cet_ref[...] = cour_ref[0].reshape(rows, n_x).T
    ce_right = rcopy(cet_ref.at[pl.ds(n_x - 2, 2), :], ceh_ref.at[pl.ds(n_x - 2, 2), :], S_CE_R, (right, lat, lev))
    ce_left = rcopy(cet_ref.at[pl.ds(0, 2), :], ceh_ref.at[pl.ds(0, 2), :], S_CE_L, (left, lat, lev))
    cn_up = rcopy(
        cyp_ref.at[:, pl.ds(PAD + n_y - 2, 2), :], cyp_ref.at[:, pl.ds(PAD - 2, 2), :], S_CN_U, (lon, up, lev)
    )
    cn_down = rcopy(
        cyp_ref.at[:, pl.ds(PAD, 2), :], cyp_ref.at[:, pl.ds(PAD + n_y, 2), :], S_CN_D, (lon, down, lev)
    )
    mix_x = rcopy(mix_ref.at[pl.ds(edge_z, 1)], mh_ref, S_MIX, (lon, lat, partner))

    def start_coefficient_halos():
        mix_x.start()
        ce_right.start()
        ce_left.start()

        @pl.when(has_up)
        def _():
            cn_up.start()

        @pl.when(has_down)
        def _():
            cn_down.start()

    def fix_vertical_coefficients():
        mix_x.wait()
        below = jnp.where(low_half, vc_ref[1, 0], mh_ref[0])
        vc_ref[1, 0] = below
        vc_ref[2, 0] = jnp.where(low_half, vc_ref[2, 0], 1.0 - vc_ref[0, 0] - below)

    def build_vertical_coefficients():
        dep = jnp.where(low_half, 0.1 + 0.3 * land_ref[...].astype(jnp.float32), 0.0)
        below = jnp.zeros((n_y, n_x), jnp.float32)
        for z in range(n_z):
            above = mix_ref[z]
            if z == n_z - 1:
                above = jnp.where(low_half, above, 0.0)
            base = 1.0 - above - below
            if z == 0:
                base = base - dep
            vc_ref[0, z] = above
            vc_ref[1, z] = below
            vc_ref[2, z] = base
            below = above

    def build_transport_coefficients():
        ce_right.wait()
        ce_left.wait()

        @pl.when(has_up)
        def _():
            cn_up.wait_send()
            cn_down.wait_recv()

        @pl.when(has_down)
        def _():
            cn_down.wait_send()
            cn_up.wait_recv()

        he = ceh_ref[...].T.reshape(n_z, n_y, n_x)
        for z in range(n_z):
            c = cour_ref[0, z]
            hz = he[z]
            c_p1 = jnp.where(lane == n_x - 1, pltpu.roll(hz, n_x - 1, 1), pltpu.roll(c, n_x - 1, 1))
            c_m1 = jnp.where(lane == 0, pltpu.roll(hz, 1, 1), pltpu.roll(c, 1, 1))
            c_m2 = jnp.where(lane <= 1, pltpu.roll(hz, 2, 1), pltpu.roll(c, 2, 1))
            cx_ref[0, z] = -1.5 * jnp.maximum(c, 0.0)
            cx_ref[1, z] = 0.5 * jnp.maximum(c_p1, 0.0)
            cx_ref[2, z] = -1.5 * jnp.minimum(c_m1, 0.0)
            cx_ref[3, z] = 0.5 * jnp.minimum(c_m2, 0.0)
            cy_ref[0, z] = -1.5 * jnp.maximum(cyp_ref[z, PAD : PAD + n_y, :], 0.0)
            cy_ref[1, z] = 0.5 * jnp.maximum(cyp_ref[z, PAD + 1 : PAD + 1 + n_y, :], 0.0)
            cy_ref[2, z] = -1.5 * jnp.minimum(cyp_ref[z, PAD - 1 : PAD - 1 + n_y, :], 0.0)
            cy_ref[3, z] = 0.5 * jnp.minimum(cyp_ref[z, PAD - 2 : PAD - 2 + n_y, :], 0.0)

    eo_ref[...] = jnp.zeros(eo_ref.shape, jnp.float32)
    src_mask = srcm_ref[...].astype(jnp.float32)
    adj_in.wait()
    build_vertical_coefficients()
    emis_copy = rcopy(eo_ref, ep_ref, S_EMIS, (lon, lat, partner))

    def lat_fix(k, t, z):
        h = lh_ref[k, t, z, 0:4, :]
        am2 = h[0:1]
        am1 = h[1:2]
        ap1 = h[2:3]
        ap2 = h[3:4]
        c_lo = cy_ref[:, z, 0:2, :]
        c_hi = cy_ref[:, z, n_y - 2 : n_y, :]
        r0 = c_lo[2, 0:1] * am1 + c_lo[3, 0:1] * (am2 - am1)
        r1 = c_lo[3, 1:2] * am1
        r14 = -c_hi[1, 0:1] * ap1
        r15 = c_hi[1, 1:2] * (ap1 - ap2) - c_hi[0, 1:2] * ap1
        out_ref[t, z, 0:2, :] = out_ref[t, z, 0:2, :] + jnp.concatenate([r0, r1], axis=0)
        out_ref[t, z, n_y - 2 : n_y, :] = out_ref[t, z, n_y - 2 : n_y, :] + jnp.concatenate([r14, r15], axis=0)

    for k in range(steps - 1, -1, -1):
        first = k == steps - 1
        traj_in[k].wait()

        def coag_level(zz, acc):
            z = jnp.where(low_half, n_z - 1 - zz, zz)
            zg = level0 + z
            if not first:
                for t in range(n_t):
                    lat_fix(k + 1, t, z)
            lam = [out_ref[t, z] for t in range(n_t)]
            st = [traj_ref[k, t, z].astype(jnp.float32) for t in range(n_t)]
            new_acc = []
            for m in range(3):
                part = acc[m]
                for j in range(3):
                    part = part + (ecoef_ref[3 * m + j] * prof_ref[zg]) * lam[3 * m + j]
                new_acc.append(part)
            k0, k1, k2, k01, k02, k12 = [rates_ref[i, zg] for i in range(6)]
            n0, v0, w0, n1, v1, w1, n2, v2, w2 = st
            ln0, lv0, lw0, ln1, lv1, lw1, ln2, lv2, lw2 = lam
            a01 = k01 * n1
            a02 = k02 * n2
            a12 = k12 * n2
            s0 = a01 + a02
            g_n0 = ln0 * (-2.0 * k0 * n0 - s0)
            g_v0 = (
                (lv1 * a01 + lv2 * a02 - lv0 * s0)
                + 2.0 * (lw0 * (k0 * v0) + lw1 * (k01 * v1) + lw2 * (k02 * v2))
            )
            g_w0 = lw1 * a01 + lw2 * a02 - lw0 * s0
            g_n1 = (
                ln1 * (-2.0 * k1 * n1 - a12)
                - ln0 * (k01 * n0)
                + (lv1 - lv0) * (k01 * v0)
                + (lw1 - lw0) * (k01 * w0)
            )
            g_v1 = (lv2 - lv1) * a12 + 2.0 * (lw1 * (k1 * v1 + k01 * v0) + lw2 * (k12 * v2))
            g_w1 = (lw2 - lw1) * a12
            g_n2 = (
                -2.0 * k2 * n2 * ln2
                - ln0 * (k02 * n0)
                - ln1 * (k12 * n1)
                + (lv2 - lv0) * (k02 * v0)
                + (lv2 - lv1) * (k12 * v1)
                + (lw2 - lw0) * (k02 * w0)
                + (lw2 - lw1) * (k12 * w1)
            )
            g_v2 = 2.0 * lw2 * (k2 * v2 + k02 * v0 + k12 * v1)
            grads = [g_n0, g_v0, g_w0, g_n1, g_v1, g_w1, g_n2, g_v2]
            for t in range(n_t - 1):
                out_ref[t, z] = lam[t] + grads[t]
            return tuple(new_acc)

        zero = jnp.zeros((n_y, n_x), jnp.float32)
        acc = coag_level(0, (zero, zero, zero))
        lev_copy = rcopy(out_ref.at[:, pl.ds(edge_z, 1)], lv_ref.at[k], S_LEV + k, (lon, lat, partner))
        if not first:
            lev_copy.start()
        acc = lax.fori_loop(1, n_z, coag_level, acc)
        for m in range(3):
            eo_ref[m] = eo_ref[m] + acc[m] * src_mask
        if k == 0:
            emis_copy.start()

        def vert_inner(t, carry):
            col = [out_ref[t, z] for z in range(n_z)]
            for z in range(n_z):
                s = speed_ref[sclass_ref[level0 + z], t]
                val = col[z] * (vc_ref[2, z] - s)
                if z > 0:
                    val = val + col[z - 1] * (vc_ref[1, z] + s)
                if z < n_z - 1:
                    val = val + col[z + 1] * vc_ref[0, z]
                pad_ref[k, t, z, PAD : PAD + n_y, :] = val
            return carry

        lax.fori_loop(0, n_t, vert_inner, 0)
        if first:
            barrier = pltpu.get_barrier_semaphore()
            for dev in ((lon, lat, partner), (left, lat, lev), (right, lat, lev)):
                pl.semaphore_signal(barrier, 1, device_id=dev, device_id_type=MESH)

            @pl.when(has_up)
            def _():
                pl.semaphore_signal(barrier, 1, device_id=(lon, up, lev), device_id_type=MESH)

            @pl.when(has_down)
            def _():
                pl.semaphore_signal(barrier, 1, device_id=(lon, down, lev), device_id_type=MESH)

            pl.semaphore_wait(barrier, 3 + has_up.astype(jnp.int32) + has_down.astype(jnp.int32))
            start_coefficient_halos()
            lev_copy.start()
            fix_vertical_coefficients()
        lev_copy.wait()

        lat_up = rcopy(
            pad_ref.at[k, :, :, pl.ds(PAD + n_y - 2, 2), :],
            lh_ref.at[k, :, :, pl.ds(0, 2), :],
            S_UP + k,
            (lon, up, lev),
        )
        lat_down = rcopy(
            pad_ref.at[k, :, :, pl.ds(PAD, 2), :],
            lh_ref.at[k, :, :, pl.ds(2, 2), :],
            S_DOWN + k,
            (lon, down, lev),
        )
        lon_right = rcopy(
            at_ref.at[k, pl.ds(n_x - 2, 2), :], ht_ref.at[k, pl.ds(n_x - 2, 2), :], S_RIGHT + k, (right, lat, lev)
        )
        lon_left = rcopy(
            at_ref.at[k, pl.ds(0, 2), :], ht_ref.at[k, pl.ds(0, 2), :], S_LEFT + k, (left, lat, lev)
        )

        for t in range(n_t):
            z = edge_z
            s = speed_ref[sclass_ref[level0 + z], t]
            a = out_ref[t, z]
            other = out_ref[t, inner_z]
            halo = lv_ref[k, t, 0]
            a_below = jnp.where(low_half, other, halo)
            a_above = jnp.where(low_half, halo, other)
            pad_ref[k, t, z, PAD : PAD + n_y, :] = (
                a * (vc_ref[2, z] - s) + a_below * (vc_ref[1, z] + s) + a_above * vc_ref[0, z]
            )
            up_t = rcopy(
                pad_ref.at[k, t, :, pl.ds(PAD + n_y - 2, 2), :],
                lh_ref.at[k, t, :, pl.ds(0, 2), :],
                S_UP + k,
                (lon, up, lev),
            )
            down_t = rcopy(
                pad_ref.at[k, t, :, pl.ds(PAD, 2), :],
                lh_ref.at[k, t, :, pl.ds(2, 2), :],
                S_DOWN + k,
                (lon, down, lev),
            )

            @pl.when(has_up)
            def _():
                up_t.start()

            @pl.when(has_down)
            def _():
                down_t.start()

        for t in range(n_t):
            blk = pad_ref[k, t, :, PAD : PAD + n_y, :].reshape(rows, n_x)
            cols = pl.ds(t * rows, rows)
            at_ref[k, :, cols] = blk.T
            rcopy(
                at_ref.at[k, pl.ds(n_x - 2, 2), cols], ht_ref.at[k, pl.ds(n_x - 2, 2), cols], S_RIGHT + k,
                (right, lat, lev),
            ).start()
            rcopy(
                at_ref.at[k, pl.ds(0, 2), cols], ht_ref.at[k, pl.ds(0, 2), cols], S_LEFT + k, (left, lat, lev)
            ).start()

        if k == steps - 1:
            build_transport_coefficients()

        def transport(t, carry):
            for z in range(n_z):
                a = pad_ref[k, t, z, PAD : PAD + n_y, :]
                y_p1 = pad_ref[k, t, z, PAD + 1 : PAD + 1 + n_y, :]
                y_p2 = pad_ref[k, t, z, PAD + 2 : PAD + 2 + n_y, :]
                y_m1 = pad_ref[k, t, z, PAD - 1 : PAD - 1 + n_y, :]
                y_m2 = pad_ref[k, t, z, PAD - 2 : PAD - 2 + n_y, :]
                x_p1 = pltpu.roll(a, n_x - 1, 1)
                x_p2 = pltpu.roll(a, n_x - 2, 1)
                x_m1 = pltpu.roll(a, 1, 1)
                x_m2 = pltpu.roll(a, 2, 1)
                lon_part = (
                    cx_ref[0, z] * (a - x_p1)
                    + cx_ref[1, z] * (x_p1 - x_p2)
                    + cx_ref[2, z] * (x_m1 - a)
                    + cx_ref[3, z] * (x_m2 - x_m1)
                )
                lat_part = (
                    cy_ref[0, z] * (a - y_p1)
                    + cy_ref[1, z] * (y_p1 - y_p2)
                    + cy_ref[2, z] * (y_m1 - a)
                    + cy_ref[3, z] * (y_m2 - y_m1)
                )
                out_ref[t, z] = a + lon_part + lat_part
            return carry

        lax.fori_loop(0, n_t, transport, 0)

        lon_right.wait()
        lon_left.wait()

        def lon_edges(t, carry):
            cols = pl.ds(pl.multiple_of(t * rows, rows), rows)
            h_t = ht_ref[k, :, cols].T.reshape(n_z, n_y, n_x)
            for z in range(n_z):
                a = pad_ref[k, t, z, PAD : PAD + n_y, :]
                d = h_t[z] - a
                d_m1 = pltpu.roll(d, 1, 1)
                d_m2 = pltpu.roll(d, 2, 1)
                d_p1 = pltpu.roll(d, n_x - 1, 1)
                d_p2 = pltpu.roll(d, n_x - 2, 1)
                cx0 = cx_ref[0, z]
                cx1 = cx_ref[1, z]
                cxm1 = cx_ref[2, z]
                cxm2 = cx_ref[3, z]
                low = cxm2 * d_m2 + jnp.where(lane == 0, (cxm1 - cxm2) * d_m1, 0.0)
                high = jnp.where(lane == n_x - 1, (cx1 - cx0) * d_p1, 0.0) - cx1 * d_p2
                corr = jnp.where(lane <= 1, low, jnp.where(lane >= n_x - 2, high, 0.0))
                out_ref[t, z] = out_ref[t, z] + corr
            return carry

        lax.fori_loop(0, n_t, lon_edges, 0)

        @pl.when(has_up)
        def _():
            lat_up.wait_send()
            lat_down.wait_recv()

        @pl.when(has_down)
        def _():
            lat_down.wait_send()
            lat_up.wait_recv()

        if k == 0:
            def lat_edges(t, carry):
                for z in range(n_z):
                    lat_fix(k, t, z)
                return carry

            lax.fori_loop(0, n_t, lat_edges, 0)

    emis_copy.wait()
    emis_ref[...] = eo_ref[...] + ep_ref[...]
    out_copy = pltpu.make_async_copy(out_ref, out_hbm, local_sem.at[0])
    emis_out = pltpu.make_async_copy(emis_ref, emis_hbm, local_sem.at[1])
    out_copy.start()
    emis_out.start()
    out_copy.wait()
    emis_out.wait()


def hand_over(adj_hbm, emis_hbm, adj_out, emis_out, adj_buf, emis_buf, sem):
    ins = [
        pltpu.make_async_copy(adj_hbm, adj_buf, sem.at[0]),
        pltpu.make_async_copy(emis_hbm, emis_buf, sem.at[1]),
    ]
    for c in ins:
        c.start()
    outs = [
        pltpu.make_async_copy(adj_buf, adj_out, sem.at[2]),
        pltpu.make_async_copy(emis_buf, emis_out, sem.at[3]),
    ]
    for c, o in zip(ins, outs):
        c.wait()
        o.start()
    for o in outs:
        o.wait()


def shards(
    adjoint_in,
    trajectory,
    courant,
    mixing,
    coag_rates,
    settle_speed,
    settle_class,
    emis_profile,
    emis_coef,
    land_mask,
    source_mask,
):
    n_t, n_z, n_y, n_x = adjoint_in.shape
    steps = trajectory.shape[0]
    rows = n_z * n_y
    hbm = pl.BlockSpec(memory_space=pl.ANY)
    vmem = pl.BlockSpec(memory_space=pltpu.VMEM)
    smem = pl.BlockSpec(memory_space=pltpu.SMEM)
    f32 = jnp.float32
    adj_out, emis_out = pl.pallas_call(
        kernel,
        out_shape=(
            jax.ShapeDtypeStruct(adjoint_in.shape, f32),
            jax.ShapeDtypeStruct((3, n_y, n_x), f32),
        ),
        in_specs=[hbm] * 11,
        out_specs=(hbm, hbm),
        scratch_shapes=[
            pltpu.VMEM(adjoint_in.shape, f32),
            pltpu.VMEM((3, n_y, n_x), f32),
            pltpu.VMEM(land_mask.shape, land_mask.dtype),
            pltpu.VMEM(source_mask.shape, source_mask.dtype),
            pltpu.SMEM(coag_rates.shape, f32),
            pltpu.SMEM(settle_speed.shape, f32),
            pltpu.SMEM(settle_class.shape, settle_class.dtype),
            pltpu.SMEM(emis_profile.shape, f32),
            pltpu.SMEM(emis_coef.shape, f32),
            pltpu.VMEM(trajectory.shape, trajectory.dtype),
            pltpu.VMEM(courant.shape, f32),
            pltpu.VMEM(mixing.shape, f32),
            pltpu.VMEM((steps, n_t, n_z, n_y + 2 * PAD, n_x), f32),
            pltpu.VMEM((steps, n_t, n_z, PAD, n_x), f32),
            pltpu.VMEM((steps, n_x, n_t * rows), f32),
            pltpu.VMEM((steps, n_x, n_t * rows), f32),
            pltpu.VMEM((n_t, n_z, n_y, n_x), f32),
            pltpu.VMEM((steps, n_t, 1, n_y, n_x), f32),
            pltpu.VMEM((3, n_y, n_x), f32),
            pltpu.VMEM((3, n_y, n_x), f32),
            pltpu.VMEM((4, n_z, n_y, n_x), f32),
            pltpu.VMEM((4, n_z, n_y, n_x), f32),
            pltpu.VMEM((3, n_z, n_y, n_x), f32),
            pltpu.VMEM((n_x, rows), f32),
            pltpu.VMEM((n_x, rows), f32),
            pltpu.VMEM((n_z, n_y + 2 * PAD, n_x), f32),
            pltpu.VMEM((1, n_y, n_x), f32),
            pltpu.SemaphoreType.DMA((N_REMOTE,)),
            pltpu.SemaphoreType.DMA((N_REMOTE,)),
            pltpu.SemaphoreType.DMA((10 + steps,)),
        ],
        compiler_params=pltpu.CompilerParams(
            collective_id=0, has_side_effects=True, vmem_limit_bytes=67043328
        ),
    )(
        adjoint_in, trajectory, courant, mixing, land_mask, source_mask,
        coag_rates, settle_speed, settle_class, emis_profile, emis_coef,
    )
    return pl.pallas_call(
        hand_over,
        out_shape=(
            jax.ShapeDtypeStruct(adj_out.shape, f32),
            jax.ShapeDtypeStruct(emis_out.shape, f32),
        ),
        in_specs=[hbm, hbm],
        out_specs=(hbm, hbm),
        scratch_shapes=[
            pltpu.VMEM(adj_out.shape, f32),
            pltpu.VMEM(emis_out.shape, f32),
            pltpu.SemaphoreType.DMA((4,)),
        ],
    )(adj_out, emis_out)


def solution(mesh):
    return jax.shard_map(
        shards,
        mesh=mesh,
        in_specs=(
            P(None, "lev", "lat", "lon"),
            P(None, None, "lev", "lat", "lon"),
            P(None, "lev", "lat", "lon"),
            P("lev", "lat", "lon"),
            P(),
            P(),
            P(),
            P(),
            P(),
            P("lat", "lon"),
            P("lat", "lon"),
        ),
        out_specs=(P(None, "lev", "lat", "lon"), P(None, "lat", "lon")),
        check_vma=False,
    )
```

```python
import jax
import jax.numpy as jnp
from jax import lax
from jax.experimental import pallas as pl
from jax.experimental.pallas import tpu as pltpu
from jax.sharding import PartitionSpec as P

MESH = pl.DeviceIdType.MESH
PAD = 8

S_LEV, S_UP, S_DOWN, S_RIGHT, S_LEFT = 0, 3, 6, 9, 12
S_EMIS, S_CE_R, S_CE_L, S_CN_U, S_CN_D, S_MIX = 15, 16, 17, 18, 19, 20
N_REMOTE = 21


def kernel(
    adj_hbm, traj_hbm, cour_hbm, mix_hbm, land_hbm, srcm_hbm,
    rates_hbm, speed_hbm, sclass_hbm, prof_hbm, ecoef_hbm,
    out_hbm, emis_hbm,
    out_ref, emis_ref, land_ref, srcm_ref, rates_ref, speed_ref, sclass_ref, prof_ref, ecoef_ref,
    traj_ref, cour_ref, mix_ref, pad_ref, lh_ref, at_ref, ht_ref, hb_ref, lv_ref, eo_ref, ep_ref,
    cx_ref, cy_ref, vc_ref, cet_ref, ceh_ref, cyp_ref, mh_ref,
    send_sem, recv_sem, local_sem,
):
    n_t, n_z, n_y, n_x = out_ref.shape
    steps = traj_hbm.shape[0]
    rows = n_z * n_y
    lon = lax.axis_index("lon")
    lat = lax.axis_index("lat")
    lev = lax.axis_index("lev")
    n_lon = lax.axis_size("lon")
    n_lat = lax.axis_size("lat")
    right = lax.rem(lon + 1, n_lon)
    left = lax.rem(lon + n_lon - 1, n_lon)
    has_up = lat < n_lat - 1
    has_down = lat > 0
    up = jnp.minimum(lat + 1, n_lat - 1)
    down = jnp.maximum(lat - 1, 0)
    partner = 1 - lev
    low_half = lev == 0
    edge_z = jnp.where(low_half, n_z - 1, 0)
    inner_z = jnp.where(low_half, n_z - 2, 1)
    level0 = lev * n_z

    adj_in = pltpu.make_async_copy(adj_hbm, out_ref, local_sem.at[0])
    cour_in = pltpu.make_async_copy(cour_hbm, cour_ref, local_sem.at[1])
    mix_in = pltpu.make_async_copy(mix_hbm, mix_ref, local_sem.at[2])
    traj_in = [
        pltpu.make_async_copy(traj_hbm.at[k], traj_ref.at[k], local_sem.at[3 + k]) for k in range(steps)
    ]
    small_in = [
        pltpu.make_async_copy(src, dst, local_sem.at[3 + steps + i])
        for i, (src, dst) in enumerate(
            (
                (rates_hbm, rates_ref),
                (speed_hbm, speed_ref),
                (sclass_hbm, sclass_ref),
                (prof_hbm, prof_ref),
                (ecoef_hbm, ecoef_ref),
                (land_hbm, land_ref),
                (srcm_hbm, srcm_ref),
            )
        )
    ]
    for c in small_in:
        c.start()
    cour_in.start()
    mix_in.start()
    adj_in.start()
    for k in range(steps - 1, -1, -1):
        traj_in[k].start()

    zeros_pad = jnp.zeros((n_t, n_z, PAD, n_x), jnp.float32)
    for k in range(steps):
        pad_ref[k, :, :, 0:PAD, :] = zeros_pad
        pad_ref[k, :, :, PAD + n_y : 2 * PAD + n_y, :] = zeros_pad
        lh_ref[k] = zeros_pad
    zeros_c = jnp.zeros((n_z, PAD, n_x), jnp.float32)
    cyp_ref[:, 0:PAD, :] = zeros_c
    cyp_ref[:, PAD + n_y : 2 * PAD + n_y, :] = zeros_c

    def rcopy(src, dst, idx, dev):
        return pltpu.make_async_remote_copy(
            src, dst, send_sem.at[idx], recv_sem.at[idx], device_id=dev, device_id_type=MESH
        )

    lane = lax.broadcasted_iota(jnp.int32, (n_y, n_x), 1)
    row = lax.broadcasted_iota(jnp.int32, (n_y, n_x), 0)

    cour_in.wait()
    mix_in.wait()
    for c in small_in:
        c.wait()
    top_row = jnp.logical_and(lat == n_lat - 1, row == n_y - 1)
    for z in range(n_z):
        cyp_ref[z, PAD : PAD + n_y, :] = jnp.where(top_row, 0.0, cour_ref[1, z])
    cet_ref[...] = cour_ref[0].reshape(rows, n_x).T
    ce_right = rcopy(cet_ref.at[pl.ds(n_x - 2, 2), :], ceh_ref.at[pl.ds(n_x - 2, 2), :], S_CE_R, (right, lat, lev))
    ce_left = rcopy(cet_ref.at[pl.ds(0, 2), :], ceh_ref.at[pl.ds(0, 2), :], S_CE_L, (left, lat, lev))
    cn_up = rcopy(
        cyp_ref.at[:, pl.ds(PAD + n_y - 2, 2), :], cyp_ref.at[:, pl.ds(PAD - 2, 2), :], S_CN_U, (lon, up, lev)
    )
    cn_down = rcopy(
        cyp_ref.at[:, pl.ds(PAD, 2), :], cyp_ref.at[:, pl.ds(PAD + n_y, 2), :], S_CN_D, (lon, down, lev)
    )
    mix_x = rcopy(mix_ref.at[pl.ds(edge_z, 1)], mh_ref, S_MIX, (lon, lat, partner))

    def start_coefficient_halos():
        mix_x.start()
        ce_right.start()
        ce_left.start()

        @pl.when(has_up)
        def _():
            cn_up.start()

        @pl.when(has_down)
        def _():
            cn_down.start()

    def fix_vertical_coefficients():
        mix_x.wait()
        below = jnp.where(low_half, vc_ref[1, 0], mh_ref[0])
        vc_ref[1, 0] = below
        vc_ref[2, 0] = jnp.where(low_half, vc_ref[2, 0], 1.0 - vc_ref[0, 0] - below)

    def build_vertical_coefficients():
        dep = jnp.where(low_half, 0.1 + 0.3 * land_ref[...].astype(jnp.float32), 0.0)
        below = jnp.zeros((n_y, n_x), jnp.float32)
        for z in range(n_z):
            above = mix_ref[z]
            if z == n_z - 1:
                above = jnp.where(low_half, above, 0.0)
            base = 1.0 - above - below
            if z == 0:
                base = base - dep
            vc_ref[0, z] = above
            vc_ref[1, z] = below
            vc_ref[2, z] = base
            below = above

    def build_transport_coefficients():
        ce_right.wait()
        ce_left.wait()

        @pl.when(has_up)
        def _():
            cn_up.wait_send()
            cn_down.wait_recv()

        @pl.when(has_down)
        def _():
            cn_down.wait_send()
            cn_up.wait_recv()

        he = ceh_ref[...].T.reshape(n_z, n_y, n_x)
        for z in range(n_z):
            c = cour_ref[0, z]
            hz = he[z]
            c_p1 = jnp.where(lane == n_x - 1, pltpu.roll(hz, n_x - 1, 1), pltpu.roll(c, n_x - 1, 1))
            c_m1 = jnp.where(lane == 0, pltpu.roll(hz, 1, 1), pltpu.roll(c, 1, 1))
            c_m2 = jnp.where(lane <= 1, pltpu.roll(hz, 2, 1), pltpu.roll(c, 2, 1))
            cx_ref[0, z] = -1.5 * jnp.maximum(c, 0.0)
            cx_ref[1, z] = 0.5 * jnp.maximum(c_p1, 0.0)
            cx_ref[2, z] = -1.5 * jnp.minimum(c_m1, 0.0)
            cx_ref[3, z] = 0.5 * jnp.minimum(c_m2, 0.0)
            cy_ref[0, z] = -1.5 * jnp.maximum(cyp_ref[z, PAD : PAD + n_y, :], 0.0)
            cy_ref[1, z] = 0.5 * jnp.maximum(cyp_ref[z, PAD + 1 : PAD + 1 + n_y, :], 0.0)
            cy_ref[2, z] = -1.5 * jnp.minimum(cyp_ref[z, PAD - 1 : PAD - 1 + n_y, :], 0.0)
            cy_ref[3, z] = 0.5 * jnp.minimum(cyp_ref[z, PAD - 2 : PAD - 2 + n_y, :], 0.0)

    eo_ref[...] = jnp.zeros(eo_ref.shape, jnp.float32)
    src_mask = srcm_ref[...].astype(jnp.float32)
    adj_in.wait()
    build_vertical_coefficients()
    emis_copy = rcopy(eo_ref, ep_ref, S_EMIS, (lon, lat, partner))

    def lat_fix(k, t, z):
        h = lh_ref[k, t, z, 0:4, :]
        am2 = h[0:1]
        am1 = h[1:2]
        ap1 = h[2:3]
        ap2 = h[3:4]
        c_lo = cy_ref[:, z, 0:2, :]
        c_hi = cy_ref[:, z, n_y - 2 : n_y, :]
        r0 = c_lo[2, 0:1] * am1 + c_lo[3, 0:1] * (am2 - am1)
        r1 = c_lo[3, 1:2] * am1
        r14 = -c_hi[1, 0:1] * ap1
        r15 = c_hi[1, 1:2] * (ap1 - ap2) - c_hi[0, 1:2] * ap1
        out_ref[t, z, 0:2, :] = out_ref[t, z, 0:2, :] + jnp.concatenate([r0, r1], axis=0)
        out_ref[t, z, n_y - 2 : n_y, :] = out_ref[t, z, n_y - 2 : n_y, :] + jnp.concatenate([r14, r15], axis=0)

    for k in range(steps - 1, -1, -1):
        first = k == steps - 1
        traj_in[k].wait()

        def coag_level(zz, acc):
            z = jnp.where(low_half, n_z - 1 - zz, zz)
            zg = level0 + z
            if not first:
                for t in range(n_t):
                    lat_fix(k + 1, t, z)
            lam = [out_ref[t, z] for t in range(n_t)]
            st = [traj_ref[k, t, z].astype(jnp.float32) for t in range(n_t)]
            new_acc = []
            for m in range(3):
                part = acc[m]
                for j in range(3):
                    part = part + (ecoef_ref[3 * m + j] * prof_ref[zg]) * lam[3 * m + j]
                new_acc.append(part)
            k0, k1, k2, k01, k02, k12 = [rates_ref[i, zg] for i in range(6)]
            n0, v0, w0, n1, v1, w1, n2, v2, w2 = st
            ln0, lv0, lw0, ln1, lv1, lw1, ln2, lv2, lw2 = lam
            a01 = k01 * n1
            a02 = k02 * n2
            a12 = k12 * n2
            s0 = a01 + a02
            g_n0 = ln0 * (-2.0 * k0 * n0 - s0)
            g_v0 = (
                (lv1 * a01 + lv2 * a02 - lv0 * s0)
                + 2.0 * (lw0 * (k0 * v0) + lw1 * (k01 * v1) + lw2 * (k02 * v2))
            )
            g_w0 = lw1 * a01 + lw2 * a02 - lw0 * s0
            g_n1 = (
                ln1 * (-2.0 * k1 * n1 - a12)
                - ln0 * (k01 * n0)
                + (lv1 - lv0) * (k01 * v0)
                + (lw1 - lw0) * (k01 * w0)
            )
            g_v1 = (lv2 - lv1) * a12 + 2.0 * (lw1 * (k1 * v1 + k01 * v0) + lw2 * (k12 * v2))
            g_w1 = (lw2 - lw1) * a12
            g_n2 = (
                -2.0 * k2 * n2 * ln2
                - ln0 * (k02 * n0)
                - ln1 * (k12 * n1)
                + (lv2 - lv0) * (k02 * v0)
                + (lv2 - lv1) * (k12 * v1)
                + (lw2 - lw0) * (k02 * w0)
                + (lw2 - lw1) * (k12 * w1)
            )
            g_v2 = 2.0 * lw2 * (k2 * v2 + k02 * v0 + k12 * v1)
            grads = [g_n0, g_v0, g_w0, g_n1, g_v1, g_w1, g_n2, g_v2]
            for t in range(n_t - 1):
                out_ref[t, z] = lam[t] + grads[t]
            return tuple(new_acc)

        zero = jnp.zeros((n_y, n_x), jnp.float32)
        acc = coag_level(0, (zero, zero, zero))
        lev_copy = rcopy(out_ref.at[:, pl.ds(edge_z, 1)], lv_ref.at[k], S_LEV + k, (lon, lat, partner))
        if not first:
            lev_copy.start()
        acc = lax.fori_loop(1, n_z, coag_level, acc)
        for m in range(3):
            eo_ref[m] = eo_ref[m] + acc[m] * src_mask
        if k == 0:
            emis_copy.start()

        def vert_inner(t, carry):
            col = [out_ref[t, z] for z in range(n_z)]
            for z in range(n_z):
                s = speed_ref[sclass_ref[level0 + z], t]
                val = col[z] * (vc_ref[2, z] - s)
                if z > 0:
                    val = val + col[z - 1] * (vc_ref[1, z] + s)
                if z < n_z - 1:
                    val = val + col[z + 1] * vc_ref[0, z]
                pad_ref[k, t, z, PAD : PAD + n_y, :] = val
            return carry

        lax.fori_loop(0, n_t, vert_inner, 0)
        if first:
            barrier = pltpu.get_barrier_semaphore()
            for dev in ((lon, lat, partner), (left, lat, lev), (right, lat, lev)):
                pl.semaphore_signal(barrier, 1, device_id=dev, device_id_type=MESH)

            @pl.when(has_up)
            def _():
                pl.semaphore_signal(barrier, 1, device_id=(lon, up, lev), device_id_type=MESH)

            @pl.when(has_down)
            def _():
                pl.semaphore_signal(barrier, 1, device_id=(lon, down, lev), device_id_type=MESH)

            pl.semaphore_wait(barrier, 3 + has_up.astype(jnp.int32) + has_down.astype(jnp.int32))
            start_coefficient_halos()
            lev_copy.start()
            fix_vertical_coefficients()
        lev_copy.wait()

        lat_up = rcopy(
            pad_ref.at[k, :, :, pl.ds(PAD + n_y - 2, 2), :],
            lh_ref.at[k, :, :, pl.ds(0, 2), :],
            S_UP + k,
            (lon, up, lev),
        )
        lat_down = rcopy(
            pad_ref.at[k, :, :, pl.ds(PAD, 2), :],
            lh_ref.at[k, :, :, pl.ds(2, 2), :],
            S_DOWN + k,
            (lon, down, lev),
        )
        lon_right = rcopy(
            at_ref.at[k, pl.ds(n_x - 2, 2), :], ht_ref.at[k, pl.ds(n_x - 2, 2), :], S_RIGHT + k, (right, lat, lev)
        )
        lon_left = rcopy(
            at_ref.at[k, pl.ds(0, 2), :], ht_ref.at[k, pl.ds(0, 2), :], S_LEFT + k, (left, lat, lev)
        )

        for t in range(n_t):
            z = edge_z
            s = speed_ref[sclass_ref[level0 + z], t]
            a = out_ref[t, z]
            other = out_ref[t, inner_z]
            halo = lv_ref[k, t, 0]
            a_below = jnp.where(low_half, other, halo)
            a_above = jnp.where(low_half, halo, other)
            pad_ref[k, t, z, PAD : PAD + n_y, :] = (
                a * (vc_ref[2, z] - s) + a_below * (vc_ref[1, z] + s) + a_above * vc_ref[0, z]
            )
            up_t = rcopy(
                pad_ref.at[k, t, :, pl.ds(PAD + n_y - 2, 2), :],
                lh_ref.at[k, t, :, pl.ds(0, 2), :],
                S_UP + k,
                (lon, up, lev),
            )
            down_t = rcopy(
                pad_ref.at[k, t, :, pl.ds(PAD, 2), :],
                lh_ref.at[k, t, :, pl.ds(2, 2), :],
                S_DOWN + k,
                (lon, down, lev),
            )

            @pl.when(has_up)
            def _():
                up_t.start()

            @pl.when(has_down)
            def _():
                down_t.start()

        for t in range(n_t):
            blk = pad_ref[k, t, :, PAD : PAD + n_y, :].reshape(rows, n_x)
            cols = pl.ds(t * rows, rows)
            at_ref[k, :, cols] = blk.T
            rcopy(
                at_ref.at[k, pl.ds(n_x - 2, 2), cols], ht_ref.at[k, pl.ds(n_x - 2, 2), cols], S_RIGHT + k,
                (right, lat, lev),
            ).start()
            rcopy(
                at_ref.at[k, pl.ds(0, 2), cols], ht_ref.at[k, pl.ds(0, 2), cols], S_LEFT + k, (left, lat, lev)
            ).start()

        if k == steps - 1:
            build_transport_coefficients()

        def transport(t, carry):
            for z in range(n_z):
                a = pad_ref[k, t, z, PAD : PAD + n_y, :]
                y_p1 = pad_ref[k, t, z, PAD + 1 : PAD + 1 + n_y, :]
                y_p2 = pad_ref[k, t, z, PAD + 2 : PAD + 2 + n_y, :]
                y_m1 = pad_ref[k, t, z, PAD - 1 : PAD - 1 + n_y, :]
                y_m2 = pad_ref[k, t, z, PAD - 2 : PAD - 2 + n_y, :]
                x_p1 = pltpu.roll(a, n_x - 1, 1)
                x_p2 = pltpu.roll(a, n_x - 2, 1)
                x_m1 = pltpu.roll(a, 1, 1)
                x_m2 = pltpu.roll(a, 2, 1)
                lon_part = (
                    cx_ref[0, z] * (a - x_p1)
                    + cx_ref[1, z] * (x_p1 - x_p2)
                    + cx_ref[2, z] * (x_m1 - a)
                    + cx_ref[3, z] * (x_m2 - x_m1)
                )
                lat_part = (
                    cy_ref[0, z] * (a - y_p1)
                    + cy_ref[1, z] * (y_p1 - y_p2)
                    + cy_ref[2, z] * (y_m1 - a)
                    + cy_ref[3, z] * (y_m2 - y_m1)
                )
                out_ref[t, z] = a + lon_part + lat_part
            return carry

        lax.fori_loop(0, n_t, transport, 0)

        lon_right.wait()
        lon_left.wait()

        def lon_edges(t, carry):
            cols = pl.ds(pl.multiple_of(t * rows, rows), rows)
            h_t = ht_ref[k, :, cols].T.reshape(n_z, n_y, n_x)
            for z in range(n_z):
                a = pad_ref[k, t, z, PAD : PAD + n_y, :]
                d = h_t[z] - a
                d_m1 = pltpu.roll(d, 1, 1)
                d_m2 = pltpu.roll(d, 2, 1)
                d_p1 = pltpu.roll(d, n_x - 1, 1)
                d_p2 = pltpu.roll(d, n_x - 2, 1)
                cx0 = cx_ref[0, z]
                cx1 = cx_ref[1, z]
                cxm1 = cx_ref[2, z]
                cxm2 = cx_ref[3, z]
                low = cxm2 * d_m2 + jnp.where(lane == 0, (cxm1 - cxm2) * d_m1, 0.0)
                high = jnp.where(lane == n_x - 1, (cx1 - cx0) * d_p1, 0.0) - cx1 * d_p2
                corr = jnp.where(lane <= 1, low, jnp.where(lane >= n_x - 2, high, 0.0))
                out_ref[t, z] = out_ref[t, z] + corr
            return carry

        lax.fori_loop(0, n_t, lon_edges, 0)

        @pl.when(has_up)
        def _():
            lat_up.wait_send()
            lat_down.wait_recv()

        @pl.when(has_down)
        def _():
            lat_down.wait_send()
            lat_up.wait_recv()

        if k == 0:
            def lat_edges(t, carry):
                for z in range(n_z):
                    lat_fix(k, t, z)
                pltpu.make_async_copy(out_ref.at[t], out_hbm.at[t], local_sem.at[0]).start()
                return carry

            lax.fori_loop(0, n_t, lat_edges, 0)

    emis_copy.wait()
    emis_ref[...] = eo_ref[...] + ep_ref[...]
    out_copy = pltpu.make_async_copy(out_ref, out_hbm, local_sem.at[0])
    emis_out = pltpu.make_async_copy(emis_ref, emis_hbm, local_sem.at[1])
    emis_out.start()
    out_copy.wait()
    emis_out.wait()


def hand_over(adj_hbm, emis_hbm, adj_out, emis_out, adj_buf, emis_buf, sem):
    ins = [
        pltpu.make_async_copy(adj_hbm, adj_buf, sem.at[0]),
        pltpu.make_async_copy(emis_hbm, emis_buf, sem.at[1]),
    ]
    for c in ins:
        c.start()
    outs = [
        pltpu.make_async_copy(adj_buf, adj_out, sem.at[2]),
        pltpu.make_async_copy(emis_buf, emis_out, sem.at[3]),
    ]
    for c, o in zip(ins, outs):
        c.wait()
        o.start()
    for o in outs:
        o.wait()


def shards(
    adjoint_in,
    trajectory,
    courant,
    mixing,
    coag_rates,
    settle_speed,
    settle_class,
    emis_profile,
    emis_coef,
    land_mask,
    source_mask,
):
    n_t, n_z, n_y, n_x = adjoint_in.shape
    steps = trajectory.shape[0]
    rows = n_z * n_y
    hbm = pl.BlockSpec(memory_space=pl.ANY)
    vmem = pl.BlockSpec(memory_space=pltpu.VMEM)
    smem = pl.BlockSpec(memory_space=pltpu.SMEM)
    f32 = jnp.float32
    adj_out, emis_out = pl.pallas_call(
        kernel,
        out_shape=(
            jax.ShapeDtypeStruct(adjoint_in.shape, f32),
            jax.ShapeDtypeStruct((3, n_y, n_x), f32),
        ),
        in_specs=[hbm] * 11,
        out_specs=(hbm, hbm),
        scratch_shapes=[
            pltpu.VMEM(adjoint_in.shape, f32),
            pltpu.VMEM((3, n_y, n_x), f32),
            pltpu.VMEM(land_mask.shape, land_mask.dtype),
            pltpu.VMEM(source_mask.shape, source_mask.dtype),
            pltpu.SMEM(coag_rates.shape, f32),
            pltpu.SMEM(settle_speed.shape, f32),
            pltpu.SMEM(settle_class.shape, settle_class.dtype),
            pltpu.SMEM(emis_profile.shape, f32),
            pltpu.SMEM(emis_coef.shape, f32),
            pltpu.VMEM(trajectory.shape, trajectory.dtype),
            pltpu.VMEM(courant.shape, f32),
            pltpu.VMEM(mixing.shape, f32),
            pltpu.VMEM((steps, n_t, n_z, n_y + 2 * PAD, n_x), f32),
            pltpu.VMEM((steps, n_t, n_z, PAD, n_x), f32),
            pltpu.VMEM((steps, n_x, n_t * rows), f32),
            pltpu.VMEM((steps, n_x, n_t * rows), f32),
            pltpu.VMEM((n_t, n_z, n_y, n_x), f32),
            pltpu.VMEM((steps, n_t, 1, n_y, n_x), f32),
            pltpu.VMEM((3, n_y, n_x), f32),
            pltpu.VMEM((3, n_y, n_x), f32),
            pltpu.VMEM((4, n_z, n_y, n_x), f32),
            pltpu.VMEM((4, n_z, n_y, n_x), f32),
            pltpu.VMEM((3, n_z, n_y, n_x), f32),
            pltpu.VMEM((n_x, rows), f32),
            pltpu.VMEM((n_x, rows), f32),
            pltpu.VMEM((n_z, n_y + 2 * PAD, n_x), f32),
            pltpu.VMEM((1, n_y, n_x), f32),
            pltpu.SemaphoreType.DMA((N_REMOTE,)),
            pltpu.SemaphoreType.DMA((N_REMOTE,)),
            pltpu.SemaphoreType.DMA((10 + steps,)),
        ],
        compiler_params=pltpu.CompilerParams(
            collective_id=0, has_side_effects=True, vmem_limit_bytes=67043328
        ),
    )(
        adjoint_in, trajectory, courant, mixing, land_mask, source_mask,
        coag_rates, settle_speed, settle_class, emis_profile, emis_coef,
    )
    return pl.pallas_call(
        hand_over,
        out_shape=(
            jax.ShapeDtypeStruct(adj_out.shape, f32),
            jax.ShapeDtypeStruct(emis_out.shape, f32),
        ),
        in_specs=[hbm, hbm],
        out_specs=(hbm, hbm),
        scratch_shapes=[
            pltpu.VMEM(adj_out.shape, f32),
            pltpu.VMEM(emis_out.shape, f32),
            pltpu.SemaphoreType.DMA((4,)),
        ],
    )(adj_out, emis_out)


def solution(mesh):
    return jax.shard_map(
        shards,
        mesh=mesh,
        in_specs=(
            P(None, "lev", "lat", "lon"),
            P(None, None, "lev", "lat", "lon"),
            P(None, "lev", "lat", "lon"),
            P("lev", "lat", "lon"),
            P(),
            P(),
            P(),
            P(),
            P(),
            P("lat", "lon"),
            P("lat", "lon"),
        ),
        out_specs=(P(None, "lev", "lat", "lon"), P(None, "lat", "lon")),
        check_vma=False,
    )
```

```python
import jax
import jax.numpy as jnp
from jax import lax
from jax.experimental import pallas as pl
from jax.experimental.pallas import tpu as pltpu
from jax.sharding import PartitionSpec as P

MESH = pl.DeviceIdType.MESH
PAD = 8

S_LEV, S_UP, S_DOWN, S_RIGHT, S_LEFT = 0, 3, 6, 9, 12
S_EMIS, S_CE_R, S_CE_L, S_CN_U, S_CN_D, S_MIX = 15, 16, 17, 18, 19, 20
N_REMOTE = 21


def kernel(
    adj_hbm, traj_hbm, cour_hbm, mix_hbm, land_hbm, srcm_hbm,
    rates_hbm, speed_hbm, sclass_hbm, prof_hbm, ecoef_hbm,
    out_hbm, emis_hbm,
    out_ref, emis_ref, land_ref, srcm_ref, rates_ref, speed_ref, sclass_ref, prof_ref, ecoef_ref,
    traj_ref, cour_ref, mix_ref, pad_ref, lh_ref, at_ref, ht_ref, hb_ref, lv_ref, eo_ref, ep_ref,
    cx_ref, cy_ref, vc_ref, cet_ref, ceh_ref, cyp_ref, mh_ref,
    send_sem, recv_sem, local_sem,
):
    n_t, n_z, n_y, n_x = out_ref.shape
    steps = traj_hbm.shape[0]
    rows = n_z * n_y
    lon = lax.axis_index("lon")
    lat = lax.axis_index("lat")
    lev = lax.axis_index("lev")
    n_lon = lax.axis_size("lon")
    n_lat = lax.axis_size("lat")
    right = lax.rem(lon + 1, n_lon)
    left = lax.rem(lon + n_lon - 1, n_lon)
    has_up = lat < n_lat - 1
    has_down = lat > 0
    up = jnp.minimum(lat + 1, n_lat - 1)
    down = jnp.maximum(lat - 1, 0)
    partner = 1 - lev
    low_half = lev == 0
    edge_z = jnp.where(low_half, n_z - 1, 0)
    inner_z = jnp.where(low_half, n_z - 2, 1)
    level0 = lev * n_z

    adj_in = pltpu.make_async_copy(adj_hbm, out_ref, local_sem.at[0])
    cour_in = pltpu.make_async_copy(cour_hbm, cour_ref, local_sem.at[1])
    mix_in = pltpu.make_async_copy(mix_hbm, mix_ref, local_sem.at[2])
    traj_in = [
        pltpu.make_async_copy(traj_hbm.at[k], traj_ref.at[k], local_sem.at[3 + k]) for k in range(steps)
    ]
    small_in = [
        pltpu.make_async_copy(src, dst, local_sem.at[3 + steps + i])
        for i, (src, dst) in enumerate(
            (
                (rates_hbm, rates_ref),
                (speed_hbm, speed_ref),
                (sclass_hbm, sclass_ref),
                (prof_hbm, prof_ref),
                (ecoef_hbm, ecoef_ref),
                (land_hbm, land_ref),
                (srcm_hbm, srcm_ref),
            )
        )
    ]
    for c in small_in:
        c.start()
    cour_in.start()
    mix_in.start()
    adj_in.start()
    for k in range(steps - 1, -1, -1):
        traj_in[k].start()

    zeros_pad = jnp.zeros((n_t, n_z, PAD, n_x), jnp.float32)
    for k in range(steps):
        pad_ref[k, :, :, 0:PAD, :] = zeros_pad
        pad_ref[k, :, :, PAD + n_y : 2 * PAD + n_y, :] = zeros_pad
        lh_ref[k] = zeros_pad
    zeros_c = jnp.zeros((n_z, PAD, n_x), jnp.float32)
    cyp_ref[:, 0:PAD, :] = zeros_c
    cyp_ref[:, PAD + n_y : 2 * PAD + n_y, :] = zeros_c

    def rcopy(src, dst, idx, dev):
        return pltpu.make_async_remote_copy(
            src, dst, send_sem.at[idx], recv_sem.at[idx], device_id=dev, device_id_type=MESH
        )

    lane = lax.broadcasted_iota(jnp.int32, (n_y, n_x), 1)
    row = lax.broadcasted_iota(jnp.int32, (n_y, n_x), 0)

    cour_in.wait()
    mix_in.wait()
    for c in small_in:
        c.wait()
    top_row = jnp.logical_and(lat == n_lat - 1, row == n_y - 1)
    for z in range(n_z):
        cyp_ref[z, PAD : PAD + n_y, :] = jnp.where(top_row, 0.0, cour_ref[1, z])
    cet_ref[...] = cour_ref[0].reshape(rows, n_x).T
    ce_right = rcopy(cet_ref.at[pl.ds(n_x - 2, 2), :], ceh_ref.at[pl.ds(n_x - 2, 2), :], S_CE_R, (right, lat, lev))
    ce_left = rcopy(cet_ref.at[pl.ds(0, 2), :], ceh_ref.at[pl.ds(0, 2), :], S_CE_L, (left, lat, lev))
    cn_up = rcopy(
        cyp_ref.at[:, pl.ds(PAD + n_y - 2, 2), :], cyp_ref.at[:, pl.ds(PAD - 2, 2), :], S_CN_U, (lon, up, lev)
    )
    cn_down = rcopy(
        cyp_ref.at[:, pl.ds(PAD, 2), :], cyp_ref.at[:, pl.ds(PAD + n_y, 2), :], S_CN_D, (lon, down, lev)
    )
    mix_x = rcopy(mix_ref.at[pl.ds(edge_z, 1)], mh_ref, S_MIX, (lon, lat, partner))

    def start_coefficient_halos():
        mix_x.start()
        ce_right.start()
        ce_left.start()

        @pl.when(has_up)
        def _():
            cn_up.start()

        @pl.when(has_down)
        def _():
            cn_down.start()

    def fix_vertical_coefficients():
        mix_x.wait()
        below = jnp.where(low_half, vc_ref[1, 0], mh_ref[0])
        vc_ref[1, 0] = below
        vc_ref[2, 0] = jnp.where(low_half, vc_ref[2, 0], 1.0 - vc_ref[0, 0] - below)

    def build_vertical_coefficients():
        dep = jnp.where(low_half, 0.1 + 0.3 * land_ref[...].astype(jnp.float32), 0.0)
        below = jnp.zeros((n_y, n_x), jnp.float32)
        for z in range(n_z):
            above = mix_ref[z]
            if z == n_z - 1:
                above = jnp.where(low_half, above, 0.0)
            base = 1.0 - above - below
            if z == 0:
                base = base - dep
            vc_ref[0, z] = above
            vc_ref[1, z] = below
            vc_ref[2, z] = base
            below = above

    def build_transport_coefficients():
        ce_right.wait()
        ce_left.wait()

        @pl.when(has_up)
        def _():
            cn_up.wait_send()
            cn_down.wait_recv()

        @pl.when(has_down)
        def _():
            cn_down.wait_send()
            cn_up.wait_recv()

        he = ceh_ref[...].T.reshape(n_z, n_y, n_x)
        for z in range(n_z):
            c = cour_ref[0, z]
            hz = he[z]
            c_p1 = jnp.where(lane == n_x - 1, pltpu.roll(hz, n_x - 1, 1), pltpu.roll(c, n_x - 1, 1))
            c_m1 = jnp.where(lane == 0, pltpu.roll(hz, 1, 1), pltpu.roll(c, 1, 1))
            c_m2 = jnp.where(lane <= 1, pltpu.roll(hz, 2, 1), pltpu.roll(c, 2, 1))
            cx_ref[0, z] = -1.5 * jnp.maximum(c, 0.0)
            cx_ref[1, z] = 0.5 * jnp.maximum(c_p1, 0.0)
            cx_ref[2, z] = -1.5 * jnp.minimum(c_m1, 0.0)
            cx_ref[3, z] = 0.5 * jnp.minimum(c_m2, 0.0)
            cy_ref[0, z] = -1.5 * jnp.maximum(cyp_ref[z, PAD : PAD + n_y, :], 0.0)
            cy_ref[1, z] = 0.5 * jnp.maximum(cyp_ref[z, PAD + 1 : PAD + 1 + n_y, :], 0.0)
            cy_ref[2, z] = -1.5 * jnp.minimum(cyp_ref[z, PAD - 1 : PAD - 1 + n_y, :], 0.0)
            cy_ref[3, z] = 0.5 * jnp.minimum(cyp_ref[z, PAD - 2 : PAD - 2 + n_y, :], 0.0)

    eo_ref[...] = jnp.zeros(eo_ref.shape, jnp.float32)
    src_mask = srcm_ref[...].astype(jnp.float32)
    adj_in.wait()
    build_vertical_coefficients()
    emis_copy = rcopy(eo_ref, ep_ref, S_EMIS, (lon, lat, partner))

    def lat_fix(k, t, z):
        h = lh_ref[k, t, z, 0:4, :]
        am2 = h[0:1]
        am1 = h[1:2]
        ap1 = h[2:3]
        ap2 = h[3:4]
        c_lo = cy_ref[:, z, 0:2, :]
        c_hi = cy_ref[:, z, n_y - 2 : n_y, :]
        r0 = c_lo[2, 0:1] * am1 + c_lo[3, 0:1] * (am2 - am1)
        r1 = c_lo[3, 1:2] * am1
        r14 = -c_hi[1, 0:1] * ap1
        r15 = c_hi[1, 1:2] * (ap1 - ap2) - c_hi[0, 1:2] * ap1
        out_ref[t, z, 0:2, :] = out_ref[t, z, 0:2, :] + jnp.concatenate([r0, r1], axis=0)
        out_ref[t, z, n_y - 2 : n_y, :] = out_ref[t, z, n_y - 2 : n_y, :] + jnp.concatenate([r14, r15], axis=0)

    for k in range(steps - 1, -1, -1):
        first = k == steps - 1
        traj_in[k].wait()

        def coag_level(zz, acc):
            z = jnp.where(low_half, n_z - 1 - zz, zz)
            zg = level0 + z
            if not first:
                for t in range(n_t):
                    lat_fix(k + 1, t, z)
            lam = [out_ref[t, z] for t in range(n_t)]
            st = [traj_ref[k, t, z].astype(jnp.float32) for t in range(n_t)]
            new_acc = []
            for m in range(3):
                part = acc[m]
                for j in range(3):
                    part = part + (ecoef_ref[3 * m + j] * prof_ref[zg]) * lam[3 * m + j]
                new_acc.append(part)
            k0, k1, k2, k01, k02, k12 = [rates_ref[i, zg] for i in range(6)]
            n0, v0, w0, n1, v1, w1, n2, v2, w2 = st
            ln0, lv0, lw0, ln1, lv1, lw1, ln2, lv2, lw2 = lam
            a01 = k01 * n1
            a02 = k02 * n2
            a12 = k12 * n2
            s0 = a01 + a02
            g_n0 = ln0 * (-2.0 * k0 * n0 - s0)
            g_v0 = (
                (lv1 * a01 + lv2 * a02 - lv0 * s0)
                + 2.0 * (lw0 * (k0 * v0) + lw1 * (k01 * v1) + lw2 * (k02 * v2))
            )
            g_w0 = lw1 * a01 + lw2 * a02 - lw0 * s0
            g_n1 = (
                ln1 * (-2.0 * k1 * n1 - a12)
                - ln0 * (k01 * n0)
                + (lv1 - lv0) * (k01 * v0)
                + (lw1 - lw0) * (k01 * w0)
            )
            g_v1 = (lv2 - lv1) * a12 + 2.0 * (lw1 * (k1 * v1 + k01 * v0) + lw2 * (k12 * v2))
            g_w1 = (lw2 - lw1) * a12
            g_n2 = (
                -2.0 * k2 * n2 * ln2
                - ln0 * (k02 * n0)
                - ln1 * (k12 * n1)
                + (lv2 - lv0) * (k02 * v0)
                + (lv2 - lv1) * (k12 * v1)
                + (lw2 - lw0) * (k02 * w0)
                + (lw2 - lw1) * (k12 * w1)
            )
            g_v2 = 2.0 * lw2 * (k2 * v2 + k02 * v0 + k12 * v1)
            grads = [g_n0, g_v0, g_w0, g_n1, g_v1, g_w1, g_n2, g_v2]
            for t in range(n_t - 1):
                out_ref[t, z] = lam[t] + grads[t]
            return tuple(new_acc)

        zero = jnp.zeros((n_y, n_x), jnp.float32)
        acc = coag_level(0, (zero, zero, zero))
        lev_copy = rcopy(out_ref.at[:, pl.ds(edge_z, 1)], lv_ref.at[k], S_LEV + k, (lon, lat, partner))
        if not first:
            lev_copy.start()
        acc = lax.fori_loop(1, n_z, coag_level, acc)
        for m in range(3):
            eo_ref[m] = eo_ref[m] + acc[m] * src_mask
        if k == 0:
            emis_copy.start()

        def vert_inner(t, carry):
            col = [out_ref[t, z] for z in range(n_z)]
            for z in range(n_z):
                s = speed_ref[sclass_ref[level0 + z], t]
                val = col[z] * (vc_ref[2, z] - s)
                if z > 0:
                    val = val + col[z - 1] * (vc_ref[1, z] + s)
                if z < n_z - 1:
                    val = val + col[z + 1] * vc_ref[0, z]
                pad_ref[k, t, z, PAD : PAD + n_y, :] = val
            return carry

        lax.fori_loop(0, n_t, vert_inner, 0, unroll=3)
        if first:
            barrier = pltpu.get_barrier_semaphore()
            for dev in ((lon, lat, partner), (left, lat, lev), (right, lat, lev)):
                pl.semaphore_signal(barrier, 1, device_id=dev, device_id_type=MESH)

            @pl.when(has_up)
            def _():
                pl.semaphore_signal(barrier, 1, device_id=(lon, up, lev), device_id_type=MESH)

            @pl.when(has_down)
            def _():
                pl.semaphore_signal(barrier, 1, device_id=(lon, down, lev), device_id_type=MESH)

            pl.semaphore_wait(barrier, 3 + has_up.astype(jnp.int32) + has_down.astype(jnp.int32))
            start_coefficient_halos()
            lev_copy.start()
            fix_vertical_coefficients()
        lev_copy.wait()

        lat_up = rcopy(
            pad_ref.at[k, :, :, pl.ds(PAD + n_y - 2, 2), :],
            lh_ref.at[k, :, :, pl.ds(0, 2), :],
            S_UP + k,
            (lon, up, lev),
        )
        lat_down = rcopy(
            pad_ref.at[k, :, :, pl.ds(PAD, 2), :],
            lh_ref.at[k, :, :, pl.ds(2, 2), :],
            S_DOWN + k,
            (lon, down, lev),
        )
        lon_right = rcopy(
            at_ref.at[k, pl.ds(n_x - 2, 2), :], ht_ref.at[k, pl.ds(n_x - 2, 2), :], S_RIGHT + k, (right, lat, lev)
        )
        lon_left = rcopy(
            at_ref.at[k, pl.ds(0, 2), :], ht_ref.at[k, pl.ds(0, 2), :], S_LEFT + k, (left, lat, lev)
        )

        for t in range(n_t):
            z = edge_z
            s = speed_ref[sclass_ref[level0 + z], t]
            a = out_ref[t, z]
            other = out_ref[t, inner_z]
            halo = lv_ref[k, t, 0]
            a_below = jnp.where(low_half, other, halo)
            a_above = jnp.where(low_half, halo, other)
            pad_ref[k, t, z, PAD : PAD + n_y, :] = (
                a * (vc_ref[2, z] - s) + a_below * (vc_ref[1, z] + s) + a_above * vc_ref[0, z]
            )
            up_t = rcopy(
                pad_ref.at[k, t, :, pl.ds(PAD + n_y - 2, 2), :],
                lh_ref.at[k, t, :, pl.ds(0, 2), :],
                S_UP + k,
                (lon, up, lev),
            )
            down_t = rcopy(
                pad_ref.at[k, t, :, pl.ds(PAD, 2), :],
                lh_ref.at[k, t, :, pl.ds(2, 2), :],
                S_DOWN + k,
                (lon, down, lev),
            )

            @pl.when(has_up)
            def _():
                up_t.start()

            @pl.when(has_down)
            def _():
                down_t.start()

        for t in range(n_t):
            blk = pad_ref[k, t, :, PAD : PAD + n_y, :].reshape(rows, n_x)
            cols = pl.ds(t * rows, rows)
            at_ref[k, :, cols] = blk.T
            rcopy(
                at_ref.at[k, pl.ds(n_x - 2, 2), cols], ht_ref.at[k, pl.ds(n_x - 2, 2), cols], S_RIGHT + k,
                (right, lat, lev),
            ).start()
            rcopy(
                at_ref.at[k, pl.ds(0, 2), cols], ht_ref.at[k, pl.ds(0, 2), cols], S_LEFT + k, (left, lat, lev)
            ).start()

        if k == steps - 1:
            build_transport_coefficients()

        def transport(t, carry):
            for z in range(n_z):
                a = pad_ref[k, t, z, PAD : PAD + n_y, :]
                y_p1 = pad_ref[k, t, z, PAD + 1 : PAD + 1 + n_y, :]
                y_p2 = pad_ref[k, t, z, PAD + 2 : PAD + 2 + n_y, :]
                y_m1 = pad_ref[k, t, z, PAD - 1 : PAD - 1 + n_y, :]
                y_m2 = pad_ref[k, t, z, PAD - 2 : PAD - 2 + n_y, :]
                x_p1 = pltpu.roll(a, n_x - 1, 1)
                x_p2 = pltpu.roll(a, n_x - 2, 1)
                x_m1 = pltpu.roll(a, 1, 1)
                x_m2 = pltpu.roll(a, 2, 1)
                lon_part = (
                    cx_ref[0, z] * (a - x_p1)
                    + cx_ref[1, z] * (x_p1 - x_p2)
                    + cx_ref[2, z] * (x_m1 - a)
                    + cx_ref[3, z] * (x_m2 - x_m1)
                )
                lat_part = (
                    cy_ref[0, z] * (a - y_p1)
                    + cy_ref[1, z] * (y_p1 - y_p2)
                    + cy_ref[2, z] * (y_m1 - a)
                    + cy_ref[3, z] * (y_m2 - y_m1)
                )
                out_ref[t, z] = a + lon_part + lat_part
            return carry

        lax.fori_loop(0, n_t, transport, 0)

        lon_right.wait()
        lon_left.wait()

        def lon_edges(t, carry):
            cols = pl.ds(pl.multiple_of(t * rows, rows), rows)
            h_t = ht_ref[k, :, cols].T.reshape(n_z, n_y, n_x)
            for z in range(n_z):
                a = pad_ref[k, t, z, PAD : PAD + n_y, :]
                d = h_t[z] - a
                d_m1 = pltpu.roll(d, 1, 1)
                d_m2 = pltpu.roll(d, 2, 1)
                d_p1 = pltpu.roll(d, n_x - 1, 1)
                d_p2 = pltpu.roll(d, n_x - 2, 1)
                cx0 = cx_ref[0, z]
                cx1 = cx_ref[1, z]
                cxm1 = cx_ref[2, z]
                cxm2 = cx_ref[3, z]
                low = cxm2 * d_m2 + jnp.where(lane == 0, (cxm1 - cxm2) * d_m1, 0.0)
                high = jnp.where(lane == n_x - 1, (cx1 - cx0) * d_p1, 0.0) - cx1 * d_p2
                corr = jnp.where(lane <= 1, low, jnp.where(lane >= n_x - 2, high, 0.0))
                out_ref[t, z] = out_ref[t, z] + corr
            return carry

        lax.fori_loop(0, n_t, lon_edges, 0)

        @pl.when(has_up)
        def _():
            lat_up.wait_send()
            lat_down.wait_recv()

        @pl.when(has_down)
        def _():
            lat_down.wait_send()
            lat_up.wait_recv()

        if k == 0:
            def lat_edges(t, carry):
                for z in range(n_z):
                    lat_fix(k, t, z)
                return carry

            lax.fori_loop(0, n_t, lat_edges, 0)

    emis_copy.wait()
    emis_ref[...] = eo_ref[...] + ep_ref[...]
    out_copy = pltpu.make_async_copy(out_ref, out_hbm, local_sem.at[0])
    emis_out = pltpu.make_async_copy(emis_ref, emis_hbm, local_sem.at[1])
    out_copy.start()
    emis_out.start()
    out_copy.wait()
    emis_out.wait()


def hand_over(adj_hbm, emis_hbm, adj_out, emis_out, adj_buf, emis_buf, sem):
    ins = [
        pltpu.make_async_copy(adj_hbm, adj_buf, sem.at[0]),
        pltpu.make_async_copy(emis_hbm, emis_buf, sem.at[1]),
    ]
    for c in ins:
        c.start()
    outs = [
        pltpu.make_async_copy(adj_buf, adj_out, sem.at[2]),
        pltpu.make_async_copy(emis_buf, emis_out, sem.at[3]),
    ]
    for c, o in zip(ins, outs):
        c.wait()
        o.start()
    for o in outs:
        o.wait()


def shards(
    adjoint_in,
    trajectory,
    courant,
    mixing,
    coag_rates,
    settle_speed,
    settle_class,
    emis_profile,
    emis_coef,
    land_mask,
    source_mask,
):
    n_t, n_z, n_y, n_x = adjoint_in.shape
    steps = trajectory.shape[0]
    rows = n_z * n_y
    hbm = pl.BlockSpec(memory_space=pl.ANY)
    vmem = pl.BlockSpec(memory_space=pltpu.VMEM)
    smem = pl.BlockSpec(memory_space=pltpu.SMEM)
    f32 = jnp.float32
    adj_out, emis_out = pl.pallas_call(
        kernel,
        out_shape=(
            jax.ShapeDtypeStruct(adjoint_in.shape, f32),
            jax.ShapeDtypeStruct((3, n_y, n_x), f32),
        ),
        in_specs=[hbm] * 11,
        out_specs=(hbm, hbm),
        scratch_shapes=[
            pltpu.VMEM(adjoint_in.shape, f32),
            pltpu.VMEM((3, n_y, n_x), f32),
            pltpu.VMEM(land_mask.shape, land_mask.dtype),
            pltpu.VMEM(source_mask.shape, source_mask.dtype),
            pltpu.SMEM(coag_rates.shape, f32),
            pltpu.SMEM(settle_speed.shape, f32),
            pltpu.SMEM(settle_class.shape, settle_class.dtype),
            pltpu.SMEM(emis_profile.shape, f32),
            pltpu.SMEM(emis_coef.shape, f32),
            pltpu.VMEM(trajectory.shape, trajectory.dtype),
            pltpu.VMEM(courant.shape, f32),
            pltpu.VMEM(mixing.shape, f32),
            pltpu.VMEM((steps, n_t, n_z, n_y + 2 * PAD, n_x), f32),
            pltpu.VMEM((steps, n_t, n_z, PAD, n_x), f32),
            pltpu.VMEM((steps, n_x, n_t * rows), f32),
            pltpu.VMEM((steps, n_x, n_t * rows), f32),
            pltpu.VMEM((n_t, n_z, n_y, n_x), f32),
            pltpu.VMEM((steps, n_t, 1, n_y, n_x), f32),
            pltpu.VMEM((3, n_y, n_x), f32),
            pltpu.VMEM((3, n_y, n_x), f32),
            pltpu.VMEM((4, n_z, n_y, n_x), f32),
            pltpu.VMEM((4, n_z, n_y, n_x), f32),
            pltpu.VMEM((3, n_z, n_y, n_x), f32),
            pltpu.VMEM((n_x, rows), f32),
            pltpu.VMEM((n_x, rows), f32),
            pltpu.VMEM((n_z, n_y + 2 * PAD, n_x), f32),
            pltpu.VMEM((1, n_y, n_x), f32),
            pltpu.SemaphoreType.DMA((N_REMOTE,)),
            pltpu.SemaphoreType.DMA((N_REMOTE,)),
            pltpu.SemaphoreType.DMA((10 + steps,)),
        ],
        compiler_params=pltpu.CompilerParams(
            collective_id=0, has_side_effects=True, vmem_limit_bytes=67043328
        ),
    )(
        adjoint_in, trajectory, courant, mixing, land_mask, source_mask,
        coag_rates, settle_speed, settle_class, emis_profile, emis_coef,
    )
    return pl.pallas_call(
        hand_over,
        out_shape=(
            jax.ShapeDtypeStruct(adj_out.shape, f32),
            jax.ShapeDtypeStruct(emis_out.shape, f32),
        ),
        in_specs=[hbm, hbm],
        out_specs=(hbm, hbm),
        scratch_shapes=[
            pltpu.VMEM(adj_out.shape, f32),
            pltpu.VMEM(emis_out.shape, f32),
            pltpu.SemaphoreType.DMA((4,)),
        ],
    )(adj_out, emis_out)


def solution(mesh):
    return jax.shard_map(
        shards,
        mesh=mesh,
        in_specs=(
            P(None, "lev", "lat", "lon"),
            P(None, None, "lev", "lat", "lon"),
            P(None, "lev", "lat", "lon"),
            P("lev", "lat", "lon"),
            P(),
            P(),
            P(),
            P(),
            P(),
            P("lat", "lon"),
            P("lat", "lon"),
        ),
        out_specs=(P(None, "lev", "lat", "lon"), P(None, "lat", "lon")),
        check_vma=False,
    )
```

```python
import jax
import jax.numpy as jnp
from jax import lax
from jax.experimental import pallas as pl
from jax.experimental.pallas import tpu as pltpu
from jax.sharding import PartitionSpec as P

MESH = pl.DeviceIdType.MESH
PAD = 8

S_LEV, S_UP, S_DOWN, S_RIGHT, S_LEFT = 0, 3, 6, 9, 12
S_EMIS, S_CE_R, S_CE_L, S_CN_U, S_CN_D, S_MIX = 15, 16, 17, 18, 19, 20
N_REMOTE = 21


def kernel(
    adj_hbm, traj_hbm, cour_hbm, mix_hbm, land_hbm, srcm_hbm,
    rates_hbm, speed_hbm, sclass_hbm, prof_hbm, ecoef_hbm,
    out_hbm, emis_hbm,
    out_ref, emis_ref, land_ref, srcm_ref, rates_ref, speed_ref, sclass_ref, prof_ref, ecoef_ref,
    traj_ref, cour_ref, mix_ref, pad_ref, lh_ref, at_ref, ht_ref, hb_ref, lv_ref, eo_ref, ep_ref,
    cx_ref, cy_ref, vc_ref, cet_ref, ceh_ref, cyp_ref, mh_ref,
    send_sem, recv_sem, local_sem,
):
    n_t, n_z, n_y, n_x = out_ref.shape
    steps = traj_hbm.shape[0]
    rows = n_z * n_y
    lon = lax.axis_index("lon")
    lat = lax.axis_index("lat")
    lev = lax.axis_index("lev")
    n_lon = lax.axis_size("lon")
    n_lat = lax.axis_size("lat")
    right = lax.rem(lon + 1, n_lon)
    left = lax.rem(lon + n_lon - 1, n_lon)
    has_up = lat < n_lat - 1
    has_down = lat > 0
    up = jnp.minimum(lat + 1, n_lat - 1)
    down = jnp.maximum(lat - 1, 0)
    partner = 1 - lev
    low_half = lev == 0
    edge_z = jnp.where(low_half, n_z - 1, 0)
    inner_z = jnp.where(low_half, n_z - 2, 1)
    level0 = lev * n_z

    adj_in = pltpu.make_async_copy(adj_hbm, out_ref, local_sem.at[0])
    cour_in = pltpu.make_async_copy(cour_hbm, cour_ref, local_sem.at[1])
    mix_in = pltpu.make_async_copy(mix_hbm, mix_ref, local_sem.at[2])
    traj_in = [
        pltpu.make_async_copy(traj_hbm.at[k], traj_ref.at[k], local_sem.at[3 + k]) for k in range(steps)
    ]
    small_in = [
        pltpu.make_async_copy(src, dst, local_sem.at[3 + steps + i])
        for i, (src, dst) in enumerate(
            (
                (rates_hbm, rates_ref),
                (speed_hbm, speed_ref),
                (sclass_hbm, sclass_ref),
                (prof_hbm, prof_ref),
                (ecoef_hbm, ecoef_ref),
                (land_hbm, land_ref),
                (srcm_hbm, srcm_ref),
            )
        )
    ]
    for c in small_in:
        c.start()
    cour_in.start()
    mix_in.start()
    adj_in.start()
    for k in range(steps - 1, -1, -1):
        traj_in[k].start()

    zeros_pad = jnp.zeros((n_t, n_z, PAD, n_x), jnp.float32)
    for k in range(steps):
        pad_ref[k, :, :, 0:PAD, :] = zeros_pad
        pad_ref[k, :, :, PAD + n_y : 2 * PAD + n_y, :] = zeros_pad
        lh_ref[k] = zeros_pad
    zeros_c = jnp.zeros((n_z, PAD, n_x), jnp.float32)
    cyp_ref[:, 0:PAD, :] = zeros_c
    cyp_ref[:, PAD + n_y : 2 * PAD + n_y, :] = zeros_c

    def rcopy(src, dst, idx, dev):
        return pltpu.make_async_remote_copy(
            src, dst, send_sem.at[idx], recv_sem.at[idx], device_id=dev, device_id_type=MESH
        )

    lane = lax.broadcasted_iota(jnp.int32, (n_y, n_x), 1)
    row = lax.broadcasted_iota(jnp.int32, (n_y, n_x), 0)

    cour_in.wait()
    mix_in.wait()
    for c in small_in:
        c.wait()
    top_row = jnp.logical_and(lat == n_lat - 1, row == n_y - 1)
    for z in range(n_z):
        cyp_ref[z, PAD : PAD + n_y, :] = jnp.where(top_row, 0.0, cour_ref[1, z])
    cet_ref[...] = cour_ref[0].reshape(rows, n_x).T
    ce_right = rcopy(cet_ref.at[pl.ds(n_x - 2, 2), :], ceh_ref.at[pl.ds(n_x - 2, 2), :], S_CE_R, (right, lat, lev))
    ce_left = rcopy(cet_ref.at[pl.ds(0, 2), :], ceh_ref.at[pl.ds(0, 2), :], S_CE_L, (left, lat, lev))
    cn_up = rcopy(
        cyp_ref.at[:, pl.ds(PAD + n_y - 2, 2), :], cyp_ref.at[:, pl.ds(PAD - 2, 2), :], S_CN_U, (lon, up, lev)
    )
    cn_down = rcopy(
        cyp_ref.at[:, pl.ds(PAD, 2), :], cyp_ref.at[:, pl.ds(PAD + n_y, 2), :], S_CN_D, (lon, down, lev)
    )
    mix_x = rcopy(mix_ref.at[pl.ds(edge_z, 1)], mh_ref, S_MIX, (lon, lat, partner))

    def start_coefficient_halos():
        mix_x.start()
        ce_right.start()
        ce_left.start()

        @pl.when(has_up)
        def _():
            cn_up.start()

        @pl.when(has_down)
        def _():
            cn_down.start()

    def fix_vertical_coefficients():
        mix_x.wait()
        below = jnp.where(low_half, vc_ref[1, 0], mh_ref[0])
        vc_ref[1, 0] = below
        vc_ref[2, 0] = jnp.where(low_half, vc_ref[2, 0], 1.0 - vc_ref[0, 0] - below)

    def build_vertical_coefficients():
        dep = jnp.where(low_half, 0.1 + 0.3 * land_ref[...].astype(jnp.float32), 0.0)
        below = jnp.zeros((n_y, n_x), jnp.float32)
        for z in range(n_z):
            above = mix_ref[z]
            if z == n_z - 1:
                above = jnp.where(low_half, above, 0.0)
            base = 1.0 - above - below
            if z == 0:
                base = base - dep
            vc_ref[0, z] = above
            vc_ref[1, z] = below
            vc_ref[2, z] = base
            below = above

    def build_transport_coefficients():
        ce_right.wait()
        ce_left.wait()

        @pl.when(has_up)
        def _():
            cn_up.wait_send()
            cn_down.wait_recv()

        @pl.when(has_down)
        def _():
            cn_down.wait_send()
            cn_up.wait_recv()

        he = ceh_ref[...].T.reshape(n_z, n_y, n_x)
        for z in range(n_z):
            c = cour_ref[0, z]
            hz = he[z]
            c_p1 = jnp.where(lane == n_x - 1, pltpu.roll(hz, n_x - 1, 1), pltpu.roll(c, n_x - 1, 1))
            c_m1 = jnp.where(lane == 0, pltpu.roll(hz, 1, 1), pltpu.roll(c, 1, 1))
            c_m2 = jnp.where(lane <= 1, pltpu.roll(hz, 2, 1), pltpu.roll(c, 2, 1))
            cx_ref[0, z] = -1.5 * jnp.maximum(c, 0.0)
            cx_ref[1, z] = 0.5 * jnp.maximum(c_p1, 0.0)
            cx_ref[2, z] = -1.5 * jnp.minimum(c_m1, 0.0)
            cx_ref[3, z] = 0.5 * jnp.minimum(c_m2, 0.0)
            cy_ref[0, z] = -1.5 * jnp.maximum(cyp_ref[z, PAD : PAD + n_y, :], 0.0)
            cy_ref[1, z] = 0.5 * jnp.maximum(cyp_ref[z, PAD + 1 : PAD + 1 + n_y, :], 0.0)
            cy_ref[2, z] = -1.5 * jnp.minimum(cyp_ref[z, PAD - 1 : PAD - 1 + n_y, :], 0.0)
            cy_ref[3, z] = 0.5 * jnp.minimum(cyp_ref[z, PAD - 2 : PAD - 2 + n_y, :], 0.0)

    eo_ref[...] = jnp.zeros(eo_ref.shape, jnp.float32)
    src_mask = srcm_ref[...].astype(jnp.float32)
    adj_in.wait()
    build_vertical_coefficients()
    emis_copy = rcopy(eo_ref, ep_ref, S_EMIS, (lon, lat, partner))

    def lat_fix(k, t, z):
        h = lh_ref[k, t, z, 0:4, :]
        am2 = h[0:1]
        am1 = h[1:2]
        ap1 = h[2:3]
        ap2 = h[3:4]
        c_lo = cy_ref[:, z, 0:2, :]
        c_hi = cy_ref[:, z, n_y - 2 : n_y, :]
        r0 = c_lo[2, 0:1] * am1 + c_lo[3, 0:1] * (am2 - am1)
        r1 = c_lo[3, 1:2] * am1
        r14 = -c_hi[1, 0:1] * ap1
        r15 = c_hi[1, 1:2] * (ap1 - ap2) - c_hi[0, 1:2] * ap1
        out_ref[t, z, 0:2, :] = out_ref[t, z, 0:2, :] + jnp.concatenate([r0, r1], axis=0)
        out_ref[t, z, n_y - 2 : n_y, :] = out_ref[t, z, n_y - 2 : n_y, :] + jnp.concatenate([r14, r15], axis=0)

    for k in range(steps - 1, -1, -1):
        first = k == steps - 1
        traj_in[k].wait()

        def coag_level(zz, acc):
            z = jnp.where(low_half, n_z - 1 - zz, zz)
            zg = level0 + z
            if not first:
                for t in range(n_t):
                    lat_fix(k + 1, t, z)
            lam = [out_ref[t, z] for t in range(n_t)]
            st = [traj_ref[k, t, z].astype(jnp.float32) for t in range(n_t)]
            new_acc = []
            for m in range(3):
                part = acc[m]
                for j in range(3):
                    part = part + (ecoef_ref[3 * m + j] * prof_ref[zg]) * lam[3 * m + j]
                new_acc.append(part)
            k0, k1, k2, k01, k02, k12 = [rates_ref[i, zg] for i in range(6)]
            n0, v0, w0, n1, v1, w1, n2, v2, w2 = st
            ln0, lv0, lw0, ln1, lv1, lw1, ln2, lv2, lw2 = lam
            a01 = k01 * n1
            a02 = k02 * n2
            a12 = k12 * n2
            s0 = a01 + a02
            g_n0 = ln0 * (-2.0 * k0 * n0 - s0)
            g_v0 = (
                (lv1 * a01 + lv2 * a02 - lv0 * s0)
                + 2.0 * (lw0 * (k0 * v0) + lw1 * (k01 * v1) + lw2 * (k02 * v2))
            )
            g_w0 = lw1 * a01 + lw2 * a02 - lw0 * s0
            g_n1 = (
                ln1 * (-2.0 * k1 * n1 - a12)
                - ln0 * (k01 * n0)
                + (lv1 - lv0) * (k01 * v0)
                + (lw1 - lw0) * (k01 * w0)
            )
            g_v1 = (lv2 - lv1) * a12 + 2.0 * (lw1 * (k1 * v1 + k01 * v0) + lw2 * (k12 * v2))
            g_w1 = (lw2 - lw1) * a12
            g_n2 = (
                -2.0 * k2 * n2 * ln2
                - ln0 * (k02 * n0)
                - ln1 * (k12 * n1)
                + (lv2 - lv0) * (k02 * v0)
                + (lv2 - lv1) * (k12 * v1)
                + (lw2 - lw0) * (k02 * w0)
                + (lw2 - lw1) * (k12 * w1)
            )
            g_v2 = 2.0 * lw2 * (k2 * v2 + k02 * v0 + k12 * v1)
            grads = [g_n0, g_v0, g_w0, g_n1, g_v1, g_w1, g_n2, g_v2]
            for t in range(n_t - 1):
                out_ref[t, z] = lam[t] + grads[t]
            return tuple(new_acc)

        zero = jnp.zeros((n_y, n_x), jnp.float32)
        acc = coag_level(0, (zero, zero, zero))
        lev_copy = rcopy(out_ref.at[:, pl.ds(edge_z, 1)], lv_ref.at[k], S_LEV + k, (lon, lat, partner))
        if not first:
            lev_copy.start()
        acc = lax.fori_loop(1, n_z, coag_level, acc)
        for m in range(3):
            eo_ref[m] = eo_ref[m] + acc[m] * src_mask
        if k == 0:
            emis_copy.start()

        def vert_inner(t, carry):
            col = [out_ref[t, z] for z in range(n_z)]
            for z in range(n_z):
                s = speed_ref[sclass_ref[level0 + z], t]
                val = col[z] * (vc_ref[2, z] - s)
                if z > 0:
                    val = val + col[z - 1] * (vc_ref[1, z] + s)
                if z < n_z - 1:
                    val = val + col[z + 1] * vc_ref[0, z]
                pad_ref[k, t, z, PAD : PAD + n_y, :] = val
            return carry

        lax.fori_loop(0, n_t, vert_inner, 0)
        if first:
            barrier = pltpu.get_barrier_semaphore()
            for dev in ((lon, lat, partner), (left, lat, lev), (right, lat, lev)):
                pl.semaphore_signal(barrier, 1, device_id=dev, device_id_type=MESH)

            @pl.when(has_up)
            def _():
                pl.semaphore_signal(barrier, 1, device_id=(lon, up, lev), device_id_type=MESH)

            @pl.when(has_down)
            def _():
                pl.semaphore_signal(barrier, 1, device_id=(lon, down, lev), device_id_type=MESH)

            pl.semaphore_wait(barrier, 3 + has_up.astype(jnp.int32) + has_down.astype(jnp.int32))
            start_coefficient_halos()
            lev_copy.start()
            fix_vertical_coefficients()
        lev_copy.wait()

        lat_up = rcopy(
            pad_ref.at[k, :, :, pl.ds(PAD + n_y - 2, 2), :],
            lh_ref.at[k, :, :, pl.ds(0, 2), :],
            S_UP + k,
            (lon, up, lev),
        )
        lat_down = rcopy(
            pad_ref.at[k, :, :, pl.ds(PAD, 2), :],
            lh_ref.at[k, :, :, pl.ds(2, 2), :],
            S_DOWN + k,
            (lon, down, lev),
        )
        lon_right = rcopy(
            at_ref.at[k, pl.ds(n_x - 2, 2), :], ht_ref.at[k, pl.ds(n_x - 2, 2), :], S_RIGHT + k, (right, lat, lev)
        )
        lon_left = rcopy(
            at_ref.at[k, pl.ds(0, 2), :], ht_ref.at[k, pl.ds(0, 2), :], S_LEFT + k, (left, lat, lev)
        )

        for t in range(n_t):
            z = edge_z
            s = speed_ref[sclass_ref[level0 + z], t]
            a = out_ref[t, z]
            other = out_ref[t, inner_z]
            halo = lv_ref[k, t, 0]
            a_below = jnp.where(low_half, other, halo)
            a_above = jnp.where(low_half, halo, other)
            pad_ref[k, t, z, PAD : PAD + n_y, :] = (
                a * (vc_ref[2, z] - s) + a_below * (vc_ref[1, z] + s) + a_above * vc_ref[0, z]
            )
            up_t = rcopy(
                pad_ref.at[k, t, :, pl.ds(PAD + n_y - 2, 2), :],
                lh_ref.at[k, t, :, pl.ds(0, 2), :],
                S_UP + k,
                (lon, up, lev),
            )
            down_t = rcopy(
                pad_ref.at[k, t, :, pl.ds(PAD, 2), :],
                lh_ref.at[k, t, :, pl.ds(2, 2), :],
                S_DOWN + k,
                (lon, down, lev),
            )

            @pl.when(has_up)
            def _():
                up_t.start()

            @pl.when(has_down)
            def _():
                down_t.start()

        for t in range(n_t):
            blk = pad_ref[k, t, :, PAD : PAD + n_y, :].reshape(rows, n_x)
            cols = pl.ds(t * rows, rows)
            at_ref[k, :, cols] = blk.T
            rcopy(
                at_ref.at[k, pl.ds(n_x - 2, 2), cols], ht_ref.at[k, pl.ds(n_x - 2, 2), cols], S_RIGHT + k,
                (right, lat, lev),
            ).start()
            rcopy(
                at_ref.at[k, pl.ds(0, 2), cols], ht_ref.at[k, pl.ds(0, 2), cols], S_LEFT + k, (left, lat, lev)
            ).start()

        if k == steps - 1:
            build_transport_coefficients()

        def transport(t, carry):
            for z in range(n_z):
                a = pad_ref[k, t, z, PAD : PAD + n_y, :]
                y_p1 = pad_ref[k, t, z, PAD + 1 : PAD + 1 + n_y, :]
                y_p2 = pad_ref[k, t, z, PAD + 2 : PAD + 2 + n_y, :]
                y_m1 = pad_ref[k, t, z, PAD - 1 : PAD - 1 + n_y, :]
                y_m2 = pad_ref[k, t, z, PAD - 2 : PAD - 2 + n_y, :]
                x_p1 = pltpu.roll(a, n_x - 1, 1)
                x_p2 = pltpu.roll(a, n_x - 2, 1)
                x_m1 = pltpu.roll(a, 1, 1)
                x_m2 = pltpu.roll(a, 2, 1)
                lon_part = (
                    cx_ref[0, z] * (a - x_p1)
                    + cx_ref[1, z] * (x_p1 - x_p2)
                    + cx_ref[2, z] * (x_m1 - a)
                    + cx_ref[3, z] * (x_m2 - x_m1)
                )
                lat_part = (
                    cy_ref[0, z] * (a - y_p1)
                    + cy_ref[1, z] * (y_p1 - y_p2)
                    + cy_ref[2, z] * (y_m1 - a)
                    + cy_ref[3, z] * (y_m2 - y_m1)
                )
                out_ref[t, z] = a + lon_part + lat_part
            return carry

        lax.fori_loop(0, n_t, transport, 0)

        lon_right.wait()
        lon_left.wait()

        def lon_edges(t, carry):
            cols = pl.ds(pl.multiple_of(t * rows, rows), rows)
            h_t = ht_ref[k, :, cols].T.reshape(n_z, n_y, n_x)
            for z in range(n_z):
                a = pad_ref[k, t, z, PAD : PAD + n_y, :]
                d = h_t[z] - a
                d_m1 = pltpu.roll(d, 1, 1)
                d_m2 = pltpu.roll(d, 2, 1)
                d_p1 = pltpu.roll(d, n_x - 1, 1)
                d_p2 = pltpu.roll(d, n_x - 2, 1)
                cx0 = cx_ref[0, z]
                cx1 = cx_ref[1, z]
                cxm1 = cx_ref[2, z]
                cxm2 = cx_ref[3, z]
                low = cxm2 * d_m2 + jnp.where(lane == 0, (cxm1 - cxm2) * d_m1, 0.0)
                high = jnp.where(lane == n_x - 1, (cx1 - cx0) * d_p1, 0.0) - cx1 * d_p2
                corr = jnp.where(lane <= 1, low, jnp.where(lane >= n_x - 2, high, 0.0))
                out_ref[t, z] = out_ref[t, z] + corr
            return carry

        lax.fori_loop(0, n_t, lon_edges, 0, unroll=3)

        @pl.when(has_up)
        def _():
            lat_up.wait_send()
            lat_down.wait_recv()

        @pl.when(has_down)
        def _():
            lat_down.wait_send()
            lat_up.wait_recv()

        if k == 0:
            def lat_edges(t, carry):
                for z in range(n_z):
                    lat_fix(k, t, z)
                return carry

            lax.fori_loop(0, n_t, lat_edges, 0)

    emis_copy.wait()
    emis_ref[...] = eo_ref[...] + ep_ref[...]
    out_copy = pltpu.make_async_copy(out_ref, out_hbm, local_sem.at[0])
    emis_out = pltpu.make_async_copy(emis_ref, emis_hbm, local_sem.at[1])
    out_copy.start()
    emis_out.start()
    out_copy.wait()
    emis_out.wait()


def hand_over(adj_hbm, emis_hbm, adj_out, emis_out, adj_buf, emis_buf, sem):
    ins = [
        pltpu.make_async_copy(adj_hbm, adj_buf, sem.at[0]),
        pltpu.make_async_copy(emis_hbm, emis_buf, sem.at[1]),
    ]
    for c in ins:
        c.start()
    outs = [
        pltpu.make_async_copy(adj_buf, adj_out, sem.at[2]),
        pltpu.make_async_copy(emis_buf, emis_out, sem.at[3]),
    ]
    for c, o in zip(ins, outs):
        c.wait()
        o.start()
    for o in outs:
        o.wait()


def shards(
    adjoint_in,
    trajectory,
    courant,
    mixing,
    coag_rates,
    settle_speed,
    settle_class,
    emis_profile,
    emis_coef,
    land_mask,
    source_mask,
):
    n_t, n_z, n_y, n_x = adjoint_in.shape
    steps = trajectory.shape[0]
    rows = n_z * n_y
    hbm = pl.BlockSpec(memory_space=pl.ANY)
    vmem = pl.BlockSpec(memory_space=pltpu.VMEM)
    smem = pl.BlockSpec(memory_space=pltpu.SMEM)
    f32 = jnp.float32
    adj_out, emis_out = pl.pallas_call(
        kernel,
        out_shape=(
            jax.ShapeDtypeStruct(adjoint_in.shape, f32),
            jax.ShapeDtypeStruct((3, n_y, n_x), f32),
        ),
        in_specs=[hbm] * 11,
        out_specs=(hbm, hbm),
        scratch_shapes=[
            pltpu.VMEM(adjoint_in.shape, f32),
            pltpu.VMEM((3, n_y, n_x), f32),
            pltpu.VMEM(land_mask.shape, land_mask.dtype),
            pltpu.VMEM(source_mask.shape, source_mask.dtype),
            pltpu.SMEM(coag_rates.shape, f32),
            pltpu.SMEM(settle_speed.shape, f32),
            pltpu.SMEM(settle_class.shape, settle_class.dtype),
            pltpu.SMEM(emis_profile.shape, f32),
            pltpu.SMEM(emis_coef.shape, f32),
            pltpu.VMEM(trajectory.shape, trajectory.dtype),
            pltpu.VMEM(courant.shape, f32),
            pltpu.VMEM(mixing.shape, f32),
            pltpu.VMEM((steps, n_t, n_z, n_y + 2 * PAD, n_x), f32),
            pltpu.VMEM((steps, n_t, n_z, PAD, n_x), f32),
            pltpu.VMEM((steps, n_x, n_t * rows), f32),
            pltpu.VMEM((steps, n_x, n_t * rows), f32),
            pltpu.VMEM((n_t, n_z, n_y, n_x), f32),
            pltpu.VMEM((steps, n_t, 1, n_y, n_x), f32),
            pltpu.VMEM((3, n_y, n_x), f32),
            pltpu.VMEM((3, n_y, n_x), f32),
            pltpu.VMEM((4, n_z, n_y, n_x), f32),
            pltpu.VMEM((4, n_z, n_y, n_x), f32),
            pltpu.VMEM((3, n_z, n_y, n_x), f32),
            pltpu.VMEM((n_x, rows), f32),
            pltpu.VMEM((n_x, rows), f32),
            pltpu.VMEM((n_z, n_y + 2 * PAD, n_x), f32),
            pltpu.VMEM((1, n_y, n_x), f32),
            pltpu.SemaphoreType.DMA((N_REMOTE,)),
            pltpu.SemaphoreType.DMA((N_REMOTE,)),
            pltpu.SemaphoreType.DMA((10 + steps,)),
        ],
        compiler_params=pltpu.CompilerParams(
            collective_id=0, has_side_effects=True, vmem_limit_bytes=67043328
        ),
    )(
        adjoint_in, trajectory, courant, mixing, land_mask, source_mask,
        coag_rates, settle_speed, settle_class, emis_profile, emis_coef,
    )
    return pl.pallas_call(
        hand_over,
        out_shape=(
            jax.ShapeDtypeStruct(adj_out.shape, f32),
            jax.ShapeDtypeStruct(emis_out.shape, f32),
        ),
        in_specs=[hbm, hbm],
        out_specs=(hbm, hbm),
        scratch_shapes=[
            pltpu.VMEM(adj_out.shape, f32),
            pltpu.VMEM(emis_out.shape, f32),
            pltpu.SemaphoreType.DMA((4,)),
        ],
    )(adj_out, emis_out)


def solution(mesh):
    return jax.shard_map(
        shards,
        mesh=mesh,
        in_specs=(
            P(None, "lev", "lat", "lon"),
            P(None, None, "lev", "lat", "lon"),
            P(None, "lev", "lat", "lon"),
            P("lev", "lat", "lon"),
            P(),
            P(),
            P(),
            P(),
            P(),
            P("lat", "lon"),
            P("lat", "lon"),
        ),
        out_specs=(P(None, "lev", "lat", "lon"), P(None, "lat", "lon")),
        check_vma=False,
    )
```

```python
import jax
import jax.numpy as jnp
from jax import lax
from jax.experimental import pallas as pl
from jax.experimental.pallas import tpu as pltpu
from jax.sharding import PartitionSpec as P

MESH = pl.DeviceIdType.MESH
PAD = 8

S_LEV, S_UP, S_DOWN, S_RIGHT, S_LEFT = 0, 3, 6, 9, 12
S_EMIS, S_CE_R, S_CE_L, S_CN_U, S_CN_D, S_MIX = 15, 16, 17, 18, 19, 20
N_REMOTE = 21


def kernel(
    adj_hbm, traj_hbm, cour_hbm, mix_hbm, land_hbm, srcm_hbm,
    rates_hbm, speed_hbm, sclass_hbm, prof_hbm, ecoef_hbm,
    out_hbm, emis_hbm,
    out_ref, emis_ref, land_ref, srcm_ref, rates_ref, speed_ref, sclass_ref, prof_ref, ecoef_ref,
    traj_ref, cour_ref, mix_ref, pad_ref, lh_ref, at_ref, ht_ref, hb_ref, lv_ref, eo_ref, ep_ref,
    cx_ref, cy_ref, vc_ref, cet_ref, ceh_ref, cyp_ref, mh_ref,
    send_sem, recv_sem, local_sem,
):
    n_t, n_z, n_y, n_x = out_ref.shape
    steps = traj_hbm.shape[0]
    rows = n_z * n_y
    lon = lax.axis_index("lon")
    lat = lax.axis_index("lat")
    lev = lax.axis_index("lev")
    n_lon = lax.axis_size("lon")
    n_lat = lax.axis_size("lat")
    right = lax.rem(lon + 1, n_lon)
    left = lax.rem(lon + n_lon - 1, n_lon)
    has_up = lat < n_lat - 1
    has_down = lat > 0
    up = jnp.minimum(lat + 1, n_lat - 1)
    down = jnp.maximum(lat - 1, 0)
    partner = 1 - lev
    low_half = lev == 0
    edge_z = jnp.where(low_half, n_z - 1, 0)
    inner_z = jnp.where(low_half, n_z - 2, 1)
    level0 = lev * n_z

    adj_in = pltpu.make_async_copy(adj_hbm, out_ref, local_sem.at[0])
    cour_in = pltpu.make_async_copy(cour_hbm, cour_ref, local_sem.at[1])
    mix_in = pltpu.make_async_copy(mix_hbm, mix_ref, local_sem.at[2])
    traj_in = [
        pltpu.make_async_copy(traj_hbm.at[k], traj_ref.at[k], local_sem.at[3 + k]) for k in range(steps)
    ]
    small_in = [
        pltpu.make_async_copy(src, dst, local_sem.at[3 + steps + i])
        for i, (src, dst) in enumerate(
            (
                (rates_hbm, rates_ref),
                (speed_hbm, speed_ref),
                (sclass_hbm, sclass_ref),
                (prof_hbm, prof_ref),
                (ecoef_hbm, ecoef_ref),
                (land_hbm, land_ref),
                (srcm_hbm, srcm_ref),
            )
        )
    ]
    for c in small_in:
        c.start()
    cour_in.start()
    mix_in.start()
    adj_in.start()
    for k in range(steps - 1, -1, -1):
        traj_in[k].start()

    zeros_pad = jnp.zeros((n_t, n_z, PAD, n_x), jnp.float32)
    for k in range(steps):
        pad_ref[k, :, :, 0:PAD, :] = zeros_pad
        pad_ref[k, :, :, PAD + n_y : 2 * PAD + n_y, :] = zeros_pad
        lh_ref[k] = zeros_pad
    zeros_c = jnp.zeros((n_z, PAD, n_x), jnp.float32)
    cyp_ref[:, 0:PAD, :] = zeros_c
    cyp_ref[:, PAD + n_y : 2 * PAD + n_y, :] = zeros_c

    def rcopy(src, dst, idx, dev):
        return pltpu.make_async_remote_copy(
            src, dst, send_sem.at[idx], recv_sem.at[idx], device_id=dev, device_id_type=MESH
        )

    lane = lax.broadcasted_iota(jnp.int32, (n_y, n_x), 1)
    row = lax.broadcasted_iota(jnp.int32, (n_y, n_x), 0)

    cour_in.wait()
    mix_in.wait()
    for c in small_in:
        c.wait()
    top_row = jnp.logical_and(lat == n_lat - 1, row == n_y - 1)
    for z in range(n_z):
        cyp_ref[z, PAD : PAD + n_y, :] = jnp.where(top_row, 0.0, cour_ref[1, z])
    cet_ref[...] = cour_ref[0].reshape(rows, n_x).T
    ce_right = rcopy(cet_ref.at[pl.ds(n_x - 2, 2), :], ceh_ref.at[pl.ds(n_x - 2, 2), :], S_CE_R, (right, lat, lev))
    ce_left = rcopy(cet_ref.at[pl.ds(0, 2), :], ceh_ref.at[pl.ds(0, 2), :], S_CE_L, (left, lat, lev))
    cn_up = rcopy(
        cyp_ref.at[:, pl.ds(PAD + n_y - 2, 2), :], cyp_ref.at[:, pl.ds(PAD - 2, 2), :], S_CN_U, (lon, up, lev)
    )
    cn_down = rcopy(
        cyp_ref.at[:, pl.ds(PAD, 2), :], cyp_ref.at[:, pl.ds(PAD + n_y, 2), :], S_CN_D, (lon, down, lev)
    )
    mix_x = rcopy(mix_ref.at[pl.ds(edge_z, 1)], mh_ref, S_MIX, (lon, lat, partner))

    def start_coefficient_halos():
        mix_x.start()
        ce_right.start()
        ce_left.start()

        @pl.when(has_up)
        def _():
            cn_up.start()

        @pl.when(has_down)
        def _():
            cn_down.start()

    def fix_vertical_coefficients():
        mix_x.wait()
        below = jnp.where(low_half, vc_ref[1, 0], mh_ref[0])
        vc_ref[1, 0] = below
        vc_ref[2, 0] = jnp.where(low_half, vc_ref[2, 0], 1.0 - vc_ref[0, 0] - below)

    def build_vertical_coefficients():
        dep = jnp.where(low_half, 0.1 + 0.3 * land_ref[...].astype(jnp.float32), 0.0)
        below = jnp.zeros((n_y, n_x), jnp.float32)
        for z in range(n_z):
            above = mix_ref[z]
            if z == n_z - 1:
                above = jnp.where(low_half, above, 0.0)
            base = 1.0 - above - below
            if z == 0:
                base = base - dep
            vc_ref[0, z] = above
            vc_ref[1, z] = below
            vc_ref[2, z] = base
            below = above

    def build_transport_coefficients():
        ce_right.wait()
        ce_left.wait()

        @pl.when(has_up)
        def _():
            cn_up.wait_send()
            cn_down.wait_recv()

        @pl.when(has_down)
        def _():
            cn_down.wait_send()
            cn_up.wait_recv()

        he = ceh_ref[...].T.reshape(n_z, n_y, n_x)
        for z in range(n_z):
            c = cour_ref[0, z]
            hz = he[z]
            c_p1 = jnp.where(lane == n_x - 1, pltpu.roll(hz, n_x - 1, 1), pltpu.roll(c, n_x - 1, 1))
            c_m1 = jnp.where(lane == 0, pltpu.roll(hz, 1, 1), pltpu.roll(c, 1, 1))
            c_m2 = jnp.where(lane <= 1, pltpu.roll(hz, 2, 1), pltpu.roll(c, 2, 1))
            cx_ref[0, z] = -1.5 * jnp.maximum(c, 0.0)
            cx_ref[1, z] = 0.5 * jnp.maximum(c_p1, 0.0)
            cx_ref[2, z] = -1.5 * jnp.minimum(c_m1, 0.0)
            cx_ref[3, z] = 0.5 * jnp.minimum(c_m2, 0.0)
            cy_ref[0, z] = -1.5 * jnp.maximum(cyp_ref[z, PAD : PAD + n_y, :], 0.0)
            cy_ref[1, z] = 0.5 * jnp.maximum(cyp_ref[z, PAD + 1 : PAD + 1 + n_y, :], 0.0)
            cy_ref[2, z] = -1.5 * jnp.minimum(cyp_ref[z, PAD - 1 : PAD - 1 + n_y, :], 0.0)
            cy_ref[3, z] = 0.5 * jnp.minimum(cyp_ref[z, PAD - 2 : PAD - 2 + n_y, :], 0.0)

    eo_ref[...] = jnp.zeros(eo_ref.shape, jnp.float32)
    src_mask = srcm_ref[...].astype(jnp.float32)
    adj_in.wait()
    build_vertical_coefficients()
    emis_copy = rcopy(eo_ref, ep_ref, S_EMIS, (lon, lat, partner))

    def lat_fix(k, t, z):
        h = lh_ref[k, t, z, 0:4, :]
        am2 = h[0:1]
        am1 = h[1:2]
        ap1 = h[2:3]
        ap2 = h[3:4]
        c_lo = cy_ref[:, z, 0:2, :]
        c_hi = cy_ref[:, z, n_y - 2 : n_y, :]
        r0 = c_lo[2, 0:1] * am1 + c_lo[3, 0:1] * (am2 - am1)
        r1 = c_lo[3, 1:2] * am1
        r14 = -c_hi[1, 0:1] * ap1
        r15 = c_hi[1, 1:2] * (ap1 - ap2) - c_hi[0, 1:2] * ap1
        out_ref[t, z, 0:2, :] = out_ref[t, z, 0:2, :] + jnp.concatenate([r0, r1], axis=0)
        out_ref[t, z, n_y - 2 : n_y, :] = out_ref[t, z, n_y - 2 : n_y, :] + jnp.concatenate([r14, r15], axis=0)

    for k in range(steps - 1, -1, -1):
        first = k == steps - 1
        traj_in[k].wait()

        def coag_level(zz, acc):
            z = jnp.where(low_half, n_z - 1 - zz, zz)
            zg = level0 + z
            if not first:
                for t in range(n_t):
                    lat_fix(k + 1, t, z)
            lam = [out_ref[t, z] for t in range(n_t)]
            st = [traj_ref[k, t, z].astype(jnp.float32) for t in range(n_t)]
            new_acc = []
            for m in range(3):
                part = acc[m]
                for j in range(3):
                    part = part + (ecoef_ref[3 * m + j] * prof_ref[zg]) * lam[3 * m + j]
                new_acc.append(part)
            k0, k1, k2, k01, k02, k12 = [rates_ref[i, zg] for i in range(6)]
            n0, v0, w0, n1, v1, w1, n2, v2, w2 = st
            ln0, lv0, lw0, ln1, lv1, lw1, ln2, lv2, lw2 = lam
            a01 = k01 * n1
            a02 = k02 * n2
            a12 = k12 * n2
            s0 = a01 + a02
            g_n0 = ln0 * (-2.0 * k0 * n0 - s0)
            g_v0 = (
                (lv1 * a01 + lv2 * a02 - lv0 * s0)
                + 2.0 * (lw0 * (k0 * v0) + lw1 * (k01 * v1) + lw2 * (k02 * v2))
            )
            g_w0 = lw1 * a01 + lw2 * a02 - lw0 * s0
            g_n1 = (
                ln1 * (-2.0 * k1 * n1 - a12)
                - ln0 * (k01 * n0)
                + (lv1 - lv0) * (k01 * v0)
                + (lw1 - lw0) * (k01 * w0)
            )
            g_v1 = (lv2 - lv1) * a12 + 2.0 * (lw1 * (k1 * v1 + k01 * v0) + lw2 * (k12 * v2))
            g_w1 = (lw2 - lw1) * a12
            g_n2 = (
                -2.0 * k2 * n2 * ln2
                - ln0 * (k02 * n0)
                - ln1 * (k12 * n1)
                + (lv2 - lv0) * (k02 * v0)
                + (lv2 - lv1) * (k12 * v1)
                + (lw2 - lw0) * (k02 * w0)
                + (lw2 - lw1) * (k12 * w1)
            )
            g_v2 = 2.0 * lw2 * (k2 * v2 + k02 * v0 + k12 * v1)
            grads = [g_n0, g_v0, g_w0, g_n1, g_v1, g_w1, g_n2, g_v2]
            for t in range(n_t - 1):
                out_ref[t, z] = lam[t] + grads[t]
            return tuple(new_acc)

        zero = jnp.zeros((n_y, n_x), jnp.float32)
        acc = coag_level(0, (zero, zero, zero))
        lev_copy = rcopy(out_ref.at[:, pl.ds(edge_z, 1)], lv_ref.at[k], S_LEV + k, (lon, lat, partner))
        if not first:
            lev_copy.start()
        acc = lax.fori_loop(1, n_z, coag_level, acc)
        for m in range(3):
            eo_ref[m] = eo_ref[m] + acc[m] * src_mask
        if k == 0:
            emis_copy.start()

        def vert_inner(t, carry):
            col = [out_ref[t, z] for z in range(n_z)]
            for z in range(n_z):
                s = speed_ref[sclass_ref[level0 + z], t]
                val = col[z] * (vc_ref[2, z] - s)
                if z > 0:
                    val = val + col[z - 1] * (vc_ref[1, z] + s)
                if z < n_z - 1:
                    val = val + col[z + 1] * vc_ref[0, z]
                pad_ref[k, t, z, PAD : PAD + n_y, :] = val
            return carry

        lax.fori_loop(0, n_t, vert_inner, 0)
        if first:
            barrier = pltpu.get_barrier_semaphore()
            for dev in ((lon, lat, partner), (left, lat, lev), (right, lat, lev)):
                pl.semaphore_signal(barrier, 1, device_id=dev, device_id_type=MESH)

            @pl.when(has_up)
            def _():
                pl.semaphore_signal(barrier, 1, device_id=(lon, up, lev), device_id_type=MESH)

            @pl.when(has_down)
            def _():
                pl.semaphore_signal(barrier, 1, device_id=(lon, down, lev), device_id_type=MESH)

            pl.semaphore_wait(barrier, 3 + has_up.astype(jnp.int32) + has_down.astype(jnp.int32))
            start_coefficient_halos()
            lev_copy.start()
            fix_vertical_coefficients()
        lev_copy.wait()

        lat_up = rcopy(
            pad_ref.at[k, :, :, pl.ds(PAD + n_y - 2, 2), :],
            lh_ref.at[k, :, :, pl.ds(0, 2), :],
            S_UP + k,
            (lon, up, lev),
        )
        lat_down = rcopy(
            pad_ref.at[k, :, :, pl.ds(PAD, 2), :],
            lh_ref.at[k, :, :, pl.ds(2, 2), :],
            S_DOWN + k,
            (lon, down, lev),
        )
        lon_right = rcopy(
            at_ref.at[k, pl.ds(n_x - 2, 2), :], ht_ref.at[k, pl.ds(n_x - 2, 2), :], S_RIGHT + k, (right, lat, lev)
        )
        lon_left = rcopy(
            at_ref.at[k, pl.ds(0, 2), :], ht_ref.at[k, pl.ds(0, 2), :], S_LEFT + k, (left, lat, lev)
        )

        for t in range(n_t):
            z = edge_z
            s = speed_ref[sclass_ref[level0 + z], t]
            a = out_ref[t, z]
            other = out_ref[t, inner_z]
            halo = lv_ref[k, t, 0]
            a_below = jnp.where(low_half, other, halo)
            a_above = jnp.where(low_half, halo, other)
            pad_ref[k, t, z, PAD : PAD + n_y, :] = (
                a * (vc_ref[2, z] - s) + a_below * (vc_ref[1, z] + s) + a_above * vc_ref[0, z]
            )
            up_t = rcopy(
                pad_ref.at[k, t, :, pl.ds(PAD + n_y - 2, 2), :],
                lh_ref.at[k, t, :, pl.ds(0, 2), :],
                S_UP + k,
                (lon, up, lev),
            )
            down_t = rcopy(
                pad_ref.at[k, t, :, pl.ds(PAD, 2), :],
                lh_ref.at[k, t, :, pl.ds(2, 2), :],
                S_DOWN + k,
                (lon, down, lev),
            )

            @pl.when(has_up)
            def _():
                up_t.start()

            @pl.when(has_down)
            def _():
                down_t.start()

        for t in range(n_t):
            blk = pad_ref[k, t, :, PAD : PAD + n_y, :].reshape(rows, n_x)
            cols = pl.ds(t * rows, rows)
            at_ref[k, :, cols] = blk.T
            rcopy(
                at_ref.at[k, pl.ds(n_x - 2, 2), cols], ht_ref.at[k, pl.ds(n_x - 2, 2), cols], S_RIGHT + k,
                (right, lat, lev),
            ).start()
            rcopy(
                at_ref.at[k, pl.ds(0, 2), cols], ht_ref.at[k, pl.ds(0, 2), cols], S_LEFT + k, (left, lat, lev)
            ).start()

        if k == steps - 1:
            build_transport_coefficients()

        def transport(t, carry):
            for z in range(n_z):
                a = pad_ref[k, t, z, PAD : PAD + n_y, :]
                y_p1 = pad_ref[k, t, z, PAD + 1 : PAD + 1 + n_y, :]
                y_p2 = pad_ref[k, t, z, PAD + 2 : PAD + 2 + n_y, :]
                y_m1 = pad_ref[k, t, z, PAD - 1 : PAD - 1 + n_y, :]
                y_m2 = pad_ref[k, t, z, PAD - 2 : PAD - 2 + n_y, :]
                x_p1 = pltpu.roll(a, n_x - 1, 1)
                x_p2 = pltpu.roll(a, n_x - 2, 1)
                x_m1 = pltpu.roll(a, 1, 1)
                x_m2 = pltpu.roll(a, 2, 1)
                lon_part = (
                    cx_ref[0, z] * (a - x_p1)
                    + cx_ref[1, z] * (x_p1 - x_p2)
                    + cx_ref[2, z] * (x_m1 - a)
                    + cx_ref[3, z] * (x_m2 - x_m1)
                )
                lat_part = (
                    cy_ref[0, z] * (a - y_p1)
                    + cy_ref[1, z] * (y_p1 - y_p2)
                    + cy_ref[2, z] * (y_m1 - a)
                    + cy_ref[3, z] * (y_m2 - y_m1)
                )
                out_ref[t, z] = a + lon_part + lat_part
            return carry

        lax.fori_loop(0, n_t, transport, 0, unroll=3)

        lon_right.wait()
        lon_left.wait()

        def lon_edges(t, carry):
            cols = pl.ds(pl.multiple_of(t * rows, rows), rows)
            h_t = ht_ref[k, :, cols].T.reshape(n_z, n_y, n_x)
            for z in range(n_z):
                a = pad_ref[k, t, z, PAD : PAD + n_y, :]
                d = h_t[z] - a
                d_m1 = pltpu.roll(d, 1, 1)
                d_m2 = pltpu.roll(d, 2, 1)
                d_p1 = pltpu.roll(d, n_x - 1, 1)
                d_p2 = pltpu.roll(d, n_x - 2, 1)
                cx0 = cx_ref[0, z]
                cx1 = cx_ref[1, z]
                cxm1 = cx_ref[2, z]
                cxm2 = cx_ref[3, z]
                low = cxm2 * d_m2 + jnp.where(lane == 0, (cxm1 - cxm2) * d_m1, 0.0)
                high = jnp.where(lane == n_x - 1, (cx1 - cx0) * d_p1, 0.0) - cx1 * d_p2
                corr = jnp.where(lane <= 1, low, jnp.where(lane >= n_x - 2, high, 0.0))
                out_ref[t, z] = out_ref[t, z] + corr
            return carry

        lax.fori_loop(0, n_t, lon_edges, 0, unroll=3)

        @pl.when(has_up)
        def _():
            lat_up.wait_send()
            lat_down.wait_recv()

        @pl.when(has_down)
        def _():
            lat_down.wait_send()
            lat_up.wait_recv()

        if k == 0:
            def lat_edges(t, carry):
                for z in range(n_z):
                    lat_fix(k, t, z)
                return carry

            lax.fori_loop(0, n_t, lat_edges, 0)

    emis_copy.wait()
    emis_ref[...] = eo_ref[...] + ep_ref[...]
    out_copy = pltpu.make_async_copy(out_ref, out_hbm, local_sem.at[0])
    emis_out = pltpu.make_async_copy(emis_ref, emis_hbm, local_sem.at[1])
    out_copy.start()
    emis_out.start()
    out_copy.wait()
    emis_out.wait()


def hand_over(adj_hbm, emis_hbm, adj_out, emis_out, adj_buf, emis_buf, sem):
    ins = [
        pltpu.make_async_copy(adj_hbm, adj_buf, sem.at[0]),
        pltpu.make_async_copy(emis_hbm, emis_buf, sem.at[1]),
    ]
    for c in ins:
        c.start()
    outs = [
        pltpu.make_async_copy(adj_buf, adj_out, sem.at[2]),
        pltpu.make_async_copy(emis_buf, emis_out, sem.at[3]),
    ]
    for c, o in zip(ins, outs):
        c.wait()
        o.start()
    for o in outs:
        o.wait()


def shards(
    adjoint_in,
    trajectory,
    courant,
    mixing,
    coag_rates,
    settle_speed,
    settle_class,
    emis_profile,
    emis_coef,
    land_mask,
    source_mask,
):
    n_t, n_z, n_y, n_x = adjoint_in.shape
    steps = trajectory.shape[0]
    rows = n_z * n_y
    hbm = pl.BlockSpec(memory_space=pl.ANY)
    vmem = pl.BlockSpec(memory_space=pltpu.VMEM)
    smem = pl.BlockSpec(memory_space=pltpu.SMEM)
    f32 = jnp.float32
    adj_out, emis_out = pl.pallas_call(
        kernel,
        out_shape=(
            jax.ShapeDtypeStruct(adjoint_in.shape, f32),
            jax.ShapeDtypeStruct((3, n_y, n_x), f32),
        ),
        in_specs=[hbm] * 11,
        out_specs=(hbm, hbm),
        scratch_shapes=[
            pltpu.VMEM(adjoint_in.shape, f32),
            pltpu.VMEM((3, n_y, n_x), f32),
            pltpu.VMEM(land_mask.shape, land_mask.dtype),
            pltpu.VMEM(source_mask.shape, source_mask.dtype),
            pltpu.SMEM(coag_rates.shape, f32),
            pltpu.SMEM(settle_speed.shape, f32),
            pltpu.SMEM(settle_class.shape, settle_class.dtype),
            pltpu.SMEM(emis_profile.shape, f32),
            pltpu.SMEM(emis_coef.shape, f32),
            pltpu.VMEM(trajectory.shape, trajectory.dtype),
            pltpu.VMEM(courant.shape, f32),
            pltpu.VMEM(mixing.shape, f32),
            pltpu.VMEM((steps, n_t, n_z, n_y + 2 * PAD, n_x), f32),
            pltpu.VMEM((steps, n_t, n_z, PAD, n_x), f32),
            pltpu.VMEM((steps, n_x, n_t * rows), f32),
            pltpu.VMEM((steps, n_x, n_t * rows), f32),
            pltpu.VMEM((n_t, n_z, n_y, n_x), f32),
            pltpu.VMEM((steps, n_t, 1, n_y, n_x), f32),
            pltpu.VMEM((3, n_y, n_x), f32),
            pltpu.VMEM((3, n_y, n_x), f32),
            pltpu.VMEM((4, n_z, n_y, n_x), f32),
            pltpu.VMEM((4, n_z, n_y, n_x), f32),
            pltpu.VMEM((3, n_z, n_y, n_x), f32),
            pltpu.VMEM((n_x, rows), f32),
            pltpu.VMEM((n_x, rows), f32),
            pltpu.VMEM((n_z, n_y + 2 * PAD, n_x), f32),
            pltpu.VMEM((1, n_y, n_x), f32),
            pltpu.SemaphoreType.DMA((N_REMOTE,)),
            pltpu.SemaphoreType.DMA((N_REMOTE,)),
            pltpu.SemaphoreType.DMA((10 + steps,)),
        ],
        compiler_params=pltpu.CompilerParams(
            collective_id=0, has_side_effects=True, vmem_limit_bytes=67043328
        ),
    )(
        adjoint_in, trajectory, courant, mixing, land_mask, source_mask,
        coag_rates, settle_speed, settle_class, emis_profile, emis_coef,
    )
    return pl.pallas_call(
        hand_over,
        out_shape=(
            jax.ShapeDtypeStruct(adj_out.shape, f32),
            jax.ShapeDtypeStruct(emis_out.shape, f32),
        ),
        in_specs=[hbm, hbm],
        out_specs=(hbm, hbm),
        scratch_shapes=[
            pltpu.VMEM(adj_out.shape, f32),
            pltpu.VMEM(emis_out.shape, f32),
            pltpu.SemaphoreType.DMA((4,)),
        ],
    )(adj_out, emis_out)


def solution(mesh):
    return jax.shard_map(
        shards,
        mesh=mesh,
        in_specs=(
            P(None, "lev", "lat", "lon"),
            P(None, None, "lev", "lat", "lon"),
            P(None, "lev", "lat", "lon"),
            P("lev", "lat", "lon"),
            P(),
            P(),
            P(),
            P(),
            P(),
            P("lat", "lon"),
            P("lat", "lon"),
        ),
        out_specs=(P(None, "lev", "lat", "lon"), P(None, "lat", "lon")),
        check_vma=False,
    )
```
